32 devices in a mesh: dp: 4 (over z), row: 4 (over x, core), col: 2 (over y).
Axes of the slice: x: 2, y: 2, z: 4, core: 2. Of those that a mesh axis runs over, the one named last changes fastest.
Arguments:
- tokens: bfloat16 [4096, 1024], P(('dp', 'col'), 'row'), may hold values from -6 to 6
- cotangent: bfloat16 [4096, 1024], P(('dp', 'col'), 'row'), may hold values from -6 to 6
- seg_ids: int32 [4, 1024], P('dp'), may hold values from 0 to 6, never falling along the last dimension, each value on 1 to 256 neighbouring positions
- norm_one: float32 [1024], P('row'), may hold values from 0.1 to 1.9
- wq: bfloat16 [1024, 1024], P('row', 'col'), may hold values from -0.1875 to 0.1875
- wk: bfloat16 [1024, 1024], P('row', 'col'), may hold values from -0.1875 to 0.1875
- wv: bfloat16 [1024, 1024], P('row', 'col'), may hold values from -0.1875 to 0.1875
- wo: bfloat16 [1024, 1024], P('col', 'row'), may hold values from -2 to 2
- norm_two: float32 [1024], P('row'), may hold values from 0.1 to 1.9
- w_gate: bfloat16 [1024, 2816], P('row', 'col'), may hold values from -0.1875 to 0.1875
- w_up: bfloat16 [1024, 2816], P('row', 'col'), may hold values from -0.1875 to 0.1875
- w_down: bfloat16 [2816, 1024], P('col', 'row'), may hold values from -0.109375 to 0.109375
Outputs:
- output: bfloat16 [4096, 1024], P(('dp', 'col'), 'row')
- grad_input: float32 [4096, 1024], P(('dp', 'col'), 'row')
- grad_norm_one: float32 [1024], P('row')
- grad_wq: float32 [1024, 1024], P('row', 'col')
- grad_wk: float32 [1024, 1024], P('row', 'col')
- grad_wv: float32 [1024, 1024], P('row', 'col')
- grad_wo: float32 [1024, 1024], P('col', 'row')
- grad_norm_two: float32 [1024], P('row')
- grad_gate: float32 [1024, 2816], P('row', 'col')
- grad_up: float32 [1024, 2816], P('row', 'col')
- grad_down: float32 [2816, 1024], P('col', 'row')
The draws below stay inside these ranges and needn't reach their ends.
Inputs may be any that keep to these rules, and one draw needn't show every extreme that they name: Along each row of seg_ids the ids start at 0 and never fall; each sequence covers 1 to 256 positions and one covers exactly 256.
All inputs are finite; a program needn't handle non-finite values.
Results may differ from the reference program's by a relative error of at most 0.04.
Values may be sent and summed in bfloat16 or wider, within the bound.
A program may use at most 128 MiB of HBM per device.

```python
import math
import jax
import jax.numpy as jnp
import numpy as np
from jax import lax

D = 1024
HEADS = 16
HEAD_DIM = 64
FF = 2816
GROUPS = 4
GROUP_TOK = 1024
TOKENS = 4096
SEQ_MOST = 256
SEGS = 7
QUERY_BLOCK = 256


def levels(rng, shape, split, least, top_value):
    def one(dim, blocks):
        draws = jax.random.uniform(jax.random.fold_in(jax.random.fold_in(rng, 6), dim), (blocks,), jnp.float32, least / len(split), top_value / len(split))
        return jnp.repeat(jnp.exp(draws), shape[dim] // blocks).reshape((-1,) + (1,) * (len(shape) - dim - 1))

    factor_of = one(*split[0])
    for cut in split[1:]:
        factor_of = factor_of * one(*cut)
    return factor_of


def profile(amount, total, limit, skew):
    weights = [(1 << 20) // math.isqrt(rank ** skew) + 1 for rank in range(2, amount + 1)]
    rest, counts = total - limit - (amount - 1), [1] * (amount - 1)
    while rest > 0:
        candidates = [i for i in range(amount - 1) if counts[i] < limit]
        whole, left = sum([weights[i] for i in candidates]), rest
        for i in candidates:
            more = min(limit - counts[i], max(1, left * weights[i] // whole), rest)
            counts[i] = counts[i] + more
            rest = rest - more
    return np.array([limit] + counts)


def uneven_parts(rng, count, total, reach, lean):
    if count == 2:
        one = jax.random.randint(rng, (), max(1, total - reach), min(reach, total - 1) + 1)
        return jnp.stack([one, total - one])
    sizes = jnp.asarray(profile(count, total, reach, lean), jnp.int32)
    couples = (count - 1) // 2
    giver, receiver = sizes[1:1 + 2 * couples:2], sizes[2:2 + 2 * couples:2]
    margin = jnp.minimum(giver - 1, reach - receiver)
    passed = jax.random.randint(jax.random.fold_in(rng, 1), (couples,), 0, 1 << 20) % (margin + 1)
    sizes = sizes.at[1:1 + 2 * couples:2].set(giver - passed).at[2:2 + 2 * couples:2].set(receiver + passed)
    return sizes[jax.random.permutation(jax.random.fold_in(rng, 2), count)]


def noise(own_key, shape, width, bound, shards=(), kind=jnp.bfloat16):
    array = width * jax.random.normal(own_key, shape, jnp.float32)
    if shards:
        array = array * levels(own_key, shape, shards, -0.22, 0.18)
    return jnp.clip(array, -bound, bound).astype(kind)


def setup_inputs(seed: int = 0) -> dict:
    streams_of = jax.random.split(jax.random.key(seed), 13)
    return {
        "tokens": noise(streams_of[0], (TOKENS, D), 1.0, 6.0, ((0, 8), (1, 4))),
        "cotangent": noise(streams_of[1], (TOKENS, D), 1.0, 6.0, ((0, 8), (1, 4))),
        "seg_ids": jax.vmap(lambda own: jnp.searchsorted(jnp.cumsum(uneven_parts(own, SEGS, GROUP_TOK, SEQ_MOST, 1)), jnp.arange(GROUP_TOK), side="right"))(jax.random.split(streams_of[2], GROUPS)).reshape((GROUPS, GROUP_TOK)).astype(jnp.int32),
        "norm_one": jnp.clip(1.0 + 0.18 * jax.random.normal(streams_of[3], (D,), jnp.float32), 0.1, 1.9),
        "wq": noise(streams_of[4], (D, D), D ** -0.5, 0.1875, ((0, 4), (1, 2))),
        "wk": noise(streams_of[5], (D, D), D ** -0.5, 0.1875, ((0, 4), (1, 2))),
        "wv": noise(streams_of[6], (D, D), D ** -0.5, 0.1875, ((0, 4), (1, 2))),
        "wo": noise(streams_of[7], (D, D), (max(D // 128, 1)) ** -0.5, 2.0, ((0, 2), (1, 4))),
        "norm_two": jnp.clip(1.0 + 0.18 * jax.random.normal(streams_of[8], (D,), jnp.float32), 0.1, 1.9),
        "w_gate": noise(streams_of[9], (D, FF), D ** -0.5, 0.1875, ((0, 4), (1, 2))),
        "w_up": noise(streams_of[10], (D, FF), D ** -0.5, 0.1875, ((0, 4), (1, 2))),
        "w_down": noise(streams_of[11], (FF, D), FF ** -0.5, 0.109375, ((0, 2), (1, 4))),
    }


EPSILON = 1e-05
NEGATIVE = -1e+30

@jax.custom_vjp
def low(v):
    return lax.optimization_barrier(v.astype(jnp.bfloat16)).astype(jnp.float32)

@jax.custom_vjp
def low_back(v):
    return v

def low_keep(v):
    return (low(v), None)

def low_pass(kept, grad):
    return (grad,)

def back_keep(v):
    return (v, None)

def back_low(kept, grad):
    return (low(grad),)
low.defvjp(low_keep, low_pass)
low_back.defvjp(back_keep, back_low)

def product(first_op, second_op):
    return jnp.dot(first_op, second_op, precision=lax.Precision.HIGHEST)

def normalize(array_in, gain):
    return array_in * lax.rsqrt(lax.optimization_barrier(jnp.mean(array_in * array_in, axis=-1, keepdims=True)) + EPSILON) * gain

def attention(queries, keys, values, seg_ids):
    zero_rows = jnp.zeros((GROUPS, SEQ_MOST, D), jnp.float32)
    keys_pad = jnp.concatenate([zero_rows, keys], axis=1)
    values_pad = jnp.concatenate([zero_rows, values], axis=1)
    ids_pad = jnp.concatenate([jnp.full((GROUPS, SEQ_MOST), -1, jnp.int32), seg_ids.astype(jnp.int32)], axis=1)
    per_group = GROUP_TOK // QUERY_BLOCK
    window = SEQ_MOST + QUERY_BLOCK
    inv_root = HEAD_DIM ** (-0.5)
    anchor = jnp.zeros((), jnp.int32)

    def one_block(block_index):
        group_index = (block_index // per_group).astype(jnp.int32)
        offset = (block_index % per_group * QUERY_BLOCK).astype(jnp.int32)
        q_blk = lax.dynamic_slice(queries, (group_index, offset, anchor), (1, QUERY_BLOCK, D))[0]
        k_blk = lax.dynamic_slice(keys_pad, (group_index, offset, anchor), (1, window, D))[0]
        v_blk = lax.dynamic_slice(values_pad, (group_index, offset, anchor), (1, window, D))[0]
        q_blk = q_blk.reshape(QUERY_BLOCK, HEADS, HEAD_DIM)
        k_blk = k_blk.reshape(window, HEADS, HEAD_DIM)
        v_blk = v_blk.reshape(window, HEADS, HEAD_DIM)
        q_ids = lax.dynamic_slice(ids_pad, (group_index, offset + SEQ_MOST), (1, QUERY_BLOCK))[0]
        k_ids = lax.dynamic_slice(ids_pad, (group_index, offset), (1, window))[0]
        q_pos = lax.iota(jnp.int32, QUERY_BLOCK)
        k_pos = lax.iota(jnp.int32, window) - SEQ_MOST
        allowed = (q_ids[:, None] == k_ids[None, :]) & (k_pos[None, :] <= q_pos[:, None])
        scores = low_back(jnp.einsum('qhd,khd->hqk', q_blk, k_blk, precision=lax.Precision.HIGHEST) * inv_root)
        scores = jnp.where(allowed[None], scores, NEGATIVE)
        row_max = lax.optimization_barrier(jnp.max(scores, axis=2, keepdims=True))
        expo = jnp.exp(scores - row_max)
        prob_full = expo / lax.optimization_barrier(jnp.sum(expo, axis=2, keepdims=True))
        mixed_out = jnp.einsum('hqk,khd->qhd', low(prob_full), v_blk, precision=lax.Precision.HIGHEST)
        return mixed_out.reshape(QUERY_BLOCK, D)
    blocks = lax.map(jax.checkpoint(one_block), lax.iota(jnp.int32, GROUPS * per_group))
    return blocks.reshape(GROUPS, GROUP_TOK, D)

def forward_layer(token_vals, norm_one, wq, wk, wv, wo, norm_two, w_gate, w_up, w_down, seg_ids):
    normed = low(normalize(token_vals, norm_one))
    queries = low(low_back(product(normed, wq)))
    keys = low(low_back(product(normed, wk)))
    values = low(low_back(product(normed, wv)))
    group_shape = (GROUPS, GROUP_TOK, D)
    mixed_out = attention(queries.reshape(group_shape), keys.reshape(group_shape), values.reshape(group_shape), seg_ids)
    attn_out = low(low_back(mixed_out.reshape(TOKENS, D)))
    residual = token_vals + low_back(product(attn_out, wo))
    hidden_in = low(normalize(residual, norm_two))
    gate_pre = low_back(product(hidden_in, w_gate))
    up_pre = low_back(product(hidden_in, w_up))
    act_low = low(jax.nn.silu(gate_pre) * up_pre)
    return residual + product(act_low, w_down)

def reference(tokens, cotangent, seg_ids, norm_one, wq, wk, wv, wo, norm_two, w_gate, w_up, w_down):
    floats = tuple((item.astype(jnp.float32) for item in (tokens, norm_one, wq, wk, wv, wo, norm_two, w_gate, w_up, w_down)))

    def layer_of(token_vals, gain_one, query_w, key_w, value_w, out_w, gain_two, gate_w, up_w, down_w):
        return forward_layer(token_vals, gain_one, query_w, key_w, value_w, out_w, gain_two, gate_w, up_w, down_w, seg_ids)
    result, pullback = jax.vjp(layer_of, *floats)
    gradients = pullback(cotangent.astype(jnp.float32))
    return (result.astype(jnp.bfloat16), gradients[0], gradients[1], gradients[2], gradients[3], gradients[4], gradients[5], gradients[6], gradients[7], gradients[8], gradients[9])
```

```python
import functools

import jax
import jax.numpy as jnp
from jax import lax
from jax.experimental import pallas as pl
from jax.experimental.pallas import tpu as pltpu
from jax.sharding import PartitionSpec as P

D = 1024
HEAD_DIM = 64


EPSILON = 1e-05
NEGATIVE = -1e30


def for_sending(array):

    def short(part):
        return part.astype(jnp.bfloat16) if part.dtype == jnp.float32 else part

    return jax.tree.map(short, array)


def shifted(block, axis, distance):
    devices = range(lax.axis_size(axis))
    route = [(i - distance, i) for i in devices if i - distance in devices]
    return lax.ppermute(block, axis, route)


def matmul(first_op, second_op):
    return jnp.dot(first_op, second_op, preferred_element_type=jnp.float32)


def matmul_tn(first_op, second_op):
    return lax.dot_general(
        first_op, second_op, (((0,), (0,)), ((), ())), preferred_element_type=jnp.float32
    )


def matmul_nt(first_op, second_op):
    return lax.dot_general(
        first_op, second_op, (((1,), (1,)), ((), ())), preferred_element_type=jnp.float32
    )


def tokens_col(array_in):
    return lax.all_gather(array_in, "col", axis=0, tiled=True)


def tokens_row(array_in):
    return lax.all_gather(for_sending(array_in), "row", axis=0, tiled=True).astype(array_in.dtype)


def summed_row(array_in):
    return lax.psum_scatter(
        array_in.astype(jnp.bfloat16), "row", scatter_dimension=0, tiled=True
    ).astype(jnp.float32)


def summed_col(array_in):
    return lax.psum_scatter(
        array_in.astype(jnp.bfloat16), "col", scatter_dimension=0, tiled=True
    ).astype(jnp.float32)


def feature_total(array_in):
    return lax.psum(array_in, "row")


def window_parts(queries, keys_all, ids_ext, offset, head_cols):
    t_local = queries.shape[0]
    block_rows = min(512, t_local)
    key_reach = min(2048, t_local)
    window = key_reach + block_rows
    head_count = head_cols // HEAD_DIM
    anchor = offset + t_local - key_reach
    q_blk = lax.dynamic_slice_in_dim(queries, offset, block_rows, 0).reshape(
        block_rows, head_count, HEAD_DIM
    )
    k_win = lax.dynamic_slice_in_dim(keys_all, anchor, window, 0)
    k_blk = k_win[:, :head_cols].reshape(window, head_count, HEAD_DIM)
    v_blk = k_win[:, head_cols:].reshape(window, head_count, HEAD_DIM)
    q_ids = lax.dynamic_slice_in_dim(ids_ext, offset + t_local, block_rows, 0)
    k_ids = lax.dynamic_slice_in_dim(ids_ext, anchor, window, 0)
    q_pos = offset + lax.iota(jnp.int32, block_rows)
    k_pos = offset - key_reach + lax.iota(jnp.int32, window)
    allowed = (q_ids[:, None] == k_ids[None, :]) & (k_pos[None, :] <= q_pos[:, None])
    scores = jnp.einsum(
        "qhd,khd->hqk", q_blk, k_blk, preferred_element_type=jnp.float32
    ) * HEAD_DIM ** (-0.5)
    scores = jnp.where(allowed[None], scores, NEGATIVE)
    return (q_blk, k_blk, v_blk, scores)


def forward(tokens, seg_ids, norm_one, wq, wk, wv, wo, norm_two, w_gate, w_up, w_down):
    token_vals = tokens.astype(jnp.float32)
    scale_one = lax.rsqrt(feature_total(jnp.sum(token_vals * token_vals, axis=1)) / D + EPSILON)
    normed = (token_vals * scale_one[:, None] * norm_one).astype(jnp.bfloat16)
    normed_all = tokens_col(normed)
    w_qkv = jnp.concatenate([wq, wk, wv], axis=1)
    head_cols = wq.shape[1]
    qkv = summed_row(matmul(normed_all, w_qkv)).astype(jnp.bfloat16)
    queries = qkv[:, :head_cols]
    kv_local = qkv[:, head_cols:]
    prior_keys = shifted(kv_local, "row", 1)
    keys_all = jnp.concatenate([prior_keys, kv_local], axis=0)
    t_local = queries.shape[0]
    block_rows = min(512, t_local)
    padded_ids = jnp.concatenate([jnp.full((t_local,), -1, jnp.int32), seg_ids[0]])
    ids_ext = lax.dynamic_slice_in_dim(padded_ids, lax.axis_index("row") * t_local, 2 * t_local, 0)

    def attend(offset):
        q_blk, k_blk, v_blk, scores = window_parts(queries, keys_all, ids_ext, offset, head_cols)
        row_max = jnp.max(scores, axis=2, keepdims=True)
        exp_total = jnp.sum(jnp.exp(scores - row_max), axis=2, keepdims=True)
        log_total = row_max + jnp.log(exp_total)
        prob_low = jnp.exp(scores - log_total).astype(jnp.bfloat16)
        mixed_out = jnp.einsum("hqk,khd->qhd", prob_low, v_blk, preferred_element_type=jnp.float32)
        return (mixed_out.reshape(block_rows, head_cols).astype(jnp.bfloat16), log_total[:, :, 0])

    offsets = lax.iota(jnp.int32, t_local // block_rows) * block_rows
    pieces, log_totals = lax.map(attend, offsets)
    attn_out = pieces.reshape(t_local, head_cols)
    attn_all = tokens_row(attn_out)
    residual = token_vals + summed_col(matmul(attn_all, wo))
    stored = {
        "token_vals": token_vals,
        "scale_one": scale_one,
        "normed_all": normed_all,
        "queries": queries,
        "keys_all": keys_all,
        "ids_ext": ids_ext,
        "log_totals": log_totals,
        "attn_all": attn_all,
        "offsets": offsets,
    }
    f_col = w_gate.shape[1]
    scale_two = lax.rsqrt(feature_total(jnp.sum(residual * residual, axis=1)) / D + EPSILON)
    hidden_in = (residual * scale_two[:, None] * norm_two).astype(jnp.bfloat16)
    hidden_all = tokens_col(hidden_in)
    w_pair = jnp.concatenate([w_gate, w_up], axis=1)
    pair_sum = summed_row(matmul(hidden_all, w_pair))
    gate_pre = pair_sum[:, :f_col]
    up_pre = pair_sum[:, f_col:]
    act_low = (jax.nn.silu(gate_pre) * up_pre).astype(jnp.bfloat16)
    act_all = tokens_row(act_low)
    final_sum = residual + summed_col(matmul(act_all, w_down))
    stored.update(
        {
            "residual": residual,
            "scale_two": scale_two,
            "hidden_all": hidden_all,
            "gate_pre": gate_pre,
            "up_pre": up_pre,
            "act_all": act_all,
        }
    )
    return (final_sum.astype(jnp.bfloat16), stored)


def swiglu_grads(dact, gate_pre, up_pre):
    sigmoid_gate = jax.nn.sigmoid(gate_pre)
    gate_grad = (dact * up_pre * sigmoid_gate * (1.0 + gate_pre * (1.0 - sigmoid_gate))).astype(
        jnp.bfloat16
    )
    up_grad = (dact * gate_pre * sigmoid_gate).astype(jnp.bfloat16)
    return (gate_grad, up_grad)


def per_device(
    tokens, cotangent, seg_ids, norm_one, wq, wk, wv, wo, norm_two, w_gate, w_up, w_down
):
    weights = (tokens, seg_ids, norm_one, wq, wk, wv, wo, norm_two, w_gate, w_up, w_down)
    output, stored = forward(*weights)
    f_col = w_gate.shape[1]
    grad_out = cotangent.astype(jnp.float32)
    grad_all = tokens_col(cotangent)
    dact = summed_row(matmul_nt(grad_all, w_down))
    grad_down = matmul_tn(stored["act_all"], grad_all)
    gate_grad, up_grad = swiglu_grads(dact, stored["gate_pre"], stored["up_pre"])
    dpair = jnp.concatenate([gate_grad, up_grad], axis=1)
    dpair_all = tokens_row(dpair)
    w_pair = jnp.concatenate([w_gate, w_up], axis=1)
    dhidden = summed_col(matmul_nt(dpair_all, w_pair))
    grad_pair = matmul_tn(stored["hidden_all"], dpair_all)
    grad_gate = grad_pair[:, :f_col]
    grad_up = grad_pair[:, f_col:]
    residual = stored["residual"]
    scale_two = stored["scale_two"]
    weighted = dhidden * norm_two
    inner_sum = feature_total(jnp.sum(weighted * residual, axis=1)) / D
    dresid = (
        grad_out + scale_two[:, None] * weighted - residual * (scale_two**3 * inner_sum)[:, None]
    )
    grad_norm_two = jnp.sum(dhidden * residual * scale_two[:, None], axis=0)
    dbranch = dresid.astype(jnp.bfloat16)
    dbranch_all = tokens_col(dbranch)
    attn_grad = summed_row(matmul_nt(dbranch_all, wo)).astype(jnp.bfloat16)
    grad_wo = matmul_tn(stored["attn_all"], dbranch_all)
    queries = stored["queries"]
    keys_all = stored["keys_all"]
    ids_ext = stored["ids_ext"]
    head_cols = wq.shape[1]
    head_count = head_cols // HEAD_DIM
    t_local = queries.shape[0]
    block_rows = min(512, t_local)
    key_reach = min(2048, t_local)
    window = key_reach + block_rows
    inv_root = HEAD_DIM ** (-0.5)

    def attend_back(accum_dkv, inputs):
        offset, log_total = inputs
        q_blk, k_blk, v_blk, scores = window_parts(queries, keys_all, ids_ext, offset, head_cols)
        prob_full = jnp.exp(scores - log_total[:, :, None])
        prob_low = prob_full.astype(jnp.bfloat16)
        d_blk = lax.dynamic_slice_in_dim(attn_grad, offset, block_rows, 0).reshape(
            block_rows, head_count, HEAD_DIM
        )
        dprobs = jnp.einsum("qhd,khd->hqk", d_blk, v_blk, preferred_element_type=jnp.float32)
        dvalue = jnp.einsum("hqk,qhd->khd", prob_low, d_blk, preferred_element_type=jnp.float32)
        center = jnp.sum(prob_full * dprobs, axis=2, keepdims=True)
        dscores = (prob_full * (dprobs - center)).astype(jnp.bfloat16)
        dquery = (
            jnp.einsum("hqk,khd->qhd", dscores, k_blk, preferred_element_type=jnp.float32)
            * inv_root
        )
        dkey = (
            jnp.einsum("hqk,qhd->khd", dscores, q_blk, preferred_element_type=jnp.float32)
            * inv_root
        )
        update = jnp.concatenate(
            [dkey.reshape(window, head_cols), dvalue.reshape(window, head_cols)], axis=1
        )
        anchor = offset + t_local - key_reach
        current = lax.dynamic_slice_in_dim(accum_dkv, anchor, window, 0)
        accum_dkv = lax.dynamic_update_slice_in_dim(accum_dkv, current + update, anchor, 0)
        return (accum_dkv, dquery.reshape(block_rows, head_cols))

    start_grads = jnp.zeros((2 * t_local, 2 * head_cols), jnp.float32)
    accum_dkv, query_grads = lax.scan(
        attend_back, start_grads, (stored["offsets"], stored["log_totals"])
    )
    returned = shifted(accum_dkv[:t_local].astype(jnp.bfloat16), "row", -1).astype(jnp.float32)
    key_grads = accum_dkv[t_local:] + returned
    dqkv = jnp.concatenate([query_grads.reshape(t_local, head_cols), key_grads], axis=1).astype(
        jnp.bfloat16
    )
    dqkv_all = tokens_row(dqkv)
    w_qkv = jnp.concatenate([wq, wk, wv], axis=1)
    dnormed = summed_col(matmul_nt(dqkv_all, w_qkv))
    grad_qkv = matmul_tn(stored["normed_all"], dqkv_all)
    grad_wq = grad_qkv[:, :head_cols]
    grad_wk = grad_qkv[:, head_cols : 2 * head_cols]
    grad_wv = grad_qkv[:, 2 * head_cols :]
    token_vals = stored["token_vals"]
    scale_one = stored["scale_one"]
    weighted_one = dnormed * norm_one
    inner_one = feature_total(jnp.sum(weighted_one * token_vals, axis=1)) / D
    grad_input = (
        dresid
        + scale_one[:, None] * weighted_one
        - token_vals * (scale_one**3 * inner_one)[:, None]
    )
    grad_norm_one = jnp.sum(dnormed * token_vals * scale_one[:, None], axis=0)
    grad_sums = (
        lax.psum(grad_wq.astype(jnp.bfloat16), "dp").astype(jnp.float32),
        lax.psum(grad_wk.astype(jnp.bfloat16), "dp").astype(jnp.float32),
        lax.psum(grad_wv.astype(jnp.bfloat16), "dp").astype(jnp.float32),
        lax.psum(grad_wo.astype(jnp.bfloat16), "dp").astype(jnp.float32),
        lax.psum(grad_gate.astype(jnp.bfloat16), "dp").astype(jnp.float32),
        lax.psum(grad_up.astype(jnp.bfloat16), "dp").astype(jnp.float32),
        lax.psum(grad_down.astype(jnp.bfloat16), "dp").astype(jnp.float32),
    )
    gain_sums = lax.psum((grad_norm_one, grad_norm_two), ("dp", "col"))
    return (
        output,
        grad_input,
        gain_sums[0],
        grad_sums[0],
        grad_sums[1],
        grad_sums[2],
        grad_sums[3],
        gain_sums[1],
        grad_sums[4],
        grad_sums[5],
        grad_sums[6],
    )


MESH = pl.DeviceIdType.MESH
BF = jnp.bfloat16
F32 = jnp.float32
NPLANE = 8


def contract(a, b, ca, cb):
    return lax.dot_general(a, b, (((ca,), (cb,)), ((), ())), preferred_element_type=F32)


class Copies:
    def __init__(self, send, recv):
        self.send, self.recv, self.used, self.open = send, recv, 0, []

    def take(self, amount=1):
        base = self.used
        self.used += amount
        return base

    def make(self, src, dst, to, site=None):
        site = self.take() if site is None else site
        return pltpu.make_async_remote_copy(
            src_ref=src,
            dst_ref=dst,
            send_sem=self.send.at[site],
            recv_sem=self.recv.at[site],
            device_id=to,
            device_id_type=MESH,
        )

    def start(self, copy, when=None):
        self.open.append((copy, when))
        if when is None:
            copy.start()
        else:
            pl.when(when)(copy.start)

    def finish(self):
        for copy, when in self.open:
            if when is None:
                copy.wait_send()
            else:
                pl.when(when)(copy.wait_send)
        self.open = []


def layer_kernel(nz, ff_half, ff_cut, *refs):
    it = iter(refs)
    take = lambda n: [next(it) for _ in range(n)]
    tok, cot, seg, n1, wq, wk, wv, wo, n2, wg, wu, wd = take(12)
    out, gin, gn1, gwq, gwk, gwv, gwo, gn2, gwg, gwu, gwd = take(11)
    X, G, WQKV, WO, WG, WU, WD, NG1, NG2 = take(9)
    XN, Q, K, V, BIAS, PM, A = take(7)
    PART, RY, RX, SX = take(4)
    HN, RES, DRES, ACT, DGA, DUP, DB, DAT = take(8)
    DK, DV, DQKV, HS, HR = take(5)
    OS, GS, GP, GR, GZ, GZS = take(6)
    zbufs = [take(5) for _ in range(5)]
    OFQ, OFO, OFF1, OFF2, OFD = take(5)
    send, recv, loc = take(3)

    z, row, y = lax.axis_index("dp"), lax.axis_index("row"), lax.axis_index("col")
    x, c = row // 2, row % 2
    net = Copies(send, recv)
    nloc = [0]

    def local(src, dst):
        nloc[0] += 1
        return pltpu.make_async_copy(src, dst, loc.at[nloc[0] - 1])

    def dev(zz, xx, yy, cc):
        return (zz, 2 * xx + cc, yy)

    core_nb, x_nb, y_nb = dev(z, x, y, 1 - c), dev(z, 1 - x, y, c), dev(z, x, 1 - y, c)
    z_up, z_dn = dev(z + 1, x, y, c), dev(z - 1, x, y, c)
    lanes = lambda i, n=256: pl.ds(pl.multiple_of(i * n, 128), n)
    rows = lambda i, n: pl.ds(pl.multiple_of(i * n, n if n % 16 else 16), n)
    flip = lambda v, bit: 1 - v if bit else v

    barrier = pltpu.get_barrier_semaphore()
    for d in range(1, NPLANE):
        pl.semaphore_signal(
            barrier, inc=1, device_id=dev(z, flip(x, d & 1), flip(y, d & 2), flip(c, d & 4)), device_id_type=MESH
        )
    for d in range(1, nz):
        pl.semaphore_signal(barrier, inc=1, device_id=dev((z + d) % nz, x, y, c), device_id_type=MESH)
    pl.semaphore_wait(barrier, NPLANE - 1 + nz - 1)

    def gather_tokens(src, buf):
        col = lambda rr: buf.at[:, lanes(rr)]
        mine = c == y
        keep = local(src, col(row))
        pl.when(mine)(keep.start)
        over = net.make(src, col(row), core_nb)
        bx, by, bf = net.take(2), net.take(2), net.take(2)
        net.start(net.make(src, col(row), dev(z, 1 - x, y, y), bx + c))
        net.start(net.make(src, col(row), dev(z, x, 1 - y, y), by + c))
        net.start(over, jnp.logical_not(mine))
        fw = [net.make(col(2 * (1 - x) + k), col(2 * (1 - x) + k), y_nb, bf + k) for k in range(2)]
        inx = [net.make(src, col(row), core_nb, bx + k) for k in range(2)]
        iny = [net.make(src, col(row), core_nb, by + k) for k in range(2)]

        def arrive():
            @pl.when(mine)
            def _():
                for k in range(2):
                    inx[k].wait_recv()
                    fw[k].start()
                over.wait_recv()
                keep.wait()

            net.open += [(f, mine) for f in fw]

        def rest():
            @pl.when(jnp.logical_not(mine))
            def _():
                for k in range(2):
                    iny[k].wait_recv()
                for k in range(2):
                    fw[k].wait_recv()

        return arrive, rest

    def relay(src_of, dst_of):
        keep = local(src_of(x), dst_of(row))
        across = net.make(src_of(x), dst_of(row), core_nb)
        far = net.make(src_of(1 - x), dst_of(row), x_nb)
        theirs = dst_of(2 * (1 - x) + c)
        fwd = net.make(theirs, theirs, core_nb)

        def start():
            keep.start()
            net.start(far)
            net.start(across)

        def arrive():
            far.wait_recv()
            net.start(fwd)

        def rest():
            keep.wait()
            across.wait_recv()
            fwd.wait_recv()

        return start, arrive, rest

    def gather_gain(src, dst):
        keep = local(src, dst.at[:, lanes(row)])
        keep.start()
        got = []
        for to in (core_nb, x_nb, dev(z, 1 - x, y, 1 - c)):
            got.append(net.make(src, dst.at[:, lanes(row)], to))
            net.start(got[-1])

        def rest():
            keep.wait()
            for g in got:
                g.wait_recv()

        return rest

    gx = gather_tokens(tok, X)
    rq = [
        relay(
            lambda xx, w=w: w.at[:, lanes(xx)],
            lambda rr, i=i: WQKV.at[rows(rr, 256), pl.ds(i * 256, 256)],
        )
        for i, w in enumerate((wq, wk, wv))
    ]
    for r in rq:
        r[0]()
    ga = [gather_gain(n1, NG1), gather_gain(n2, NG2)]
    gx[0]()
    gg = gather_tokens(cot, G)
    ro = relay(lambda xx: wo.at[rows(xx, 256), :], lambda rr: WO.at[:, lanes(rr)])
    rg = relay(lambda xx: wg.at[:, pl.ds(pl.multiple_of(xx * ff_cut, 128), ff_half)], lambda rr: WG.at[rows(rr, 256), :])
    ru = relay(lambda xx: wu.at[:, pl.ds(pl.multiple_of(xx * ff_cut, 128), ff_half)], lambda rr: WU.at[rows(rr, 256), :])
    rd = relay(lambda xx: wd.at[pl.ds(pl.multiple_of(xx * ff_cut, 128), ff_half), :], lambda rr: WD.at[:, lanes(rr)])
    for r in rq:
        r[1]()
    for r in (ro, rg, ru, rd):
        r[0]()
    for _, _, ZR, _, _ in zbufs:

        @pl.when(z == 0)
        def _(ZR=ZR):
            ZR[0, nz - 2] = jnp.zeros(ZR.shape[2:], BF)

        @pl.when(z == nz - 1)
        def _(ZR=ZR):
            ZR[1, nz - 2] = jnp.zeros(ZR.shape[2:], BF)

    seg_f = seg[...].astype(F32)
    own = jnp.where(c == 0, seg_f[:, :512], seg_f[:, 512:])
    before = jnp.where(c == 0, jnp.full((1, 256), -1.0, F32), seg_f[:, 256:512])
    ids = jnp.concatenate([before, own], axis=1)
    for b in range(2):
        k_id = jnp.broadcast_to(ids[:, b * 256 : b * 256 + 512], (256, 512))
        q_id = jnp.broadcast_to(ids[:, 256 + b * 256 : 512 + b * 256], (512, 256)).T
        q_pos = lax.broadcasted_iota(jnp.int32, (256, 512), 0) + 256
        k_pos = lax.broadcasted_iota(jnp.int32, (256, 512), 1)
        BIAS[b] = jnp.where((q_id == k_id) & (k_pos <= q_pos), 0.0, NEGATIVE)

    @pl.when(c == 0)
    def _():
        K[0:256, :] = jnp.zeros((256, 256), BF)
        V[0:256, :] = jnp.zeros((256, 256), BF)

    for g in ga:
        g()
    gx[1]()
    for t in range(4):
        v = X[t * 128 : t * 128 + 128, :].astype(F32)
        scale = lax.rsqrt(jnp.mean(v * v, axis=1, keepdims=True) + EPSILON)
        XN[t * 128 : t * 128 + 128, :] = (v * scale * NG1[...]).astype(BF)
    for r in rq:
        r[2]()
    K[256:768, :] = contract(XN[...], WQKV[:, 256:512], 1, 0).astype(BF)
    V[256:768, :] = contract(XN[...], WQKV[:, 512:768], 1, 0).astype(BF)
    hk = net.make(K.at[pl.ds(512, 256), :], K.at[pl.ds(0, 256), :], core_nb)
    hv = net.make(V.at[pl.ds(512, 256), :], V.at[pl.ds(0, 256), :], core_nb)
    net.start(hk, c == 0)
    net.start(hv, c == 0)
    Q[...] = (contract(XN[...], WQKV[:, 0:256], 1, 0).astype(BF) * 0.125).astype(BF)

    gg[0]()
    @pl.when(c == 1)
    def _():
        hk.wait_recv()
        hv.wait_recv()

    lane_id = lax.broadcasted_iota(jnp.int32, (1, 128), 1)
    head_mask = [jnp.where(lane_id < 64, 1.0, 0.0).astype(BF), jnp.where(lane_id < 64, 0.0, 1.0).astype(BF)]

    def attend(b, carry):
        for hp in range(2):
            cols = slice(hp * 128, hp * 128 + 128)
            q_b = Q[pl.ds(pl.multiple_of(b * 256, 256), 256), cols]
            k_b = K[pl.ds(pl.multiple_of(b * 256, 256), 512), cols]
            v_b = V[pl.ds(pl.multiple_of(b * 256, 256), 512), cols]
            total = None
            for h in range(2):
                s = contract(q_b * head_mask[h], k_b, 1, 1) + BIAS[b]
                e = jnp.exp(s - jnp.max(s, axis=1, keepdims=True))
                p = e * (1.0 / jnp.sum(e, axis=1, keepdims=True))
                PM[b * 4 + hp * 2 + h] = p
                part = contract(p.astype(BF), v_b * head_mask[h], 1, 0)
                total = part if total is None else total + part
            A[pl.ds(pl.multiple_of(b * 256, 256), 256), cols] = total.astype(BF)
        return carry

    lax.fori_loop(0, 2, attend, 0)
    for r in (ro, rg, ru, rd):
        r[1]()

    j = 2 * x + y
    shard = lambda buf, jj: buf.at[rows(jj, 128), :]

    def reduce_start(k, p):
        part = PART.at[p]
        a = net.make(shard(part, 2 * (1 - x) + 1 - y), RY.at[k, 0], y_nb)
        b = net.make(shard(part, 2 * x + 1 - y), RY.at[k, 1], y_nb)
        d = net.make(SX.at[k], RX.at[k], x_nb)
        a.start()
        b.start()

        def mid():
            a.wait_recv()
            SX[k] = (PART[p, rows(2 * (1 - x) + y, 128), :].astype(F32) + RY[k, 0].astype(F32)).astype(BF)
            d.start()

        def end():
            b.wait_recv()
            d.wait_recv()
            for copy in (a, b, d):
                copy.wait_send()
            return PART[p, rows(j, 128), :].astype(F32) + RY[k, 1].astype(F32) + RX[k].astype(F32)

        return mid, end

    def gather_start(buf):
        a = net.make(shard(buf, j), shard(buf, j), x_nb)
        b = net.make(shard(buf, j), shard(buf, j), y_nb)
        jx = 2 * (1 - x) + y
        f = net.make(shard(buf, jx), shard(buf, jx), y_nb)
        net.start(a)
        net.start(b)

        def mid():
            a.wait_recv()
            net.start(f)

        def end():
            b.wait_recv()
            f.wait_recv()

        return mid, end

    def send_blocks(src, dst):
        base_r = net.take(4)
        waits = []
        for dx in range(2):
            for cc in range(2):
                xx = flip(x, dx)
                piece, place = src.at[:, lanes(2 * xx + cc)], dst.at[rows(j, 128), :]
                s = net.take()
                copy = pltpu.make_async_remote_copy(
                    src_ref=piece,
                    dst_ref=place,
                    send_sem=net.send.at[s],
                    recv_sem=net.recv.at[base_r + dx * 2 + y],
                    device_id=dev(z, xx, c, cc),
                    device_id_type=MESH,
                )
                if dx == 0:
                    here = (c == y) & (c == cc)
                    keep = local(piece, place)
                    pl.when(here)(keep.start)
                    net.start(copy, jnp.logical_not(here))
                    waits.append((keep, here))
                else:
                    net.start(copy)
        piece, place = src.at[:, pl.ds(0, 256)], dst.at[pl.ds(0, 128), :]
        arrivals = [
            (net.make(piece, place, core_nb, base_r + dx * 2 + yy), jnp.logical_not((c == y) & (y == yy)) if dx == 0 else None)
            for dx in range(2)
            for yy in range(2)
        ]

        def end():
            for keep, here in waits:
                pl.when(here)(keep.wait)
            for got, when in arrivals:
                if when is None:
                    got.wait_recv()
                else:
                    pl.when(when)(got.wait_recv)

        return end

    def along_z(bufs, deliver):
        GB, CR, ZR, RL, FF = bufs
        n_rows = CR.shape[1] // nz
        part = lambda q: CR.at[:, rows(q, n_rows), :]
        over = net.make(GB.at[1 - c], CR, core_nb)
        ends = []
        net.start(over)
        yield
        over.wait_recv()
        for xx in range(2):
            CR[xx] = (CR[xx].astype(F32) + GB[c, xx].astype(F32)).astype(BF)
        up = [net.take() for _ in range(nz - 1)]
        dn = [net.take() for _ in range(nz - 1)]
        for s in range(1, nz):
            for way, sites, to in ((0, up, z_up), (1, dn, z_dn)):
                zz = z if way == 0 else nz - 1 - z
                q = nz - s + zz
                q = q if way == 0 else nz - 1 - q
                go = (zz < nz - 1) & (zz <= s - 1)
                first, later = go & (zz == 0), go & (zz > 0)
                net.start(net.make(part(q), ZR.at[way, s - 1], to, sites[s - 1]), first)
                if s >= 2:
                    acc = ZR.at[way, s - 2]
                    got = net.make(acc, acc, to, sites[s - 2])

                    @pl.when(later)
                    def _(got=got, acc=acc, q=q):
                        got.wait_recv()
                        acc[...] = (acc[...].astype(F32) + CR[:, rows(q, n_rows), :].astype(F32)).astype(BF)

                    net.start(net.make(acc, ZR.at[way, s - 1], to, sites[s - 1]), later)
            yield
        for way, sites in ((0, up), (1, dn)):
            zz = z if way == 0 else nz - 1 - z
            last = ZR.at[way, nz - 2]
            pl.when(zz > 0)(net.make(last, last, z_up, sites[nz - 2]).wait_recv)
        total = lambda xx: (
            CR[xx, rows(z, n_rows), :].astype(F32) + ZR[0, nz - 2, xx].astype(F32) + ZR[1, nz - 2, xx].astype(F32)
        ).astype(BF)
        RL[...] = total(1 - x)
        side = net.make(RL, FF.at[z, x], x_nb)
        net.start(side)
        FF[z, x] = total(x)
        yield
        side.wait_recv()
        up = [net.take() for _ in range(nz - 1)]
        dn = [net.take() for _ in range(nz - 1)]
        net.start(net.make(FF.at[z], FF.at[z], z_up, up[0]), z < nz - 1)
        net.start(net.make(FF.at[z], FF.at[z], z_dn, dn[0]), z > 0)
        yield
        for s in range(2, nz + 1):
            for way, sites, to in ((0, up, z_up), (1, dn, z_dn)):
                zz = z if way == 0 else nz - 1 - z
                q = z - (s - 1) if way == 0 else z + (s - 1)
                have = zz >= s - 1
                got = net.make(FF.at[q], FF.at[q], to, sites[s - 2])
                pl.when(have)(got.wait_recv)
                if s < nz:
                    net.start(net.make(FF.at[q], FF.at[q], to, sites[s - 1]), have & (zz < nz - 1))
            yield
        deliver(FF)
        yield

    def flush(buf, dst):
        copy = local(buf, dst)
        copy.start()
        flushes.append(copy)

    flushes = []
    over_cut = ff_half - ff_cut

    def deliver_qkv(FF):
        for i, dst in enumerate((gwq, gwk, gwv)):
            for q in range(nz):
                for xx in range(2):
                    OFQ[i, q * 64 : q * 64 + 64, xx * 256 : xx * 256 + 256] = FF[q, xx, :, i * 256 : i * 256 + 256].astype(F32)
            flush(OFQ.at[i], dst)

    def deliver_wo(FF):
        for q in range(nz):
            for xx in range(2):
                OFO[xx * 256 + q * 64 : xx * 256 + q * 64 + 64, :] = FF[q, xx].astype(F32)
        flush(OFO, gwo)

    def deliver_pair(buf, dst):
        def run(FF):
            for q in range(nz):
                buf[q * 64 : q * 64 + 64, 0:ff_half] = FF[q, 0].astype(F32)
                buf[q * 64 : q * 64 + 64, ff_half:] = FF[q, 1, :, over_cut:].astype(F32)
            flush(buf, dst)

        return run

    def deliver_down(FF):
        n = ff_half // nz
        for q in range(nz):
            OFD[q * n : q * n + n, :] = FF[q, 0].astype(F32)
            skip = max(0, min(n, over_cut - q * n))
            if skip < n:
                OFD[ff_cut + q * n + skip : ff_cut + q * n + n, :] = FF[q, 1, skip:, :].astype(F32)
        flush(OFD, gwd)

    lines = []

    def tick(n=1):
        for _ in range(n):
            for line in lines:
                next(line, None)

    ro[2]()
    for n in range(4):
        PART[0, :, n * 256 : n * 256 + 256] = contract(A[...], WO[:, n * 256 : n * 256 + 256], 1, 0).astype(BF)
    mid, end = reduce_start(0, 0)
    mid()
    gg[1]()
    res = X[rows(j, 128), :].astype(F32) + end()
    RES[...] = res
    scale = lax.rsqrt(jnp.mean(res * res, axis=1, keepdims=True) + EPSILON)
    HN[rows(j, 128), :] = (res * scale * NG2[...]).astype(BF)
    mid, end = gather_start(HN)
    mid()
    for r in (rg, ru, rd):
        r[2]()
    end()

    skip = (lax.broadcasted_iota(jnp.int32, (1, 256), 1) < over_cut) & (x == 1)
    for n in range(ff_half // 256):
        cols = slice(n * 256, n * 256 + 256)
        gate = contract(HN[...], WG[:, cols], 1, 0)
        up = contract(HN[...], WU[:, cols], 1, 0)
        dact = contract(G[...], WD[cols, :], 1, 1)
        sig = jax.nn.sigmoid(gate)
        silu = gate * sig
        act, dgate, dup = silu * up, dact * up * sig * (1.0 + gate * (1.0 - sig)), dact * silu
        if n == 0:
            act, dgate, dup = (jnp.where(skip, 0.0, v) for v in (act, dgate, dup))
        ACT[:, cols] = act.astype(BF)
        DGA[:, cols] = dgate.astype(BF)
        DUP[:, cols] = dup.astype(BF)
    for n in range(4):
        cols = slice(n * 256, n * 256 + 256)
        PART[1, :, cols] = (contract(DGA[...], WG[cols, :], 1, 1) + contract(DUP[...], WU[cols, :], 1, 1)).astype(BF)
    hid = reduce_start(1, 1)
    for r in range(4):
        zbufs[0][0][r % 2, r // 2] = contract(ACT[...], G[:, r * 256 : r * 256 + 256], 0, 0).astype(BF)
    lines.append(along_z(zbufs[0], deliver_down))
    tick()
    for n in range(4):
        cols = slice(n * 256, n * 256 + 256)
        PART[2, :, cols] = contract(ACT[...], WD[:, cols], 1, 0).astype(BF)
    hid[0]()
    fin = reduce_start(2, 2)
    tick()
    for r in range(4):
        zbufs[1][0][r % 2, r // 2] = contract(HN[:, r * 256 : r * 256 + 256], DGA[...], 0, 0).astype(BF)
    lines.append(along_z(zbufs[1], deliver_pair(OFF1, gwg)))
    dh = hid[1]()
    res = RES[...]
    scale = lax.rsqrt(jnp.mean(res * res, axis=1, keepdims=True) + EPSILON)
    w = dh * NG2[...]
    inner = jnp.mean(w * res, axis=1, keepdims=True)
    dres = G[rows(j, 128), :].astype(F32) + scale * w - res * (scale * scale * scale * inner)
    DRES[...] = dres
    GP[...] = jnp.zeros_like(GP)
    GP[1:2, :] = jnp.sum(dh * res * scale, axis=0, keepdims=True)
    DB[rows(j, 128), :] = dres.astype(BF)
    dbg = gather_start(DB)
    tick()
    for r in range(4):
        zbufs[2][0][r % 2, r // 2] = contract(HN[:, r * 256 : r * 256 + 256], DUP[...], 0, 0).astype(BF)
    dbg[0]()
    lines.append(along_z(zbufs[2], deliver_pair(OFF2, gwu)))
    tick()
    fin[0]()
    OS[...] = (RES[...] + fin[1]()).astype(BF)
    sent = send_blocks(OS, out)
    dbg[1]()

    DAT[...] = contract(DB[...], WO[...], 1, 1).astype(BF)
    for r in range(4):
        zbufs[3][0][r % 2, r // 2] = contract(A[...], DB[:, r * 256 : r * 256 + 256], 0, 0).astype(BF)
    tick()
    DK[...] = jnp.zeros_like(DK)
    DV[...] = jnp.zeros_like(DV)

    def attend_back(b, carry):
        qs, ks = pl.ds(pl.multiple_of(b * 256, 256), 256), pl.ds(pl.multiple_of(b * 256, 256), 512)
        for hp in range(2):
            cols = slice(hp * 128, hp * 128 + 128)
            q_b, k_b, v_b, d_b = Q[qs, cols], K[ks, cols], V[ks, cols], DAT[qs, cols]
            dq = dk = dv = None
            for h in range(2):
                m = head_mask[h]
                d_h = d_b * m
                p = PM[b * 4 + hp * 2 + h]
                dp = contract(d_h, v_b, 1, 1)
                ds = (p * (dp - jnp.sum(p * dp, axis=1, keepdims=True))).astype(BF)
                one = (contract(ds, k_b * m, 1, 0), contract(ds, q_b * m, 0, 0), contract(p.astype(BF), d_h, 0, 0))
                dq, dk, dv = one if dq is None else (dq + one[0], dk + one[1], dv + one[2])
            DQKV[qs, cols] = (dq * 0.125).astype(BF)
            DK[ks, cols] += dk
            DV[ks, cols] += dv
        return carry

    lax.fori_loop(0, 2, attend_back, 0)
    HS[:, 0:256] = DK[0:256, :].astype(BF)
    HS[:, 256:512] = DV[0:256, :].astype(BF)
    back = net.make(HS, HR, core_nb)
    net.start(back, c == 1)
    tick()

    @pl.when(c == 0)
    def _():
        back.wait_recv()
        DK[512:768, :] += HR[:, 0:256].astype(F32)
        DV[512:768, :] += HR[:, 256:512].astype(F32)

    DQKV[:, 256:512] = DK[256:768, :].astype(BF)
    DQKV[:, 512:768] = DV[256:768, :].astype(BF)
    for n in range(4):
        cols = slice(n * 256, n * 256 + 256)
        PART[0, :, cols] = contract(DQKV[...], WQKV[cols, :], 1, 1).astype(BF)
    last = reduce_start(3, 0)
    for r in range(4):
        zbufs[4][0][r % 2, r // 2] = contract(XN[:, r * 256 : r * 256 + 256], DQKV[...], 0, 0).astype(BF)
    lines.append(along_z(zbufs[4], deliver_qkv))
    lines.append(along_z(zbufs[3], deliver_wo))
    tick()
    last[0]()
    tick()
    dx = last[1]()
    v = X[rows(j, 128), :].astype(F32)
    scale = lax.rsqrt(jnp.mean(v * v, axis=1, keepdims=True) + EPSILON)
    w = dx * NG1[...]
    inner = jnp.mean(w * v, axis=1, keepdims=True)
    GS[...] = DRES[...] + scale * w - v * (scale * scale * scale * inner)
    GP[0:1, :] = jnp.sum(dx * v * scale, axis=0, keepdims=True)
    sent_in = send_blocks(GS, gin)

    me = 4 * x + 2 * y + c
    got = []
    for d in range(1, NPLANE):
        xx, yy, cc = flip(x, d & 1), flip(y, d & 2), flip(c, d & 4)
        copy = net.make(GP.at[:, lanes(2 * xx + cc)], GR.at[me], dev(z, xx, yy, cc))
        net.start(copy)
        got.append(copy)
    keep = local(GP.at[:, lanes(row)], GR.at[me])
    keep.start()
    tick()
    keep.wait()
    for copy in got:
        copy.wait_recv()
    total = GR[0]
    for d in range(1, NPLANE):
        total = total + GR[d]
    GZS[...] = total
    got = []
    for d in range(1, nz):
        copy = net.make(GZS, GZ.at[z], dev((z + d) % nz, x, y, c))
        net.start(copy)
        got.append(copy)
    keep = local(GZS, GZ.at[z])
    keep.start()
    tick(2)
    keep.wait()
    for copy in got:
        copy.wait_recv()
    total = GZ[0]
    for d in range(1, nz):
        total = total + GZ[d]
    gn1[...] = total[0:1, :]
    gn2[...] = total[1:2, :]
    tick(30)
    sent()
    sent_in()
    for copy in flushes:
        copy.wait()
    net.finish()


def fused(nz, tokens, cotangent, seg_ids, norm_one, wq, wk, wv, wo, norm_two, w_gate, w_up, w_down):
    ff = w_gate.shape[1]
    ff_half = -(-ff // 512) * 256
    ff_cut = ff - ff_half
    vm = pltpu.VMEM
    zshapes = [(256 * ff_half // 256, 256), (256, ff_half), (256, ff_half), (256, 256), (256, 768)]
    zscratch = []
    for rows, cols in zshapes:
        zscratch += [
            vm((2, 2, rows, cols), BF),
            vm((2, rows, cols), BF),
            vm((2, nz - 1, 2, rows // nz, cols), BF),
            vm((rows // nz, cols), BF),
            vm((nz, 2, rows // nz, cols), BF),
        ]
    scratch = [
        vm((512, D), BF), vm((512, D), BF), vm((D, 768), BF), vm((256, D), BF),
        vm((D, ff_half), BF), vm((D, ff_half), BF), vm((ff_half, D), BF), vm((1, D), F32), vm((1, D), F32),
        vm((512, D), BF), vm((512, 256), BF), vm((768, 256), BF), vm((768, 256), BF), vm((2, 256, 512), F32),
        vm((8, 256, 512), F32), vm((512, 256), BF),
        vm((3, 512, D), BF), vm((4, 2, 128, D), BF), vm((4, 128, D), BF), vm((4, 128, D), BF),
        vm((512, D), BF), vm((128, D), F32), vm((128, D), F32), vm((512, ff_half), BF), vm((512, ff_half), BF),
        vm((512, ff_half), BF), vm((512, D), BF), vm((512, 256), BF),
        vm((768, 256), F32), vm((768, 256), F32), vm((512, 768), BF), vm((256, 512), BF), vm((256, 512), BF),
        vm((128, D), BF), vm((128, D), F32), vm((8, D), F32), vm((8, 8, 256), F32), vm((nz, 8, 256), F32), vm((8, 256), F32),
        *zscratch,
        vm((3, 256, 512), F32), vm((512, 256), F32), vm((256, ff), F32), vm((256, ff), F32), vm((ff, 256), F32),
        pltpu.SemaphoreType.DMA((220,)), pltpu.SemaphoreType.DMA((220,)), pltpu.SemaphoreType.DMA((40,)),
    ]
    hbm, vmem = pl.BlockSpec(memory_space=pl.ANY), pl.BlockSpec(memory_space=pltpu.VMEM)
    sds = jax.ShapeDtypeStruct
    outs = (
        sds((512, 256), BF), sds((512, 256), F32), sds((1, 256), F32),
        sds((256, 512), F32), sds((256, 512), F32), sds((256, 512), F32), sds((512, 256), F32),
        sds((1, 256), F32), sds((256, ff), F32), sds((256, ff), F32), sds((ff, 256), F32),
    )
    res = pl.pallas_call(
        functools.partial(layer_kernel, nz, ff_half, ff_cut),
        out_shape=outs,
        in_specs=[hbm, hbm, vmem, vmem, hbm, hbm, hbm, hbm, vmem, hbm, hbm, hbm],
        out_specs=(hbm, hbm, vmem, hbm, hbm, hbm, hbm, vmem, hbm, hbm, hbm),
        scratch_shapes=scratch,
        compiler_params=pltpu.CompilerParams(collective_id=0, has_side_effects=True, vmem_limit_bytes=62 << 20),
        name="layer",
    )(
        tokens, cotangent, seg_ids, norm_one[None], wq, wk, wv, wo, norm_two[None], w_gate, w_up, w_down,
    )
    res = list(res)
    res[2], res[7] = res[2][0], res[7][0]
    return tuple(res)


def solution(mesh):
    in_specs = (
        P(("dp", "col"), "row"),
        P(("dp", "col"), "row"),
        P("dp", None),
        P("row"),
        P("row", "col"),
        P("row", "col"),
        P("row", "col"),
        P("col", "row"),
        P("row"),
        P("row", "col"),
        P("row", "col"),
        P("col", "row"),
    )
    out_specs = (
        P(("dp", "col"), "row"),
        P(("dp", "col"), "row"),
        P("row"),
        P("row", "col"),
        P("row", "col"),
        P("row", "col"),
        P("col", "row"),
        P("row"),
        P("row", "col"),
        P("row", "col"),
        P("col", "row"),
    )
    sizes = dict(mesh.shape)
    body = per_device
    if sizes["row"] == 4 and sizes["col"] == 2:
        body = functools.partial(fused, sizes["dp"])
    return jax.shard_map(
        body, mesh=mesh, in_specs=in_specs, out_specs=out_specs, check_vma=False
    )
```

```python
import functools

import jax
import jax.numpy as jnp
from jax import lax
from jax.experimental import pallas as pl
from jax.experimental.pallas import tpu as pltpu
from jax.sharding import PartitionSpec as P

D = 1024
HEAD_DIM = 64


EPSILON = 1e-05
NEGATIVE = -1e30


def for_sending(array):

    def short(part):
        return part.astype(jnp.bfloat16) if part.dtype == jnp.float32 else part

    return jax.tree.map(short, array)


def shifted(block, axis, distance):
    devices = range(lax.axis_size(axis))
    route = [(i - distance, i) for i in devices if i - distance in devices]
    return lax.ppermute(block, axis, route)


def matmul(first_op, second_op):
    return jnp.dot(first_op, second_op, preferred_element_type=jnp.float32)


def matmul_tn(first_op, second_op):
    return lax.dot_general(
        first_op, second_op, (((0,), (0,)), ((), ())), preferred_element_type=jnp.float32
    )


def matmul_nt(first_op, second_op):
    return lax.dot_general(
        first_op, second_op, (((1,), (1,)), ((), ())), preferred_element_type=jnp.float32
    )


def tokens_col(array_in):
    return lax.all_gather(array_in, "col", axis=0, tiled=True)


def tokens_row(array_in):
    return lax.all_gather(for_sending(array_in), "row", axis=0, tiled=True).astype(array_in.dtype)


def summed_row(array_in):
    return lax.psum_scatter(
        array_in.astype(jnp.bfloat16), "row", scatter_dimension=0, tiled=True
    ).astype(jnp.float32)


def summed_col(array_in):
    return lax.psum_scatter(
        array_in.astype(jnp.bfloat16), "col", scatter_dimension=0, tiled=True
    ).astype(jnp.float32)


def feature_total(array_in):
    return lax.psum(array_in, "row")


def window_parts(queries, keys_all, ids_ext, offset, head_cols):
    t_local = queries.shape[0]
    block_rows = min(512, t_local)
    key_reach = min(2048, t_local)
    window = key_reach + block_rows
    head_count = head_cols // HEAD_DIM
    anchor = offset + t_local - key_reach
    q_blk = lax.dynamic_slice_in_dim(queries, offset, block_rows, 0).reshape(
        block_rows, head_count, HEAD_DIM
    )
    k_win = lax.dynamic_slice_in_dim(keys_all, anchor, window, 0)
    k_blk = k_win[:, :head_cols].reshape(window, head_count, HEAD_DIM)
    v_blk = k_win[:, head_cols:].reshape(window, head_count, HEAD_DIM)
    q_ids = lax.dynamic_slice_in_dim(ids_ext, offset + t_local, block_rows, 0)
    k_ids = lax.dynamic_slice_in_dim(ids_ext, anchor, window, 0)
    q_pos = offset + lax.iota(jnp.int32, block_rows)
    k_pos = offset - key_reach + lax.iota(jnp.int32, window)
    allowed = (q_ids[:, None] == k_ids[None, :]) & (k_pos[None, :] <= q_pos[:, None])
    scores = jnp.einsum(
        "qhd,khd->hqk", q_blk, k_blk, preferred_element_type=jnp.float32
    ) * HEAD_DIM ** (-0.5)
    scores = jnp.where(allowed[None], scores, NEGATIVE)
    return (q_blk, k_blk, v_blk, scores)


def forward(tokens, seg_ids, norm_one, wq, wk, wv, wo, norm_two, w_gate, w_up, w_down):
    token_vals = tokens.astype(jnp.float32)
    scale_one = lax.rsqrt(feature_total(jnp.sum(token_vals * token_vals, axis=1)) / D + EPSILON)
    normed = (token_vals * scale_one[:, None] * norm_one).astype(jnp.bfloat16)
    normed_all = tokens_col(normed)
    w_qkv = jnp.concatenate([wq, wk, wv], axis=1)
    head_cols = wq.shape[1]
    qkv = summed_row(matmul(normed_all, w_qkv)).astype(jnp.bfloat16)
    queries = qkv[:, :head_cols]
    kv_local = qkv[:, head_cols:]
    prior_keys = shifted(kv_local, "row", 1)
    keys_all = jnp.concatenate([prior_keys, kv_local], axis=0)
    t_local = queries.shape[0]
    block_rows = min(512, t_local)
    padded_ids = jnp.concatenate([jnp.full((t_local,), -1, jnp.int32), seg_ids[0]])
    ids_ext = lax.dynamic_slice_in_dim(padded_ids, lax.axis_index("row") * t_local, 2 * t_local, 0)

    def attend(offset):
        q_blk, k_blk, v_blk, scores = window_parts(queries, keys_all, ids_ext, offset, head_cols)
        row_max = jnp.max(scores, axis=2, keepdims=True)
        exp_total = jnp.sum(jnp.exp(scores - row_max), axis=2, keepdims=True)
        log_total = row_max + jnp.log(exp_total)
        prob_low = jnp.exp(scores - log_total).astype(jnp.bfloat16)
        mixed_out = jnp.einsum("hqk,khd->qhd", prob_low, v_blk, preferred_element_type=jnp.float32)
        return (mixed_out.reshape(block_rows, head_cols).astype(jnp.bfloat16), log_total[:, :, 0])

    offsets = lax.iota(jnp.int32, t_local // block_rows) * block_rows
    pieces, log_totals = lax.map(attend, offsets)
    attn_out = pieces.reshape(t_local, head_cols)
    attn_all = tokens_row(attn_out)
    residual = token_vals + summed_col(matmul(attn_all, wo))
    stored = {
        "token_vals": token_vals,
        "scale_one": scale_one,
        "normed_all": normed_all,
        "queries": queries,
        "keys_all": keys_all,
        "ids_ext": ids_ext,
        "log_totals": log_totals,
        "attn_all": attn_all,
        "offsets": offsets,
    }
    f_col = w_gate.shape[1]
    scale_two = lax.rsqrt(feature_total(jnp.sum(residual * residual, axis=1)) / D + EPSILON)
    hidden_in = (residual * scale_two[:, None] * norm_two).astype(jnp.bfloat16)
    hidden_all = tokens_col(hidden_in)
    w_pair = jnp.concatenate([w_gate, w_up], axis=1)
    pair_sum = summed_row(matmul(hidden_all, w_pair))
    gate_pre = pair_sum[:, :f_col]
    up_pre = pair_sum[:, f_col:]
    act_low = (jax.nn.silu(gate_pre) * up_pre).astype(jnp.bfloat16)
    act_all = tokens_row(act_low)
    final_sum = residual + summed_col(matmul(act_all, w_down))
    stored.update(
        {
            "residual": residual,
            "scale_two": scale_two,
            "hidden_all": hidden_all,
            "gate_pre": gate_pre,
            "up_pre": up_pre,
            "act_all": act_all,
        }
    )
    return (final_sum.astype(jnp.bfloat16), stored)


def swiglu_grads(dact, gate_pre, up_pre):
    sigmoid_gate = jax.nn.sigmoid(gate_pre)
    gate_grad = (dact * up_pre * sigmoid_gate * (1.0 + gate_pre * (1.0 - sigmoid_gate))).astype(
        jnp.bfloat16
    )
    up_grad = (dact * gate_pre * sigmoid_gate).astype(jnp.bfloat16)
    return (gate_grad, up_grad)


def per_device(
    tokens, cotangent, seg_ids, norm_one, wq, wk, wv, wo, norm_two, w_gate, w_up, w_down
):
    weights = (tokens, seg_ids, norm_one, wq, wk, wv, wo, norm_two, w_gate, w_up, w_down)
    output, stored = forward(*weights)
    f_col = w_gate.shape[1]
    grad_out = cotangent.astype(jnp.float32)
    grad_all = tokens_col(cotangent)
    dact = summed_row(matmul_nt(grad_all, w_down))
    grad_down = matmul_tn(stored["act_all"], grad_all)
    gate_grad, up_grad = swiglu_grads(dact, stored["gate_pre"], stored["up_pre"])
    dpair = jnp.concatenate([gate_grad, up_grad], axis=1)
    dpair_all = tokens_row(dpair)
    w_pair = jnp.concatenate([w_gate, w_up], axis=1)
    dhidden = summed_col(matmul_nt(dpair_all, w_pair))
    grad_pair = matmul_tn(stored["hidden_all"], dpair_all)
    grad_gate = grad_pair[:, :f_col]
    grad_up = grad_pair[:, f_col:]
    residual = stored["residual"]
    scale_two = stored["scale_two"]
    weighted = dhidden * norm_two
    inner_sum = feature_total(jnp.sum(weighted * residual, axis=1)) / D
    dresid = (
        grad_out + scale_two[:, None] * weighted - residual * (scale_two**3 * inner_sum)[:, None]
    )
    grad_norm_two = jnp.sum(dhidden * residual * scale_two[:, None], axis=0)
    dbranch = dresid.astype(jnp.bfloat16)
    dbranch_all = tokens_col(dbranch)
    attn_grad = summed_row(matmul_nt(dbranch_all, wo)).astype(jnp.bfloat16)
    grad_wo = matmul_tn(stored["attn_all"], dbranch_all)
    queries = stored["queries"]
    keys_all = stored["keys_all"]
    ids_ext = stored["ids_ext"]
    head_cols = wq.shape[1]
    head_count = head_cols // HEAD_DIM
    t_local = queries.shape[0]
    block_rows = min(512, t_local)
    key_reach = min(2048, t_local)
    window = key_reach + block_rows
    inv_root = HEAD_DIM ** (-0.5)

    def attend_back(accum_dkv, inputs):
        offset, log_total = inputs
        q_blk, k_blk, v_blk, scores = window_parts(queries, keys_all, ids_ext, offset, head_cols)
        prob_full = jnp.exp(scores - log_total[:, :, None])
        prob_low = prob_full.astype(jnp.bfloat16)
        d_blk = lax.dynamic_slice_in_dim(attn_grad, offset, block_rows, 0).reshape(
            block_rows, head_count, HEAD_DIM
        )
        dprobs = jnp.einsum("qhd,khd->hqk", d_blk, v_blk, preferred_element_type=jnp.float32)
        dvalue = jnp.einsum("hqk,qhd->khd", prob_low, d_blk, preferred_element_type=jnp.float32)
        center = jnp.sum(prob_full * dprobs, axis=2, keepdims=True)
        dscores = (prob_full * (dprobs - center)).astype(jnp.bfloat16)
        dquery = (
            jnp.einsum("hqk,khd->qhd", dscores, k_blk, preferred_element_type=jnp.float32)
            * inv_root
        )
        dkey = (
            jnp.einsum("hqk,qhd->khd", dscores, q_blk, preferred_element_type=jnp.float32)
            * inv_root
        )
        update = jnp.concatenate(
            [dkey.reshape(window, head_cols), dvalue.reshape(window, head_cols)], axis=1
        )
        anchor = offset + t_local - key_reach
        current = lax.dynamic_slice_in_dim(accum_dkv, anchor, window, 0)
        accum_dkv = lax.dynamic_update_slice_in_dim(accum_dkv, current + update, anchor, 0)
        return (accum_dkv, dquery.reshape(block_rows, head_cols))

    start_grads = jnp.zeros((2 * t_local, 2 * head_cols), jnp.float32)
    accum_dkv, query_grads = lax.scan(
        attend_back, start_grads, (stored["offsets"], stored["log_totals"])
    )
    returned = shifted(accum_dkv[:t_local].astype(jnp.bfloat16), "row", -1).astype(jnp.float32)
    key_grads = accum_dkv[t_local:] + returned
    dqkv = jnp.concatenate([query_grads.reshape(t_local, head_cols), key_grads], axis=1).astype(
        jnp.bfloat16
    )
    dqkv_all = tokens_row(dqkv)
    w_qkv = jnp.concatenate([wq, wk, wv], axis=1)
    dnormed = summed_col(matmul_nt(dqkv_all, w_qkv))
    grad_qkv = matmul_tn(stored["normed_all"], dqkv_all)
    grad_wq = grad_qkv[:, :head_cols]
    grad_wk = grad_qkv[:, head_cols : 2 * head_cols]
    grad_wv = grad_qkv[:, 2 * head_cols :]
    token_vals = stored["token_vals"]
    scale_one = stored["scale_one"]
    weighted_one = dnormed * norm_one
    inner_one = feature_total(jnp.sum(weighted_one * token_vals, axis=1)) / D
    grad_input = (
        dresid
        + scale_one[:, None] * weighted_one
        - token_vals * (scale_one**3 * inner_one)[:, None]
    )
    grad_norm_one = jnp.sum(dnormed * token_vals * scale_one[:, None], axis=0)
    grad_sums = (
        lax.psum(grad_wq.astype(jnp.bfloat16), "dp").astype(jnp.float32),
        lax.psum(grad_wk.astype(jnp.bfloat16), "dp").astype(jnp.float32),
        lax.psum(grad_wv.astype(jnp.bfloat16), "dp").astype(jnp.float32),
        lax.psum(grad_wo.astype(jnp.bfloat16), "dp").astype(jnp.float32),
        lax.psum(grad_gate.astype(jnp.bfloat16), "dp").astype(jnp.float32),
        lax.psum(grad_up.astype(jnp.bfloat16), "dp").astype(jnp.float32),
        lax.psum(grad_down.astype(jnp.bfloat16), "dp").astype(jnp.float32),
    )
    gain_sums = lax.psum((grad_norm_one, grad_norm_two), ("dp", "col"))
    return (
        output,
        grad_input,
        gain_sums[0],
        grad_sums[0],
        grad_sums[1],
        grad_sums[2],
        grad_sums[3],
        gain_sums[1],
        grad_sums[4],
        grad_sums[5],
        grad_sums[6],
    )


MESH = pl.DeviceIdType.MESH
BF = jnp.bfloat16
F32 = jnp.float32
NPLANE = 8


def contract(a, b, ca, cb):
    return lax.dot_general(a, b, (((ca,), (cb,)), ((), ())), preferred_element_type=F32)


class Copies:
    def __init__(self, send, recv):
        self.send, self.recv, self.used, self.open = send, recv, 0, []

    def take(self, amount=1):
        base = self.used
        self.used += amount
        return base

    def make(self, src, dst, to, site=None):
        site = self.take() if site is None else site
        return pltpu.make_async_remote_copy(
            src_ref=src,
            dst_ref=dst,
            send_sem=self.send.at[site],
            recv_sem=self.recv.at[site],
            device_id=to,
            device_id_type=MESH,
        )

    def start(self, copy, when=None):
        self.open.append((copy, when))
        if when is None:
            copy.start()
        else:
            pl.when(when)(copy.start)

    def finish(self):
        for copy, when in self.open:
            if when is None:
                copy.wait_send()
            else:
                pl.when(when)(copy.wait_send)
        self.open = []


def layer_kernel(nz, ff_half, ff_cut, *refs):
    it = iter(refs)
    take = lambda n: [next(it) for _ in range(n)]
    tok, cot, seg, n1, wq, wk, wv, wo, n2, wg, wu, wd = take(12)
    out, gin, gains, fd, fg, fu, fo, fq = take(8)
    X, G, WQKV, WO, WG, WU, WD, NG1, NG2 = take(9)
    XN, Q, K, V, BIAS, PM, AF = take(7)
    PART, RA, RB, R2, S2 = take(5)
    HN, RES, DRES, ACT, DGA, DUP, DB, DAT = take(8)
    DK, DV, DQKV, HS, HR = take(5)
    OS, GS, GP, GR, GZ, GZS = take(6)
    zbufs = [take(5) for _ in range(5)]
    send, recv, loc = take(3)

    z, row, y = lax.axis_index("dp"), lax.axis_index("row"), lax.axis_index("col")
    x, c = row // 2, row % 2
    net = Copies(send, recv)
    nloc = [0]

    def local(src, dst):
        nloc[0] += 1
        return pltpu.make_async_copy(src, dst, loc.at[nloc[0] - 1])

    def dev(zz, xx, yy, cc):
        return (zz, 2 * xx + cc, yy)

    core_nb, x_nb, y_nb = dev(z, x, y, 1 - c), dev(z, 1 - x, y, c), dev(z, x, 1 - y, c)
    z_up, z_dn = dev(z + 1, x, y, c), dev(z - 1, x, y, c)
    lanes = lambda i, n=256: pl.ds(pl.multiple_of(i * n, 128), n)
    rows = lambda i, n: pl.ds(pl.multiple_of(i * n, n if n % 16 else 16), n)
    flip = lambda v, bit: 1 - v if bit else v

    barrier = pltpu.get_barrier_semaphore()
    for d in range(1, NPLANE):
        pl.semaphore_signal(
            barrier, inc=1, device_id=dev(z, flip(x, d & 1), flip(y, d & 2), flip(c, d & 4)), device_id_type=MESH
        )
    for d in range(1, nz):
        pl.semaphore_signal(barrier, inc=1, device_id=dev((z + d) % nz, x, y, c), device_id_type=MESH)
    pl.semaphore_wait(barrier, NPLANE - 1 + nz - 1)

    def gather_tokens(src, buf):
        col = lambda rr: buf.at[:, lanes(rr)]
        mine = c == y
        other = jnp.logical_not(mine)
        keep = local(src, col(row))
        over = net.make(src, col(row), core_nb)
        bx, by = net.take(2), net.take(2)
        to_x = net.make(src, col(row), dev(z, 1 - x, y, y), bx + c)
        to_y = net.make(src, col(row), dev(z, x, 1 - y, y), by + c)
        far = 2 * (1 - x)
        by_y = net.make(col(far), col(far), y_nb)
        by_x = net.make(col(2 * x + 1), col(2 * x + 1), x_nb)
        got_x = [net.make(src, col(row), core_nb, bx + k) for k in range(2)]
        got_y = [net.make(src, col(row), core_nb, by + k) for k in range(2)]

        def start():
            pl.when(mine)(keep.start)
            net.start(to_x)
            net.start(to_y)
            net.start(over, other)

        def arrive():
            @pl.when(mine)
            def _():
                got_x[0].wait_recv()
                by_y.start()

            @pl.when(other)
            def _():
                got_y[1].wait_recv()
                by_x.start()

            net.open += [(by_y, mine), (by_x, other)]

        def rest():
            @pl.when(mine)
            def _():
                got_x[1].wait_recv()
                over.wait_recv()
                keep.wait()

            @pl.when(other)
            def _():
                got_y[0].wait_recv()
                by_y.wait_recv()
                by_x.wait_recv()

        return start, arrive, rest

    def relay(src_of, dst_of):
        keep = local(src_of(x), dst_of(row))
        across = net.make(src_of(x), dst_of(row), core_nb)
        far = net.make(src_of(1 - x), dst_of(row), x_nb)
        theirs = dst_of(2 * (1 - x) + c)
        fwd = net.make(theirs, theirs, core_nb)

        def start():
            keep.start()
            net.start(far)
            net.start(across)

        def arrive():
            far.wait_recv()
            net.start(fwd)

        def rest():
            keep.wait()
            across.wait_recv()
            fwd.wait_recv()

        return start, arrive, rest

    def relay_z(src_of, dst_of, n_rows):
        n = n_rows // nz
        keep = local(src_of(x, 0, n_rows), dst_of(row, 0, n_rows))
        across = net.make(src_of(x, 0, n_rows), dst_of(row, 0, n_rows), core_nb)
        far = net.make(src_of(1 - x, z * n, n), dst_of(row, z * n, n), x_nb)
        theirs = lambda q: dst_of(2 * (1 - x) + c, q * n, n)
        spread = [net.make(theirs(z), theirs(z), dev((z + d) % nz, x, y, c)) for d in range(1, nz)]
        whole = dst_of(2 * (1 - x) + c, 0, n_rows)
        fwd = net.make(whole, whole, core_nb)

        def start():
            net.start(far)
            keep.start()
            net.start(across)

        def arrive():
            far.wait_recv()
            for copy in spread:
                net.start(copy)

        def pass_on():
            for copy in spread:
                copy.wait_recv()
            net.start(fwd)

        def rest():
            keep.wait()
            across.wait_recv()
            fwd.wait_recv()

        return start, arrive, pass_on, rest

    def gather_wo():
        at = lambda yy, rr: WO.at[rows(yy, 512), lanes(rr)]
        keep = local(wo, at(y, row))
        across = net.make(wo, at(y, row), core_nb)
        to_x, to_y = net.make(wo, at(y, row), x_nb), net.make(wo, at(y, row), y_nb)
        rx = 2 * (1 - x) + c
        on_y = net.make(at(y, rx), at(y, rx), y_nb)
        others = (at(y, rx), at(1 - y, row), at(1 - y, rx))
        fwd = [net.make(ref, ref, core_nb) for ref in others]

        def start():
            net.start(to_x)
            net.start(to_y)
            keep.start()
            net.start(across)

        def arrive():
            to_x.wait_recv()
            net.start(on_y)
            net.start(fwd[0])

        def pass_on():
            to_y.wait_recv()
            net.start(fwd[1])
            on_y.wait_recv()
            net.start(fwd[2])

        def rest():
            keep.wait()
            across.wait_recv()
            for copy in fwd:
                copy.wait_recv()

        return start, arrive, pass_on, rest

    def gather_gain(src, dst):
        keep = local(src, dst.at[:, lanes(row)])
        keep.start()
        got = []
        for to in (core_nb, x_nb, dev(z, 1 - x, y, 1 - c)):
            got.append(net.make(src, dst.at[:, lanes(row)], to))
            net.start(got[-1])

        def rest():
            keep.wait()
            for g in got:
                g.wait_recv()

        return rest

    gx, gg = gather_tokens(tok, X), gather_tokens(cot, G)
    qkv_at = lambda rr, r0, n, i: WQKV.at[pl.ds(pl.multiple_of(rr * 256 + r0, 16), n), pl.ds(i * 256, 256)]
    rq = relay(lambda xx: wq.at[:, lanes(xx)], lambda rr: WQKV.at[rows(rr, 256), pl.ds(0, 256)])
    rkv = [
        relay_z(
            lambda xx, r0, n, w=w: w.at[pl.ds(pl.multiple_of(r0, 16), n), lanes(xx)],
            lambda rr, r0, n, i=i: qkv_at(rr, r0, n, i),
            256,
        )
        for i, w in ((1, wk), (2, wv))
    ]
    ro = gather_wo()
    cut = lambda xx: pl.multiple_of(xx * ff_cut, 128)
    rff = [
        relay_z(
            lambda xx, r0, n, w=w: w.at[pl.ds(pl.multiple_of(r0, 16), n), pl.ds(cut(xx), ff_half)],
            lambda rr, r0, n, W=W: W.at[pl.ds(pl.multiple_of(rr * 256 + r0, 16), n), :],
            256,
        )
        for w, W in ((wg, WG), (wu, WU))
    ]
    rd = relay_z(
        lambda xx, r0, n: wd.at[pl.ds(pl.multiple_of(xx * ff_cut + r0, 16), n), :],
        lambda rr, r0, n: WD.at[pl.ds(pl.multiple_of(r0, 16), n), lanes(rr)],
        ff_half,
    )
    for r in rkv:
        r[0]()
    gx[0]()
    rq[0]()
    ga = [gather_gain(n1, NG1), gather_gain(n2, NG2)]
    for r in rkv:
        r[1]()
    ro[0]()
    for r in rff:
        r[0]()
    gx[1]()
    for _, _, ZR, _, _ in zbufs:

        @pl.when(z == 0)
        def _(ZR=ZR):
            ZR[0, nz - 2] = jnp.zeros(ZR.shape[2:], BF)

        @pl.when(z == nz - 1)
        def _(ZR=ZR):
            ZR[1, nz - 2] = jnp.zeros(ZR.shape[2:], BF)

    seg_f = seg[...].astype(F32)
    own = jnp.where(c == 0, seg_f[:, :512], seg_f[:, 512:])
    before = jnp.where(c == 0, jnp.full((1, 256), -1.0, F32), seg_f[:, 256:512])
    ids = jnp.concatenate([before, own], axis=1)
    for b in range(2):
        k_id = jnp.broadcast_to(ids[:, b * 256 : b * 256 + 512], (256, 512))
        q_id = jnp.broadcast_to(ids[:, 256 + b * 256 : 512 + b * 256], (512, 256)).T
        q_pos = lax.broadcasted_iota(jnp.int32, (256, 512), 0) + 256
        k_pos = lax.broadcasted_iota(jnp.int32, (256, 512), 1)
        BIAS[b] = jnp.where((q_id == k_id) & (k_pos <= q_pos), 0.0, NEGATIVE)

    @pl.when(c == 0)
    def _():
        K[0:256, :] = jnp.zeros((256, 256), BF)
        V[0:256, :] = jnp.zeros((256, 256), BF)

    for g in ga:
        g()
    gx[2]()
    for t in range(4):
        v = X[t * 128 : t * 128 + 128, :].astype(F32)
        scale = lax.rsqrt(jnp.mean(v * v, axis=1, keepdims=True) + EPSILON)
        XN[t * 128 : t * 128 + 128, :] = (v * scale * NG1[...]).astype(BF)
    for r in rkv:
        r[2]()
    for r in rff:
        r[1]()
    rd[0]()
    gg[0]()
    for r in rkv:
        r[3]()
    K[256:768, :] = contract(XN[...], WQKV[:, 256:512], 1, 0).astype(BF)
    V[256:768, :] = contract(XN[...], WQKV[:, 512:768], 1, 0).astype(BF)
    hk = net.make(K.at[pl.ds(512, 256), :], K.at[pl.ds(0, 256), :], core_nb)
    hv = net.make(V.at[pl.ds(512, 256), :], V.at[pl.ds(0, 256), :], core_nb)
    net.start(hk, c == 0)
    net.start(hv, c == 0)
    rq[1]()
    rq[2]()
    Q[...] = (contract(XN[...], WQKV[:, 0:256], 1, 0).astype(BF) * 0.125).astype(BF)
    ro[1]()

    @pl.when(c == 1)
    def _():
        hk.wait_recv()
        hv.wait_recv()

    lane_id = lax.broadcasted_iota(jnp.int32, (1, 128), 1)
    head_mask = [jnp.where(lane_id < 64, 1.0, 0.0).astype(BF), jnp.where(lane_id < 64, 0.0, 1.0).astype(BF)]

    heads_at = lambda xx, yy, b: AF.at[pl.ds(b * 256, 256), lanes(2 * yy + xx)]
    a_x = [net.make(heads_at(x, y, b), heads_at(x, y, b), x_nb) for b in range(2)]
    a_y = [net.make(heads_at(x, y, b), heads_at(x, y, b), y_nb) for b in range(2)]
    a_far = (
        net.make(heads_at(1 - x, y, 0), heads_at(1 - x, y, 0), y_nb),
        net.make(heads_at(x, 1 - y, 1), heads_at(x, 1 - y, 1), x_nb),
    )
    base = (2 * y + x) * 256
    for b in range(2):
        for hp in range(2):
            cols = slice(hp * 128, hp * 128 + 128)
            q_b, k_b, v_b = Q[b * 256 : b * 256 + 256, cols], K[b * 256 : b * 256 + 512, cols], V[b * 256 : b * 256 + 512, cols]
            total = None
            for h in range(2):
                s = contract(q_b * head_mask[h], k_b, 1, 1) + BIAS[b]
                e = jnp.exp(s - jnp.max(s, axis=1, keepdims=True))
                p = e * (1.0 / jnp.sum(e, axis=1, keepdims=True))
                PM[b * 4 + hp * 2 + h] = p
                part = contract(p.astype(BF), v_b * head_mask[h], 1, 0)
                total = part if total is None else total + part
            AF[b * 256 : b * 256 + 256, pl.ds(pl.multiple_of(base + hp * 128, 128), 128)] = total.astype(BF)
        net.start(a_x[b])
        net.start(a_y[b])
    for r in rff:
        r[2]()
    rd[1]()
    ro[2]()
    a_x[0].wait_recv()
    net.start(a_far[0])
    a_y[1].wait_recv()
    net.start(a_far[1])
    gg[1]()

    j = 2 * x + y
    shard = lambda buf, jj: buf.at[rows(jj, 128), :]

    def half(jj, h):
        return pl.ds(pl.multiple_of(jj * 128 + h * 64, 64), 64)

    def reduce_start(k, p):
        part = PART.at[p]
        j_f, j_x, j_y = 2 * (1 - x) + 1 - y, 2 * (1 - x) + y, 2 * x + 1 - y
        a = [net.make(part.at[half(q, 0), :], RA.at[k, i], y_nb) for i, q in enumerate((j_f, j_y))]
        b = [net.make(part.at[half(q, 1), :], RB.at[k, i], x_nb) for i, q in enumerate((j_f, j_x))]
        sa, sb = net.make(S2.at[k, 0], R2.at[k, 0], x_nb), net.make(S2.at[k, 1], R2.at[k, 1], y_nb)
        for copy in (a[0], b[0], a[1], b[1]):
            copy.start()

        def mid():
            a[0].wait_recv()
            S2[k, 0] = (PART[p, half(j_x, 0), :].astype(F32) + RA[k, 0].astype(F32)).astype(BF)
            sa.start()
            b[0].wait_recv()
            S2[k, 1] = (PART[p, half(j_y, 1), :].astype(F32) + RB[k, 0].astype(F32)).astype(BF)
            sb.start()

        def end():
            a[1].wait_recv()
            b[1].wait_recv()
            sa.wait_recv()
            sb.wait_recv()
            for copy in (*a, *b, sa, sb):
                copy.wait_send()
            first = PART[p, half(j, 0), :].astype(F32) + RA[k, 1].astype(F32) + R2[k, 0].astype(F32)
            second = PART[p, half(j, 1), :].astype(F32) + RB[k, 1].astype(F32) + R2[k, 1].astype(F32)
            return jnp.concatenate([first, second], axis=0)

        return mid, end

    def gather_start(buf):
        piece = lambda jj, h: buf.at[half(jj, h), :]
        to_x = [net.make(piece(j, h), piece(j, h), x_nb) for h in range(2)]
        to_y = [net.make(piece(j, h), piece(j, h), y_nb) for h in range(2)]
        j_x, j_y = 2 * (1 - x) + y, 2 * x + 1 - y
        on_y, on_x = net.make(piece(j_x, 0), piece(j_x, 0), y_nb), net.make(piece(j_y, 1), piece(j_y, 1), x_nb)
        for copy in (to_x[0], to_y[1], to_x[1], to_y[0]):
            net.start(copy)

        def mid():
            to_x[0].wait_recv()
            net.start(on_y)
            to_y[1].wait_recv()
            net.start(on_x)

        def end():
            for copy in (to_x[1], to_y[0], on_x, on_y):
                copy.wait_recv()

        return mid, end

    def send_blocks(src, dst):
        base_r = net.take(4)
        waits = []
        for dx in range(2):
            for cc in range(2):
                xx = flip(x, dx)
                piece, place = src.at[:, lanes(2 * xx + cc)], dst.at[rows(j, 128), :]
                s = net.take()
                copy = pltpu.make_async_remote_copy(
                    src_ref=piece,
                    dst_ref=place,
                    send_sem=net.send.at[s],
                    recv_sem=net.recv.at[base_r + dx * 2 + y],
                    device_id=dev(z, xx, c, cc),
                    device_id_type=MESH,
                )
                if dx == 0:
                    here = (c == y) & (c == cc)
                    keep = local(piece, place)
                    pl.when(here)(keep.start)
                    net.start(copy, jnp.logical_not(here))
                    waits.append((keep, here))
                else:
                    net.start(copy)
        piece, place = src.at[:, pl.ds(0, 256)], dst.at[pl.ds(0, 128), :]
        arrivals = [
            (net.make(piece, place, core_nb, base_r + dx * 2 + yy), jnp.logical_not((c == y) & (y == yy)) if dx == 0 else None)
            for dx in range(2)
            for yy in range(2)
        ]

        def end():
            for keep, here in waits:
                pl.when(here)(keep.wait)
            for got, when in arrivals:
                if when is None:
                    got.wait_recv()
                else:
                    pl.when(when)(got.wait_recv)

        return end

    def along_z(bufs, dst):
        GB, CR, ZR, RL, FF = bufs
        n_rows = CR.shape[1] // nz
        n = n_rows // 2
        part = lambda q, i: pl.ds(pl.multiple_of(q * n_rows + i * n, 16), n)
        own = lambda i: pl.ds(i * n, n)
        over = net.make(GB.at[1 - c], CR, core_nb)
        net.start(over)
        yield
        over.wait_recv()
        for xx in range(2):
            CR[xx] = (CR[xx].astype(F32) + GB[c, xx].astype(F32)).astype(BF)
        sites = [[net.take(nz - 1) for _ in range(2)] for _ in range(2)]
        for s in range(1, nz):
            for i in range(2):
                for way, to in ((0, z_up), (1, z_dn)):
                    zz = z if way == 0 else nz - 1 - z
                    q = nz - s + zz
                    q = q if way == 0 else nz - 1 - q
                    go = (zz < nz - 1) & (zz <= s - 1)
                    first, later = go & (zz == 0), go & (zz > 0)
                    site = sites[way][i] + s - 1
                    there = ZR.at[way, s - 1, :, own(i), :]
                    net.start(net.make(CR.at[:, part(q, i), :], there, to, site), first)
                    if s >= 2:
                        acc = ZR.at[way, s - 2, :, own(i), :]
                        got = net.make(acc, acc, to, site - 1)

                        @pl.when(later)
                        def _(got=got, acc=acc, q=q, i=i):
                            got.wait_recv()
                            acc[...] = (acc[...].astype(F32) + CR[:, part(q, i), :].astype(F32)).astype(BF)

                        net.start(net.make(acc, there, to, site), later)
            yield
        side = []
        for i in range(2):
            for way in range(2):
                zz = z if way == 0 else nz - 1 - z
                acc = ZR.at[way, nz - 2, :, own(i), :]
                pl.when(zz > 0)(net.make(acc, acc, z_up, sites[way][i] + nz - 2).wait_recv)
            total = lambda xx: (
                CR[xx, part(z, i), :].astype(F32)
                + ZR[0, nz - 2, xx, own(i), :].astype(F32)
                + ZR[1, nz - 2, xx, own(i), :].astype(F32)
            ).astype(BF)
            RL[own(i), :] = total(1 - x)
            side.append(net.make(RL.at[own(i), :], FF.at[z, x, own(i), :], x_nb))
            net.start(side[i])
            FF[z, x, own(i), :] = total(x)
        yield
        sites = [[net.take(nz - 1) for _ in range(2)] for _ in range(2)]
        here = lambda q, i: FF.at[q, :, own(i), :]
        for i in range(2):
            side[i].wait_recv()
            net.start(net.make(here(z, i), here(z, i), z_up, sites[0][i]), z < nz - 1)
            net.start(net.make(here(z, i), here(z, i), z_dn, sites[1][i]), z > 0)
        yield
        for s in range(2, nz + 1):
            for i in range(2):
                for way, to in ((0, z_up), (1, z_dn)):
                    zz = z if way == 0 else nz - 1 - z
                    q = z - (s - 1) if way == 0 else z + (s - 1)
                    have = zz >= s - 1
                    ref = here(q, i)
                    pl.when(have)(net.make(ref, ref, to, sites[way][i] + s - 2).wait_recv)
                    if s < nz:
                        net.start(net.make(ref, ref, to, sites[way][i] + s - 1), have & (zz < nz - 1))
            yield
        flush(FF, dst)
        yield

    def flush(buf, dst):
        copy = local(buf, dst)
        copy.start()
        flushes.append(copy)

    flushes = []
    over_cut = ff_half - ff_cut

    lines = []

    def begin(i, dst, wait):
        line = along_z(zbufs[i], dst)
        next(line)
        lines.append([line, wait])

    def tick(n=1):
        for _ in range(n):
            for line in lines:
                if line[1] > 0:
                    line[1] -= 1
                else:
                    next(line[0], None)

    ro[3]()
    for copy in (a_x[1], a_y[0], *a_far):
        copy.wait_recv()
    for t in range(4):
        tile = slice(t * 128, t * 128 + 128)
        res = X[tile, :].astype(F32) + contract(AF[tile, :], WO[...], 1, 0)
        RES[tile, :] = res
        scale = lax.rsqrt(jnp.mean(res * res, axis=1, keepdims=True) + EPSILON)
        HN[tile, :] = (res * scale * NG2[...]).astype(BF)
    for r in rff:
        r[3]()
    rd[2]()
    gg[2]()
    rd[3]()
    skip = (lax.broadcasted_iota(jnp.int32, (1, 256), 1) < over_cut) & (x == 1)
    for n in range(ff_half // 256):
        cols = slice(n * 256, n * 256 + 256)
        gate = contract(HN[...], WG[:, cols], 1, 0)
        up = contract(HN[...], WU[:, cols], 1, 0)
        dact = contract(G[...], WD[cols, :], 1, 1)
        sig = jax.nn.sigmoid(gate)
        silu = gate * sig
        act, dgate, dup = silu * up, dact * up * sig * (1.0 + gate * (1.0 - sig)), dact * silu
        if n == 0:
            act, dgate, dup = (jnp.where(skip, 0.0, v) for v in (act, dgate, dup))
        ACT[:, cols] = act.astype(BF)
        DGA[:, cols] = dgate.astype(BF)
        DUP[:, cols] = dup.astype(BF)
    blocks = lambda i, f: [zbufs[i][0].__setitem__((r % 2, r // 2), f(slice(r * 256, r * 256 + 256)).astype(BF)) for r in range(4)]
    blocks(0, lambda cols: contract(ACT[...], G[:, cols], 0, 0))
    begin(0, fd, 0)
    blocks(1, lambda cols: contract(HN[:, cols], DGA[...], 0, 0))
    tick()
    begin(1, fg, 3)
    for n in range(4):
        cols = slice(n * 256, n * 256 + 256)
        PART[0, :, cols] = (contract(DGA[...], WG[cols, :], 1, 1) + contract(DUP[...], WU[cols, :], 1, 1)).astype(BF)
    hid = reduce_start(0, 0)
    blocks(2, lambda cols: contract(HN[:, cols], DUP[...], 0, 0))
    begin(2, fu, 7)
    tick()
    for n in range(4):
        cols = slice(n * 256, n * 256 + 256)
        PART[1, :, cols] = contract(ACT[...], WD[:, cols], 1, 0).astype(BF)
    hid[0]()
    tick()
    dh = hid[1]()
    res = RES[rows(j, 128), :]
    scale = lax.rsqrt(jnp.mean(res * res, axis=1, keepdims=True) + EPSILON)
    w = dh * NG2[...]
    inner = jnp.mean(w * res, axis=1, keepdims=True)
    dres = G[rows(j, 128), :].astype(F32) + scale * w - res * (scale * scale * scale * inner)
    DRES[...] = dres
    GP[...] = jnp.zeros_like(GP)
    GP[1:2, :] = jnp.sum(dh * res * scale, axis=0, keepdims=True)
    DB[rows(j, 128), :] = dres.astype(BF)
    dbg = gather_start(DB)
    tick()
    dbg[0]()
    fin = reduce_start(1, 1)
    tick()
    dbg[1]()

    DAT[...] = contract(DB[...], WO[pl.ds(pl.multiple_of(base, 256), 256), :], 1, 1).astype(BF)
    own_heads = AF[:, pl.ds(pl.multiple_of(base, 256), 256)]
    blocks(3, lambda cols: contract(own_heads, DB[:, cols], 0, 0))
    begin(3, fo, 8)
    fin[0]()
    tick()
    DK[...] = jnp.zeros_like(DK)
    DV[...] = jnp.zeros_like(DV)

    def attend_back(b, carry):
        qs, ks = pl.ds(pl.multiple_of(b * 256, 256), 256), pl.ds(pl.multiple_of(b * 256, 256), 512)
        for hp in range(2):
            cols = slice(hp * 128, hp * 128 + 128)
            q_b, k_b, v_b, d_b = Q[qs, cols], K[ks, cols], V[ks, cols], DAT[qs, cols]
            dq = dk = dv = None
            for h in range(2):
                m = head_mask[h]
                d_h = d_b * m
                p = PM[b * 4 + hp * 2 + h]
                dp = contract(d_h, v_b, 1, 1)
                ds = (p * (dp - jnp.sum(p * dp, axis=1, keepdims=True))).astype(BF)
                one = (contract(ds, k_b * m, 1, 0), contract(ds, q_b * m, 0, 0), contract(p.astype(BF), d_h, 0, 0))
                dq, dk, dv = one if dq is None else (dq + one[0], dk + one[1], dv + one[2])
            DQKV[qs, cols] = (dq * 0.125).astype(BF)
            DK[ks, cols] += dk
            DV[ks, cols] += dv
        return carry

    lax.fori_loop(0, 2, attend_back, 0)
    HS[:, 0:256] = DK[0:256, :].astype(BF)
    HS[:, 256:512] = DV[0:256, :].astype(BF)
    back = net.make(HS, HR, core_nb)
    net.start(back, c == 1)
    tick()
    OS[...] = (RES[rows(j, 128), :] + fin[1]()).astype(BF)
    sent = send_blocks(OS, out)

    @pl.when(c == 0)
    def _():
        back.wait_recv()
        DK[512:768, :] += HR[:, 0:256].astype(F32)
        DV[512:768, :] += HR[:, 256:512].astype(F32)

    DQKV[:, 256:512] = DK[256:768, :].astype(BF)
    DQKV[:, 512:768] = DV[256:768, :].astype(BF)
    blocks(4, lambda cols: contract(XN[:, cols], DQKV[...], 0, 0))
    begin(4, fq, 4)
    for n in range(4):
        cols = slice(n * 256, n * 256 + 256)
        PART[0, :, cols] = contract(DQKV[...], WQKV[cols, :], 1, 1).astype(BF)
    last = reduce_start(2, 0)
    tick()
    last[0]()
    tick()
    dx = last[1]()
    v = X[rows(j, 128), :].astype(F32)
    scale = lax.rsqrt(jnp.mean(v * v, axis=1, keepdims=True) + EPSILON)
    w = dx * NG1[...]
    inner = jnp.mean(w * v, axis=1, keepdims=True)
    GS[...] = DRES[...] + scale * w - v * (scale * scale * scale * inner)
    GP[0:1, :] = jnp.sum(dx * v * scale, axis=0, keepdims=True)
    sent_in = send_blocks(GS, gin)

    me = 4 * x + 2 * y + c
    got = []
    for d in range(1, NPLANE):
        xx, yy, cc = flip(x, d & 1), flip(y, d & 2), flip(c, d & 4)
        copy = net.make(GP.at[:, lanes(2 * xx + cc)], GR.at[me], dev(z, xx, yy, cc))
        net.start(copy)
        got.append(copy)
    keep = local(GP.at[:, lanes(row)], GR.at[me])
    keep.start()
    tick()
    keep.wait()
    for copy in got:
        copy.wait_recv()
    total = GR[0]
    for d in range(1, NPLANE):
        total = total + GR[d]
    GZS[...] = total
    got = []
    for d in range(1, nz):
        copy = net.make(GZS, GZ.at[z], dev((z + d) % nz, x, y, c))
        net.start(copy)
        got.append(copy)
    keep = local(GZS, GZ.at[z])
    keep.start()
    tick(2)
    keep.wait()
    for copy in got:
        copy.wait_recv()
    total = GZ[0]
    for d in range(1, nz):
        total = total + GZ[d]
    gains[...] = total
    tick()
    tick()
    tick()
    tick()
    tick()
    tick()
    tick()
    tick()
    tick()
    tick()
    tick()
    tick()
    tick(20)
    sent()
    sent_in()
    for copy in flushes:
        copy.wait()
    net.finish()


def spread_kernel(nz, ff_half, ff_cut, fd, fg, fu, fo, fq, out_in, gin_in, gains, *refs):
    out, gin, gn1, gwq, gwk, gwv, gwo, gn2, gwg, gwu, gwd = refs[:11]
    ID, IG, IU, IO, IQ, OD, OG, OU, OO, OQ, sem, sem_out = refs[11:]
    over_cut = ff_half - ff_cut
    passed = [pltpu.make_async_copy(a, b, sem_out.at[i]) for i, (a, b) in enumerate(((out_in, out), (gin_in, gin)))]
    loads = [pltpu.make_async_copy(a, b, sem.at[i]) for i, (a, b) in enumerate(((fd, ID), (fg, IG), (fu, IU), (fo, IO), (fq, IQ)))]
    for copy in (*loads, *passed):
        copy.start()
    stores = []

    def store(buf, dst):
        stores.append(pltpu.make_async_copy(buf, dst, sem_out.at[2 + len(stores)]))
        stores[-1].start()

    gn1[...] = gains[0:1, :]
    gn2[...] = gains[1:2, :]
    loads[0].wait()
    n = ff_half // nz
    for q in range(nz):
        OD[q * n : q * n + n, :] = ID[q, 0].astype(F32)
        skip = max(0, min(n, over_cut - q * n))
        if skip < n:
            OD[ff_cut + q * n + skip : ff_cut + q * n + n, :] = ID[q, 1, skip:, :].astype(F32)
    store(OD, gwd)
    for k, (I, O, dst) in enumerate(((IG, OG, gwg), (IU, OU, gwu))):
        loads[1 + k].wait()
        for q in range(nz):
            O[q * 64 : q * 64 + 64, 0:ff_half] = I[q, 0].astype(F32)
            O[q * 64 : q * 64 + 64, ff_half:] = I[q, 1, :, over_cut:].astype(F32)
        store(O, dst)
    loads[3].wait()
    for q in range(nz):
        for xx in range(2):
            OO[xx * 256 + q * 64 : xx * 256 + q * 64 + 64, :] = IO[q, xx].astype(F32)
    store(OO, gwo)
    loads[4].wait()
    for i, dst in enumerate((gwq, gwk, gwv)):
        for q in range(nz):
            for xx in range(2):
                OQ[i, q * 64 : q * 64 + 64, xx * 256 : xx * 256 + 256] = IQ[q, xx, :, i * 256 : i * 256 + 256].astype(F32)
        store(OQ.at[i], dst)
    for copy in (*passed, *stores):
        copy.wait()


def fused(nz, tokens, cotangent, seg_ids, norm_one, wq, wk, wv, wo, norm_two, w_gate, w_up, w_down):
    ff = w_gate.shape[1]
    ff_half = -(-ff // 512) * 256
    ff_cut = ff - ff_half
    vm = pltpu.VMEM
    zshapes = [(ff_half, 256), (256, ff_half), (256, ff_half), (256, 256), (256, 768)]
    zscratch, fshapes = [], []
    for rows, cols in zshapes:
        fshapes.append((nz, 2, rows // nz, cols))
        zscratch += [
            vm((2, 2, rows, cols), BF),
            vm((2, rows, cols), BF),
            vm((2, nz - 1, 2, rows // nz, cols), BF),
            vm((rows // nz, cols), BF),
            vm(fshapes[-1], BF),
        ]
    scratch = [
        vm((512, D), BF), vm((512, D), BF), vm((D, 768), BF), vm((D, D), BF),
        vm((D, ff_half), BF), vm((D, ff_half), BF), vm((ff_half, D), BF), vm((1, D), F32), vm((1, D), F32),
        vm((512, D), BF), vm((512, 256), BF), vm((768, 256), BF), vm((768, 256), BF), vm((2, 256, 512), F32),
        vm((8, 256, 512), F32), vm((512, D), BF),
        vm((2, 512, D), BF), vm((3, 2, 64, D), BF), vm((3, 2, 64, D), BF), vm((3, 2, 64, D), BF), vm((3, 2, 64, D), BF),
        vm((512, D), BF), vm((512, D), F32), vm((128, D), F32), vm((512, ff_half), BF), vm((512, ff_half), BF),
        vm((512, ff_half), BF), vm((512, D), BF), vm((512, 256), BF),
        vm((768, 256), F32), vm((768, 256), F32), vm((512, 768), BF), vm((256, 512), BF), vm((256, 512), BF),
        vm((128, D), BF), vm((128, D), F32), vm((8, D), F32), vm((8, 8, 256), F32), vm((nz, 8, 256), F32), vm((8, 256), F32),
        *zscratch,
        pltpu.SemaphoreType.DMA((280,)), pltpu.SemaphoreType.DMA((280,)), pltpu.SemaphoreType.DMA((40,)),
    ]
    hbm, vmem = pl.BlockSpec(memory_space=pl.ANY), pl.BlockSpec(memory_space=pltpu.VMEM)
    sds = jax.ShapeDtypeStruct
    done = pl.pallas_call(
        functools.partial(layer_kernel, nz, ff_half, ff_cut),
        out_shape=(sds((512, 256), BF), sds((512, 256), F32), sds((8, 256), F32), *(sds(f, BF) for f in fshapes)),
        in_specs=[hbm, hbm, vmem, vmem, hbm, hbm, hbm, hbm, vmem, hbm, hbm, hbm],
        out_specs=(hbm, hbm, vmem, *(hbm for f in fshapes)),
        scratch_shapes=scratch,
        compiler_params=pltpu.CompilerParams(collective_id=0, has_side_effects=True, vmem_limit_bytes=62 << 20),
        name="layer",
    )(
        tokens, cotangent, seg_ids, norm_one[None], wq, wk, wv, wo, norm_two[None], w_gate, w_up, w_down,
    )
    out, gin, gains, *sums = done
    grads = (
        sds((512, 256), BF), sds((512, 256), F32), sds((1, 256), F32),
        sds((256, 512), F32), sds((256, 512), F32), sds((256, 512), F32), sds((512, 256), F32),
        sds((1, 256), F32), sds((256, ff), F32), sds((256, ff), F32), sds((ff, 256), F32),
    )
    res = pl.pallas_call(
        functools.partial(spread_kernel, nz, ff_half, ff_cut),
        out_shape=grads,
        in_specs=[hbm] * 7 + [vmem],
        out_specs=tuple(vmem if i in (2, 7) else hbm for i in range(11)),
        scratch_shapes=[vm(f, BF) for f in fshapes]
        + [vm((ff, 256), F32), vm((256, ff), F32), vm((256, ff), F32), vm((512, 256), F32), vm((3, 256, 512), F32)]
        + [pltpu.SemaphoreType.DMA((5,)), pltpu.SemaphoreType.DMA((9,))],
        compiler_params=pltpu.CompilerParams(vmem_limit_bytes=32 << 20),
        name="spread",
    )(*sums, out, gin, gains)
    res = list(res)
    res[2], res[7] = res[2][0], res[7][0]
    return tuple(res)


def solution(mesh):
    in_specs = (
        P(("dp", "col"), "row"),
        P(("dp", "col"), "row"),
        P("dp", None),
        P("row"),
        P("row", "col"),
        P("row", "col"),
        P("row", "col"),
        P("col", "row"),
        P("row"),
        P("row", "col"),
        P("row", "col"),
        P("col", "row"),
    )
    out_specs = (
        P(("dp", "col"), "row"),
        P(("dp", "col"), "row"),
        P("row"),
        P("row", "col"),
        P("row", "col"),
        P("row", "col"),
        P("col", "row"),
        P("row"),
        P("row", "col"),
        P("row", "col"),
        P("col", "row"),
    )
    sizes = dict(mesh.shape)
    body = per_device
    if sizes["row"] == 4 and sizes["col"] == 2:
        body = functools.partial(fused, sizes["dp"])
    return jax.shard_map(
        body, mesh=mesh, in_specs=in_specs, out_specs=out_specs, check_vma=False
    )
```

```python
import functools

import jax
import jax.numpy as jnp
from jax import lax
from jax.experimental import pallas as pl
from jax.experimental.pallas import tpu as pltpu
from jax.sharding import PartitionSpec as P

D = 1024
HEAD_DIM = 64


EPSILON = 1e-05
NEGATIVE = -1e30


def for_sending(array):

    def short(part):
        return part.astype(jnp.bfloat16) if part.dtype == jnp.float32 else part

    return jax.tree.map(short, array)


def shifted(block, axis, distance):
    devices = range(lax.axis_size(axis))
    route = [(i - distance, i) for i in devices if i - distance in devices]
    return lax.ppermute(block, axis, route)


def matmul(first_op, second_op):
    return jnp.dot(first_op, second_op, preferred_element_type=jnp.float32)


def matmul_tn(first_op, second_op):
    return lax.dot_general(
        first_op, second_op, (((0,), (0,)), ((), ())), preferred_element_type=jnp.float32
    )


def matmul_nt(first_op, second_op):
    return lax.dot_general(
        first_op, second_op, (((1,), (1,)), ((), ())), preferred_element_type=jnp.float32
    )


def tokens_col(array_in):
    return lax.all_gather(array_in, "col", axis=0, tiled=True)


def tokens_row(array_in):
    return lax.all_gather(for_sending(array_in), "row", axis=0, tiled=True).astype(array_in.dtype)


def summed_row(array_in):
    return lax.psum_scatter(
        array_in.astype(jnp.bfloat16), "row", scatter_dimension=0, tiled=True
    ).astype(jnp.float32)


def summed_col(array_in):
    return lax.psum_scatter(
        array_in.astype(jnp.bfloat16), "col", scatter_dimension=0, tiled=True
    ).astype(jnp.float32)


def feature_total(array_in):
    return lax.psum(array_in, "row")


def window_parts(queries, keys_all, ids_ext, offset, head_cols):
    t_local = queries.shape[0]
    block_rows = min(512, t_local)
    key_reach = min(2048, t_local)
    window = key_reach + block_rows
    head_count = head_cols // HEAD_DIM
    anchor = offset + t_local - key_reach
    q_blk = lax.dynamic_slice_in_dim(queries, offset, block_rows, 0).reshape(
        block_rows, head_count, HEAD_DIM
    )
    k_win = lax.dynamic_slice_in_dim(keys_all, anchor, window, 0)
    k_blk = k_win[:, :head_cols].reshape(window, head_count, HEAD_DIM)
    v_blk = k_win[:, head_cols:].reshape(window, head_count, HEAD_DIM)
    q_ids = lax.dynamic_slice_in_dim(ids_ext, offset + t_local, block_rows, 0)
    k_ids = lax.dynamic_slice_in_dim(ids_ext, anchor, window, 0)
    q_pos = offset + lax.iota(jnp.int32, block_rows)
    k_pos = offset - key_reach + lax.iota(jnp.int32, window)
    allowed = (q_ids[:, None] == k_ids[None, :]) & (k_pos[None, :] <= q_pos[:, None])
    scores = jnp.einsum(
        "qhd,khd->hqk", q_blk, k_blk, preferred_element_type=jnp.float32
    ) * HEAD_DIM ** (-0.5)
    scores = jnp.where(allowed[None], scores, NEGATIVE)
    return (q_blk, k_blk, v_blk, scores)


def forward(tokens, seg_ids, norm_one, wq, wk, wv, wo, norm_two, w_gate, w_up, w_down):
    token_vals = tokens.astype(jnp.float32)
    scale_one = lax.rsqrt(feature_total(jnp.sum(token_vals * token_vals, axis=1)) / D + EPSILON)
    normed = (token_vals * scale_one[:, None] * norm_one).astype(jnp.bfloat16)
    normed_all = tokens_col(normed)
    w_qkv = jnp.concatenate([wq, wk, wv], axis=1)
    head_cols = wq.shape[1]
    qkv = summed_row(matmul(normed_all, w_qkv)).astype(jnp.bfloat16)
    queries = qkv[:, :head_cols]
    kv_local = qkv[:, head_cols:]
    prior_keys = shifted(kv_local, "row", 1)
    keys_all = jnp.concatenate([prior_keys, kv_local], axis=0)
    t_local = queries.shape[0]
    block_rows = min(512, t_local)
    padded_ids = jnp.concatenate([jnp.full((t_local,), -1, jnp.int32), seg_ids[0]])
    ids_ext = lax.dynamic_slice_in_dim(padded_ids, lax.axis_index("row") * t_local, 2 * t_local, 0)

    def attend(offset):
        q_blk, k_blk, v_blk, scores = window_parts(queries, keys_all, ids_ext, offset, head_cols)
        row_max = jnp.max(scores, axis=2, keepdims=True)
        exp_total = jnp.sum(jnp.exp(scores - row_max), axis=2, keepdims=True)
        log_total = row_max + jnp.log(exp_total)
        prob_low = jnp.exp(scores - log_total).astype(jnp.bfloat16)
        mixed_out = jnp.einsum("hqk,khd->qhd", prob_low, v_blk, preferred_element_type=jnp.float32)
        return (mixed_out.reshape(block_rows, head_cols).astype(jnp.bfloat16), log_total[:, :, 0])

    offsets = lax.iota(jnp.int32, t_local // block_rows) * block_rows
    pieces, log_totals = lax.map(attend, offsets)
    attn_out = pieces.reshape(t_local, head_cols)
    attn_all = tokens_row(attn_out)
    residual = token_vals + summed_col(matmul(attn_all, wo))
    stored = {
        "token_vals": token_vals,
        "scale_one": scale_one,
        "normed_all": normed_all,
        "queries": queries,
        "keys_all": keys_all,
        "ids_ext": ids_ext,
        "log_totals": log_totals,
        "attn_all": attn_all,
        "offsets": offsets,
    }
    f_col = w_gate.shape[1]
    scale_two = lax.rsqrt(feature_total(jnp.sum(residual * residual, axis=1)) / D + EPSILON)
    hidden_in = (residual * scale_two[:, None] * norm_two).astype(jnp.bfloat16)
    hidden_all = tokens_col(hidden_in)
    w_pair = jnp.concatenate([w_gate, w_up], axis=1)
    pair_sum = summed_row(matmul(hidden_all, w_pair))
    gate_pre = pair_sum[:, :f_col]
    up_pre = pair_sum[:, f_col:]
    act_low = (jax.nn.silu(gate_pre) * up_pre).astype(jnp.bfloat16)
    act_all = tokens_row(act_low)
    final_sum = residual + summed_col(matmul(act_all, w_down))
    stored.update(
        {
            "residual": residual,
            "scale_two": scale_two,
            "hidden_all": hidden_all,
            "gate_pre": gate_pre,
            "up_pre": up_pre,
            "act_all": act_all,
        }
    )
    return (final_sum.astype(jnp.bfloat16), stored)


def swiglu_grads(dact, gate_pre, up_pre):
    sigmoid_gate = jax.nn.sigmoid(gate_pre)
    gate_grad = (dact * up_pre * sigmoid_gate * (1.0 + gate_pre * (1.0 - sigmoid_gate))).astype(
        jnp.bfloat16
    )
    up_grad = (dact * gate_pre * sigmoid_gate).astype(jnp.bfloat16)
    return (gate_grad, up_grad)


def per_device(
    tokens, cotangent, seg_ids, norm_one, wq, wk, wv, wo, norm_two, w_gate, w_up, w_down
):
    weights = (tokens, seg_ids, norm_one, wq, wk, wv, wo, norm_two, w_gate, w_up, w_down)
    output, stored = forward(*weights)
    f_col = w_gate.shape[1]
    grad_out = cotangent.astype(jnp.float32)
    grad_all = tokens_col(cotangent)
    dact = summed_row(matmul_nt(grad_all, w_down))
    grad_down = matmul_tn(stored["act_all"], grad_all)
    gate_grad, up_grad = swiglu_grads(dact, stored["gate_pre"], stored["up_pre"])
    dpair = jnp.concatenate([gate_grad, up_grad], axis=1)
    dpair_all = tokens_row(dpair)
    w_pair = jnp.concatenate([w_gate, w_up], axis=1)
    dhidden = summed_col(matmul_nt(dpair_all, w_pair))
    grad_pair = matmul_tn(stored["hidden_all"], dpair_all)
    grad_gate = grad_pair[:, :f_col]
    grad_up = grad_pair[:, f_col:]
    residual = stored["residual"]
    scale_two = stored["scale_two"]
    weighted = dhidden * norm_two
    inner_sum = feature_total(jnp.sum(weighted * residual, axis=1)) / D
    dresid = (
        grad_out + scale_two[:, None] * weighted - residual * (scale_two**3 * inner_sum)[:, None]
    )
    grad_norm_two = jnp.sum(dhidden * residual * scale_two[:, None], axis=0)
    dbranch = dresid.astype(jnp.bfloat16)
    dbranch_all = tokens_col(dbranch)
    attn_grad = summed_row(matmul_nt(dbranch_all, wo)).astype(jnp.bfloat16)
    grad_wo = matmul_tn(stored["attn_all"], dbranch_all)
    queries = stored["queries"]
    keys_all = stored["keys_all"]
    ids_ext = stored["ids_ext"]
    head_cols = wq.shape[1]
    head_count = head_cols // HEAD_DIM
    t_local = queries.shape[0]
    block_rows = min(512, t_local)
    key_reach = min(2048, t_local)
    window = key_reach + block_rows
    inv_root = HEAD_DIM ** (-0.5)

    def attend_back(accum_dkv, inputs):
        offset, log_total = inputs
        q_blk, k_blk, v_blk, scores = window_parts(queries, keys_all, ids_ext, offset, head_cols)
        prob_full = jnp.exp(scores - log_total[:, :, None])
        prob_low = prob_full.astype(jnp.bfloat16)
        d_blk = lax.dynamic_slice_in_dim(attn_grad, offset, block_rows, 0).reshape(
            block_rows, head_count, HEAD_DIM
        )
        dprobs = jnp.einsum("qhd,khd->hqk", d_blk, v_blk, preferred_element_type=jnp.float32)
        dvalue = jnp.einsum("hqk,qhd->khd", prob_low, d_blk, preferred_element_type=jnp.float32)
        center = jnp.sum(prob_full * dprobs, axis=2, keepdims=True)
        dscores = (prob_full * (dprobs - center)).astype(jnp.bfloat16)
        dquery = (
            jnp.einsum("hqk,khd->qhd", dscores, k_blk, preferred_element_type=jnp.float32)
            * inv_root
        )
        dkey = (
            jnp.einsum("hqk,qhd->khd", dscores, q_blk, preferred_element_type=jnp.float32)
            * inv_root
        )
        update = jnp.concatenate(
            [dkey.reshape(window, head_cols), dvalue.reshape(window, head_cols)], axis=1
        )
        anchor = offset + t_local - key_reach
        current = lax.dynamic_slice_in_dim(accum_dkv, anchor, window, 0)
        accum_dkv = lax.dynamic_update_slice_in_dim(accum_dkv, current + update, anchor, 0)
        return (accum_dkv, dquery.reshape(block_rows, head_cols))

    start_grads = jnp.zeros((2 * t_local, 2 * head_cols), jnp.float32)
    accum_dkv, query_grads = lax.scan(
        attend_back, start_grads, (stored["offsets"], stored["log_totals"])
    )
    returned = shifted(accum_dkv[:t_local].astype(jnp.bfloat16), "row", -1).astype(jnp.float32)
    key_grads = accum_dkv[t_local:] + returned
    dqkv = jnp.concatenate([query_grads.reshape(t_local, head_cols), key_grads], axis=1).astype(
        jnp.bfloat16
    )
    dqkv_all = tokens_row(dqkv)
    w_qkv = jnp.concatenate([wq, wk, wv], axis=1)
    dnormed = summed_col(matmul_nt(dqkv_all, w_qkv))
    grad_qkv = matmul_tn(stored["normed_all"], dqkv_all)
    grad_wq = grad_qkv[:, :head_cols]
    grad_wk = grad_qkv[:, head_cols : 2 * head_cols]
    grad_wv = grad_qkv[:, 2 * head_cols :]
    token_vals = stored["token_vals"]
    scale_one = stored["scale_one"]
    weighted_one = dnormed * norm_one
    inner_one = feature_total(jnp.sum(weighted_one * token_vals, axis=1)) / D
    grad_input = (
        dresid
        + scale_one[:, None] * weighted_one
        - token_vals * (scale_one**3 * inner_one)[:, None]
    )
    grad_norm_one = jnp.sum(dnormed * token_vals * scale_one[:, None], axis=0)
    grad_sums = (
        lax.psum(grad_wq.astype(jnp.bfloat16), "dp").astype(jnp.float32),
        lax.psum(grad_wk.astype(jnp.bfloat16), "dp").astype(jnp.float32),
        lax.psum(grad_wv.astype(jnp.bfloat16), "dp").astype(jnp.float32),
        lax.psum(grad_wo.astype(jnp.bfloat16), "dp").astype(jnp.float32),
        lax.psum(grad_gate.astype(jnp.bfloat16), "dp").astype(jnp.float32),
        lax.psum(grad_up.astype(jnp.bfloat16), "dp").astype(jnp.float32),
        lax.psum(grad_down.astype(jnp.bfloat16), "dp").astype(jnp.float32),
    )
    gain_sums = lax.psum((grad_norm_one, grad_norm_two), ("dp", "col"))
    return (
        output,
        grad_input,
        gain_sums[0],
        grad_sums[0],
        grad_sums[1],
        grad_sums[2],
        grad_sums[3],
        gain_sums[1],
        grad_sums[4],
        grad_sums[5],
        grad_sums[6],
    )


MESH = pl.DeviceIdType.MESH
BF = jnp.bfloat16
F32 = jnp.float32
NPLANE = 8
FWAIT, OWAIT, QWAIT = (0, 4, 8), 6, 2


def contract(a, b, ca, cb):
    return lax.dot_general(a, b, (((ca,), (cb,)), ((), ())), preferred_element_type=F32)


class Copies:
    def __init__(self, send, recv):
        self.send, self.recv, self.used, self.kept, self.open = send, recv, 0, 1, []

    def take(self, amount=1):
        base = self.used
        self.used += amount
        return base

    def make(self, src, dst, to, site=None, own=False):
        site = self.take() if site is None else site
        self.kept += own
        return pltpu.make_async_remote_copy(
            src_ref=src,
            dst_ref=dst,
            send_sem=self.send.at[self.kept - 1 if own else 0],
            recv_sem=self.recv.at[site],
            device_id=to,
            device_id_type=MESH,
        )

    def start(self, copy, when=None):
        self.open.append((copy, when))
        if when is None:
            copy.start()
        else:
            pl.when(when)(copy.start)

    def finish(self):
        for copy, when in self.open:
            if when is None:
                copy.wait_send()
            else:
                pl.when(when)(copy.wait_send)
        self.open = []


def layer_kernel(nz, ff_half, ff_cut, *refs):
    it = iter(refs)
    take = lambda n: [next(it) for _ in range(n)]
    tok, cot, seg, n1, wq, wk, wv, wo, n2, wg, wu, wd = take(12)
    out, gin, gains, f0, f1, f2, fo, fq = take(8)
    X, G, WQKV, WO, WG, WU, WD, NG1, NG2 = take(9)
    XN, Q, K, V, BIAS, PM, AF = take(7)
    PART, RX = take(2)
    HN, RES, DRES, ACT, DGA, DUP, DB, DAT, BYG, BYU = take(10)
    DK, DV, DQKV, HS, HR = take(5)
    OS, GS, GP, GR, GZ, GZS = take(6)
    zbufs = [take(5) for _ in range(5)]
    send, recv, loc = take(3)

    z, row, y = lax.axis_index("dp"), lax.axis_index("row"), lax.axis_index("col")
    x, c = row // 2, row % 2
    net = Copies(send, recv)
    nloc = [0]

    def local(src, dst):
        nloc[0] += 1
        return pltpu.make_async_copy(src, dst, loc.at[nloc[0] - 1])

    def dev(zz, xx, yy, cc):
        return (zz, 2 * xx + cc, yy)

    core_nb, x_nb, y_nb = dev(z, x, y, 1 - c), dev(z, 1 - x, y, c), dev(z, x, 1 - y, c)
    z_up, z_dn = dev(z + 1, x, y, c), dev(z - 1, x, y, c)
    lanes = lambda i, n=256: pl.ds(pl.multiple_of(i * n, 128), n)
    rows = lambda i, n: pl.ds(pl.multiple_of(i * n, n if n % 16 else 16), n)
    flip = lambda v, bit: 1 - v if bit else v

    barrier = pltpu.get_barrier_semaphore()
    for d in range(1, NPLANE):
        pl.semaphore_signal(
            barrier, inc=1, device_id=dev(z, flip(x, d & 1), flip(y, d & 2), flip(c, d & 4)), device_id_type=MESH
        )
    for d in range(1, nz):
        pl.semaphore_signal(barrier, inc=1, device_id=dev((z + d) % nz, x, y, c), device_id_type=MESH)
    for _, _, ZR, _, _ in zbufs:

        @pl.when(z == 0)
        def _(ZR=ZR):
            ZR[0, nz - 2] = jnp.zeros(ZR.shape[2:], BF)

        @pl.when(z == nz - 1)
        def _(ZR=ZR):
            ZR[1, nz - 2] = jnp.zeros(ZR.shape[2:], BF)

    seg_f = seg[...].astype(F32)
    own = jnp.where(c == 0, seg_f[:, :512], seg_f[:, 512:])
    before = jnp.where(c == 0, jnp.full((1, 256), -1.0, F32), seg_f[:, 256:512])
    ids = jnp.concatenate([before, own], axis=1)
    for b in range(2):
        k_id = jnp.broadcast_to(ids[:, b * 256 : b * 256 + 512], (256, 512))
        q_id = jnp.broadcast_to(ids[:, 256 + b * 256 : 512 + b * 256], (512, 256)).T
        q_pos = lax.broadcasted_iota(jnp.int32, (256, 512), 0) + 256
        k_pos = lax.broadcasted_iota(jnp.int32, (256, 512), 1)
        BIAS[b] = jnp.where((q_id == k_id) & (k_pos <= q_pos), 0.0, NEGATIVE)

    @pl.when(c == 0)
    def _():
        K[0:256, :] = jnp.zeros((256, 256), BF)
        V[0:256, :] = jnp.zeros((256, 256), BF)

    pl.semaphore_wait(barrier, NPLANE - 1 + nz - 1)

    def gather_tokens(src, buf):
        col = lambda rr: buf.at[:, lanes(rr)]
        mine = c == y
        other = jnp.logical_not(mine)
        keep = local(src, col(row))
        over = net.make(src, col(row), core_nb)
        bx, by = net.take(2), net.take(2)
        to_x = net.make(src, col(row), dev(z, 1 - x, y, y), bx + c)
        to_y = net.make(src, col(row), dev(z, x, 1 - y, y), by + c)
        far = 2 * (1 - x)
        by_y = net.make(col(far), col(far), y_nb)
        by_x = net.make(col(2 * x + 1), col(2 * x + 1), x_nb)
        got_x = [net.make(src, col(row), core_nb, bx + k) for k in range(2)]
        got_y = [net.make(src, col(row), core_nb, by + k) for k in range(2)]

        def start():
            pl.when(mine)(keep.start)
            net.start(to_x)
            net.start(to_y)
            net.start(over, other)

        def arrive():
            @pl.when(mine)
            def _():
                got_x[0].wait_recv()
                by_y.start()

            @pl.when(other)
            def _():
                got_y[1].wait_recv()
                by_x.start()

            net.open += [(by_y, mine), (by_x, other)]

        def rest():
            @pl.when(mine)
            def _():
                got_x[1].wait_recv()
                over.wait_recv()
                keep.wait()

            @pl.when(other)
            def _():
                got_y[0].wait_recv()
                by_y.wait_recv()
                by_x.wait_recv()

        return start, arrive, rest

    def relay(src_of, dst_of):
        keep = local(src_of(x), dst_of(row))
        across = net.make(src_of(x), dst_of(row), core_nb)
        far = net.make(src_of(1 - x), dst_of(row), x_nb)
        theirs = dst_of(2 * (1 - x) + c)
        fwd = net.make(theirs, theirs, core_nb)

        def start():
            keep.start()
            net.start(far)
            net.start(across)

        def arrive():
            far.wait_recv()
            net.start(fwd)

        def rest():
            keep.wait()
            across.wait_recv()
            fwd.wait_recv()

        return start, arrive, rest

    def z_gather(at):
        sites = (net.take(nz - 1), net.take(nz - 1))

        def step(s):
            for way, to in ((0, z_up), (1, z_dn)):
                zz = z if way == 0 else nz - 1 - z
                ref = at(z - s if way == 0 else z + s)
                have = zz >= s
                if s > 0:
                    pl.when(have)(net.make(ref, ref, to, sites[way] + s - 1).wait_recv)
                if s < nz - 1:
                    net.start(net.make(ref, ref, to, sites[way] + s), have & (zz < nz - 1))

        return step

    def relay_z(src_of, dst_of, n_rows):
        n = n_rows // nz
        keep = local(src_of(x, 0, n_rows), dst_of(row, 0, n_rows))
        across = net.make(src_of(x, 0, n_rows), dst_of(row, 0, n_rows), core_nb)
        far = net.make(src_of(1 - x, z * n, n), dst_of(row, z * n, n), x_nb)
        hop = z_gather(lambda q: dst_of(2 * (1 - x) + c, q * n, n))
        whole = dst_of(2 * (1 - x) + c, 0, n_rows)
        fwd = net.make(whole, whole, core_nb)

        def begin():
            net.start(far)
            keep.start()
            net.start(across)

        def step(s):
            if s == 0:
                far.wait_recv()
            hop(s)
            if s == nz - 1:
                net.start(fwd)

        def rest():
            keep.wait()
            across.wait_recv()
            fwd.wait_recv()

        return begin, step, rest

    def gather_wo():
        at = lambda yy, rr: WO.at[rows(yy, 512), lanes(rr)]
        keep = local(wo, at(y, row))
        across = net.make(wo, at(y, row), core_nb)
        to_x, to_y = net.make(wo, at(y, row), x_nb), net.make(wo, at(y, row), y_nb)
        rx = 2 * (1 - x) + c
        on_y = net.make(at(y, rx), at(y, rx), y_nb)
        others = (at(y, rx), at(1 - y, row), at(1 - y, rx))
        fwd = [net.make(ref, ref, core_nb) for ref in others]

        def start():
            net.start(to_x)
            net.start(to_y)
            keep.start()
            net.start(across)

        def arrive():
            to_x.wait_recv()
            net.start(on_y)
            net.start(fwd[0])

        def pass_on():
            to_y.wait_recv()
            net.start(fwd[1])
            on_y.wait_recv()
            net.start(fwd[2])

        def rest():
            keep.wait()
            across.wait_recv()
            for copy in fwd:
                copy.wait_recv()

        return start, arrive, pass_on, rest

    def gather_gain(src, dst):
        keep = local(src, dst.at[:, lanes(row)])
        keep.start()
        got = []
        for to in (core_nb, x_nb, dev(z, 1 - x, y, 1 - c)):
            got.append(net.make(src, dst.at[:, lanes(row)], to))
            net.start(got[-1])

        def rest():
            keep.wait()
            for g in got:
                g.wait_recv()

        return rest

    gx, gg = gather_tokens(tok, X), gather_tokens(cot, G)
    qkv_at = lambda rr, r0, n, i: WQKV.at[pl.ds(pl.multiple_of(rr * 256 + r0, 16), n), pl.ds(i * 256, 256)]
    rqkv = [
        relay_z(
            lambda xx, r0, n, w=w: w.at[pl.ds(pl.multiple_of(r0, 16), n), lanes(xx)],
            lambda rr, r0, n, i=i: qkv_at(rr, r0, n, i),
            256,
        )
        for i, w in ((1, wk), (2, wv), (0, wq))
    ]
    ro = gather_wo()
    cut = lambda xx: pl.multiple_of(xx * ff_cut, 128)
    rff = [
        relay_z(
            lambda xx, r0, n, w=w: w.at[pl.ds(pl.multiple_of(r0, 16), n), pl.ds(cut(xx), ff_half)],
            lambda rr, r0, n, W=W: W.at[pl.ds(pl.multiple_of(rr * 256 + r0, 16), n), :],
            256,
        )
        for w, W in ((wg, WG), (wu, WU))
    ]
    rd = relay_z(
        lambda xx, r0, n: wd.at[pl.ds(pl.multiple_of(xx * ff_cut + r0, 16), n), :],
        lambda rr, r0, n: WD.at[pl.ds(pl.multiple_of(r0, 16), n), lanes(rr)],
        ff_half,
    )
    for r in rqkv:
        r[0]()
    gx[0]()
    ga = [gather_gain(n1, NG1), gather_gain(n2, NG2)]
    for r in rqkv:
        r[1](0)
    gx[1]()
    for s in range(1, nz):
        for r in rqkv:
            r[1](s)
    for g in ga:
        g()
    gx[2]()
    for r in rff:
        r[0]()
    ro[0]()
    for t in range(4):
        v = X[t * 128 : t * 128 + 128, :].astype(F32)
        scale = lax.rsqrt(jnp.mean(v * v, axis=1, keepdims=True) + EPSILON)
        XN[t * 128 : t * 128 + 128, :] = (v * scale * NG1[...]).astype(BF)
    for r in rqkv:
        r[2]()
    K[256:768, :] = contract(XN[...], WQKV[:, 256:512], 1, 0).astype(BF)
    V[256:768, :] = contract(XN[...], WQKV[:, 512:768], 1, 0).astype(BF)
    hk = net.make(K.at[pl.ds(512, 256), :], K.at[pl.ds(0, 256), :], core_nb)
    hv = net.make(V.at[pl.ds(512, 256), :], V.at[pl.ds(0, 256), :], core_nb)
    net.start(hk, c == 0)
    net.start(hv, c == 0)
    Q[...] = (contract(XN[...], WQKV[:, 0:256], 1, 0).astype(BF) * 0.125).astype(BF)
    @pl.when(c == 1)
    def _():
        hk.wait_recv()
        hv.wait_recv()

    lane_id = lax.broadcasted_iota(jnp.int32, (1, 128), 1)
    head_mask = [jnp.where(lane_id < 64, 1.0, 0.0).astype(BF), jnp.where(lane_id < 64, 0.0, 1.0).astype(BF)]

    heads_at = lambda xx, yy, b: AF.at[pl.ds(b * 256, 256), lanes(2 * yy + xx)]
    a_x = [net.make(heads_at(x, y, b), heads_at(x, y, b), x_nb) for b in range(2)]
    a_y = [net.make(heads_at(x, y, b), heads_at(x, y, b), y_nb) for b in range(2)]
    a_far = (
        net.make(heads_at(1 - x, y, 0), heads_at(1 - x, y, 0), y_nb),
        net.make(heads_at(x, 1 - y, 1), heads_at(x, 1 - y, 1), x_nb),
    )
    base = (2 * y + x) * 256
    for b in range(2):
        for hp in range(2):
            cols = slice(hp * 128, hp * 128 + 128)
            q_b, k_b, v_b = Q[b * 256 : b * 256 + 256, cols], K[b * 256 : b * 256 + 512, cols], V[b * 256 : b * 256 + 512, cols]
            total = None
            for h in range(2):
                s = contract(q_b * head_mask[h], k_b, 1, 1) + BIAS[b]
                e = jnp.exp(s - jnp.max(s, axis=1, keepdims=True))
                p = e * (1.0 / jnp.sum(e, axis=1, keepdims=True))
                PM[b * 4 + hp * 2 + h] = p
                part = contract(p.astype(BF), v_b * head_mask[h], 1, 0)
                total = part if total is None else total + part
            AF[b * 256 : b * 256 + 256, pl.ds(pl.multiple_of(base + hp * 128, 128), 128)] = total.astype(BF)
        net.start(a_x[b])
        net.start(a_y[b])
        if b == 0:
            for r in rff:
                r[1](0)
    rd[0]()
    for r in rff:
        r[1](1)
    ro[1]()
    a_x[0].wait_recv()
    net.start(a_far[0])
    a_y[1].wait_recv()
    net.start(a_far[1])
    gg[0]()
    for r in rff:
        r[1](2)
    rd[1](0)
    ro[2]()
    for r in rff:
        r[1](3)
    rd[1](1)

    j = 2 * x + y
    shard = lambda buf, jj: buf.at[rows(jj, 128), :]

    peers = ((x_nb, 2 * (1 - x) + y), (y_nb, 2 * x + 1 - y), (dev(z, 1 - x, 1 - y, c), 2 * (1 - x) + 1 - y))

    def reduce_start(k, p):
        sent = [net.make(shard(PART.at[p], jj), RX.at[k, i], to, own=True) for i, (to, jj) in enumerate(peers)]
        for copy in (sent[2], sent[0], sent[1]):
            copy.start()

        def end():
            for copy in sent:
                copy.wait_recv()
            for copy in sent:
                copy.wait_send()
            total = PART[p, rows(j, 128), :].astype(F32)
            for i in range(3):
                total = total + RX[k, i].astype(F32)
            return total

        return end

    def gather_start(buf):
        sent = [net.make(shard(buf, j), shard(buf, j), to) for to, _ in peers]
        for copy in (sent[2], sent[0], sent[1]):
            net.start(copy)

        def end():
            for copy in sent:
                copy.wait_recv()

        return end

    def send_blocks(src, dst):
        base_r = net.take(4)
        waits = []
        for dx in range(2):
            for cc in range(2):
                xx = flip(x, dx)
                piece, place = src.at[:, lanes(2 * xx + cc)], dst.at[rows(j, 128), :]
                copy = pltpu.make_async_remote_copy(
                    src_ref=piece,
                    dst_ref=place,
                    send_sem=net.send.at[0],
                    recv_sem=net.recv.at[base_r + dx * 2 + y],
                    device_id=dev(z, xx, c, cc),
                    device_id_type=MESH,
                )
                if dx == 0:
                    here = (c == y) & (c == cc)
                    keep = local(piece, place)
                    pl.when(here)(keep.start)
                    net.start(copy, jnp.logical_not(here))
                    waits.append((keep, here))
                else:
                    net.start(copy)
        piece, place = src.at[:, pl.ds(0, 256)], dst.at[pl.ds(0, 128), :]
        arrivals = [
            (net.make(piece, place, core_nb, base_r + dx * 2 + yy), jnp.logical_not((c == y) & (y == yy)) if dx == 0 else None)
            for dx in range(2)
            for yy in range(2)
        ]

        def end():
            for keep, here in waits:
                pl.when(here)(keep.wait)
            for got, when in arrivals:
                if when is None:
                    got.wait_recv()
                else:
                    pl.when(when)(got.wait_recv)

        return end

    def along_z(tag, dst):
        GB, CR, ZR, RL, FF = zbufs[tag]
        n_rows = CR.shape[1] // nz
        n = n_rows // 2
        part = lambda q, i: pl.ds(pl.multiple_of(q * n_rows + i * n, 16), n)
        own = lambda i: pl.ds(i * n, n)
        over = net.make(GB.at[1 - c], CR, core_nb)
        net.start(over)
        yield
        over.wait_recv()
        for xx in range(2):
            CR[xx] = (CR[xx].astype(F32) + GB[c, xx].astype(F32)).astype(BF)
        sites = [[net.take(nz - 1) for _ in range(2)] for _ in range(2)]
        for s in range(1, nz):
            for i in range(2):
                for way, to in ((0, z_up), (1, z_dn)):
                    zz = z if way == 0 else nz - 1 - z
                    q = nz - s + zz
                    q = q if way == 0 else nz - 1 - q
                    go = (zz < nz - 1) & (zz <= s - 1)
                    first, later = go & (zz == 0), go & (zz > 0)
                    site = sites[way][i] + s - 1
                    there = ZR.at[way, s - 1, :, own(i), :]
                    net.start(net.make(CR.at[:, part(q, i), :], there, to, site), first)
                    if s >= 2:
                        acc = ZR.at[way, s - 2, :, own(i), :]
                        got = net.make(acc, acc, to, site - 1)

                        @pl.when(later)
                        def _(got=got, acc=acc, q=q, i=i):
                            got.wait_recv()
                            acc[...] = (acc[...].astype(F32) + CR[:, part(q, i), :].astype(F32)).astype(BF)

                        net.start(net.make(acc, there, to, site), later)
                yield
        side = []
        for i in range(2):
            for way in range(2):
                zz = z if way == 0 else nz - 1 - z
                acc = ZR.at[way, nz - 2, :, own(i), :]
                pl.when(zz > 0)(net.make(acc, acc, z_up, sites[way][i] + nz - 2).wait_recv)
            total = lambda xx: (
                CR[xx, part(z, i), :].astype(F32)
                + ZR[0, nz - 2, xx, own(i), :].astype(F32)
                + ZR[1, nz - 2, xx, own(i), :].astype(F32)
            ).astype(BF)
            RL[own(i), :] = total(1 - x)
            side.append(net.make(RL.at[own(i), :], FF.at[z, x, own(i), :], x_nb))
            net.start(side[i])
            FF[z, x, own(i), :] = total(x)
            yield
        sites = [[net.take(nz - 1) for _ in range(2)] for _ in range(2)]
        here = lambda q, i: FF.at[q, :, own(i), :]
        for i in range(2):
            side[i].wait_recv()
            net.start(net.make(here(z, i), here(z, i), z_up, sites[0][i]), z < nz - 1)
            net.start(net.make(here(z, i), here(z, i), z_dn, sites[1][i]), z > 0)
            yield
        for s in range(2, nz + 1):
            for i in range(2):
                for way, to in ((0, z_up), (1, z_dn)):
                    zz = z if way == 0 else nz - 1 - z
                    q = z - (s - 1) if way == 0 else z + (s - 1)
                    have = zz >= s - 1
                    ref = here(q, i)
                    pl.when(have)(net.make(ref, ref, to, sites[way][i] + s - 2).wait_recv)
                    if s < nz:
                        net.start(net.make(ref, ref, to, sites[way][i] + s - 1), have & (zz < nz - 1))
                yield
        flush(FF, dst)
        yield

    def flush(buf, dst):
        copy = local(buf, dst)
        copy.start()
        flushes.append(copy)

    flushes = []
    over_cut = ff_half - ff_cut

    lines = []

    def begin(i, dst, wait):
        line = along_z(i, dst)
        next(line)
        lines.append([line, wait])

    def tick(n=1):
        for _ in range(n):
            for _ in range(2):
                for line in lines:
                    if line[1] > 0:
                        line[1] -= 1
                    else:
                        next(line[0], None)

    ro[3]()
    for copy in (a_x[1], a_y[0], *a_far):
        copy.wait_recv()
    for t in range(4):
        tile = slice(t * 128, t * 128 + 128)
        res = X[tile, :].astype(F32) + contract(AF[tile, :], WO[...], 1, 0)
        RES[tile, :] = res
        scale = lax.rsqrt(jnp.mean(res * res, axis=1, keepdims=True) + EPSILON)
        HN[tile, :] = (res * scale * NG2[...]).astype(BF)
    rd[1](2)
    gg[1]()
    for r in rff:
        r[2]()
    skip = (lax.broadcasted_iota(jnp.int32, (1, 256), 1) < over_cut) & (x == 1)
    def tile_grads(n):
        cols = slice(n * 256, n * 256 + 256)
        GB = zbufs[n][0]
        for i, made in enumerate((DGA, DUP)):
            whole = contract(HN[...], made[:, cols], 0, 0)
            for r in range(4):
                GB[r % 2, r // 2, :, i * 256 : i * 256 + 256] = whole[r * 256 : r * 256 + 256].astype(BF)
        whole = contract(ACT[:, cols], G[...], 0, 0)
        for r in range(4):
            GB[r % 2, r // 2, :, 512:768] = whole[:, r * 256 : r * 256 + 256].astype(BF)
        begin(n, (f0, f1, f2)[n], FWAIT[n])

    for n in range(ff_half // 256):
        cols = slice(n * 256, n * 256 + 256)
        gate = contract(HN[...], WG[:, cols], 1, 0)
        up = contract(HN[...], WU[:, cols], 1, 0)
        sig = jax.nn.sigmoid(gate)
        silu = gate * sig
        act, by_gate = silu * up, up * sig * (1.0 + gate * (1.0 - sig))
        if n == 0:
            act, by_gate, silu = (jnp.where(skip, 0.0, v) for v in (act, by_gate, silu))
        ACT[:, cols] = act.astype(BF)
        BYG[:, cols] = by_gate
        BYU[:, cols] = silu
    rd[1](3)
    gg[2]()
    rd[2]()
    for n in range(ff_half // 256):
        cols = slice(n * 256, n * 256 + 256)
        dact = contract(G[...], WD[cols, :], 1, 1)
        DGA[:, cols] = (dact * BYG[:, cols]).astype(BF)
        DUP[:, cols] = (dact * BYU[:, cols]).astype(BF)
        tile_grads(n)
        if n == 1:
            tick()
    blocks = lambda i, f: [zbufs[i][0].__setitem__((r % 2, r // 2), f(slice(r * 256, r * 256 + 256)).astype(BF)) for r in range(4)]
    tick()
    for n in range(4):
        cols = slice(n * 256, n * 256 + 256)
        PART[0, :, cols] = (contract(DGA[...], WG[cols, :], 1, 1) + contract(DUP[...], WU[cols, :], 1, 1)).astype(BF)
    hid = reduce_start(0, 0)
    tick()
    for n in range(4):
        cols = slice(n * 256, n * 256 + 256)
        PART[1, :, cols] = contract(ACT[...], WD[:, cols], 1, 0).astype(BF)
    tick()
    dh = hid()
    res = RES[rows(j, 128), :]
    scale = lax.rsqrt(jnp.mean(res * res, axis=1, keepdims=True) + EPSILON)
    w = dh * NG2[...]
    inner = jnp.mean(w * res, axis=1, keepdims=True)
    dres = G[rows(j, 128), :].astype(F32) + scale * w - res * (scale * scale * scale * inner)
    DRES[...] = dres
    GP[...] = jnp.zeros_like(GP)
    GP[1:2, :] = jnp.sum(dh * res * scale, axis=0, keepdims=True)
    DB[rows(j, 128), :] = dres.astype(BF)
    dbg = gather_start(DB)
    tick()
    tick()
    dbg()
    fin = reduce_start(1, 1)

    DAT[...] = contract(DB[...], WO[pl.ds(pl.multiple_of(base, 256), 256), :], 1, 1).astype(BF)
    own_heads = AF[:, pl.ds(pl.multiple_of(base, 256), 256)]
    blocks(3, lambda cols: contract(own_heads, DB[:, cols], 0, 0))
    begin(3, fo, OWAIT)
    tick()
    DK[...] = jnp.zeros_like(DK)
    DV[...] = jnp.zeros_like(DV)

    def attend_back(b):
        qs, ks = pl.ds(b * 256, 256), pl.ds(b * 256, 512)
        for hp in range(2):
            cols = slice(hp * 128, hp * 128 + 128)
            q_b, k_b, v_b, d_b = Q[qs, cols], K[ks, cols], V[ks, cols], DAT[qs, cols]
            dq = dk = dv = None
            for h in range(2):
                m = head_mask[h]
                d_h = d_b * m
                p = PM[b * 4 + hp * 2 + h]
                dp = contract(d_h, v_b, 1, 1)
                ds = (p * (dp - jnp.sum(p * dp, axis=1, keepdims=True))).astype(BF)
                one = (contract(ds, k_b * m, 1, 0), contract(ds, q_b * m, 0, 0), contract(p.astype(BF), d_h, 0, 0))
                dq, dk, dv = one if dq is None else (dq + one[0], dk + one[1], dv + one[2])
            DQKV[qs, cols] = (dq * 0.125).astype(BF)
            DK[ks, cols] += dk
            DV[ks, cols] += dv

    attend_back(0)
    tick()
    attend_back(1)
    HS[:, 0:256] = DK[0:256, :].astype(BF)
    HS[:, 256:512] = DV[0:256, :].astype(BF)
    back = net.make(HS, HR, core_nb)
    net.start(back, c == 1)

    @pl.when(c == 0)
    def _():
        back.wait_recv()
        DK[512:768, :] += HR[:, 0:256].astype(F32)
        DV[512:768, :] += HR[:, 256:512].astype(F32)

    DQKV[:, 256:512] = DK[256:768, :].astype(BF)
    DQKV[:, 512:768] = DV[256:768, :].astype(BF)
    blocks(4, lambda cols: contract(XN[:, cols], DQKV[...], 0, 0))
    begin(4, fq, QWAIT)
    tick()
    OS[...] = (RES[rows(j, 128), :] + fin()).astype(BF)
    sent = send_blocks(OS, out)
    for n in range(4):
        cols = slice(n * 256, n * 256 + 256)
        PART[0, :, cols] = contract(DQKV[...], WQKV[cols, :], 1, 1).astype(BF)
    last = reduce_start(2, 0)
    tick(3)
    dx = last()
    v = X[rows(j, 128), :].astype(F32)
    scale = lax.rsqrt(jnp.mean(v * v, axis=1, keepdims=True) + EPSILON)
    w = dx * NG1[...]
    inner = jnp.mean(w * v, axis=1, keepdims=True)
    GS[...] = DRES[...] + scale * w - v * (scale * scale * scale * inner)
    GP[0:1, :] = jnp.sum(dx * v * scale, axis=0, keepdims=True)
    sent_in = send_blocks(GS, gin)

    me = 4 * x + 2 * y + c
    got = []
    for d in range(1, NPLANE):
        xx, yy, cc = flip(x, d & 1), flip(y, d & 2), flip(c, d & 4)
        copy = net.make(GP.at[:, lanes(2 * xx + cc)], GR.at[me], dev(z, xx, yy, cc))
        net.start(copy)
        got.append(copy)
    keep = local(GP.at[:, lanes(row)], GR.at[me])
    keep.start()
    tick(2)
    keep.wait()
    for copy in got:
        copy.wait_recv()
    total = GR[0]
    for d in range(1, NPLANE):
        total = total + GR[d]
    GZS[...] = total
    got = []
    for d in range(1, nz):
        copy = net.make(GZS, GZ.at[z], dev((z + d) % nz, x, y, c))
        net.start(copy)
        got.append(copy)
    keep = local(GZS, GZ.at[z])
    keep.start()
    tick(30)
    keep.wait()
    for copy in got:
        copy.wait_recv()
    total = GZ[0]
    for d in range(1, nz):
        total = total + GZ[d]
    gains[...] = total
    sent()
    sent_in()
    for copy in flushes:
        copy.wait()
    net.finish()


def spread_kernel(nz, ff_half, ff_cut, f0, f1, f2, fo, fq, out_in, gin_in, gains, *refs):
    out, gin, gn1, gwq, gwk, gwv, gwo, gn2, gwg, gwu, gwd = refs[:11]
    I0, I1, I2, IO, IQ, OG, OU, OD, OO, OQ, PO, PG, sem, sem_out = refs[11:]
    over_cut = ff_half - ff_cut
    moves = ((f0, I0), (f1, I1), (f2, I2), (fo, IO), (fq, IQ), (out_in, PO), (gin_in, PG))
    loads = [pltpu.make_async_copy(a, b, sem.at[i]) for i, (a, b) in enumerate(moves)]
    for copy in loads:
        copy.start()
    stores = []

    def store(buf, dst):
        stores.append(pltpu.make_async_copy(buf, dst, sem_out.at[len(stores)]))
        stores[-1].start()

    gn1[...] = gains[0:1, :]
    gn2[...] = gains[1:2, :]
    for n, I in enumerate((I0, I1, I2)):
        loads[n].wait()
        for q in range(nz):
            for xx in range(2):
                at = xx * ff_cut + n * 256
                skip = over_cut if xx == 1 and n == 0 else 0
                OG[q * 64 : q * 64 + 64, at + skip : at + 256] = I[q, xx, :, skip:256].astype(F32)
                OU[q * 64 : q * 64 + 64, at + skip : at + 256] = I[q, xx, :, 256 + skip : 512].astype(F32)
                if q * 64 >= skip:
                    OD[at + q * 64 : at + q * 64 + 64, :] = I[q, xx, :, 512:768].astype(F32)
    for buf, dst in ((OG, gwg), (OU, gwu), (OD, gwd)):
        store(buf, dst)
    loads[3].wait()
    for q in range(nz):
        for xx in range(2):
            OO[xx * 256 + q * 64 : xx * 256 + q * 64 + 64, :] = IO[q, xx].astype(F32)
    store(OO, gwo)
    loads[4].wait()
    for i, dst in enumerate((gwq, gwk, gwv)):
        for q in range(nz):
            for xx in range(2):
                OQ[i, q * 64 : q * 64 + 64, xx * 256 : xx * 256 + 256] = IQ[q, xx, :, i * 256 : i * 256 + 256].astype(F32)
        store(OQ.at[i], dst)
    for load, buf, dst in ((loads[5], PO, out), (loads[6], PG, gin)):
        load.wait()
        store(buf, dst)
    for copy in stores:
        copy.wait()


def fused(nz, tokens, cotangent, seg_ids, norm_one, wq, wk, wv, wo, norm_two, w_gate, w_up, w_down):
    ff = w_gate.shape[1]
    ff_half = -(-ff // 512) * 256
    ff_cut = ff - ff_half
    vm = pltpu.VMEM
    zshapes = [(256, 768)] * 3 + [(256, 256), (256, 768)]
    zscratch, fshapes = [], []
    for rows, cols in zshapes:
        fshapes.append((nz, 2, rows // nz, cols))
        zscratch += [
            vm((2, 2, rows, cols), BF),
            vm((2, rows, cols), BF),
            vm((2, nz - 1, 2, rows // nz, cols), BF),
            vm((rows // nz, cols), BF),
            vm(fshapes[-1], BF),
        ]
    scratch = [
        vm((512, D), BF), vm((512, D), BF), vm((D, 768), BF), vm((D, D), BF),
        vm((D, ff_half), BF), vm((D, ff_half), BF), vm((ff_half, D), BF), vm((1, D), F32), vm((1, D), F32),
        vm((512, D), BF), vm((512, 256), BF), vm((768, 256), BF), vm((768, 256), BF), vm((2, 256, 512), F32),
        vm((8, 256, 512), F32), vm((512, D), BF),
        vm((2, 512, D), BF), vm((3, 3, 128, D), BF),
        vm((512, D), BF), vm((512, D), F32), vm((128, D), F32), vm((512, ff_half), BF), vm((512, ff_half), BF),
        vm((512, ff_half), BF), vm((512, D), BF), vm((512, 256), BF), vm((512, ff_half), F32), vm((512, ff_half), F32),
        vm((768, 256), F32), vm((768, 256), F32), vm((512, 768), BF), vm((256, 512), BF), vm((256, 512), BF),
        vm((128, D), BF), vm((128, D), F32), vm((8, D), F32), vm((8, 8, 256), F32), vm((nz, 8, 256), F32), vm((8, 256), F32),
        *zscratch,
        pltpu.SemaphoreType.DMA((10,)), pltpu.SemaphoreType.DMA((255,)), pltpu.SemaphoreType.DMA((22,)),
    ]
    hbm, vmem = pl.BlockSpec(memory_space=pl.ANY), pl.BlockSpec(memory_space=pltpu.VMEM)
    sds = jax.ShapeDtypeStruct
    done = pl.pallas_call(
        functools.partial(layer_kernel, nz, ff_half, ff_cut),
        out_shape=(sds((512, 256), BF), sds((512, 256), F32), sds((8, 256), F32), *(sds(f, BF) for f in fshapes)),
        in_specs=[hbm, hbm, vmem, vmem, hbm, hbm, hbm, hbm, vmem, hbm, hbm, hbm],
        out_specs=(hbm, hbm, vmem, *(hbm for f in fshapes)),
        scratch_shapes=scratch,
        compiler_params=pltpu.CompilerParams(collective_id=0, has_side_effects=True, vmem_limit_bytes=62 << 20),
        name="layer",
    )(
        tokens, cotangent, seg_ids, norm_one[None], wq, wk, wv, wo, norm_two[None], w_gate, w_up, w_down,
    )
    out, gin, gains, *sums = done
    grads = (
        sds((512, 256), BF), sds((512, 256), F32), sds((1, 256), F32),
        sds((256, 512), F32), sds((256, 512), F32), sds((256, 512), F32), sds((512, 256), F32),
        sds((1, 256), F32), sds((256, ff), F32), sds((256, ff), F32), sds((ff, 256), F32),
    )
    res = pl.pallas_call(
        functools.partial(spread_kernel, nz, ff_half, ff_cut),
        out_shape=grads,
        in_specs=[hbm] * 7 + [vmem],
        out_specs=tuple(vmem if i in (2, 7) else hbm for i in range(11)),
        scratch_shapes=[vm(f, BF) for f in fshapes]
        + [vm((256, ff), F32), vm((256, ff), F32), vm((ff, 256), F32), vm((512, 256), F32), vm((3, 256, 512), F32)]
        + [vm((512, 256), BF), vm((512, 256), F32), pltpu.SemaphoreType.DMA((7,)), pltpu.SemaphoreType.DMA((9,))],
        compiler_params=pltpu.CompilerParams(vmem_limit_bytes=63 << 20),
        name="spread",
    )(*sums, out, gin, gains)
    res = list(res)
    res[2], res[7] = res[2][0], res[7][0]
    return tuple(res)


def solution(mesh):
    in_specs = (
        P(("dp", "col"), "row"),
        P(("dp", "col"), "row"),
        P("dp", None),
        P("row"),
        P("row", "col"),
        P("row", "col"),
        P("row", "col"),
        P("col", "row"),
        P("row"),
        P("row", "col"),
        P("row", "col"),
        P("col", "row"),
    )
    out_specs = (
        P(("dp", "col"), "row"),
        P(("dp", "col"), "row"),
        P("row"),
        P("row", "col"),
        P("row", "col"),
        P("row", "col"),
        P("col", "row"),
        P("row"),
        P("row", "col"),
        P("row", "col"),
        P("col", "row"),
    )
    sizes = dict(mesh.shape)
    body = per_device
    if sizes["row"] == 4 and sizes["col"] == 2:
        body = functools.partial(fused, sizes["dp"])
    return jax.shard_map(
        body, mesh=mesh, in_specs=in_specs, out_specs=out_specs, check_vma=False
    )
```

```python
import functools

import jax
import jax.numpy as jnp
from jax import lax
from jax.experimental import pallas as pl
from jax.experimental.pallas import tpu as pltpu
from jax.sharding import PartitionSpec as P

D = 1024
HEAD_DIM = 64


EPSILON = 1e-05
NEGATIVE = -1e30


def for_sending(array):

    def short(part):
        return part.astype(jnp.bfloat16) if part.dtype == jnp.float32 else part

    return jax.tree.map(short, array)


def shifted(block, axis, distance):
    devices = range(lax.axis_size(axis))
    route = [(i - distance, i) for i in devices if i - distance in devices]
    return lax.ppermute(block, axis, route)


def matmul(first_op, second_op):
    return jnp.dot(first_op, second_op, preferred_element_type=jnp.float32)


def matmul_tn(first_op, second_op):
    return lax.dot_general(
        first_op, second_op, (((0,), (0,)), ((), ())), preferred_element_type=jnp.float32
    )


def matmul_nt(first_op, second_op):
    return lax.dot_general(
        first_op, second_op, (((1,), (1,)), ((), ())), preferred_element_type=jnp.float32
    )


def tokens_col(array_in):
    return lax.all_gather(array_in, "col", axis=0, tiled=True)


def tokens_row(array_in):
    return lax.all_gather(for_sending(array_in), "row", axis=0, tiled=True).astype(array_in.dtype)


def summed_row(array_in):
    return lax.psum_scatter(
        array_in.astype(jnp.bfloat16), "row", scatter_dimension=0, tiled=True
    ).astype(jnp.float32)


def summed_col(array_in):
    return lax.psum_scatter(
        array_in.astype(jnp.bfloat16), "col", scatter_dimension=0, tiled=True
    ).astype(jnp.float32)


def feature_total(array_in):
    return lax.psum(array_in, "row")


def window_parts(queries, keys_all, ids_ext, offset, head_cols):
    t_local = queries.shape[0]
    block_rows = min(512, t_local)
    key_reach = min(2048, t_local)
    window = key_reach + block_rows
    head_count = head_cols // HEAD_DIM
    anchor = offset + t_local - key_reach
    q_blk = lax.dynamic_slice_in_dim(queries, offset, block_rows, 0).reshape(
        block_rows, head_count, HEAD_DIM
    )
    k_win = lax.dynamic_slice_in_dim(keys_all, anchor, window, 0)
    k_blk = k_win[:, :head_cols].reshape(window, head_count, HEAD_DIM)
    v_blk = k_win[:, head_cols:].reshape(window, head_count, HEAD_DIM)
    q_ids = lax.dynamic_slice_in_dim(ids_ext, offset + t_local, block_rows, 0)
    k_ids = lax.dynamic_slice_in_dim(ids_ext, anchor, window, 0)
    q_pos = offset + lax.iota(jnp.int32, block_rows)
    k_pos = offset - key_reach + lax.iota(jnp.int32, window)
    allowed = (q_ids[:, None] == k_ids[None, :]) & (k_pos[None, :] <= q_pos[:, None])
    scores = jnp.einsum(
        "qhd,khd->hqk", q_blk, k_blk, preferred_element_type=jnp.float32
    ) * HEAD_DIM ** (-0.5)
    scores = jnp.where(allowed[None], scores, NEGATIVE)
    return (q_blk, k_blk, v_blk, scores)


def forward(tokens, seg_ids, norm_one, wq, wk, wv, wo, norm_two, w_gate, w_up, w_down):
    token_vals = tokens.astype(jnp.float32)
    scale_one = lax.rsqrt(feature_total(jnp.sum(token_vals * token_vals, axis=1)) / D + EPSILON)
    normed = (token_vals * scale_one[:, None] * norm_one).astype(jnp.bfloat16)
    normed_all = tokens_col(normed)
    w_qkv = jnp.concatenate([wq, wk, wv], axis=1)
    head_cols = wq.shape[1]
    qkv = summed_row(matmul(normed_all, w_qkv)).astype(jnp.bfloat16)
    queries = qkv[:, :head_cols]
    kv_local = qkv[:, head_cols:]
    prior_keys = shifted(kv_local, "row", 1)
    keys_all = jnp.concatenate([prior_keys, kv_local], axis=0)
    t_local = queries.shape[0]
    block_rows = min(512, t_local)
    padded_ids = jnp.concatenate([jnp.full((t_local,), -1, jnp.int32), seg_ids[0]])
    ids_ext = lax.dynamic_slice_in_dim(padded_ids, lax.axis_index("row") * t_local, 2 * t_local, 0)

    def attend(offset):
        q_blk, k_blk, v_blk, scores = window_parts(queries, keys_all, ids_ext, offset, head_cols)
        row_max = jnp.max(scores, axis=2, keepdims=True)
        exp_total = jnp.sum(jnp.exp(scores - row_max), axis=2, keepdims=True)
        log_total = row_max + jnp.log(exp_total)
        prob_low = jnp.exp(scores - log_total).astype(jnp.bfloat16)
        mixed_out = jnp.einsum("hqk,khd->qhd", prob_low, v_blk, preferred_element_type=jnp.float32)
        return (mixed_out.reshape(block_rows, head_cols).astype(jnp.bfloat16), log_total[:, :, 0])

    offsets = lax.iota(jnp.int32, t_local // block_rows) * block_rows
    pieces, log_totals = lax.map(attend, offsets)
    attn_out = pieces.reshape(t_local, head_cols)
    attn_all = tokens_row(attn_out)
    residual = token_vals + summed_col(matmul(attn_all, wo))
    stored = {
        "token_vals": token_vals,
        "scale_one": scale_one,
        "normed_all": normed_all,
        "queries": queries,
        "keys_all": keys_all,
        "ids_ext": ids_ext,
        "log_totals": log_totals,
        "attn_all": attn_all,
        "offsets": offsets,
    }
    f_col = w_gate.shape[1]
    scale_two = lax.rsqrt(feature_total(jnp.sum(residual * residual, axis=1)) / D + EPSILON)
    hidden_in = (residual * scale_two[:, None] * norm_two).astype(jnp.bfloat16)
    hidden_all = tokens_col(hidden_in)
    w_pair = jnp.concatenate([w_gate, w_up], axis=1)
    pair_sum = summed_row(matmul(hidden_all, w_pair))
    gate_pre = pair_sum[:, :f_col]
    up_pre = pair_sum[:, f_col:]
    act_low = (jax.nn.silu(gate_pre) * up_pre).astype(jnp.bfloat16)
    act_all = tokens_row(act_low)
    final_sum = residual + summed_col(matmul(act_all, w_down))
    stored.update(
        {
            "residual": residual,
            "scale_two": scale_two,
            "hidden_all": hidden_all,
            "gate_pre": gate_pre,
            "up_pre": up_pre,
            "act_all": act_all,
        }
    )
    return (final_sum.astype(jnp.bfloat16), stored)


def swiglu_grads(dact, gate_pre, up_pre):
    sigmoid_gate = jax.nn.sigmoid(gate_pre)
    gate_grad = (dact * up_pre * sigmoid_gate * (1.0 + gate_pre * (1.0 - sigmoid_gate))).astype(
        jnp.bfloat16
    )
    up_grad = (dact * gate_pre * sigmoid_gate).astype(jnp.bfloat16)
    return (gate_grad, up_grad)


def per_device(
    tokens, cotangent, seg_ids, norm_one, wq, wk, wv, wo, norm_two, w_gate, w_up, w_down
):
    weights = (tokens, seg_ids, norm_one, wq, wk, wv, wo, norm_two, w_gate, w_up, w_down)
    output, stored = forward(*weights)
    f_col = w_gate.shape[1]
    grad_out = cotangent.astype(jnp.float32)
    grad_all = tokens_col(cotangent)
    dact = summed_row(matmul_nt(grad_all, w_down))
    grad_down = matmul_tn(stored["act_all"], grad_all)
    gate_grad, up_grad = swiglu_grads(dact, stored["gate_pre"], stored["up_pre"])
    dpair = jnp.concatenate([gate_grad, up_grad], axis=1)
    dpair_all = tokens_row(dpair)
    w_pair = jnp.concatenate([w_gate, w_up], axis=1)
    dhidden = summed_col(matmul_nt(dpair_all, w_pair))
    grad_pair = matmul_tn(stored["hidden_all"], dpair_all)
    grad_gate = grad_pair[:, :f_col]
    grad_up = grad_pair[:, f_col:]
    residual = stored["residual"]
    scale_two = stored["scale_two"]
    weighted = dhidden * norm_two
    inner_sum = feature_total(jnp.sum(weighted * residual, axis=1)) / D
    dresid = (
        grad_out + scale_two[:, None] * weighted - residual * (scale_two**3 * inner_sum)[:, None]
    )
    grad_norm_two = jnp.sum(dhidden * residual * scale_two[:, None], axis=0)
    dbranch = dresid.astype(jnp.bfloat16)
    dbranch_all = tokens_col(dbranch)
    attn_grad = summed_row(matmul_nt(dbranch_all, wo)).astype(jnp.bfloat16)
    grad_wo = matmul_tn(stored["attn_all"], dbranch_all)
    queries = stored["queries"]
    keys_all = stored["keys_all"]
    ids_ext = stored["ids_ext"]
    head_cols = wq.shape[1]
    head_count = head_cols // HEAD_DIM
    t_local = queries.shape[0]
    block_rows = min(512, t_local)
    key_reach = min(2048, t_local)
    window = key_reach + block_rows
    inv_root = HEAD_DIM ** (-0.5)

    def attend_back(accum_dkv, inputs):
        offset, log_total = inputs
        q_blk, k_blk, v_blk, scores = window_parts(queries, keys_all, ids_ext, offset, head_cols)
        prob_full = jnp.exp(scores - log_total[:, :, None])
        prob_low = prob_full.astype(jnp.bfloat16)
        d_blk = lax.dynamic_slice_in_dim(attn_grad, offset, block_rows, 0).reshape(
            block_rows, head_count, HEAD_DIM
        )
        dprobs = jnp.einsum("qhd,khd->hqk", d_blk, v_blk, preferred_element_type=jnp.float32)
        dvalue = jnp.einsum("hqk,qhd->khd", prob_low, d_blk, preferred_element_type=jnp.float32)
        center = jnp.sum(prob_full * dprobs, axis=2, keepdims=True)
        dscores = (prob_full * (dprobs - center)).astype(jnp.bfloat16)
        dquery = (
            jnp.einsum("hqk,khd->qhd", dscores, k_blk, preferred_element_type=jnp.float32)
            * inv_root
        )
        dkey = (
            jnp.einsum("hqk,qhd->khd", dscores, q_blk, preferred_element_type=jnp.float32)
            * inv_root
        )
        update = jnp.concatenate(
            [dkey.reshape(window, head_cols), dvalue.reshape(window, head_cols)], axis=1
        )
        anchor = offset + t_local - key_reach
        current = lax.dynamic_slice_in_dim(accum_dkv, anchor, window, 0)
        accum_dkv = lax.dynamic_update_slice_in_dim(accum_dkv, current + update, anchor, 0)
        return (accum_dkv, dquery.reshape(block_rows, head_cols))

    start_grads = jnp.zeros((2 * t_local, 2 * head_cols), jnp.float32)
    accum_dkv, query_grads = lax.scan(
        attend_back, start_grads, (stored["offsets"], stored["log_totals"])
    )
    returned = shifted(accum_dkv[:t_local].astype(jnp.bfloat16), "row", -1).astype(jnp.float32)
    key_grads = accum_dkv[t_local:] + returned
    dqkv = jnp.concatenate([query_grads.reshape(t_local, head_cols), key_grads], axis=1).astype(
        jnp.bfloat16
    )
    dqkv_all = tokens_row(dqkv)
    w_qkv = jnp.concatenate([wq, wk, wv], axis=1)
    dnormed = summed_col(matmul_nt(dqkv_all, w_qkv))
    grad_qkv = matmul_tn(stored["normed_all"], dqkv_all)
    grad_wq = grad_qkv[:, :head_cols]
    grad_wk = grad_qkv[:, head_cols : 2 * head_cols]
    grad_wv = grad_qkv[:, 2 * head_cols :]
    token_vals = stored["token_vals"]
    scale_one = stored["scale_one"]
    weighted_one = dnormed * norm_one
    inner_one = feature_total(jnp.sum(weighted_one * token_vals, axis=1)) / D
    grad_input = (
        dresid
        + scale_one[:, None] * weighted_one
        - token_vals * (scale_one**3 * inner_one)[:, None]
    )
    grad_norm_one = jnp.sum(dnormed * token_vals * scale_one[:, None], axis=0)
    grad_sums = (
        lax.psum(grad_wq.astype(jnp.bfloat16), "dp").astype(jnp.float32),
        lax.psum(grad_wk.astype(jnp.bfloat16), "dp").astype(jnp.float32),
        lax.psum(grad_wv.astype(jnp.bfloat16), "dp").astype(jnp.float32),
        lax.psum(grad_wo.astype(jnp.bfloat16), "dp").astype(jnp.float32),
        lax.psum(grad_gate.astype(jnp.bfloat16), "dp").astype(jnp.float32),
        lax.psum(grad_up.astype(jnp.bfloat16), "dp").astype(jnp.float32),
        lax.psum(grad_down.astype(jnp.bfloat16), "dp").astype(jnp.float32),
    )
    gain_sums = lax.psum((grad_norm_one, grad_norm_two), ("dp", "col"))
    return (
        output,
        grad_input,
        gain_sums[0],
        grad_sums[0],
        grad_sums[1],
        grad_sums[2],
        grad_sums[3],
        gain_sums[1],
        grad_sums[4],
        grad_sums[5],
        grad_sums[6],
    )


MESH = pl.DeviceIdType.MESH
BF = jnp.bfloat16
F32 = jnp.float32
NPLANE = 8
LATE = (1, 3, 4)
NEWFIRST, LAG = True, 4
FWAIT, OWAIT, QWAIT = (2, 6, 0), 0, 0


def contract(a, b, ca, cb):
    return lax.dot_general(a, b, (((ca,), (cb,)), ((), ())), preferred_element_type=F32)


class Copies:
    def __init__(self, send, recv):
        self.send, self.recv, self.used, self.kept, self.open = send, recv, 0, 1, []

    def take(self, amount=1):
        base = self.used
        self.used += amount
        return base

    def make(self, src, dst, to, site=None, own=False):
        site = self.take() if site is None else site
        self.kept += own
        return pltpu.make_async_remote_copy(
            src_ref=src,
            dst_ref=dst,
            send_sem=self.send.at[self.kept - 1 if own else 0],
            recv_sem=self.recv.at[site],
            device_id=to,
            device_id_type=MESH,
        )

    def start(self, copy, when=None):
        self.open.append((copy, when))
        if when is None:
            copy.start()
        else:
            pl.when(when)(copy.start)

    def finish(self):
        for copy, when in self.open:
            if when is None:
                copy.wait_send()
            else:
                pl.when(when)(copy.wait_send)
        self.open = []


def layer_kernel(nz, ff_half, ff_cut, *refs):
    it = iter(refs)
    take = lambda n: [next(it) for _ in range(n)]
    tok, cot, seg, n1, wq, wk, wv, wo, n2, wg, wu, wd = take(12)
    out, gin, gains, f0, f1, f2, fo, fq = take(8)
    X, G, WQKV, WO, WG, WU, WD, NG1, NG2 = take(9)
    XN, Q, K, V, BIAS, PM, AF = take(7)
    PART, RX = take(2)
    HN, RES, DRES, ACT, DGA, DUP, DB, DAT, BYG, BYU, T3 = take(11)
    DK, DV, DQKV, HS, HR = take(5)
    OS, GS, GP, GR, GZ, GZS = take(6)
    zbufs = [take(5) for _ in range(5)]
    send, recv, loc = take(3)

    z, row, y = lax.axis_index("dp"), lax.axis_index("row"), lax.axis_index("col")
    x, c = row // 2, row % 2
    net = Copies(send, recv)
    nloc = [0]

    def local(src, dst):
        nloc[0] += 1
        return pltpu.make_async_copy(src, dst, loc.at[nloc[0] - 1])

    def dev(zz, xx, yy, cc):
        return (zz, 2 * xx + cc, yy)

    core_nb, x_nb, y_nb = dev(z, x, y, 1 - c), dev(z, 1 - x, y, c), dev(z, x, 1 - y, c)
    z_up, z_dn = dev(z + 1, x, y, c), dev(z - 1, x, y, c)
    lanes = lambda i, n=256: pl.ds(pl.multiple_of(i * n, 128), n)
    rows = lambda i, n: pl.ds(pl.multiple_of(i * n, n if n % 16 else 16), n)
    flip = lambda v, bit: 1 - v if bit else v

    barrier = pltpu.get_barrier_semaphore()
    for d in range(1, NPLANE):
        pl.semaphore_signal(
            barrier, inc=1, device_id=dev(z, flip(x, d & 1), flip(y, d & 2), flip(c, d & 4)), device_id_type=MESH
        )
    for d in range(1, nz):
        pl.semaphore_signal(barrier, inc=1, device_id=dev((z + d) % nz, x, y, c), device_id_type=MESH)
    for _, _, ZR, _, _ in zbufs:

        @pl.when(z == 0)
        def _(ZR=ZR):
            ZR[0, nz - 2] = jnp.zeros(ZR.shape[2:], BF)

        @pl.when(z == nz - 1)
        def _(ZR=ZR):
            ZR[1, nz - 2] = jnp.zeros(ZR.shape[2:], BF)

    seg_f = seg[...].astype(F32)
    own = jnp.where(c == 0, seg_f[:, :512], seg_f[:, 512:])
    before = jnp.where(c == 0, jnp.full((1, 256), -1.0, F32), seg_f[:, 256:512])
    ids = jnp.concatenate([before, own], axis=1)
    for b in range(2):
        k_id = jnp.broadcast_to(ids[:, b * 256 : b * 256 + 512], (256, 512))
        q_id = jnp.broadcast_to(ids[:, 256 + b * 256 : 512 + b * 256], (512, 256)).T
        q_pos = lax.broadcasted_iota(jnp.int32, (256, 512), 0) + 256
        k_pos = lax.broadcasted_iota(jnp.int32, (256, 512), 1)
        BIAS[b] = jnp.where((q_id == k_id) & (k_pos <= q_pos), 0.0, NEGATIVE)

    @pl.when(c == 0)
    def _():
        K[0:256, :] = jnp.zeros((256, 256), BF)
        V[0:256, :] = jnp.zeros((256, 256), BF)

    pl.semaphore_wait(barrier, NPLANE - 1 + nz - 1)

    def gather_tokens(src, buf):
        col = lambda rr: buf.at[:, lanes(rr)]
        mine = c == y
        other = jnp.logical_not(mine)
        keep = local(src, col(row))
        over = net.make(src, col(row), core_nb)
        bx, by = net.take(2), net.take(2)
        to_x = net.make(src, col(row), dev(z, 1 - x, y, y), bx + c)
        to_y = net.make(src, col(row), dev(z, x, 1 - y, y), by + c)
        far = 2 * (1 - x)
        by_y = net.make(col(far), col(far), y_nb)
        by_x = net.make(col(2 * x + 1), col(2 * x + 1), x_nb)
        got_x = [net.make(src, col(row), core_nb, bx + k) for k in range(2)]
        got_y = [net.make(src, col(row), core_nb, by + k) for k in range(2)]

        def start():
            pl.when(mine)(keep.start)
            net.start(to_x)
            net.start(to_y)
            net.start(over, other)

        def arrive():
            @pl.when(mine)
            def _():
                got_x[0].wait_recv()
                by_y.start()

            @pl.when(other)
            def _():
                got_y[1].wait_recv()
                by_x.start()

            net.open += [(by_y, mine), (by_x, other)]

        def rest():
            @pl.when(mine)
            def _():
                got_x[1].wait_recv()
                over.wait_recv()
                keep.wait()

            @pl.when(other)
            def _():
                got_y[0].wait_recv()
                by_y.wait_recv()
                by_x.wait_recv()

        return start, arrive, rest

    def relay(src_of, dst_of):
        keep = local(src_of(x), dst_of(row))
        across = net.make(src_of(x), dst_of(row), core_nb)
        far = net.make(src_of(1 - x), dst_of(row), x_nb)
        theirs = dst_of(2 * (1 - x) + c)
        fwd = net.make(theirs, theirs, core_nb)

        def start():
            keep.start()
            net.start(far)
            net.start(across)

        def arrive():
            far.wait_recv()
            net.start(fwd)

        def rest():
            keep.wait()
            across.wait_recv()
            fwd.wait_recv()

        return start, arrive, rest

    def z_gather(at):
        sites = (net.take(nz - 1), net.take(nz - 1))

        def step(s):
            for way, to in ((0, z_up), (1, z_dn)):
                zz = z if way == 0 else nz - 1 - z
                ref = at(z - s if way == 0 else z + s)
                have = zz >= s
                if s > 0:
                    pl.when(have)(net.make(ref, ref, to, sites[way] + s - 1).wait_recv)
                if s < nz - 1:
                    net.start(net.make(ref, ref, to, sites[way] + s), have & (zz < nz - 1))

        return step

    def relay_z(pairs, whole, n_rows):
        n = n_rows // nz
        keep = [local(a, b) for a, b in pairs(x, row, 0, n_rows)]
        across = [net.make(a, b, core_nb) for a, b in pairs(x, row, 0, n_rows)]
        far = [net.make(a, b, x_nb) for a, b in pairs(1 - x, row, z * n, n)]
        hop = z_gather(lambda q: whole(2 * (1 - x) + c, q * n, n))
        theirs = whole(2 * (1 - x) + c, 0, n_rows)
        fwd = net.make(theirs, theirs, core_nb)

        def begin():
            for copy in far:
                net.start(copy)
            for copy in keep:
                copy.start()
            for copy in across:
                net.start(copy)

        def step(s):
            if s == 0:
                for copy in far:
                    copy.wait_recv()
            hop(s)
            if s == nz - 1:
                net.start(fwd)

        def rest():
            for copy in keep:
                copy.wait()
            for copy in across:
                copy.wait_recv()
            fwd.wait_recv()

        return begin, step, rest

    def gather_wo():
        at = lambda yy, rr: WO.at[rows(yy, 512), lanes(rr)]
        keep = local(wo, at(y, row))
        across = net.make(wo, at(y, row), core_nb)
        to_x, to_y = net.make(wo, at(y, row), x_nb), net.make(wo, at(y, row), y_nb)
        rx = 2 * (1 - x) + c
        on_y = net.make(at(y, rx), at(y, rx), y_nb)
        others = (at(y, rx), at(1 - y, row), at(1 - y, rx))
        fwd = [net.make(ref, ref, core_nb) for ref in others]

        def start():
            net.start(to_x)
            net.start(to_y)
            keep.start()
            net.start(across)

        def arrive():
            to_x.wait_recv()
            net.start(on_y)
            net.start(fwd[0])

        def pass_on():
            to_y.wait_recv()
            net.start(fwd[1])
            on_y.wait_recv()
            net.start(fwd[2])

        def rest():
            keep.wait()
            across.wait_recv()
            for copy in fwd:
                copy.wait_recv()

        return start, arrive, pass_on, rest

    def gather_gain(src, dst):
        keep = local(src, dst.at[:, lanes(row)])
        keep.start()
        got = []
        for to in (core_nb, x_nb, dev(z, 1 - x, y, 1 - c)):
            got.append(net.make(src, dst.at[:, lanes(row)], to))
            net.start(got[-1])

        def rest():
            keep.wait()
            for g in got:
                g.wait_recv()

        return rest

    gx, gg = gather_tokens(tok, X), gather_tokens(cot, G)
    some = lambda r0, n: pl.ds(pl.multiple_of(r0, 16), n)
    rqkv = []
    for i, w in ((1, wk), (2, wv), (0, wq)):
        at = lambda rr, r0, n, i=i: WQKV.at[some(rr * 256 + r0, n), pl.ds(i * 256, 256)]
        rqkv.append(relay_z(lambda xx, rr, r0, n, w=w, at=at: [(w.at[some(r0, n), lanes(xx)], at(rr, r0, n))], at, 256))
    ro = gather_wo()
    both = ff_half - ff_cut
    rff = []
    for w, W in ((wg, WG), (wu, WU)):
        at = lambda rr, r0, n, W=W: W.at[some(rr * 256 + r0, n), :]

        def pairs(xx, rr, r0, n, w=w, W=W):
            out = []
            for src, dst, width in ((pl.multiple_of(xx * ff_half, 128), 0, ff_cut), (ff_cut, ff_cut, both)):
                out.append((w.at[some(r0, n), pl.ds(src, width)], W.at[some(rr * 256 + r0, n), pl.ds(dst, width)]))
            return out

        rff.append(relay_z(pairs, at, 256))

    def pairs_down(xx, rr, r0, n):
        if n == ff_half:
            parts = ((xx * ff_half, 0, ff_cut), (ff_cut, ff_cut, both))
        else:
            tail = jnp.where(z == nz - 1, ff_cut, xx * ff_half + r0 + n - both)
            parts = ((xx * ff_half + r0, r0, n - both), (tail, r0 + n - both, both))
        return [(wd.at[some(src, k), :], WD.at[some(dst, k), lanes(rr)]) for src, dst, k in parts]

    rd = relay_z(pairs_down, lambda rr, r0, n: WD.at[some(r0, n), lanes(rr)], ff_half)
    for r in rqkv:
        r[0]()
    gx[0]()
    ga = [gather_gain(n1, NG1), gather_gain(n2, NG2)]
    for r in rqkv:
        r[1](0)
    gx[1]()
    for s in range(1, nz):
        for r in rqkv:
            r[1](s)
    for g in ga:
        g()
    gx[2]()
    for r in rff:
        r[0]()
    ro[0]()
    for t in range(4):
        v = X[t * 128 : t * 128 + 128, :].astype(F32)
        scale = lax.rsqrt(jnp.mean(v * v, axis=1, keepdims=True) + EPSILON)
        XN[t * 128 : t * 128 + 128, :] = (v * scale * NG1[...]).astype(BF)
    for r in rqkv:
        r[2]()
    K[256:768, :] = contract(XN[...], WQKV[:, 256:512], 1, 0).astype(BF)
    V[256:768, :] = contract(XN[...], WQKV[:, 512:768], 1, 0).astype(BF)
    hk = net.make(K.at[pl.ds(512, 256), :], K.at[pl.ds(0, 256), :], core_nb)
    hv = net.make(V.at[pl.ds(512, 256), :], V.at[pl.ds(0, 256), :], core_nb)
    net.start(hk, c == 0)
    net.start(hv, c == 0)
    Q[...] = (contract(XN[...], WQKV[:, 0:256], 1, 0).astype(BF) * 0.125).astype(BF)
    @pl.when(c == 1)
    def _():
        hk.wait_recv()
        hv.wait_recv()

    lane_id = lax.broadcasted_iota(jnp.int32, (1, 128), 1)
    head_mask = [jnp.where(lane_id < 64, 1.0, 0.0).astype(BF), jnp.where(lane_id < 64, 0.0, 1.0).astype(BF)]

    heads_at = lambda xx, yy, b: AF.at[pl.ds(b * 256, 256), lanes(2 * yy + xx)]
    a_x = [net.make(heads_at(x, y, b), heads_at(x, y, b), x_nb) for b in range(2)]
    a_y = [net.make(heads_at(x, y, b), heads_at(x, y, b), y_nb) for b in range(2)]
    a_far = (
        net.make(heads_at(1 - x, y, 0), heads_at(1 - x, y, 0), y_nb),
        net.make(heads_at(x, 1 - y, 1), heads_at(x, 1 - y, 1), x_nb),
    )
    base = (2 * y + x) * 256
    for b in range(2):
        for hp in range(2):
            cols = slice(hp * 128, hp * 128 + 128)
            q_b, k_b, v_b = Q[b * 256 : b * 256 + 256, cols], K[b * 256 : b * 256 + 512, cols], V[b * 256 : b * 256 + 512, cols]
            total = None
            for h in range(2):
                s = contract(q_b * head_mask[h], k_b, 1, 1) + BIAS[b]
                e = jnp.exp(s - jnp.max(s, axis=1, keepdims=True))
                p = e * (1.0 / jnp.sum(e, axis=1, keepdims=True))
                PM[b * 4 + hp * 2 + h] = p
                part = contract(p.astype(BF), v_b * head_mask[h], 1, 0)
                total = part if total is None else total + part
            AF[b * 256 : b * 256 + 256, pl.ds(pl.multiple_of(base + hp * 128, 128), 128)] = total.astype(BF)
        net.start(a_x[b])
        net.start(a_y[b])
        if b == 0:
            for r in rff:
                r[1](0)
    rd[0]()
    for r in rff:
        r[1](1)
    ro[1]()
    a_x[0].wait_recv()
    net.start(a_far[0])
    a_y[1].wait_recv()
    net.start(a_far[1])
    gg[0]()
    for r in rff:
        r[1](2)
    rd[1](0)
    ro[2]()
    for r in rff:
        r[1](3)
    rd[1](1)

    j = 2 * x + y
    shard = lambda buf, jj: buf.at[rows(jj, 128), :]

    peers = ((x_nb, 2 * (1 - x) + y), (y_nb, 2 * x + 1 - y), (dev(z, 1 - x, 1 - y, c), 2 * (1 - x) + 1 - y))

    def reduce_start(k, p):
        sent = [net.make(shard(PART.at[p], jj), RX.at[k, i], to, own=True) for i, (to, jj) in enumerate(peers)]
        for copy in (sent[2], sent[0], sent[1]):
            copy.start()

        def end():
            for copy in sent:
                copy.wait_recv()
            for copy in sent:
                copy.wait_send()
            total = PART[p, rows(j, 128), :].astype(F32)
            for i in range(3):
                total = total + RX[k, i].astype(F32)
            return total

        return end

    def gather_start(buf):
        sent = [net.make(shard(buf, j), shard(buf, j), to) for to, _ in peers]
        for copy in (sent[2], sent[0], sent[1]):
            net.start(copy)

        def end():
            for copy in sent:
                copy.wait_recv()

        return end

    def send_blocks(src, dst):
        base_r = net.take(4)
        waits = []
        for dx in range(2):
            for cc in range(2):
                xx = flip(x, dx)
                piece, place = src.at[:, lanes(2 * xx + cc)], dst.at[rows(j, 128), :]
                copy = pltpu.make_async_remote_copy(
                    src_ref=piece,
                    dst_ref=place,
                    send_sem=net.send.at[0],
                    recv_sem=net.recv.at[base_r + dx * 2 + y],
                    device_id=dev(z, xx, c, cc),
                    device_id_type=MESH,
                )
                if dx == 0:
                    here = (c == y) & (c == cc)
                    keep = local(piece, place)
                    pl.when(here)(keep.start)
                    net.start(copy, jnp.logical_not(here))
                    waits.append((keep, here))
                else:
                    net.start(copy)
        piece, place = src.at[:, pl.ds(0, 256)], dst.at[pl.ds(0, 128), :]
        arrivals = [
            (net.make(piece, place, core_nb, base_r + dx * 2 + yy), jnp.logical_not((c == y) & (y == yy)) if dx == 0 else None)
            for dx in range(2)
            for yy in range(2)
        ]

        def end():
            for keep, here in waits:
                pl.when(here)(keep.wait)
            for got, when in arrivals:
                if when is None:
                    got.wait_recv()
                else:
                    pl.when(when)(got.wait_recv)

        return end

    def along_z(tag, dst):
        GB, CR, ZR, RL, FF = zbufs[tag]
        n_rows = CR.shape[1] // nz
        n = n_rows // 2
        last = CR.shape[0] - 1
        part = lambda q, i: pl.ds(pl.multiple_of(q * n_rows + i * n, 16), n)
        own = lambda i: pl.ds(i * n, n)
        over = net.make(GB.at[1 - c], CR, core_nb)
        net.start(over)
        yield
        over.wait_recv()
        for u in range(CR.shape[0]):
            CR[u] = (CR[u].astype(F32) + GB[c, u].astype(F32)).astype(BF)
        sites = [[net.take(nz - 1) for _ in range(2)] for _ in range(2)]
        for s in range(1, nz):
            for i in range(2):
                for way, to in ((0, z_up), (1, z_dn)):
                    zz = z if way == 0 else nz - 1 - z
                    q = nz - s + zz
                    q = q if way == 0 else nz - 1 - q
                    go = (zz < nz - 1) & (zz <= s - 1)
                    first, later = go & (zz == 0), go & (zz > 0)
                    site = sites[way][i] + s - 1
                    there = ZR.at[way, s - 1, :, own(i), :]
                    net.start(net.make(CR.at[:, part(q, i), :], there, to, site), first)
                    if s >= 2:
                        acc = ZR.at[way, s - 2, :, own(i), :]
                        got = net.make(acc, acc, to, site - 1)

                        @pl.when(later)
                        def _(got=got, acc=acc, q=q, i=i):
                            got.wait_recv()
                            acc[...] = (acc[...].astype(F32) + CR[:, part(q, i), :].astype(F32)).astype(BF)

                        net.start(net.make(acc, there, to, site), later)
                yield
        late = len(RL.shape) == 3
        backs = [[net.take(nz - 1) for _ in range(2)] for _ in range(2)]
        here = lambda q, i: FF.at[q, :, own(i), :]
        side = []

        def send_back(i):
            net.start(net.make(here(z, i), here(z, i), z_up, backs[0][i]), z < nz - 1)
            net.start(net.make(here(z, i), here(z, i), z_dn, backs[1][i]), z > 0)

        for i in range(2):
            for way in range(2):
                zz = z if way == 0 else nz - 1 - z
                acc = ZR.at[way, nz - 2, :, own(i), :]
                pl.when(zz > 0)(net.make(acc, acc, z_up, sites[way][i] + nz - 2).wait_recv)
            total = (
                CR[:, part(z, i), :].astype(F32)
                + ZR[0, nz - 2, :, own(i), :].astype(F32)
                + ZR[1, nz - 2, :, own(i), :].astype(F32)
            ).astype(BF)
            if late:
                FF[z, :, own(i), :] = total
                send_back(i)
            else:
                RL[own(i), :] = total[-1]
                side.append(net.make(RL.at[own(i), :], FF.at[z, last, own(i), :], x_nb))
                net.start(side[i])
                FF[z, 0:last, own(i), :] = total[:-1]
            yield
        if not late:
            for i in range(2):
                side[i].wait_recv()
                send_back(i)
                if tag == 4 and i == 1:
                    gates.append(tag)
                yield
        sites = backs
        for s in range(2, nz + 1):
            for i in range(2):
                for way, to in ((0, z_up), (1, z_dn)):
                    zz = z if way == 0 else nz - 1 - z
                    q = z - (s - 1) if way == 0 else z + (s - 1)
                    have = zz >= s - 1
                    ref = here(q, i)
                    pl.when(have)(net.make(ref, ref, to, sites[way][i] + s - 2).wait_recv)
                    if s < nz:
                        net.start(net.make(ref, ref, to, sites[way][i] + s - 1), have & (zz < nz - 1))
                yield
        if late:
            trade = net.make(FF.at[:, last], RL, x_nb)
            while tag in (0, 3) and not gates:
                yield
            net.start(trade)
            for _ in range(LAG):
                yield
            trade.wait_recv()
            flush(FF.at[:, 0:last], dst.at[:, 0:last])
            flush(RL, dst.at[:, last])
        else:
            flush(FF, dst)
        yield

    def flush(buf, dst):
        copy = local(buf, dst)
        copy.start()
        flushes.append(copy)

    flushes, gates = [], []

    lines = []

    def begin(i, dst, wait):
        line = along_z(i, dst)
        next(line)
        lines.append([line, wait])

    def tick(n=1):
        for _ in range(n):
            for _ in range(2):
                for line in (lines[::-1] if NEWFIRST else lines):
                    if line[1] > 0:
                        line[1] -= 1
                    else:
                        next(line[0], None)

    ro[3]()
    for copy in (a_x[1], a_y[0], *a_far):
        copy.wait_recv()
    for t in range(4):
        tile = slice(t * 128, t * 128 + 128)
        res = X[tile, :].astype(F32) + contract(AF[tile, :], WO[...], 1, 0)
        RES[tile, :] = res
        scale = lax.rsqrt(jnp.mean(res * res, axis=1, keepdims=True) + EPSILON)
        HN[tile, :] = (res * scale * NG2[...]).astype(BF)
    rd[1](2)
    gg[1]()
    for r in rff:
        r[2]()
    unit = lambda r: jnp.where(x == r // 2, 0, 1)
    shared = (lax.broadcasted_iota(jnp.int32, (1, 256), 1) >= 256 - both) & (x == 1)

    def tile_grads(n):
        cols = slice(n * 256, n * 256 + 256)
        GB = zbufs[n][0]
        for i, made in enumerate((DGA, DUP)):
            whole = contract(HN[...], made[:, cols], 0, 0)
            for r in range(4):
                GB[r % 2, unit(r), :, i * 256 : i * 256 + 256] = whole[r * 256 : r * 256 + 256].astype(BF)
        whole = contract(ACT[:, cols], G[...], 0, 0)
        for r in range(4):
            GB[r % 2, unit(r), :, 512:768] = whole[:, r * 256 : r * 256 + 256].astype(BF)

    def last_tile_grads(n):
        GB = zbufs[n][0]

        def put(r, cols, a, b):
            GB[r % 2, jnp.where(x == r // 2, 0, 2), :, cols] = a.astype(BF)

            @pl.when(x == r // 2)
            def _():
                GB[r % 2, 1, :, cols] = b.astype(BF)

        for i in range(2):
            whole = contract(HN[...], T3[i], 0, 0)
            for r in range(4):
                rws = whole[r * 256 : r * 256 + 256]
                put(r, slice(i * 128, i * 128 + 128), rws[:, :128], rws[:, 128:])
        whole = contract(T3[2], G[...], 0, 0)
        for r in range(4):
            left, right = whole[:, r * 256 : r * 256 + 128], whole[:, r * 256 + 128 : r * 256 + 256]
            put(
                r,
                slice(256, 384),
                jnp.concatenate([left[:128], right[:128]], axis=0),
                jnp.concatenate([left[128:], right[128:]], axis=0),
            )

    tiles = ff_half // 256
    for n in range(tiles):
        cols = slice(n * 256, n * 256 + 256)
        gate = contract(HN[...], WG[:, cols], 1, 0)
        up = contract(HN[...], WU[:, cols], 1, 0)
        sig = jax.nn.sigmoid(gate)
        silu = gate * sig
        act = (silu * up).astype(BF)
        if n == tiles - 1:
            T3[2] = act
            act = jnp.where(shared, jnp.zeros_like(act), act)
        ACT[:, cols] = act
        BYG[:, cols] = up * sig * (1.0 + gate * (1.0 - sig))
        BYU[:, cols] = silu
    rd[1](3)
    gg[2]()
    rd[2]()
    for n in (tiles - 1, *range(tiles - 1)):
        cols = slice(n * 256, n * 256 + 256)
        dact = contract(G[...], WD[cols, :], 1, 1)
        dgate, dup = (dact * BYG[:, cols]).astype(BF), (dact * BYU[:, cols]).astype(BF)
        if n == tiles - 1:
            T3[0], T3[1] = dgate, dup
            dgate, dup = (jnp.where(shared, jnp.zeros_like(v), v) for v in (dgate, dup))
        DGA[:, cols] = dgate
        DUP[:, cols] = dup
        (last_tile_grads if n == tiles - 1 else tile_grads)(n)
        begin(n, (f0, f1, f2)[n], FWAIT[n])
        if n == 0:
            tick()
    blocks = lambda i, f: [zbufs[i][0].__setitem__((r % 2, unit(r)), f(slice(r * 256, r * 256 + 256)).astype(BF)) for r in range(4)]
    tick()
    for n in range(4):
        cols = slice(n * 256, n * 256 + 256)
        PART[0, :, cols] = (contract(DGA[...], WG[cols, :], 1, 1) + contract(DUP[...], WU[cols, :], 1, 1)).astype(BF)
    hid = reduce_start(0, 0)
    tick()
    for n in range(4):
        cols = slice(n * 256, n * 256 + 256)
        PART[1, :, cols] = contract(ACT[...], WD[:, cols], 1, 0).astype(BF)
    tick()
    dh = hid()
    res = RES[rows(j, 128), :]
    scale = lax.rsqrt(jnp.mean(res * res, axis=1, keepdims=True) + EPSILON)
    w = dh * NG2[...]
    inner = jnp.mean(w * res, axis=1, keepdims=True)
    dres = G[rows(j, 128), :].astype(F32) + scale * w - res * (scale * scale * scale * inner)
    DRES[...] = dres
    GP[...] = jnp.zeros_like(GP)
    GP[1:2, :] = jnp.sum(dh * res * scale, axis=0, keepdims=True)
    DB[rows(j, 128), :] = dres.astype(BF)
    dbg = gather_start(DB)
    tick()
    tick()
    dbg()
    fin = reduce_start(1, 1)

    DAT[...] = contract(DB[...], WO[pl.ds(pl.multiple_of(base, 256), 256), :], 1, 1).astype(BF)
    own_heads = AF[:, pl.ds(pl.multiple_of(base, 256), 256)]
    blocks(3, lambda cols: contract(own_heads, DB[:, cols], 0, 0))
    begin(3, fo, OWAIT)
    DK[...] = jnp.zeros_like(DK)
    DV[...] = jnp.zeros_like(DV)

    def attend_back(b):
        qs, ks = pl.ds(b * 256, 256), pl.ds(b * 256, 512)
        for hp in range(2):
            cols = slice(hp * 128, hp * 128 + 128)
            q_b, k_b, v_b, d_b = Q[qs, cols], K[ks, cols], V[ks, cols], DAT[qs, cols]
            dq = dk = dv = None
            for h in range(2):
                m = head_mask[h]
                d_h = d_b * m
                p = PM[b * 4 + hp * 2 + h]
                dp = contract(d_h, v_b, 1, 1)
                ds = (p * (dp - jnp.sum(p * dp, axis=1, keepdims=True))).astype(BF)
                one = (contract(ds, k_b * m, 1, 0), contract(ds, q_b * m, 0, 0), contract(p.astype(BF), d_h, 0, 0))
                dq, dk, dv = one if dq is None else (dq + one[0], dk + one[1], dv + one[2])
            DQKV[qs, cols] = (dq * 0.125).astype(BF)
            DK[ks, cols] += dk
            DV[ks, cols] += dv

    attend_back(0)
    tick()
    attend_back(1)
    HS[:, 0:256] = DK[0:256, :].astype(BF)
    HS[:, 256:512] = DV[0:256, :].astype(BF)
    back = net.make(HS, HR, core_nb)
    net.start(back, c == 1)

    @pl.when(c == 0)
    def _():
        back.wait_recv()
        DK[512:768, :] += HR[:, 0:256].astype(F32)
        DV[512:768, :] += HR[:, 256:512].astype(F32)

    DQKV[:, 256:512] = DK[256:768, :].astype(BF)
    DQKV[:, 512:768] = DV[256:768, :].astype(BF)
    blocks(4, lambda cols: contract(XN[:, cols], DQKV[...], 0, 0))
    begin(4, fq, QWAIT)
    tick()
    OS[...] = (RES[rows(j, 128), :] + fin()).astype(BF)
    sent = send_blocks(OS, out)
    for n in range(4):
        cols = slice(n * 256, n * 256 + 256)
        PART[0, :, cols] = contract(DQKV[...], WQKV[cols, :], 1, 1).astype(BF)
    last = reduce_start(2, 0)
    tick(3)
    dx = last()
    v = X[rows(j, 128), :].astype(F32)
    scale = lax.rsqrt(jnp.mean(v * v, axis=1, keepdims=True) + EPSILON)
    w = dx * NG1[...]
    inner = jnp.mean(w * v, axis=1, keepdims=True)
    GS[...] = DRES[...] + scale * w - v * (scale * scale * scale * inner)
    GP[0:1, :] = jnp.sum(dx * v * scale, axis=0, keepdims=True)
    sent_in = send_blocks(GS, gin)

    me = 4 * x + 2 * y + c
    got = []
    for d in range(1, NPLANE):
        xx, yy, cc = flip(x, d & 1), flip(y, d & 2), flip(c, d & 4)
        copy = net.make(GP.at[:, lanes(2 * xx + cc)], GR.at[me], dev(z, xx, yy, cc))
        net.start(copy)
        got.append(copy)
    keep = local(GP.at[:, lanes(row)], GR.at[me])
    keep.start()
    tick(2)
    keep.wait()
    for copy in got:
        copy.wait_recv()
    total = GR[0]
    for d in range(1, NPLANE):
        total = total + GR[d]
    GZS[...] = total
    got = []
    for d in range(1, nz):
        copy = net.make(GZS, GZ.at[z], dev((z + d) % nz, x, y, c))
        net.start(copy)
        got.append(copy)
    keep = local(GZS, GZ.at[z])
    keep.start()
    tick(30)
    keep.wait()
    for copy in got:
        copy.wait_recv()
    total = GZ[0]
    for d in range(1, nz):
        total = total + GZ[d]
    gains[...] = total
    sent()
    sent_in()
    for copy in flushes:
        copy.wait()
    net.finish()


def spread_kernel(nz, ff_half, ff_cut, f0, f1, f2, fo, fq, out_in, gin_in, gains, *refs):
    out, gin, gn1, gwq, gwk, gwv, gwo, gn2, gwg, gwu, gwd = refs[:11]
    I0, I1, I2, IO, IQ, OG, OU, OD, OO, OQ, PO, PG, sem, sem_out = refs[11:]
    moves = ((f0, I0), (f1, I1), (f2, I2), (fo, IO), (fq, IQ), (out_in, PO), (gin_in, PG))
    loads = [pltpu.make_async_copy(a, b, sem.at[i]) for i, (a, b) in enumerate(moves)]
    for copy in loads:
        copy.start()
    stores = []

    def store(buf, dst):
        stores.append(pltpu.make_async_copy(buf, dst, sem_out.at[len(stores)]))
        stores[-1].start()

    gn1[...] = gains[0:1, :]
    gn2[...] = gains[1:2, :]
    x = lax.axis_index("row") // 2
    chips = (x, 1 - x)
    for n, I in enumerate((I0, I1)):
        loads[n].wait()
        for u, xx in enumerate(chips):
            at = pl.multiple_of(xx * ff_half + n * 256, 128)
            for q in range(nz):
                OG[q * 64 : q * 64 + 64, pl.ds(at, 256)] = I[q, u, :, 0:256].astype(F32)
                OU[q * 64 : q * 64 + 64, pl.ds(at, 256)] = I[q, u, :, 256:512].astype(F32)
                OD[pl.ds(at + q * 64, 64), :] = I[q, u, :, 512:768].astype(F32)
    loads[2].wait()
    for u, at in enumerate((x * ff_half + ff_half - 256, ff_cut, (1 - x) * ff_half + ff_half - 256)):
        at = pl.multiple_of(at, 128) if u != 1 else at
        for q in range(nz):
            OG[q * 64 : q * 64 + 64, pl.ds(at, 128)] = I2[q, u, :, 0:128].astype(F32)
            OU[q * 64 : q * 64 + 64, pl.ds(at, 128)] = I2[q, u, :, 128:256].astype(F32)
            side = q // 2 * 128
            OD[pl.ds(at + q % 2 * 64, 64), side : side + 128] = I2[q, u, :, 256:384].astype(F32)
    for buf, dst in ((OG, gwg), (OU, gwu), (OD, gwd)):
        store(buf, dst)
    loads[3].wait()
    for u, xx in enumerate(chips):
        for q in range(nz):
            OO[pl.ds(pl.multiple_of(xx * 256, 256) + q * 64, 64), :] = IO[q, u].astype(F32)
    store(OO, gwo)
    loads[4].wait()
    for i, dst in enumerate((gwq, gwk, gwv)):
        for u, xx in enumerate(chips):
            for q in range(nz):
                OQ[i, q * 64 : q * 64 + 64, pl.ds(pl.multiple_of(xx * 256, 256), 256)] = IQ[q, u, :, i * 256 : i * 256 + 256].astype(F32)
        store(OQ.at[i], dst)
    for load, buf, dst in ((loads[5], PO, out), (loads[6], PG, gin)):
        load.wait()
        store(buf, dst)
    for copy in stores:
        copy.wait()


def fused(nz, tokens, cotangent, seg_ids, norm_one, wq, wk, wv, wo, norm_two, w_gate, w_up, w_down):
    ff = w_gate.shape[1]
    ff_half = -(-ff // 512) * 256
    ff_cut = ff - ff_half
    vm = pltpu.VMEM
    zshapes = [(2, 256, 768)] * 2 + [(3, 256, 384), (2, 256, 256), (2, 256, 768)]
    zscratch, fshapes = [], []
    for units, rows, cols in zshapes:
        fshapes.append((nz, units, rows // nz, cols))
        zscratch += [
            vm((2, units, rows, cols), BF),
            vm((units, rows, cols), BF),
            vm((2, nz - 1, units, rows // nz, cols), BF),
            vm((nz, rows // nz, cols) if len(fshapes) in LATE else (rows // nz, cols), BF),
            vm(fshapes[-1], BF),
        ]
    scratch = [
        vm((512, D), BF), vm((512, D), BF), vm((D, 768), BF), vm((D, D), BF),
        vm((D, ff_half), BF), vm((D, ff_half), BF), vm((ff_half, D), BF), vm((1, D), F32), vm((1, D), F32),
        vm((512, D), BF), vm((512, 256), BF), vm((768, 256), BF), vm((768, 256), BF), vm((2, 256, 512), F32),
        vm((8, 256, 512), F32), vm((512, D), BF),
        vm((2, 512, D), BF), vm((3, 3, 128, D), BF),
        vm((512, D), BF), vm((512, D), F32), vm((128, D), F32), vm((512, ff_half), BF), vm((512, ff_half), BF),
        vm((512, ff_half), BF), vm((512, D), BF), vm((512, 256), BF), vm((512, ff_half), F32), vm((512, ff_half), F32), vm((3, 512, 256), BF),
        vm((768, 256), F32), vm((768, 256), F32), vm((512, 768), BF), vm((256, 512), BF), vm((256, 512), BF),
        vm((128, D), BF), vm((128, D), F32), vm((8, D), F32), vm((8, 8, 256), F32), vm((nz, 8, 256), F32), vm((8, 256), F32),
        *zscratch,
        pltpu.SemaphoreType.DMA((10,)), pltpu.SemaphoreType.DMA((258,)), pltpu.SemaphoreType.DMA((28,)),
    ]
    hbm, vmem = pl.BlockSpec(memory_space=pl.ANY), pl.BlockSpec(memory_space=pltpu.VMEM)
    sds = jax.ShapeDtypeStruct
    done = pl.pallas_call(
        functools.partial(layer_kernel, nz, ff_half, ff_cut),
        out_shape=(sds((512, 256), BF), sds((512, 256), F32), sds((8, 256), F32), *(sds(f, BF) for f in fshapes)),
        in_specs=[hbm, hbm, vmem, vmem, hbm, hbm, hbm, hbm, vmem, hbm, hbm, hbm],
        out_specs=(hbm, hbm, vmem, *(hbm for f in fshapes)),
        scratch_shapes=scratch,
        compiler_params=pltpu.CompilerParams(collective_id=0, has_side_effects=True, vmem_limit_bytes=62 << 20),
        name="layer",
    )(
        tokens, cotangent, seg_ids, norm_one[None], wq, wk, wv, wo, norm_two[None], w_gate, w_up, w_down,
    )
    out, gin, gains, *sums = done
    grads = (
        sds((512, 256), BF), sds((512, 256), F32), sds((1, 256), F32),
        sds((256, 512), F32), sds((256, 512), F32), sds((256, 512), F32), sds((512, 256), F32),
        sds((1, 256), F32), sds((256, ff), F32), sds((256, ff), F32), sds((ff, 256), F32),
    )
    res = pl.pallas_call(
        functools.partial(spread_kernel, nz, ff_half, ff_cut),
        out_shape=grads,
        in_specs=[hbm] * 7 + [vmem],
        out_specs=tuple(vmem if i in (2, 7) else hbm for i in range(11)),
        scratch_shapes=[vm(f, BF) for f in fshapes]
        + [vm((256, ff), F32), vm((256, ff), F32), vm((ff, 256), F32), vm((512, 256), F32), vm((3, 256, 512), F32)]
        + [vm((512, 256), BF), vm((512, 256), F32), pltpu.SemaphoreType.DMA((7,)), pltpu.SemaphoreType.DMA((9,))],
        compiler_params=pltpu.CompilerParams(vmem_limit_bytes=63 << 20),
        name="spread",
    )(*sums, out, gin, gains)
    res = list(res)
    res[2], res[7] = res[2][0], res[7][0]
    return tuple(res)


def solution(mesh):
    in_specs = (
        P(("dp", "col"), "row"),
        P(("dp", "col"), "row"),
        P("dp", None),
        P("row"),
        P("row", "col"),
        P("row", "col"),
        P("row", "col"),
        P("col", "row"),
        P("row"),
        P("row", "col"),
        P("row", "col"),
        P("col", "row"),
    )
    out_specs = (
        P(("dp", "col"), "row"),
        P(("dp", "col"), "row"),
        P("row"),
        P("row", "col"),
        P("row", "col"),
        P("row", "col"),
        P("col", "row"),
        P("row"),
        P("row", "col"),
        P("row", "col"),
        P("col", "row"),
    )
    sizes = dict(mesh.shape)
    body = per_device
    if sizes["row"] == 4 and sizes["col"] == 2:
        body = functools.partial(fused, sizes["dp"])
    return jax.shard_map(
        body, mesh=mesh, in_specs=in_specs, out_specs=out_specs, check_vma=False
    )
```

```python
import functools

import jax
import jax.numpy as jnp
from jax import lax
from jax.experimental import pallas as pl
from jax.experimental.pallas import tpu as pltpu
from jax.sharding import PartitionSpec as P

D = 1024
HEAD_DIM = 64


EPSILON = 1e-05
NEGATIVE = -1e30


def for_sending(array):

    def short(part):
        return part.astype(jnp.bfloat16) if part.dtype == jnp.float32 else part

    return jax.tree.map(short, array)


def shifted(block, axis, distance):
    devices = range(lax.axis_size(axis))
    route = [(i - distance, i) for i in devices if i - distance in devices]
    return lax.ppermute(block, axis, route)


def matmul(first_op, second_op):
    return jnp.dot(first_op, second_op, preferred_element_type=jnp.float32)


def matmul_tn(first_op, second_op):
    return lax.dot_general(
        first_op, second_op, (((0,), (0,)), ((), ())), preferred_element_type=jnp.float32
    )


def matmul_nt(first_op, second_op):
    return lax.dot_general(
        first_op, second_op, (((1,), (1,)), ((), ())), preferred_element_type=jnp.float32
    )


def tokens_col(array_in):
    return lax.all_gather(array_in, "col", axis=0, tiled=True)


def tokens_row(array_in):
    return lax.all_gather(for_sending(array_in), "row", axis=0, tiled=True).astype(array_in.dtype)


def summed_row(array_in):
    return lax.psum_scatter(
        array_in.astype(jnp.bfloat16), "row", scatter_dimension=0, tiled=True
    ).astype(jnp.float32)


def summed_col(array_in):
    return lax.psum_scatter(
        array_in.astype(jnp.bfloat16), "col", scatter_dimension=0, tiled=True
    ).astype(jnp.float32)


def feature_total(array_in):
    return lax.psum(array_in, "row")


def window_parts(queries, keys_all, ids_ext, offset, head_cols):
    t_local = queries.shape[0]
    block_rows = min(512, t_local)
    key_reach = min(2048, t_local)
    window = key_reach + block_rows
    head_count = head_cols // HEAD_DIM
    anchor = offset + t_local - key_reach
    q_blk = lax.dynamic_slice_in_dim(queries, offset, block_rows, 0).reshape(
        block_rows, head_count, HEAD_DIM
    )
    k_win = lax.dynamic_slice_in_dim(keys_all, anchor, window, 0)
    k_blk = k_win[:, :head_cols].reshape(window, head_count, HEAD_DIM)
    v_blk = k_win[:, head_cols:].reshape(window, head_count, HEAD_DIM)
    q_ids = lax.dynamic_slice_in_dim(ids_ext, offset + t_local, block_rows, 0)
    k_ids = lax.dynamic_slice_in_dim(ids_ext, anchor, window, 0)
    q_pos = offset + lax.iota(jnp.int32, block_rows)
    k_pos = offset - key_reach + lax.iota(jnp.int32, window)
    allowed = (q_ids[:, None] == k_ids[None, :]) & (k_pos[None, :] <= q_pos[:, None])
    scores = jnp.einsum(
        "qhd,khd->hqk", q_blk, k_blk, preferred_element_type=jnp.float32
    ) * HEAD_DIM ** (-0.5)
    scores = jnp.where(allowed[None], scores, NEGATIVE)
    return (q_blk, k_blk, v_blk, scores)


def forward(tokens, seg_ids, norm_one, wq, wk, wv, wo, norm_two, w_gate, w_up, w_down):
    token_vals = tokens.astype(jnp.float32)
    scale_one = lax.rsqrt(feature_total(jnp.sum(token_vals * token_vals, axis=1)) / D + EPSILON)
    normed = (token_vals * scale_one[:, None] * norm_one).astype(jnp.bfloat16)
    normed_all = tokens_col(normed)
    w_qkv = jnp.concatenate([wq, wk, wv], axis=1)
    head_cols = wq.shape[1]
    qkv = summed_row(matmul(normed_all, w_qkv)).astype(jnp.bfloat16)
    queries = qkv[:, :head_cols]
    kv_local = qkv[:, head_cols:]
    prior_keys = shifted(kv_local, "row", 1)
    keys_all = jnp.concatenate([prior_keys, kv_local], axis=0)
    t_local = queries.shape[0]
    block_rows = min(512, t_local)
    padded_ids = jnp.concatenate([jnp.full((t_local,), -1, jnp.int32), seg_ids[0]])
    ids_ext = lax.dynamic_slice_in_dim(padded_ids, lax.axis_index("row") * t_local, 2 * t_local, 0)

    def attend(offset):
        q_blk, k_blk, v_blk, scores = window_parts(queries, keys_all, ids_ext, offset, head_cols)
        row_max = jnp.max(scores, axis=2, keepdims=True)
        exp_total = jnp.sum(jnp.exp(scores - row_max), axis=2, keepdims=True)
        log_total = row_max + jnp.log(exp_total)
        prob_low = jnp.exp(scores - log_total).astype(jnp.bfloat16)
        mixed_out = jnp.einsum("hqk,khd->qhd", prob_low, v_blk, preferred_element_type=jnp.float32)
        return (mixed_out.reshape(block_rows, head_cols).astype(jnp.bfloat16), log_total[:, :, 0])

    offsets = lax.iota(jnp.int32, t_local // block_rows) * block_rows
    pieces, log_totals = lax.map(attend, offsets)
    attn_out = pieces.reshape(t_local, head_cols)
    attn_all = tokens_row(attn_out)
    residual = token_vals + summed_col(matmul(attn_all, wo))
    stored = {
        "token_vals": token_vals,
        "scale_one": scale_one,
        "normed_all": normed_all,
        "queries": queries,
        "keys_all": keys_all,
        "ids_ext": ids_ext,
        "log_totals": log_totals,
        "attn_all": attn_all,
        "offsets": offsets,
    }
    f_col = w_gate.shape[1]
    scale_two = lax.rsqrt(feature_total(jnp.sum(residual * residual, axis=1)) / D + EPSILON)
    hidden_in = (residual * scale_two[:, None] * norm_two).astype(jnp.bfloat16)
    hidden_all = tokens_col(hidden_in)
    w_pair = jnp.concatenate([w_gate, w_up], axis=1)
    pair_sum = summed_row(matmul(hidden_all, w_pair))
    gate_pre = pair_sum[:, :f_col]
    up_pre = pair_sum[:, f_col:]
    act_low = (jax.nn.silu(gate_pre) * up_pre).astype(jnp.bfloat16)
    act_all = tokens_row(act_low)
    final_sum = residual + summed_col(matmul(act_all, w_down))
    stored.update(
        {
            "residual": residual,
            "scale_two": scale_two,
            "hidden_all": hidden_all,
            "gate_pre": gate_pre,
            "up_pre": up_pre,
            "act_all": act_all,
        }
    )
    return (final_sum.astype(jnp.bfloat16), stored)


def swiglu_grads(dact, gate_pre, up_pre):
    sigmoid_gate = jax.nn.sigmoid(gate_pre)
    gate_grad = (dact * up_pre * sigmoid_gate * (1.0 + gate_pre * (1.0 - sigmoid_gate))).astype(
        jnp.bfloat16
    )
    up_grad = (dact * gate_pre * sigmoid_gate).astype(jnp.bfloat16)
    return (gate_grad, up_grad)


def per_device(
    tokens, cotangent, seg_ids, norm_one, wq, wk, wv, wo, norm_two, w_gate, w_up, w_down
):
    weights = (tokens, seg_ids, norm_one, wq, wk, wv, wo, norm_two, w_gate, w_up, w_down)
    output, stored = forward(*weights)
    f_col = w_gate.shape[1]
    grad_out = cotangent.astype(jnp.float32)
    grad_all = tokens_col(cotangent)
    dact = summed_row(matmul_nt(grad_all, w_down))
    grad_down = matmul_tn(stored["act_all"], grad_all)
    gate_grad, up_grad = swiglu_grads(dact, stored["gate_pre"], stored["up_pre"])
    dpair = jnp.concatenate([gate_grad, up_grad], axis=1)
    dpair_all = tokens_row(dpair)
    w_pair = jnp.concatenate([w_gate, w_up], axis=1)
    dhidden = summed_col(matmul_nt(dpair_all, w_pair))
    grad_pair = matmul_tn(stored["hidden_all"], dpair_all)
    grad_gate = grad_pair[:, :f_col]
    grad_up = grad_pair[:, f_col:]
    residual = stored["residual"]
    scale_two = stored["scale_two"]
    weighted = dhidden * norm_two
    inner_sum = feature_total(jnp.sum(weighted * residual, axis=1)) / D
    dresid = (
        grad_out + scale_two[:, None] * weighted - residual * (scale_two**3 * inner_sum)[:, None]
    )
    grad_norm_two = jnp.sum(dhidden * residual * scale_two[:, None], axis=0)
    dbranch = dresid.astype(jnp.bfloat16)
    dbranch_all = tokens_col(dbranch)
    attn_grad = summed_row(matmul_nt(dbranch_all, wo)).astype(jnp.bfloat16)
    grad_wo = matmul_tn(stored["attn_all"], dbranch_all)
    queries = stored["queries"]
    keys_all = stored["keys_all"]
    ids_ext = stored["ids_ext"]
    head_cols = wq.shape[1]
    head_count = head_cols // HEAD_DIM
    t_local = queries.shape[0]
    block_rows = min(512, t_local)
    key_reach = min(2048, t_local)
    window = key_reach + block_rows
    inv_root = HEAD_DIM ** (-0.5)

    def attend_back(accum_dkv, inputs):
        offset, log_total = inputs
        q_blk, k_blk, v_blk, scores = window_parts(queries, keys_all, ids_ext, offset, head_cols)
        prob_full = jnp.exp(scores - log_total[:, :, None])
        prob_low = prob_full.astype(jnp.bfloat16)
        d_blk = lax.dynamic_slice_in_dim(attn_grad, offset, block_rows, 0).reshape(
            block_rows, head_count, HEAD_DIM
        )
        dprobs = jnp.einsum("qhd,khd->hqk", d_blk, v_blk, preferred_element_type=jnp.float32)
        dvalue = jnp.einsum("hqk,qhd->khd", prob_low, d_blk, preferred_element_type=jnp.float32)
        center = jnp.sum(prob_full * dprobs, axis=2, keepdims=True)
        dscores = (prob_full * (dprobs - center)).astype(jnp.bfloat16)
        dquery = (
            jnp.einsum("hqk,khd->qhd", dscores, k_blk, preferred_element_type=jnp.float32)
            * inv_root
        )
        dkey = (
            jnp.einsum("hqk,qhd->khd", dscores, q_blk, preferred_element_type=jnp.float32)
            * inv_root
        )
        update = jnp.concatenate(
            [dkey.reshape(window, head_cols), dvalue.reshape(window, head_cols)], axis=1
        )
        anchor = offset + t_local - key_reach
        current = lax.dynamic_slice_in_dim(accum_dkv, anchor, window, 0)
        accum_dkv = lax.dynamic_update_slice_in_dim(accum_dkv, current + update, anchor, 0)
        return (accum_dkv, dquery.reshape(block_rows, head_cols))

    start_grads = jnp.zeros((2 * t_local, 2 * head_cols), jnp.float32)
    accum_dkv, query_grads = lax.scan(
        attend_back, start_grads, (stored["offsets"], stored["log_totals"])
    )
    returned = shifted(accum_dkv[:t_local].astype(jnp.bfloat16), "row", -1).astype(jnp.float32)
    key_grads = accum_dkv[t_local:] + returned
    dqkv = jnp.concatenate([query_grads.reshape(t_local, head_cols), key_grads], axis=1).astype(
        jnp.bfloat16
    )
    dqkv_all = tokens_row(dqkv)
    w_qkv = jnp.concatenate([wq, wk, wv], axis=1)
    dnormed = summed_col(matmul_nt(dqkv_all, w_qkv))
    grad_qkv = matmul_tn(stored["normed_all"], dqkv_all)
    grad_wq = grad_qkv[:, :head_cols]
    grad_wk = grad_qkv[:, head_cols : 2 * head_cols]
    grad_wv = grad_qkv[:, 2 * head_cols :]
    token_vals = stored["token_vals"]
    scale_one = stored["scale_one"]
    weighted_one = dnormed * norm_one
    inner_one = feature_total(jnp.sum(weighted_one * token_vals, axis=1)) / D
    grad_input = (
        dresid
        + scale_one[:, None] * weighted_one
        - token_vals * (scale_one**3 * inner_one)[:, None]
    )
    grad_norm_one = jnp.sum(dnormed * token_vals * scale_one[:, None], axis=0)
    grad_sums = (
        lax.psum(grad_wq.astype(jnp.bfloat16), "dp").astype(jnp.float32),
        lax.psum(grad_wk.astype(jnp.bfloat16), "dp").astype(jnp.float32),
        lax.psum(grad_wv.astype(jnp.bfloat16), "dp").astype(jnp.float32),
        lax.psum(grad_wo.astype(jnp.bfloat16), "dp").astype(jnp.float32),
        lax.psum(grad_gate.astype(jnp.bfloat16), "dp").astype(jnp.float32),
        lax.psum(grad_up.astype(jnp.bfloat16), "dp").astype(jnp.float32),
        lax.psum(grad_down.astype(jnp.bfloat16), "dp").astype(jnp.float32),
    )
    gain_sums = lax.psum((grad_norm_one, grad_norm_two), ("dp", "col"))
    return (
        output,
        grad_input,
        gain_sums[0],
        grad_sums[0],
        grad_sums[1],
        grad_sums[2],
        grad_sums[3],
        gain_sums[1],
        grad_sums[4],
        grad_sums[5],
        grad_sums[6],
    )


MESH = pl.DeviceIdType.MESH
BF = jnp.bfloat16
F32 = jnp.float32
NPLANE = 8
TAIL, HELD = (0, 3), (0, 3)
LATE = (1, 3, 4)
NEWFIRST, LAG = True, 4
FWAIT, OWAIT, QWAIT = (2, 6, 0), 0, 0


def contract(a, b, ca, cb):
    return lax.dot_general(a, b, (((ca,), (cb,)), ((), ())), preferred_element_type=F32)


class Copies:
    def __init__(self, send, recv):
        self.send, self.recv, self.used, self.kept, self.open = send, recv, 0, 1, []

    def take(self, amount=1):
        base = self.used
        self.used += amount
        return base

    def make(self, src, dst, to, site=None, own=False):
        site = self.take() if site is None else site
        self.kept += own
        return pltpu.make_async_remote_copy(
            src_ref=src,
            dst_ref=dst,
            send_sem=self.send.at[self.kept - 1 if own else 0],
            recv_sem=self.recv.at[site],
            device_id=to,
            device_id_type=MESH,
        )

    def start(self, copy, when=None):
        self.open.append((copy, when))
        if when is None:
            copy.start()
        else:
            pl.when(when)(copy.start)

    def finish(self):
        for copy, when in self.open:
            if when is None:
                copy.wait_send()
            else:
                pl.when(when)(copy.wait_send)
        self.open = []


def layer_kernel(nz, ff_half, ff_cut, *refs):
    it = iter(refs)
    take = lambda n: [next(it) for _ in range(n)]
    tok, cot, seg, n1, wq, wk, wv, wo, n2, wg, wu, wd = take(12)
    out, gin, gains, f0, f1, f2, fo, fq = take(8)
    X, G, WQKV, WO, WG, WU, WD, NG1, NG2 = take(9)
    XN, Q, K, V, BIAS, PM, AF = take(7)
    PART, RX = take(2)
    HN, RES, DRES, ACT, DGA, DUP, DB, DAT, BYG, BYU, T3 = take(11)
    DK, DV, DQKV, HS, HR = take(5)
    OS, GS, GP, GR, GZ, GZS = take(6)
    zbufs = [take(5) for _ in range(5)]
    send, recv, loc = take(3)

    z, row, y = lax.axis_index("dp"), lax.axis_index("row"), lax.axis_index("col")
    x, c = row // 2, row % 2
    net = Copies(send, recv)
    nloc = [0]

    def local(src, dst):
        nloc[0] += 1
        return pltpu.make_async_copy(src, dst, loc.at[nloc[0] - 1])

    def dev(zz, xx, yy, cc):
        return (zz, 2 * xx + cc, yy)

    core_nb, x_nb, y_nb = dev(z, x, y, 1 - c), dev(z, 1 - x, y, c), dev(z, x, 1 - y, c)
    z_up, z_dn = dev(z + 1, x, y, c), dev(z - 1, x, y, c)
    lanes = lambda i, n=256: pl.ds(pl.multiple_of(i * n, 128), n)
    rows = lambda i, n: pl.ds(pl.multiple_of(i * n, n if n % 16 else 16), n)
    flip = lambda v, bit: 1 - v if bit else v

    barrier = pltpu.get_barrier_semaphore()
    for d in range(1, NPLANE):
        pl.semaphore_signal(
            barrier, inc=1, device_id=dev(z, flip(x, d & 1), flip(y, d & 2), flip(c, d & 4)), device_id_type=MESH
        )
    for d in range(1, nz):
        pl.semaphore_signal(barrier, inc=1, device_id=dev((z + d) % nz, x, y, c), device_id_type=MESH)
    for _, _, ZR, _, _ in zbufs:

        @pl.when(z == 0)
        def _(ZR=ZR):
            ZR[0, nz - 2] = jnp.zeros(ZR.shape[2:], BF)

        @pl.when(z == nz - 1)
        def _(ZR=ZR):
            ZR[1, nz - 2] = jnp.zeros(ZR.shape[2:], BF)

    seg_f = seg[...].astype(F32)
    own = jnp.where(c == 0, seg_f[:, :512], seg_f[:, 512:])
    before = jnp.where(c == 0, jnp.full((1, 256), -1.0, F32), seg_f[:, 256:512])
    ids = jnp.concatenate([before, own], axis=1)
    for b in range(2):
        k_id = jnp.broadcast_to(ids[:, b * 256 : b * 256 + 512], (256, 512))
        q_id = jnp.broadcast_to(ids[:, 256 + b * 256 : 512 + b * 256], (512, 256)).T
        q_pos = lax.broadcasted_iota(jnp.int32, (256, 512), 0) + 256
        k_pos = lax.broadcasted_iota(jnp.int32, (256, 512), 1)
        BIAS[b] = jnp.where((q_id == k_id) & (k_pos <= q_pos), 0.0, NEGATIVE)

    @pl.when(c == 0)
    def _():
        K[0:256, :] = jnp.zeros((256, 256), BF)
        V[0:256, :] = jnp.zeros((256, 256), BF)

    pl.semaphore_wait(barrier, NPLANE - 1 + nz - 1)

    def gather_tokens(src, buf):
        col = lambda rr: buf.at[:, lanes(rr)]
        mine = c == y
        other = jnp.logical_not(mine)
        keep = local(src, col(row))
        over = net.make(src, col(row), core_nb)
        bx, by = net.take(2), net.take(2)
        to_x = net.make(src, col(row), dev(z, 1 - x, y, y), bx + c)
        to_y = net.make(src, col(row), dev(z, x, 1 - y, y), by + c)
        far = 2 * (1 - x)
        by_y = net.make(col(far), col(far), y_nb)
        by_x = net.make(col(2 * x + 1), col(2 * x + 1), x_nb)
        got_x = [net.make(src, col(row), core_nb, bx + k) for k in range(2)]
        got_y = [net.make(src, col(row), core_nb, by + k) for k in range(2)]

        def start():
            pl.when(mine)(keep.start)
            net.start(to_x)
            net.start(to_y)
            net.start(over, other)

        def arrive():
            @pl.when(mine)
            def _():
                got_x[0].wait_recv()
                by_y.start()

            @pl.when(other)
            def _():
                got_y[1].wait_recv()
                by_x.start()

            net.open += [(by_y, mine), (by_x, other)]

        def rest():
            @pl.when(mine)
            def _():
                got_x[1].wait_recv()
                over.wait_recv()
                keep.wait()

            @pl.when(other)
            def _():
                got_y[0].wait_recv()
                by_y.wait_recv()
                by_x.wait_recv()

        return start, arrive, rest

    def relay(src_of, dst_of):
        keep = local(src_of(x), dst_of(row))
        across = net.make(src_of(x), dst_of(row), core_nb)
        far = net.make(src_of(1 - x), dst_of(row), x_nb)
        theirs = dst_of(2 * (1 - x) + c)
        fwd = net.make(theirs, theirs, core_nb)

        def start():
            keep.start()
            net.start(far)
            net.start(across)

        def arrive():
            far.wait_recv()
            net.start(fwd)

        def rest():
            keep.wait()
            across.wait_recv()
            fwd.wait_recv()

        return start, arrive, rest

    def z_gather(at):
        sites = (net.take(nz - 1), net.take(nz - 1))

        def step(s):
            for way, to in ((0, z_up), (1, z_dn)):
                zz = z if way == 0 else nz - 1 - z
                ref = at(z - s if way == 0 else z + s)
                have = zz >= s
                if s > 0:
                    pl.when(have)(net.make(ref, ref, to, sites[way] + s - 1).wait_recv)
                if s < nz - 1:
                    net.start(net.make(ref, ref, to, sites[way] + s), have & (zz < nz - 1))

        return step

    def relay_z(pairs, whole, n_rows):
        n = n_rows // nz
        keep = [local(a, b) for a, b in pairs(x, row, 0, n_rows)]
        across = [net.make(a, b, core_nb) for a, b in pairs(x, row, 0, n_rows)]
        far = [net.make(a, b, x_nb) for a, b in pairs(1 - x, row, z * n, n)]
        hop = z_gather(lambda q: whole(2 * (1 - x) + c, q * n, n))
        theirs = whole(2 * (1 - x) + c, 0, n_rows)
        fwd = net.make(theirs, theirs, core_nb)

        def begin():
            for copy in far:
                net.start(copy)
            for copy in keep:
                copy.start()
            for copy in across:
                net.start(copy)

        def step(s):
            if s == 0:
                for copy in far:
                    copy.wait_recv()
            hop(s)
            if s == nz - 1:
                net.start(fwd)

        def rest():
            for copy in keep:
                copy.wait()
            for copy in across:
                copy.wait_recv()
            fwd.wait_recv()

        return begin, step, rest

    def gather_wo():
        at = lambda yy, rr: WO.at[rows(yy, 512), lanes(rr)]
        keep = local(wo, at(y, row))
        across = net.make(wo, at(y, row), core_nb)
        to_x, to_y = net.make(wo, at(y, row), x_nb), net.make(wo, at(y, row), y_nb)
        rx = 2 * (1 - x) + c
        on_y = net.make(at(y, rx), at(y, rx), y_nb)
        others = (at(y, rx), at(1 - y, row), at(1 - y, rx))
        fwd = [net.make(ref, ref, core_nb) for ref in others]

        def start():
            net.start(to_x)
            net.start(to_y)
            keep.start()
            net.start(across)

        def arrive():
            to_x.wait_recv()
            net.start(on_y)
            net.start(fwd[0])

        def pass_on():
            to_y.wait_recv()
            net.start(fwd[1])
            on_y.wait_recv()
            net.start(fwd[2])

        def rest():
            keep.wait()
            across.wait_recv()
            for copy in fwd:
                copy.wait_recv()

        return start, arrive, pass_on, rest

    def gather_gain(src, dst):
        keep = local(src, dst.at[:, lanes(row)])
        keep.start()
        got = []
        for to in (core_nb, x_nb, dev(z, 1 - x, y, 1 - c)):
            got.append(net.make(src, dst.at[:, lanes(row)], to))
            net.start(got[-1])

        def rest():
            keep.wait()
            for g in got:
                g.wait_recv()

        return rest

    gx, gg = gather_tokens(tok, X), gather_tokens(cot, G)
    some = lambda r0, n: pl.ds(pl.multiple_of(r0, 16), n)
    rqkv = []
    for i, w in ((1, wk), (2, wv), (0, wq)):
        at = lambda rr, r0, n, i=i: WQKV.at[some(rr * 256 + r0, n), pl.ds(i * 256, 256)]
        rqkv.append(relay_z(lambda xx, rr, r0, n, w=w, at=at: [(w.at[some(r0, n), lanes(xx)], at(rr, r0, n))], at, 256))
    ro = gather_wo()
    both = ff_half - ff_cut
    rff = []
    for w, W in ((wg, WG), (wu, WU)):
        at = lambda rr, r0, n, W=W: W.at[some(rr * 256 + r0, n), :]

        def pairs(xx, rr, r0, n, w=w, W=W):
            out = []
            for src, dst, width in ((pl.multiple_of(xx * ff_half, 128), 0, ff_cut), (ff_cut, ff_cut, both)):
                out.append((w.at[some(r0, n), pl.ds(src, width)], W.at[some(rr * 256 + r0, n), pl.ds(dst, width)]))
            return out

        rff.append(relay_z(pairs, at, 256))

    def pairs_down(xx, rr, r0, n):
        if n == ff_half:
            parts = ((xx * ff_half, 0, ff_cut), (ff_cut, ff_cut, both))
        else:
            tail = jnp.where(z == nz - 1, ff_cut, xx * ff_half + r0 + n - both)
            parts = ((xx * ff_half + r0, r0, n - both), (tail, r0 + n - both, both))
        return [(wd.at[some(src, k), :], WD.at[some(dst, k), lanes(rr)]) for src, dst, k in parts]

    rd = relay_z(pairs_down, lambda rr, r0, n: WD.at[some(r0, n), lanes(rr)], ff_half)
    for r in rqkv:
        r[0]()
    gx[0]()
    ga = [gather_gain(n1, NG1), gather_gain(n2, NG2)]
    for r in rqkv:
        r[1](0)
    for r in rqkv:
        r[1](1)
    gx[1]()
    for s in range(2, nz):
        for r in rqkv:
            r[1](s)
    for g in ga:
        g()
    for r in (*rff, rd):
        r[0]()
    gx[2]()
    ro[0]()
    for t in range(4):
        v = X[t * 128 : t * 128 + 128, :].astype(F32)
        scale = lax.rsqrt(jnp.mean(v * v, axis=1, keepdims=True) + EPSILON)
        XN[t * 128 : t * 128 + 128, :] = (v * scale * NG1[...]).astype(BF)
    for r in rqkv:
        r[2]()
    K[256:768, :] = contract(XN[...], WQKV[:, 256:512], 1, 0).astype(BF)
    V[256:768, :] = contract(XN[...], WQKV[:, 512:768], 1, 0).astype(BF)
    hk = net.make(K.at[pl.ds(512, 256), :], K.at[pl.ds(0, 256), :], core_nb)
    hv = net.make(V.at[pl.ds(512, 256), :], V.at[pl.ds(0, 256), :], core_nb)
    net.start(hk, c == 0)
    net.start(hv, c == 0)
    Q[...] = (contract(XN[...], WQKV[:, 0:256], 1, 0).astype(BF) * 0.125).astype(BF)
    @pl.when(c == 1)
    def _():
        hk.wait_recv()
        hv.wait_recv()

    lane_id = lax.broadcasted_iota(jnp.int32, (1, 128), 1)
    head_mask = [jnp.where(lane_id < 64, 1.0, 0.0).astype(BF), jnp.where(lane_id < 64, 0.0, 1.0).astype(BF)]

    heads_at = lambda xx, yy, b: AF.at[pl.ds(b * 256, 256), lanes(2 * yy + xx)]
    a_x = [net.make(heads_at(x, y, b), heads_at(x, y, b), x_nb) for b in range(2)]
    a_y = [net.make(heads_at(x, y, b), heads_at(x, y, b), y_nb) for b in range(2)]
    a_far = (
        net.make(heads_at(1 - x, y, 0), heads_at(1 - x, y, 0), y_nb),
        net.make(heads_at(x, 1 - y, 1), heads_at(x, 1 - y, 1), x_nb),
    )
    base = (2 * y + x) * 256
    for b in range(2):
        for hp in range(2):
            cols = slice(hp * 128, hp * 128 + 128)
            q_b, k_b, v_b = Q[b * 256 : b * 256 + 256, cols], K[b * 256 : b * 256 + 512, cols], V[b * 256 : b * 256 + 512, cols]
            total = None
            for h in range(2):
                s = contract(q_b * head_mask[h], k_b, 1, 1) + BIAS[b]
                e = jnp.exp(s - jnp.max(s, axis=1, keepdims=True))
                p = e * (1.0 / jnp.sum(e, axis=1, keepdims=True))
                PM[b * 4 + hp * 2 + h] = p
                part = contract(p.astype(BF), v_b * head_mask[h], 1, 0)
                total = part if total is None else total + part
            AF[b * 256 : b * 256 + 256, pl.ds(pl.multiple_of(base + hp * 128, 128), 128)] = total.astype(BF)
        net.start(a_x[b])
        net.start(a_y[b])
        if b == 0:
            for r in rff:
                r[1](0)
    for r in rff:
        r[1](1)
    rd[1](0)
    ro[1]()
    a_x[0].wait_recv()
    net.start(a_far[0])
    a_y[1].wait_recv()
    net.start(a_far[1])
    gg[0]()
    for r in rff:
        r[1](2)
    rd[1](1)
    ro[2]()
    for r in rff:
        r[1](3)
    rd[1](2)

    j = 2 * x + y
    shard = lambda buf, jj: buf.at[rows(jj, 128), :]

    peers = ((x_nb, 2 * (1 - x) + y), (y_nb, 2 * x + 1 - y), (dev(z, 1 - x, 1 - y, c), 2 * (1 - x) + 1 - y))

    def reduce_start(k, p):
        sent = [net.make(shard(PART.at[p], jj), RX.at[k, i], to, own=True) for i, (to, jj) in enumerate(peers)]
        for copy in (sent[2], sent[0], sent[1]):
            copy.start()

        def end():
            for copy in sent:
                copy.wait_recv()
            for copy in sent:
                copy.wait_send()
            total = PART[p, rows(j, 128), :].astype(F32)
            for i in range(3):
                total = total + RX[k, i].astype(F32)
            return total

        return end

    def gather_start(buf):
        sent = [net.make(shard(buf, j), shard(buf, j), to) for to, _ in peers]
        for copy in (sent[2], sent[0], sent[1]):
            net.start(copy)

        def end():
            for copy in sent:
                copy.wait_recv()

        return end

    def send_blocks(src, dst):
        base_r = net.take(4)
        waits = []
        for dx in range(2):
            for cc in range(2):
                xx = flip(x, dx)
                piece, place = src.at[:, lanes(2 * xx + cc)], dst.at[rows(j, 128), :]
                copy = pltpu.make_async_remote_copy(
                    src_ref=piece,
                    dst_ref=place,
                    send_sem=net.send.at[0],
                    recv_sem=net.recv.at[base_r + dx * 2 + y],
                    device_id=dev(z, xx, c, cc),
                    device_id_type=MESH,
                )
                if dx == 0:
                    here = (c == y) & (c == cc)
                    keep = local(piece, place)
                    pl.when(here)(keep.start)
                    net.start(copy, jnp.logical_not(here))
                    waits.append((keep, here))
                else:
                    net.start(copy)
        piece, place = src.at[:, pl.ds(0, 256)], dst.at[pl.ds(0, 128), :]
        arrivals = [
            (net.make(piece, place, core_nb, base_r + dx * 2 + yy), jnp.logical_not((c == y) & (y == yy)) if dx == 0 else None)
            for dx in range(2)
            for yy in range(2)
        ]

        def end():
            for keep, here in waits:
                pl.when(here)(keep.wait)
            for got, when in arrivals:
                if when is None:
                    got.wait_recv()
                else:
                    pl.when(when)(got.wait_recv)

        return end

    def along_z(tag, dst):
        GB, CR, ZR, RL, FF = zbufs[tag]
        n_rows = CR.shape[1] // nz
        n = n_rows // 2
        last = CR.shape[0] - 1
        part = lambda q, i: pl.ds(pl.multiple_of(q * n_rows + i * n, 16), n)
        own = lambda i: pl.ds(i * n, n)
        over = net.make(GB.at[1 - c], CR, core_nb)
        net.start(over)
        yield
        over.wait_recv()
        for u in range(CR.shape[0]):
            CR[u] = (CR[u].astype(F32) + GB[c, u].astype(F32)).astype(BF)
        sites = [[net.take(nz - 1) for _ in range(2)] for _ in range(2)]
        for s in range(1, nz):
            for i in range(2):
                for way, to in ((0, z_up), (1, z_dn)):
                    zz = z if way == 0 else nz - 1 - z
                    q = nz - s + zz
                    q = q if way == 0 else nz - 1 - q
                    go = (zz < nz - 1) & (zz <= s - 1)
                    first, later = go & (zz == 0), go & (zz > 0)
                    site = sites[way][i] + s - 1
                    there = ZR.at[way, s - 1, :, own(i), :]
                    net.start(net.make(CR.at[:, part(q, i), :], there, to, site), first)
                    if s >= 2:
                        acc = ZR.at[way, s - 2, :, own(i), :]
                        got = net.make(acc, acc, to, site - 1)

                        @pl.when(later)
                        def _(got=got, acc=acc, q=q, i=i):
                            got.wait_recv()
                            acc[...] = (acc[...].astype(F32) + CR[:, part(q, i), :].astype(F32)).astype(BF)

                        net.start(net.make(acc, there, to, site), later)
                yield
        late = len(RL.shape) == 3
        backs = [[net.take(nz - 1) for _ in range(2)] for _ in range(2)]
        here = lambda q, i: FF.at[q, :, own(i), :]
        side = []

        def send_back(i):
            net.start(net.make(here(z, i), here(z, i), z_up, backs[0][i]), z < nz - 1)
            net.start(net.make(here(z, i), here(z, i), z_dn, backs[1][i]), z > 0)

        for i in range(2):
            for way in range(2):
                zz = z if way == 0 else nz - 1 - z
                acc = ZR.at[way, nz - 2, :, own(i), :]
                pl.when(zz > 0)(net.make(acc, acc, z_up, sites[way][i] + nz - 2).wait_recv)
            total = (
                CR[:, part(z, i), :].astype(F32)
                + ZR[0, nz - 2, :, own(i), :].astype(F32)
                + ZR[1, nz - 2, :, own(i), :].astype(F32)
            ).astype(BF)
            if late:
                FF[z, :, own(i), :] = total
                send_back(i)
            else:
                RL[own(i), :] = total[-1]
                side.append(net.make(RL.at[own(i), :], FF.at[z, last, own(i), :], x_nb))
                net.start(side[i])
                FF[z, 0:last, own(i), :] = total[:-1]
            yield
        if not late:
            for i in range(2):
                side[i].wait_recv()
                send_back(i)
                if tag == 4 and i == 1:
                    gates.append(tag)
                yield
        sites = backs
        for s in range(2, nz + 1):
            for i in range(2):
                for way, to in ((0, z_up), (1, z_dn)):
                    zz = z if way == 0 else nz - 1 - z
                    q = z - (s - 1) if way == 0 else z + (s - 1)
                    have = zz >= s - 1
                    ref = here(q, i)
                    pl.when(have)(net.make(ref, ref, to, sites[way][i] + s - 2).wait_recv)
                    if s < nz:
                        net.start(net.make(ref, ref, to, sites[way][i] + s - 1), have & (zz < nz - 1))
                yield
        if late:
            trade = net.make(FF.at[:, last], RL, x_nb)
            while tag in HELD and not gates:
                yield
            net.start(trade)
            for _ in range(LAG):
                yield
            trade.wait_recv()
            flush(FF.at[:, 0:last], dst.at[:, 0:last])
            flush(RL, dst.at[:, last])
        else:
            flush(FF, dst)
        yield

    def flush(buf, dst):
        copy = local(buf, dst)
        copy.start()
        flushes.append(copy)

    flushes, gates = [], []

    lines = []

    def begin(i, dst, wait):
        line = along_z(i, dst)
        next(line)
        lines.append([line, wait])

    def tick(n=1):
        for _ in range(n):
            for _ in range(2):
                for line in (lines[::-1] if NEWFIRST else lines):
                    if line[1] > 0:
                        line[1] -= 1
                    else:
                        next(line[0], None)

    ro[3]()
    for copy in (a_x[1], a_y[0], *a_far):
        copy.wait_recv()
    for t in range(4):
        tile = slice(t * 128, t * 128 + 128)
        res = X[tile, :].astype(F32) + contract(AF[tile, :], WO[...], 1, 0)
        RES[tile, :] = res
        scale = lax.rsqrt(jnp.mean(res * res, axis=1, keepdims=True) + EPSILON)
        HN[tile, :] = (res * scale * NG2[...]).astype(BF)
    gg[1]()
    for r in rff:
        r[2]()
    rd[1](3)
    unit = lambda r: jnp.where(x == r // 2, 0, 1)
    shared = (lax.broadcasted_iota(jnp.int32, (1, 256), 1) >= 256 - both) & (x == 1)

    def tile_grads(n):
        cols = slice(n * 256, n * 256 + 256)
        GB = zbufs[n][0]
        for i, made in enumerate((DGA, DUP)):
            whole = contract(HN[...], made[:, cols], 0, 0)
            for r in range(4):
                GB[r % 2, unit(r), :, i * 256 : i * 256 + 256] = whole[r * 256 : r * 256 + 256].astype(BF)
        whole = contract(ACT[:, cols], G[...], 0, 0)
        for r in range(4):
            GB[r % 2, unit(r), :, 512:768] = whole[:, r * 256 : r * 256 + 256].astype(BF)

    def last_tile_grads(n):
        GB = zbufs[n][0]

        def put(r, cols, a, b):
            GB[r % 2, jnp.where(x == r // 2, 0, 2), :, cols] = a.astype(BF)

            @pl.when(x == r // 2)
            def _():
                GB[r % 2, 1, :, cols] = b.astype(BF)

        for i in range(2):
            whole = contract(HN[...], T3[i], 0, 0)
            for r in range(4):
                rws = whole[r * 256 : r * 256 + 256]
                put(r, slice(i * 128, i * 128 + 128), rws[:, :128], rws[:, 128:])
        whole = contract(T3[2], G[...], 0, 0)
        for r in range(4):
            left, right = whole[:, r * 256 : r * 256 + 128], whole[:, r * 256 + 128 : r * 256 + 256]
            put(
                r,
                slice(256, 384),
                jnp.concatenate([left[:128], right[:128]], axis=0),
                jnp.concatenate([left[128:], right[128:]], axis=0),
            )

    tiles = ff_half // 256
    for n in range(tiles):
        cols = slice(n * 256, n * 256 + 256)
        gate = contract(HN[...], WG[:, cols], 1, 0)
        up = contract(HN[...], WU[:, cols], 1, 0)
        sig = jax.nn.sigmoid(gate)
        silu = gate * sig
        act = (silu * up).astype(BF)
        if n == tiles - 1:
            T3[2] = act
            act = jnp.where(shared, jnp.zeros_like(act), act)
        ACT[:, cols] = act
        BYG[:, cols] = up * sig * (1.0 + gate * (1.0 - sig))
        BYU[:, cols] = silu
    gg[2]()
    rd[2]()
    for n in (tiles - 1, *range(tiles - 1)):
        cols = slice(n * 256, n * 256 + 256)
        dact = contract(G[...], WD[cols, :], 1, 1)
        dgate, dup = (dact * BYG[:, cols]).astype(BF), (dact * BYU[:, cols]).astype(BF)
        if n == tiles - 1:
            T3[0], T3[1] = dgate, dup
            dgate, dup = (jnp.where(shared, jnp.zeros_like(v), v) for v in (dgate, dup))
        DGA[:, cols] = dgate
        DUP[:, cols] = dup
        (last_tile_grads if n == tiles - 1 else tile_grads)(n)
        begin(n, (f0, f1, f2)[n], FWAIT[n])
        if n == 0:
            tick()
    blocks = lambda i, f: [zbufs[i][0].__setitem__((r % 2, unit(r)), f(slice(r * 256, r * 256 + 256)).astype(BF)) for r in range(4)]
    tick()
    for n in range(4):
        cols = slice(n * 256, n * 256 + 256)
        PART[0, :, cols] = (contract(DGA[...], WG[cols, :], 1, 1) + contract(DUP[...], WU[cols, :], 1, 1)).astype(BF)
    hid = reduce_start(0, 0)
    tick()
    for n in range(4):
        cols = slice(n * 256, n * 256 + 256)
        PART[1, :, cols] = contract(ACT[...], WD[:, cols], 1, 0).astype(BF)
    tick()
    dh = hid()
    res = RES[rows(j, 128), :]
    scale = lax.rsqrt(jnp.mean(res * res, axis=1, keepdims=True) + EPSILON)
    w = dh * NG2[...]
    inner = jnp.mean(w * res, axis=1, keepdims=True)
    dres = G[rows(j, 128), :].astype(F32) + scale * w - res * (scale * scale * scale * inner)
    DRES[...] = dres
    GP[...] = jnp.zeros_like(GP)
    GP[1:2, :] = jnp.sum(dh * res * scale, axis=0, keepdims=True)
    DB[rows(j, 128), :] = dres.astype(BF)
    dbg = gather_start(DB)
    tick()
    tick()
    dbg()
    fin = reduce_start(1, 1)

    DAT[...] = contract(DB[...], WO[pl.ds(pl.multiple_of(base, 256), 256), :], 1, 1).astype(BF)
    own_heads = AF[:, pl.ds(pl.multiple_of(base, 256), 256)]
    blocks(3, lambda cols: contract(own_heads, DB[:, cols], 0, 0))
    begin(3, fo, OWAIT)
    DK[...] = jnp.zeros_like(DK)
    DV[...] = jnp.zeros_like(DV)

    def attend_back(b):
        qs, ks = pl.ds(b * 256, 256), pl.ds(b * 256, 512)
        for hp in range(2):
            cols = slice(hp * 128, hp * 128 + 128)
            q_b, k_b, v_b, d_b = Q[qs, cols], K[ks, cols], V[ks, cols], DAT[qs, cols]
            dq = dk = dv = None
            for h in range(2):
                m = head_mask[h]
                d_h = d_b * m
                p = PM[b * 4 + hp * 2 + h]
                dp = contract(d_h, v_b, 1, 1)
                ds = (p * (dp - jnp.sum(p * dp, axis=1, keepdims=True))).astype(BF)
                one = (contract(ds, k_b * m, 1, 0), contract(ds, q_b * m, 0, 0), contract(p.astype(BF), d_h, 0, 0))
                dq, dk, dv = one if dq is None else (dq + one[0], dk + one[1], dv + one[2])
            DQKV[qs, cols] = (dq * 0.125).astype(BF)
            DK[ks, cols] += dk
            DV[ks, cols] += dv

    attend_back(0)
    tick()
    attend_back(1)
    HS[:, 0:256] = DK[0:256, :].astype(BF)
    HS[:, 256:512] = DV[0:256, :].astype(BF)
    back = net.make(HS, HR, core_nb)
    net.start(back, c == 1)

    @pl.when(c == 0)
    def _():
        back.wait_recv()
        DK[512:768, :] += HR[:, 0:256].astype(F32)
        DV[512:768, :] += HR[:, 256:512].astype(F32)

    DQKV[:, 256:512] = DK[256:768, :].astype(BF)
    DQKV[:, 512:768] = DV[256:768, :].astype(BF)
    blocks(4, lambda cols: contract(XN[:, cols], DQKV[...], 0, 0))
    begin(4, fq, QWAIT)
    tick()
    OS[...] = (RES[rows(j, 128), :] + fin()).astype(BF)
    sent = send_blocks(OS, out)
    for n in range(4):
        cols = slice(n * 256, n * 256 + 256)
        PART[0, :, cols] = contract(DQKV[...], WQKV[cols, :], 1, 1).astype(BF)
    tick(TAIL[0])
    last = reduce_start(2, 0)
    tick(TAIL[1])
    dx = last()
    v = X[rows(j, 128), :].astype(F32)
    scale = lax.rsqrt(jnp.mean(v * v, axis=1, keepdims=True) + EPSILON)
    w = dx * NG1[...]
    inner = jnp.mean(w * v, axis=1, keepdims=True)
    GS[...] = (DRES[...] + scale * w - v * (scale * scale * scale * inner)).astype(BF)
    GP[0:1, :] = jnp.sum(dx * v * scale, axis=0, keepdims=True)
    sent_in = send_blocks(GS, gin)

    me = 4 * x + 2 * y + c
    got = []
    for d in range(1, NPLANE):
        xx, yy, cc = flip(x, d & 1), flip(y, d & 2), flip(c, d & 4)
        copy = net.make(GP.at[:, lanes(2 * xx + cc)], GR.at[me], dev(z, xx, yy, cc))
        net.start(copy)
        got.append(copy)
    keep = local(GP.at[:, lanes(row)], GR.at[me])
    keep.start()
    tick(2)
    keep.wait()
    for copy in got:
        copy.wait_recv()
    total = GR[0]
    for d in range(1, NPLANE):
        total = total + GR[d]
    GZS[...] = total
    got = []
    for d in range(1, nz):
        copy = net.make(GZS, GZ.at[z], dev((z + d) % nz, x, y, c))
        net.start(copy)
        got.append(copy)
    keep = local(GZS, GZ.at[z])
    keep.start()
    tick(30)
    keep.wait()
    for copy in got:
        copy.wait_recv()
    total = GZ[0]
    for d in range(1, nz):
        total = total + GZ[d]
    gains[...] = total
    sent()
    sent_in()
    for copy in flushes:
        copy.wait()
    net.finish()


def spread_kernel(nz, ff_half, ff_cut, f0, f1, f2, fo, fq, out_in, gin_in, gains, *refs):
    out, gin, gn1, gwq, gwk, gwv, gwo, gn2, gwg, gwu, gwd = refs[:11]
    I0, I1, I2, IO, IQ, OG, OU, OD, OO, OQ, PO, PG, PF, sem, sem_out = refs[11:]
    moves = ((f0, I0), (f1, I1), (f2, I2), (fo, IO), (fq, IQ), (out_in, PO), (gin_in, PG))
    loads = [pltpu.make_async_copy(a, b, sem.at[i]) for i, (a, b) in enumerate(moves)]
    for i in (5, 6, 4, 3, 0, 1, 2):
        loads[i].start()
    stores = []

    def store(buf, dst):
        stores.append(pltpu.make_async_copy(buf, dst, sem_out.at[len(stores)]))
        stores[-1].start()

    gn1[...] = gains[0:1, :]
    gn2[...] = gains[1:2, :]
    x = lax.axis_index("row") // 2
    chips = (x, 1 - x)
    loads[5].wait()
    store(PO, out)
    loads[6].wait()
    PF[...] = PG[...].astype(F32)
    store(PF, gin)
    loads[4].wait()
    for i, dst in enumerate((gwq, gwk, gwv)):
        for u, xx in enumerate(chips):
            for q in range(nz):
                OQ[i, q * 64 : q * 64 + 64, pl.ds(pl.multiple_of(xx * 256, 256), 256)] = IQ[q, u, :, i * 256 : i * 256 + 256].astype(F32)
        store(OQ.at[i], dst)
    loads[3].wait()
    for u, xx in enumerate(chips):
        for q in range(nz):
            OO[pl.ds(pl.multiple_of(xx * 256, 256) + q * 64, 64), :] = IO[q, u].astype(F32)
    store(OO, gwo)

    def store_part(at, width):
        cols = pl.ds(at, width)
        store(OG.at[:, cols], gwg.at[:, cols])
        store(OU.at[:, cols], gwu.at[:, cols])
        store(OD.at[cols, :], gwd.at[cols, :])

    for n, I in enumerate((I0, I1)):
        loads[n].wait()
        for u, xx in enumerate(chips):
            at = pl.multiple_of(xx * ff_half + n * 256, 128)
            for q in range(nz):
                OG[q * 64 : q * 64 + 64, pl.ds(at, 256)] = I[q, u, :, 0:256].astype(F32)
                OU[q * 64 : q * 64 + 64, pl.ds(at, 256)] = I[q, u, :, 256:512].astype(F32)
                OD[pl.ds(at + q * 64, 64), :] = I[q, u, :, 512:768].astype(F32)
            store_part(at, 256)
    loads[2].wait()
    for u, at in enumerate((x * ff_half + ff_half - 256, ff_cut, (1 - x) * ff_half + ff_half - 256)):
        at = pl.multiple_of(at, 128) if u != 1 else at
        for q in range(nz):
            OG[q * 64 : q * 64 + 64, pl.ds(at, 128)] = I2[q, u, :, 0:128].astype(F32)
            OU[q * 64 : q * 64 + 64, pl.ds(at, 128)] = I2[q, u, :, 128:256].astype(F32)
            side = q // 2 * 128
            OD[pl.ds(at + q % 2 * 64, 64), side : side + 128] = I2[q, u, :, 256:384].astype(F32)
        store_part(at, 128)
    for copy in stores:
        copy.wait()


def fused(nz, tokens, cotangent, seg_ids, norm_one, wq, wk, wv, wo, norm_two, w_gate, w_up, w_down):
    ff = w_gate.shape[1]
    ff_half = -(-ff // 512) * 256
    ff_cut = ff - ff_half
    vm = pltpu.VMEM
    zshapes = [(2, 256, 768)] * 2 + [(3, 256, 384), (2, 256, 256), (2, 256, 768)]
    zscratch, fshapes = [], []
    for units, rows, cols in zshapes:
        fshapes.append((nz, units, rows // nz, cols))
        zscratch += [
            vm((2, units, rows, cols), BF),
            vm((units, rows, cols), BF),
            vm((2, nz - 1, units, rows // nz, cols), BF),
            vm((nz, rows // nz, cols) if len(fshapes) in LATE else (rows // nz, cols), BF),
            vm(fshapes[-1], BF),
        ]
    scratch = [
        vm((512, D), BF), vm((512, D), BF), vm((D, 768), BF), vm((D, D), BF),
        vm((D, ff_half), BF), vm((D, ff_half), BF), vm((ff_half, D), BF), vm((1, D), F32), vm((1, D), F32),
        vm((512, D), BF), vm((512, 256), BF), vm((768, 256), BF), vm((768, 256), BF), vm((2, 256, 512), F32),
        vm((8, 256, 512), F32), vm((512, D), BF),
        vm((2, 512, D), BF), vm((3, 3, 128, D), BF),
        vm((512, D), BF), vm((512, D), F32), vm((128, D), F32), vm((512, ff_half), BF), vm((512, ff_half), BF),
        vm((512, ff_half), BF), vm((512, D), BF), vm((512, 256), BF), vm((512, ff_half), F32), vm((512, ff_half), F32), vm((3, 512, 256), BF),
        vm((768, 256), F32), vm((768, 256), F32), vm((512, 768), BF), vm((256, 512), BF), vm((256, 512), BF),
        vm((128, D), BF), vm((128, D), BF), vm((8, D), F32), vm((8, 8, 256), F32), vm((nz, 8, 256), F32), vm((8, 256), F32),
        *zscratch,
        pltpu.SemaphoreType.DMA((10,)), pltpu.SemaphoreType.DMA((258,)), pltpu.SemaphoreType.DMA((28,)),
    ]
    hbm, vmem = pl.BlockSpec(memory_space=pl.ANY), pl.BlockSpec(memory_space=pltpu.VMEM)
    sds = jax.ShapeDtypeStruct
    done = pl.pallas_call(
        functools.partial(layer_kernel, nz, ff_half, ff_cut),
        out_shape=(sds((512, 256), BF), sds((512, 256), BF), sds((8, 256), F32), *(sds(f, BF) for f in fshapes)),
        in_specs=[hbm, hbm, vmem, vmem, hbm, hbm, hbm, hbm, vmem, hbm, hbm, hbm],
        out_specs=(hbm, hbm, vmem, *(hbm for f in fshapes)),
        scratch_shapes=scratch,
        compiler_params=pltpu.CompilerParams(collective_id=0, has_side_effects=True, vmem_limit_bytes=62 << 20),
        name="layer",
    )(
        tokens, cotangent, seg_ids, norm_one[None], wq, wk, wv, wo, norm_two[None], w_gate, w_up, w_down,
    )
    out, gin, gains, *sums = done
    grads = (
        sds((512, 256), BF), sds((512, 256), F32), sds((1, 256), F32),
        sds((256, 512), F32), sds((256, 512), F32), sds((256, 512), F32), sds((512, 256), F32),
        sds((1, 256), F32), sds((256, ff), F32), sds((256, ff), F32), sds((ff, 256), F32),
    )
    res = pl.pallas_call(
        functools.partial(spread_kernel, nz, ff_half, ff_cut),
        out_shape=grads,
        in_specs=[hbm] * 7 + [vmem],
        out_specs=tuple(vmem if i in (2, 7) else hbm for i in range(11)),
        scratch_shapes=[vm(f, BF) for f in fshapes]
        + [vm((256, ff), F32), vm((256, ff), F32), vm((ff, 256), F32), vm((512, 256), F32), vm((3, 256, 512), F32)]
        + [vm((512, 256), BF), vm((512, 256), BF), vm((512, 256), F32), pltpu.SemaphoreType.DMA((7,)), pltpu.SemaphoreType.DMA((27,))],
        compiler_params=pltpu.CompilerParams(vmem_limit_bytes=63 << 20),
        name="spread",
    )(*sums, out, gin, gains)
    res = list(res)
    res[2], res[7] = res[2][0], res[7][0]
    return tuple(res)


def solution(mesh):
    in_specs = (
        P(("dp", "col"), "row"),
        P(("dp", "col"), "row"),
        P("dp", None),
        P("row"),
        P("row", "col"),
        P("row", "col"),
        P("row", "col"),
        P("col", "row"),
        P("row"),
        P("row", "col"),
        P("row", "col"),
        P("col", "row"),
    )
    out_specs = (
        P(("dp", "col"), "row"),
        P(("dp", "col"), "row"),
        P("row"),
        P("row", "col"),
        P("row", "col"),
        P("row", "col"),
        P("col", "row"),
        P("row"),
        P("row", "col"),
        P("row", "col"),
        P("col", "row"),
    )
    sizes = dict(mesh.shape)
    body = per_device
    if sizes["row"] == 4 and sizes["col"] == 2:
        body = functools.partial(fused, sizes["dp"])
    return jax.shard_map(
        body, mesh=mesh, in_specs=in_specs, out_specs=out_specs, check_vma=False
    )
```

```python
import functools

import jax
import jax.numpy as jnp
from jax import lax
from jax.experimental import pallas as pl
from jax.experimental.pallas import tpu as pltpu
from jax.sharding import PartitionSpec as P

D = 1024
HEAD_DIM = 64


EPSILON = 1e-05
NEGATIVE = -1e30


def for_sending(array):

    def short(part):
        return part.astype(jnp.bfloat16) if part.dtype == jnp.float32 else part

    return jax.tree.map(short, array)


def shifted(block, axis, distance):
    devices = range(lax.axis_size(axis))
    route = [(i - distance, i) for i in devices if i - distance in devices]
    return lax.ppermute(block, axis, route)


def matmul(first_op, second_op):
    return jnp.dot(first_op, second_op, preferred_element_type=jnp.float32)


def matmul_tn(first_op, second_op):
    return lax.dot_general(
        first_op, second_op, (((0,), (0,)), ((), ())), preferred_element_type=jnp.float32
    )


def matmul_nt(first_op, second_op):
    return lax.dot_general(
        first_op, second_op, (((1,), (1,)), ((), ())), preferred_element_type=jnp.float32
    )


def tokens_col(array_in):
    return lax.all_gather(array_in, "col", axis=0, tiled=True)


def tokens_row(array_in):
    return lax.all_gather(for_sending(array_in), "row", axis=0, tiled=True).astype(array_in.dtype)


def summed_row(array_in):
    return lax.psum_scatter(
        array_in.astype(jnp.bfloat16), "row", scatter_dimension=0, tiled=True
    ).astype(jnp.float32)


def summed_col(array_in):
    return lax.psum_scatter(
        array_in.astype(jnp.bfloat16), "col", scatter_dimension=0, tiled=True
    ).astype(jnp.float32)


def feature_total(array_in):
    return lax.psum(array_in, "row")


def window_parts(queries, keys_all, ids_ext, offset, head_cols):
    t_local = queries.shape[0]
    block_rows = min(512, t_local)
    key_reach = min(2048, t_local)
    window = key_reach + block_rows
    head_count = head_cols // HEAD_DIM
    anchor = offset + t_local - key_reach
    q_blk = lax.dynamic_slice_in_dim(queries, offset, block_rows, 0).reshape(
        block_rows, head_count, HEAD_DIM
    )
    k_win = lax.dynamic_slice_in_dim(keys_all, anchor, window, 0)
    k_blk = k_win[:, :head_cols].reshape(window, head_count, HEAD_DIM)
    v_blk = k_win[:, head_cols:].reshape(window, head_count, HEAD_DIM)
    q_ids = lax.dynamic_slice_in_dim(ids_ext, offset + t_local, block_rows, 0)
    k_ids = lax.dynamic_slice_in_dim(ids_ext, anchor, window, 0)
    q_pos = offset + lax.iota(jnp.int32, block_rows)
    k_pos = offset - key_reach + lax.iota(jnp.int32, window)
    allowed = (q_ids[:, None] == k_ids[None, :]) & (k_pos[None, :] <= q_pos[:, None])
    scores = jnp.einsum(
        "qhd,khd->hqk", q_blk, k_blk, preferred_element_type=jnp.float32
    ) * HEAD_DIM ** (-0.5)
    scores = jnp.where(allowed[None], scores, NEGATIVE)
    return (q_blk, k_blk, v_blk, scores)


def forward(tokens, seg_ids, norm_one, wq, wk, wv, wo, norm_two, w_gate, w_up, w_down):
    token_vals = tokens.astype(jnp.float32)
    scale_one = lax.rsqrt(feature_total(jnp.sum(token_vals * token_vals, axis=1)) / D + EPSILON)
    normed = (token_vals * scale_one[:, None] * norm_one).astype(jnp.bfloat16)
    normed_all = tokens_col(normed)
    w_qkv = jnp.concatenate([wq, wk, wv], axis=1)
    head_cols = wq.shape[1]
    qkv = summed_row(matmul(normed_all, w_qkv)).astype(jnp.bfloat16)
    queries = qkv[:, :head_cols]
    kv_local = qkv[:, head_cols:]
    prior_keys = shifted(kv_local, "row", 1)
    keys_all = jnp.concatenate([prior_keys, kv_local], axis=0)
    t_local = queries.shape[0]
    block_rows = min(512, t_local)
    padded_ids = jnp.concatenate([jnp.full((t_local,), -1, jnp.int32), seg_ids[0]])
    ids_ext = lax.dynamic_slice_in_dim(padded_ids, lax.axis_index("row") * t_local, 2 * t_local, 0)

    def attend(offset):
        q_blk, k_blk, v_blk, scores = window_parts(queries, keys_all, ids_ext, offset, head_cols)
        row_max = jnp.max(scores, axis=2, keepdims=True)
        exp_total = jnp.sum(jnp.exp(scores - row_max), axis=2, keepdims=True)
        log_total = row_max + jnp.log(exp_total)
        prob_low = jnp.exp(scores - log_total).astype(jnp.bfloat16)
        mixed_out = jnp.einsum("hqk,khd->qhd", prob_low, v_blk, preferred_element_type=jnp.float32)
        return (mixed_out.reshape(block_rows, head_cols).astype(jnp.bfloat16), log_total[:, :, 0])

    offsets = lax.iota(jnp.int32, t_local // block_rows) * block_rows
    pieces, log_totals = lax.map(attend, offsets)
    attn_out = pieces.reshape(t_local, head_cols)
    attn_all = tokens_row(attn_out)
    residual = token_vals + summed_col(matmul(attn_all, wo))
    stored = {
        "token_vals": token_vals,
        "scale_one": scale_one,
        "normed_all": normed_all,
        "queries": queries,
        "keys_all": keys_all,
        "ids_ext": ids_ext,
        "log_totals": log_totals,
        "attn_all": attn_all,
        "offsets": offsets,
    }
    f_col = w_gate.shape[1]
    scale_two = lax.rsqrt(feature_total(jnp.sum(residual * residual, axis=1)) / D + EPSILON)
    hidden_in = (residual * scale_two[:, None] * norm_two).astype(jnp.bfloat16)
    hidden_all = tokens_col(hidden_in)
    w_pair = jnp.concatenate([w_gate, w_up], axis=1)
    pair_sum = summed_row(matmul(hidden_all, w_pair))
    gate_pre = pair_sum[:, :f_col]
    up_pre = pair_sum[:, f_col:]
    act_low = (jax.nn.silu(gate_pre) * up_pre).astype(jnp.bfloat16)
    act_all = tokens_row(act_low)
    final_sum = residual + summed_col(matmul(act_all, w_down))
    stored.update(
        {
            "residual": residual,
            "scale_two": scale_two,
            "hidden_all": hidden_all,
            "gate_pre": gate_pre,
            "up_pre": up_pre,
            "act_all": act_all,
        }
    )
    return (final_sum.astype(jnp.bfloat16), stored)


def swiglu_grads(dact, gate_pre, up_pre):
    sigmoid_gate = jax.nn.sigmoid(gate_pre)
    gate_grad = (dact * up_pre * sigmoid_gate * (1.0 + gate_pre * (1.0 - sigmoid_gate))).astype(
        jnp.bfloat16
    )
    up_grad = (dact * gate_pre * sigmoid_gate).astype(jnp.bfloat16)
    return (gate_grad, up_grad)


def per_device(
    tokens, cotangent, seg_ids, norm_one, wq, wk, wv, wo, norm_two, w_gate, w_up, w_down
):
    weights = (tokens, seg_ids, norm_one, wq, wk, wv, wo, norm_two, w_gate, w_up, w_down)
    output, stored = forward(*weights)
    f_col = w_gate.shape[1]
    grad_out = cotangent.astype(jnp.float32)
    grad_all = tokens_col(cotangent)
    dact = summed_row(matmul_nt(grad_all, w_down))
    grad_down = matmul_tn(stored["act_all"], grad_all)
    gate_grad, up_grad = swiglu_grads(dact, stored["gate_pre"], stored["up_pre"])
    dpair = jnp.concatenate([gate_grad, up_grad], axis=1)
    dpair_all = tokens_row(dpair)
    w_pair = jnp.concatenate([w_gate, w_up], axis=1)
    dhidden = summed_col(matmul_nt(dpair_all, w_pair))
    grad_pair = matmul_tn(stored["hidden_all"], dpair_all)
    grad_gate = grad_pair[:, :f_col]
    grad_up = grad_pair[:, f_col:]
    residual = stored["residual"]
    scale_two = stored["scale_two"]
    weighted = dhidden * norm_two
    inner_sum = feature_total(jnp.sum(weighted * residual, axis=1)) / D
    dresid = (
        grad_out + scale_two[:, None] * weighted - residual * (scale_two**3 * inner_sum)[:, None]
    )
    grad_norm_two = jnp.sum(dhidden * residual * scale_two[:, None], axis=0)
    dbranch = dresid.astype(jnp.bfloat16)
    dbranch_all = tokens_col(dbranch)
    attn_grad = summed_row(matmul_nt(dbranch_all, wo)).astype(jnp.bfloat16)
    grad_wo = matmul_tn(stored["attn_all"], dbranch_all)
    queries = stored["queries"]
    keys_all = stored["keys_all"]
    ids_ext = stored["ids_ext"]
    head_cols = wq.shape[1]
    head_count = head_cols // HEAD_DIM
    t_local = queries.shape[0]
    block_rows = min(512, t_local)
    key_reach = min(2048, t_local)
    window = key_reach + block_rows
    inv_root = HEAD_DIM ** (-0.5)

    def attend_back(accum_dkv, inputs):
        offset, log_total = inputs
        q_blk, k_blk, v_blk, scores = window_parts(queries, keys_all, ids_ext, offset, head_cols)
        prob_full = jnp.exp(scores - log_total[:, :, None])
        prob_low = prob_full.astype(jnp.bfloat16)
        d_blk = lax.dynamic_slice_in_dim(attn_grad, offset, block_rows, 0).reshape(
            block_rows, head_count, HEAD_DIM
        )
        dprobs = jnp.einsum("qhd,khd->hqk", d_blk, v_blk, preferred_element_type=jnp.float32)
        dvalue = jnp.einsum("hqk,qhd->khd", prob_low, d_blk, preferred_element_type=jnp.float32)
        center = jnp.sum(prob_full * dprobs, axis=2, keepdims=True)
        dscores = (prob_full * (dprobs - center)).astype(jnp.bfloat16)
        dquery = (
            jnp.einsum("hqk,khd->qhd", dscores, k_blk, preferred_element_type=jnp.float32)
            * inv_root
        )
        dkey = (
            jnp.einsum("hqk,qhd->khd", dscores, q_blk, preferred_element_type=jnp.float32)
            * inv_root
        )
        update = jnp.concatenate(
            [dkey.reshape(window, head_cols), dvalue.reshape(window, head_cols)], axis=1
        )
        anchor = offset + t_local - key_reach
        current = lax.dynamic_slice_in_dim(accum_dkv, anchor, window, 0)
        accum_dkv = lax.dynamic_update_slice_in_dim(accum_dkv, current + update, anchor, 0)
        return (accum_dkv, dquery.reshape(block_rows, head_cols))

    start_grads = jnp.zeros((2 * t_local, 2 * head_cols), jnp.float32)
    accum_dkv, query_grads = lax.scan(
        attend_back, start_grads, (stored["offsets"], stored["log_totals"])
    )
    returned = shifted(accum_dkv[:t_local].astype(jnp.bfloat16), "row", -1).astype(jnp.float32)
    key_grads = accum_dkv[t_local:] + returned
    dqkv = jnp.concatenate([query_grads.reshape(t_local, head_cols), key_grads], axis=1).astype(
        jnp.bfloat16
    )
    dqkv_all = tokens_row(dqkv)
    w_qkv = jnp.concatenate([wq, wk, wv], axis=1)
    dnormed = summed_col(matmul_nt(dqkv_all, w_qkv))
    grad_qkv = matmul_tn(stored["normed_all"], dqkv_all)
    grad_wq = grad_qkv[:, :head_cols]
    grad_wk = grad_qkv[:, head_cols : 2 * head_cols]
    grad_wv = grad_qkv[:, 2 * head_cols :]
    token_vals = stored["token_vals"]
    scale_one = stored["scale_one"]
    weighted_one = dnormed * norm_one
    inner_one = feature_total(jnp.sum(weighted_one * token_vals, axis=1)) / D
    grad_input = (
        dresid
        + scale_one[:, None] * weighted_one
        - token_vals * (scale_one**3 * inner_one)[:, None]
    )
    grad_norm_one = jnp.sum(dnormed * token_vals * scale_one[:, None], axis=0)
    grad_sums = (
        lax.psum(grad_wq.astype(jnp.bfloat16), "dp").astype(jnp.float32),
        lax.psum(grad_wk.astype(jnp.bfloat16), "dp").astype(jnp.float32),
        lax.psum(grad_wv.astype(jnp.bfloat16), "dp").astype(jnp.float32),
        lax.psum(grad_wo.astype(jnp.bfloat16), "dp").astype(jnp.float32),
        lax.psum(grad_gate.astype(jnp.bfloat16), "dp").astype(jnp.float32),
        lax.psum(grad_up.astype(jnp.bfloat16), "dp").astype(jnp.float32),
        lax.psum(grad_down.astype(jnp.bfloat16), "dp").astype(jnp.float32),
    )
    gain_sums = lax.psum((grad_norm_one, grad_norm_two), ("dp", "col"))
    return (
        output,
        grad_input,
        gain_sums[0],
        grad_sums[0],
        grad_sums[1],
        grad_sums[2],
        grad_sums[3],
        gain_sums[1],
        grad_sums[4],
        grad_sums[5],
        grad_sums[6],
    )


MESH = pl.DeviceIdType.MESH
BF = jnp.bfloat16
F32 = jnp.float32
NPLANE = 8
TAIL, HELD = (1, 2), (0, 3)
LATE = (1, 3, 4)
NEWFIRST, LAG = True, 4
FWAIT, OWAIT, QWAIT = (4, 6, 0), 0, 0


def contract(a, b, ca, cb):
    return lax.dot_general(a, b, (((ca,), (cb,)), ((), ())), preferred_element_type=F32)


class Copies:
    def __init__(self, send, recv):
        self.send, self.recv, self.used, self.kept, self.open = send, recv, 0, 1, []

    def take(self, amount=1):
        base = self.used
        self.used += amount
        return base

    def make(self, src, dst, to, site=None, own=False):
        site = self.take() if site is None else site
        self.kept += own
        return pltpu.make_async_remote_copy(
            src_ref=src,
            dst_ref=dst,
            send_sem=self.send.at[self.kept - 1 if own else 0],
            recv_sem=self.recv.at[site],
            device_id=to,
            device_id_type=MESH,
        )

    def start(self, copy, when=None):
        self.open.append((copy, when))
        if when is None:
            copy.start()
        else:
            pl.when(when)(copy.start)

    def finish(self):
        for copy, when in self.open:
            if when is None:
                copy.wait_send()
            else:
                pl.when(when)(copy.wait_send)
        self.open = []


def layer_kernel(nz, ff_half, ff_cut, *refs):
    it = iter(refs)
    take = lambda n: [next(it) for _ in range(n)]
    tok, cot, seg, n1, wq, wk, wv, wo, n2, wg, wu, wd = take(12)
    out, gin, gains, f0, f1, f2, fo, fq = take(8)
    X, G, WQKV, WO, WG, WU, WD, NG1, NG2 = take(9)
    XN, Q, K, V, BIAS, PM, AF = take(7)
    PART, RX = take(2)
    HN, RES, DRES, ACT, DGA, DUP, DB, DAT, BYG, BYU, T3 = take(11)
    DK, DV, DQKV, HS, HR = take(5)
    OS, GS, GP, GR, GZ, GZS = take(6)
    zbufs = [take(5) for _ in range(5)]
    send, recv, loc = take(3)

    z, row, y = lax.axis_index("dp"), lax.axis_index("row"), lax.axis_index("col")
    x, c = row // 2, row % 2
    net = Copies(send, recv)
    nloc = [0]

    def local(src, dst):
        nloc[0] += 1
        return pltpu.make_async_copy(src, dst, loc.at[nloc[0] - 1])

    def dev(zz, xx, yy, cc):
        return (zz, 2 * xx + cc, yy)

    core_nb, x_nb, y_nb = dev(z, x, y, 1 - c), dev(z, 1 - x, y, c), dev(z, x, 1 - y, c)
    z_up, z_dn = dev(z + 1, x, y, c), dev(z - 1, x, y, c)
    lanes = lambda i, n=256: pl.ds(pl.multiple_of(i * n, 128), n)
    rows = lambda i, n: pl.ds(pl.multiple_of(i * n, n if n % 16 else 16), n)
    flip = lambda v, bit: 1 - v if bit else v

    barrier = pltpu.get_barrier_semaphore()
    for d in range(1, NPLANE):
        pl.semaphore_signal(
            barrier, inc=1, device_id=dev(z, flip(x, d & 1), flip(y, d & 2), flip(c, d & 4)), device_id_type=MESH
        )
    for d in range(1, nz):
        pl.semaphore_signal(barrier, inc=1, device_id=dev((z + d) % nz, x, y, c), device_id_type=MESH)
    for _, _, ZR, _, _ in zbufs:

        @pl.when(z == 0)
        def _(ZR=ZR):
            ZR[0, nz - 2] = jnp.zeros(ZR.shape[2:], BF)

        @pl.when(z == nz - 1)
        def _(ZR=ZR):
            ZR[1, nz - 2] = jnp.zeros(ZR.shape[2:], BF)

    seg_f = seg[...].astype(F32)
    own = jnp.where(c == 0, seg_f[:, :512], seg_f[:, 512:])
    before = jnp.where(c == 0, jnp.full((1, 256), -1.0, F32), seg_f[:, 256:512])
    ids = jnp.concatenate([before, own], axis=1)
    for b in range(2):
        k_id = jnp.broadcast_to(ids[:, b * 256 : b * 256 + 512], (256, 512))
        q_id = jnp.broadcast_to(ids[:, 256 + b * 256 : 512 + b * 256], (512, 256)).T
        q_pos = lax.broadcasted_iota(jnp.int32, (256, 512), 0) + 256
        k_pos = lax.broadcasted_iota(jnp.int32, (256, 512), 1)
        BIAS[b] = jnp.where((q_id == k_id) & (k_pos <= q_pos), 0.0, NEGATIVE)

    @pl.when(c == 0)
    def _():
        K[0:256, :] = jnp.zeros((256, 256), BF)
        V[0:256, :] = jnp.zeros((256, 256), BF)

    pl.semaphore_wait(barrier, NPLANE - 1 + nz - 1)

    def gather_tokens(src, buf):
        col = lambda rr: buf.at[:, lanes(rr)]
        mine = c == y
        other = jnp.logical_not(mine)
        keep = local(src, col(row))
        over = net.make(src, col(row), core_nb)
        bx, by = net.take(2), net.take(2)
        to_x = net.make(src, col(row), dev(z, 1 - x, y, y), bx + c)
        to_y = net.make(src, col(row), dev(z, x, 1 - y, y), by + c)
        far = 2 * (1 - x)
        by_y = net.make(col(far), col(far), y_nb)
        by_x = net.make(col(2 * x + 1), col(2 * x + 1), x_nb)
        got_x = [net.make(src, col(row), core_nb, bx + k) for k in range(2)]
        got_y = [net.make(src, col(row), core_nb, by + k) for k in range(2)]

        def start():
            pl.when(mine)(keep.start)
            net.start(to_x)
            net.start(to_y)
            net.start(over, other)

        def arrive():
            @pl.when(mine)
            def _():
                got_x[0].wait_recv()
                by_y.start()

            @pl.when(other)
            def _():
                got_y[1].wait_recv()
                by_x.start()

            net.open += [(by_y, mine), (by_x, other)]

        def rest():
            @pl.when(mine)
            def _():
                got_x[1].wait_recv()
                over.wait_recv()
                keep.wait()

            @pl.when(other)
            def _():
                got_y[0].wait_recv()
                by_y.wait_recv()
                by_x.wait_recv()

        return start, arrive, rest

    def relay(src_of, dst_of):
        keep = local(src_of(x), dst_of(row))
        across = net.make(src_of(x), dst_of(row), core_nb)
        far = net.make(src_of(1 - x), dst_of(row), x_nb)
        theirs = dst_of(2 * (1 - x) + c)
        fwd = net.make(theirs, theirs, core_nb)

        def start():
            keep.start()
            net.start(far)
            net.start(across)

        def arrive():
            far.wait_recv()
            net.start(fwd)

        def rest():
            keep.wait()
            across.wait_recv()
            fwd.wait_recv()

        return start, arrive, rest

    def z_gather(at):
        sites = (net.take(nz - 1), net.take(nz - 1))

        def step(s):
            for way, to in ((0, z_up), (1, z_dn)):
                zz = z if way == 0 else nz - 1 - z
                ref = at(z - s if way == 0 else z + s)
                have = zz >= s
                if s > 0:
                    pl.when(have)(net.make(ref, ref, to, sites[way] + s - 1).wait_recv)
                if s < nz - 1:
                    net.start(net.make(ref, ref, to, sites[way] + s), have & (zz < nz - 1))

        return step

    def relay_z(pairs, whole, n_rows):
        n = n_rows // nz
        keep = [local(a, b) for a, b in pairs(x, row, 0, n_rows)]
        across = [net.make(a, b, core_nb) for a, b in pairs(x, row, 0, n_rows)]
        far = [net.make(a, b, x_nb) for a, b in pairs(1 - x, row, z * n, n)]
        hop = z_gather(lambda q: whole(2 * (1 - x) + c, q * n, n))
        theirs = whole(2 * (1 - x) + c, 0, n_rows)
        fwd = net.make(theirs, theirs, core_nb)

        def begin():
            for copy in far:
                net.start(copy)
            for copy in keep:
                copy.start()
            for copy in across:
                net.start(copy)

        def step(s):
            if s == 0:
                for copy in far:
                    copy.wait_recv()
            hop(s)
            if s == nz - 1:
                net.start(fwd)

        def rest():
            for copy in keep:
                copy.wait()
            for copy in across:
                copy.wait_recv()
            fwd.wait_recv()

        return begin, step, rest

    def gather_wo():
        at = lambda yy, rr: WO.at[rows(yy, 512), lanes(rr)]
        keep = local(wo, at(y, row))
        across = net.make(wo, at(y, row), core_nb)
        to_x, to_y = net.make(wo, at(y, row), x_nb), net.make(wo, at(y, row), y_nb)
        rx = 2 * (1 - x) + c
        on_y = net.make(at(y, rx), at(y, rx), y_nb)
        others = (at(y, rx), at(1 - y, row), at(1 - y, rx))
        fwd = [net.make(ref, ref, core_nb) for ref in others]

        def start():
            net.start(to_x)
            net.start(to_y)
            keep.start()
            net.start(across)

        def arrive():
            to_x.wait_recv()
            net.start(on_y)
            net.start(fwd[0])

        def pass_on():
            to_y.wait_recv()
            net.start(fwd[1])
            on_y.wait_recv()
            net.start(fwd[2])

        def rest():
            keep.wait()
            across.wait_recv()
            for copy in fwd:
                copy.wait_recv()

        return start, arrive, pass_on, rest

    def gather_gain(src, dst):
        keep = local(src, dst.at[:, lanes(row)])
        keep.start()
        got = []
        for to in (core_nb, x_nb, dev(z, 1 - x, y, 1 - c)):
            got.append(net.make(src, dst.at[:, lanes(row)], to))
            net.start(got[-1])

        def rest():
            keep.wait()
            for g in got:
                g.wait_recv()

        return rest

    gx, gg = gather_tokens(tok, X), gather_tokens(cot, G)
    some = lambda r0, n: pl.ds(pl.multiple_of(r0, 16), n)
    rqkv = []
    for i, w in ((1, wk), (2, wv), (0, wq)):
        at = lambda rr, r0, n, i=i: WQKV.at[some(rr * 256 + r0, n), pl.ds(i * 256, 256)]
        rqkv.append(relay_z(lambda xx, rr, r0, n, w=w, at=at: [(w.at[some(r0, n), lanes(xx)], at(rr, r0, n))], at, 256))
    ro = gather_wo()
    both = ff_half - ff_cut
    rff = []
    for w, W in ((wg, WG), (wu, WU)):
        at = lambda rr, r0, n, W=W: W.at[some(rr * 256 + r0, n), :]

        def pairs(xx, rr, r0, n, w=w, W=W):
            out = []
            for src, dst, width in ((pl.multiple_of(xx * ff_half, 128), 0, ff_cut), (ff_cut, ff_cut, both)):
                out.append((w.at[some(r0, n), pl.ds(src, width)], W.at[some(rr * 256 + r0, n), pl.ds(dst, width)]))
            return out

        rff.append(relay_z(pairs, at, 256))

    def pairs_down(xx, rr, r0, n):
        if n == ff_half:
            parts = ((xx * ff_half, 0, ff_cut), (ff_cut, ff_cut, both))
        else:
            tail = jnp.where(z == nz - 1, ff_cut, xx * ff_half + r0 + n - both)
            parts = ((xx * ff_half + r0, r0, n - both), (tail, r0 + n - both, both))
        return [(wd.at[some(src, k), :], WD.at[some(dst, k), lanes(rr)]) for src, dst, k in parts]

    rd = relay_z(pairs_down, lambda rr, r0, n: WD.at[some(r0, n), lanes(rr)], ff_half)
    for r in rqkv:
        r[0]()
    gx[0]()
    ga = [gather_gain(n1, NG1), gather_gain(n2, NG2)]
    for r in rqkv:
        r[1](0)
    for r in rqkv:
        r[1](1)
    gx[1]()
    for s in range(2, nz):
        for r in rqkv:
            r[1](s)
    for g in ga:
        g()
    for r in (*rff, rd):
        r[0]()
    gx[2]()
    ro[0]()
    for t in range(4):
        v = X[t * 128 : t * 128 + 128, :].astype(F32)
        scale = lax.rsqrt(jnp.mean(v * v, axis=1, keepdims=True) + EPSILON)
        XN[t * 128 : t * 128 + 128, :] = (v * scale * NG1[...]).astype(BF)
    for r in rqkv:
        r[2]()
    K[256:768, :] = contract(XN[...], WQKV[:, 256:512], 1, 0).astype(BF)
    V[256:768, :] = contract(XN[...], WQKV[:, 512:768], 1, 0).astype(BF)
    hk = net.make(K.at[pl.ds(512, 256), :], K.at[pl.ds(0, 256), :], core_nb)
    hv = net.make(V.at[pl.ds(512, 256), :], V.at[pl.ds(0, 256), :], core_nb)
    net.start(hk, c == 0)
    net.start(hv, c == 0)
    Q[...] = (contract(XN[...], WQKV[:, 0:256], 1, 0).astype(BF) * 0.125).astype(BF)
    @pl.when(c == 1)
    def _():
        hk.wait_recv()
        hv.wait_recv()

    lane_id = lax.broadcasted_iota(jnp.int32, (1, 128), 1)
    head_mask = [jnp.where(lane_id < 64, 1.0, 0.0).astype(BF), jnp.where(lane_id < 64, 0.0, 1.0).astype(BF)]

    heads_at = lambda xx, yy, b: AF.at[pl.ds(b * 256, 256), lanes(2 * yy + xx)]
    a_x = [net.make(heads_at(x, y, b), heads_at(x, y, b), x_nb) for b in range(2)]
    a_y = [net.make(heads_at(x, y, b), heads_at(x, y, b), y_nb) for b in range(2)]
    a_far = (
        net.make(heads_at(1 - x, y, 0), heads_at(1 - x, y, 0), y_nb),
        net.make(heads_at(x, 1 - y, 1), heads_at(x, 1 - y, 1), x_nb),
    )
    base = (2 * y + x) * 256
    for b in range(2):
        for hp in range(2):
            cols = slice(hp * 128, hp * 128 + 128)
            q_b, k_b, v_b = Q[b * 256 : b * 256 + 256, cols], K[b * 256 : b * 256 + 512, cols], V[b * 256 : b * 256 + 512, cols]
            total = None
            for h in range(2):
                s = contract(q_b * head_mask[h], k_b, 1, 1) + BIAS[b]
                e = jnp.exp(s - jnp.max(s, axis=1, keepdims=True))
                p = e * (1.0 / jnp.sum(e, axis=1, keepdims=True))
                PM[b * 4 + hp * 2 + h] = p
                part = contract(p.astype(BF), v_b * head_mask[h], 1, 0)
                total = part if total is None else total + part
            AF[b * 256 : b * 256 + 256, pl.ds(pl.multiple_of(base + hp * 128, 128), 128)] = total.astype(BF)
        net.start(a_x[b])
        net.start(a_y[b])
        if b == 0:
            for r in rff:
                r[1](0)
    for r in rff:
        r[1](1)
    rd[1](0)
    ro[1]()
    a_x[0].wait_recv()
    net.start(a_far[0])
    a_y[1].wait_recv()
    net.start(a_far[1])
    gg[0]()
    for r in rff:
        r[1](2)
    rd[1](1)
    ro[2]()
    for r in rff:
        r[1](3)
    rd[1](2)

    j = 2 * x + y
    shard = lambda buf, jj: buf.at[rows(jj, 128), :]

    peers = ((x_nb, 2 * (1 - x) + y), (y_nb, 2 * x + 1 - y), (dev(z, 1 - x, 1 - y, c), 2 * (1 - x) + 1 - y))

    def reduce_start(k, p):
        sent = [net.make(shard(PART.at[p], jj), RX.at[k, i], to, own=True) for i, (to, jj) in enumerate(peers)]
        for copy in (sent[2], sent[0], sent[1]):
            copy.start()

        def end():
            for copy in sent:
                copy.wait_recv()
            for copy in sent:
                copy.wait_send()
            total = PART[p, rows(j, 128), :].astype(F32)
            for i in range(3):
                total = total + RX[k, i].astype(F32)
            return total

        return end

    def gather_start(buf):
        sent = [net.make(shard(buf, j), shard(buf, j), to) for to, _ in peers]
        for copy in (sent[2], sent[0], sent[1]):
            net.start(copy)

        def end():
            for copy in sent:
                copy.wait_recv()

        return end

    def send_blocks(src, dst):
        base_r = net.take(4)
        waits = []
        for dx in range(2):
            for cc in range(2):
                xx = flip(x, dx)
                piece, place = src.at[:, lanes(2 * xx + cc)], dst.at[rows(j, 128), :]
                copy = pltpu.make_async_remote_copy(
                    src_ref=piece,
                    dst_ref=place,
                    send_sem=net.send.at[0],
                    recv_sem=net.recv.at[base_r + dx * 2 + y],
                    device_id=dev(z, xx, c, cc),
                    device_id_type=MESH,
                )
                if dx == 0:
                    here = (c == y) & (c == cc)
                    keep = local(piece, place)
                    pl.when(here)(keep.start)
                    net.start(copy, jnp.logical_not(here))
                    waits.append((keep, here))
                else:
                    net.start(copy)
        piece, place = src.at[:, pl.ds(0, 256)], dst.at[pl.ds(0, 128), :]
        arrivals = [
            (net.make(piece, place, core_nb, base_r + dx * 2 + yy), jnp.logical_not((c == y) & (y == yy)) if dx == 0 else None)
            for dx in range(2)
            for yy in range(2)
        ]

        def end():
            for keep, here in waits:
                pl.when(here)(keep.wait)
            for got, when in arrivals:
                if when is None:
                    got.wait_recv()
                else:
                    pl.when(when)(got.wait_recv)

        return end

    def along_z(tag, dst):
        GB, CR, ZR, RL, FF = zbufs[tag]
        n_rows = CR.shape[1] // nz
        n = n_rows // 2
        last = CR.shape[0] - 1
        part = lambda q, i: pl.ds(pl.multiple_of(q * n_rows + i * n, 16), n)
        own = lambda i: pl.ds(i * n, n)
        over = net.make(GB.at[1 - c], CR, core_nb)
        net.start(over)
        yield
        over.wait_recv()
        for u in range(CR.shape[0]):
            CR[u] = (CR[u].astype(F32) + GB[c, u].astype(F32)).astype(BF)
        sites = [[net.take(nz - 1) for _ in range(2)] for _ in range(2)]
        for s in range(1, nz):
            for i in range(2):
                for way, to in ((0, z_up), (1, z_dn)):
                    zz = z if way == 0 else nz - 1 - z
                    q = nz - s + zz
                    q = q if way == 0 else nz - 1 - q
                    go = (zz < nz - 1) & (zz <= s - 1)
                    first, later = go & (zz == 0), go & (zz > 0)
                    site = sites[way][i] + s - 1
                    there = ZR.at[way, s - 1, :, own(i), :]
                    net.start(net.make(CR.at[:, part(q, i), :], there, to, site), first)
                    if s >= 2:
                        acc = ZR.at[way, s - 2, :, own(i), :]
                        got = net.make(acc, acc, to, site - 1)

                        @pl.when(later)
                        def _(got=got, acc=acc, q=q, i=i):
                            got.wait_recv()
                            acc[...] = (acc[...].astype(F32) + CR[:, part(q, i), :].astype(F32)).astype(BF)

                        net.start(net.make(acc, there, to, site), later)
                yield
        late = len(RL.shape) == 3
        backs = [[net.take(nz - 1) for _ in range(2)] for _ in range(2)]
        here = lambda q, i: FF.at[q, :, own(i), :]
        side = []

        def send_back(i):
            net.start(net.make(here(z, i), here(z, i), z_up, backs[0][i]), z < nz - 1)
            net.start(net.make(here(z, i), here(z, i), z_dn, backs[1][i]), z > 0)

        for i in range(2):
            for way in range(2):
                zz = z if way == 0 else nz - 1 - z
                acc = ZR.at[way, nz - 2, :, own(i), :]
                pl.when(zz > 0)(net.make(acc, acc, z_up, sites[way][i] + nz - 2).wait_recv)
            total = (
                CR[:, part(z, i), :].astype(F32)
                + ZR[0, nz - 2, :, own(i), :].astype(F32)
                + ZR[1, nz - 2, :, own(i), :].astype(F32)
            ).astype(BF)
            if late:
                FF[z, :, own(i), :] = total
                send_back(i)
            else:
                RL[own(i), :] = total[-1]
                side.append(net.make(RL.at[own(i), :], FF.at[z, last, own(i), :], x_nb))
                net.start(side[i])
                FF[z, 0:last, own(i), :] = total[:-1]
            yield
        if not late:
            for i in range(2):
                side[i].wait_recv()
                send_back(i)
                if tag == 4 and i == 1:
                    gates.append(tag)
                yield
        sites = backs
        for s in range(2, nz + 1):
            for i in range(2):
                for way, to in ((0, z_up), (1, z_dn)):
                    zz = z if way == 0 else nz - 1 - z
                    q = z - (s - 1) if way == 0 else z + (s - 1)
                    have = zz >= s - 1
                    ref = here(q, i)
                    pl.when(have)(net.make(ref, ref, to, sites[way][i] + s - 2).wait_recv)
                    if s < nz:
                        net.start(net.make(ref, ref, to, sites[way][i] + s - 1), have & (zz < nz - 1))
                yield
        if late:
            trade = net.make(FF.at[:, last], RL, x_nb)
            while tag in HELD and not gates:
                yield
            net.start(trade)
            for _ in range(LAG):
                yield
            trade.wait_recv()
            flush(FF.at[:, 0:last], dst.at[:, 0:last])
            flush(RL, dst.at[:, last])
        else:
            flush(FF, dst)
        yield

    def flush(buf, dst):
        copy = local(buf, dst)
        copy.start()
        flushes.append(copy)

    flushes, gates = [], []

    lines = []

    def begin(i, dst, wait):
        line = along_z(i, dst)
        next(line)
        lines.append([line, wait])

    def tick(n=1):
        for _ in range(n):
            for _ in range(2):
                for line in (lines[::-1] if NEWFIRST else lines):
                    if line[1] > 0:
                        line[1] -= 1
                    else:
                        next(line[0], None)

    ro[3]()
    for copy in (a_x[1], a_y[0], *a_far):
        copy.wait_recv()
    for t in range(4):
        tile = slice(t * 128, t * 128 + 128)
        res = X[tile, :].astype(F32) + contract(AF[tile, :], WO[...], 1, 0)
        RES[tile, :] = res
        scale = lax.rsqrt(jnp.mean(res * res, axis=1, keepdims=True) + EPSILON)
        HN[tile, :] = (res * scale * NG2[...]).astype(BF)
    gg[1]()
    for r in rff:
        r[2]()
    rd[1](3)
    unit = lambda r: jnp.where(x == r // 2, 0, 1)
    shared = (lax.broadcasted_iota(jnp.int32, (1, 256), 1) >= 256 - both) & (x == 1)

    def tile_grads(n):
        cols = slice(n * 256, n * 256 + 256)
        GB = zbufs[n][0]
        for i, made in enumerate((DGA, DUP)):
            whole = contract(HN[...], made[:, cols], 0, 0)
            for r in range(4):
                GB[r % 2, unit(r), :, i * 256 : i * 256 + 256] = whole[r * 256 : r * 256 + 256].astype(BF)
        whole = contract(ACT[:, cols], G[...], 0, 0)
        for r in range(4):
            GB[r % 2, unit(r), :, 512:768] = whole[:, r * 256 : r * 256 + 256].astype(BF)

    def last_tile_grads(n):
        GB = zbufs[n][0]

        def put(r, cols, a, b):
            GB[r % 2, jnp.where(x == r // 2, 0, 2), :, cols] = a.astype(BF)

            @pl.when(x == r // 2)
            def _():
                GB[r % 2, 1, :, cols] = b.astype(BF)

        for i in range(2):
            whole = contract(HN[...], T3[i], 0, 0)
            for r in range(4):
                rws = whole[r * 256 : r * 256 + 256]
                put(r, slice(i * 128, i * 128 + 128), rws[:, :128], rws[:, 128:])
        whole = contract(T3[2], G[...], 0, 0)
        for r in range(4):
            left, right = whole[:, r * 256 : r * 256 + 128], whole[:, r * 256 + 128 : r * 256 + 256]
            put(
                r,
                slice(256, 384),
                jnp.concatenate([left[:128], right[:128]], axis=0),
                jnp.concatenate([left[128:], right[128:]], axis=0),
            )

    tiles = ff_half // 256
    for n in range(tiles):
        cols = slice(n * 256, n * 256 + 256)
        gate = contract(HN[...], WG[:, cols], 1, 0)
        up = contract(HN[...], WU[:, cols], 1, 0)
        sig = jax.nn.sigmoid(gate)
        silu = gate * sig
        act = (silu * up).astype(BF)
        if n == tiles - 1:
            T3[2] = act
            act = jnp.where(shared, jnp.zeros_like(act), act)
        ACT[:, cols] = act
        BYG[:, cols] = up * sig * (1.0 + gate * (1.0 - sig))
        BYU[:, cols] = silu
    gg[2]()
    rd[2]()
    for n in (tiles - 1, *range(tiles - 1)):
        cols = slice(n * 256, n * 256 + 256)
        dact = contract(G[...], WD[cols, :], 1, 1)
        dgate, dup = (dact * BYG[:, cols]).astype(BF), (dact * BYU[:, cols]).astype(BF)
        if n == tiles - 1:
            T3[0], T3[1] = dgate, dup
            dgate, dup = (jnp.where(shared, jnp.zeros_like(v), v) for v in (dgate, dup))
        DGA[:, cols] = dgate
        DUP[:, cols] = dup
        (last_tile_grads if n == tiles - 1 else tile_grads)(n)
        begin(n, (f0, f1, f2)[n], FWAIT[n])
        if n == 0:
            tick()
    blocks = lambda i, f: [zbufs[i][0].__setitem__((r % 2, unit(r)), f(slice(r * 256, r * 256 + 256)).astype(BF)) for r in range(4)]
    tick()
    for n in range(4):
        cols = slice(n * 256, n * 256 + 256)
        PART[0, :, cols] = (contract(DGA[...], WG[cols, :], 1, 1) + contract(DUP[...], WU[cols, :], 1, 1)).astype(BF)
    hid = reduce_start(0, 0)
    tick()
    for n in range(4):
        cols = slice(n * 256, n * 256 + 256)
        PART[1, :, cols] = contract(ACT[...], WD[:, cols], 1, 0).astype(BF)
    tick()
    dh = hid()
    res = RES[rows(j, 128), :]
    scale = lax.rsqrt(jnp.mean(res * res, axis=1, keepdims=True) + EPSILON)
    w = dh * NG2[...]
    inner = jnp.mean(w * res, axis=1, keepdims=True)
    dres = G[rows(j, 128), :].astype(F32) + scale * w - res * (scale * scale * scale * inner)
    DRES[...] = dres
    GP[...] = jnp.zeros_like(GP)
    GP[1:2, :] = jnp.sum(dh * res * scale, axis=0, keepdims=True)
    DB[rows(j, 128), :] = dres.astype(BF)
    dbg = gather_start(DB)
    tick()
    tick()
    dbg()
    fin = reduce_start(1, 1)

    DAT[...] = contract(DB[...], WO[pl.ds(pl.multiple_of(base, 256), 256), :], 1, 1).astype(BF)
    own_heads = AF[:, pl.ds(pl.multiple_of(base, 256), 256)]
    blocks(3, lambda cols: contract(own_heads, DB[:, cols], 0, 0))
    begin(3, fo, OWAIT)
    DK[...] = jnp.zeros_like(DK)
    DV[...] = jnp.zeros_like(DV)

    def attend_back(b):
        qs, ks = pl.ds(b * 256, 256), pl.ds(b * 256, 512)
        for hp in range(2):
            cols = slice(hp * 128, hp * 128 + 128)
            q_b, k_b, v_b, d_b = Q[qs, cols], K[ks, cols], V[ks, cols], DAT[qs, cols]
            dq = dk = dv = None
            for h in range(2):
                m = head_mask[h]
                d_h = d_b * m
                p = PM[b * 4 + hp * 2 + h]
                dp = contract(d_h, v_b, 1, 1)
                ds = (p * (dp - jnp.sum(p * dp, axis=1, keepdims=True))).astype(BF)
                one = (contract(ds, k_b * m, 1, 0), contract(ds, q_b * m, 0, 0), contract(p.astype(BF), d_h, 0, 0))
                dq, dk, dv = one if dq is None else (dq + one[0], dk + one[1], dv + one[2])
            DQKV[qs, cols] = (dq * 0.125).astype(BF)
            DK[ks, cols] += dk
            DV[ks, cols] += dv

    attend_back(0)
    tick()
    attend_back(1)
    HS[:, 0:256] = DK[0:256, :].astype(BF)
    HS[:, 256:512] = DV[0:256, :].astype(BF)
    back = net.make(HS, HR, core_nb)
    net.start(back, c == 1)

    @pl.when(c == 0)
    def _():
        back.wait_recv()
        DK[512:768, :] += HR[:, 0:256].astype(F32)
        DV[512:768, :] += HR[:, 256:512].astype(F32)

    DQKV[:, 256:512] = DK[256:768, :].astype(BF)
    DQKV[:, 512:768] = DV[256:768, :].astype(BF)
    blocks(4, lambda cols: contract(XN[:, cols], DQKV[...], 0, 0))
    begin(4, fq, QWAIT)
    for n in range(4):
        cols = slice(n * 256, n * 256 + 256)
        PART[0, :, cols] = contract(DQKV[...], WQKV[cols, :], 1, 1).astype(BF)
    tick()
    OS[...] = (RES[rows(j, 128), :] + fin()).astype(BF)
    sent = send_blocks(OS, out)
    tick(TAIL[0])
    last = reduce_start(2, 0)
    tick(TAIL[1])
    dx = last()
    v = X[rows(j, 128), :].astype(F32)
    scale = lax.rsqrt(jnp.mean(v * v, axis=1, keepdims=True) + EPSILON)
    w = dx * NG1[...]
    inner = jnp.mean(w * v, axis=1, keepdims=True)
    GS[...] = (DRES[...] + scale * w - v * (scale * scale * scale * inner)).astype(BF)
    GP[0:1, :] = jnp.sum(dx * v * scale, axis=0, keepdims=True)
    sent_in = send_blocks(GS, gin)

    me = 4 * x + 2 * y + c
    got = []
    for d in range(1, NPLANE):
        xx, yy, cc = flip(x, d & 1), flip(y, d & 2), flip(c, d & 4)
        copy = net.make(GP.at[:, lanes(2 * xx + cc)], GR.at[me], dev(z, xx, yy, cc))
        net.start(copy)
        got.append(copy)
    keep = local(GP.at[:, lanes(row)], GR.at[me])
    keep.start()
    tick(2)
    keep.wait()
    for copy in got:
        copy.wait_recv()
    total = GR[0]
    for d in range(1, NPLANE):
        total = total + GR[d]
    GZS[...] = total
    got = []
    for d in range(1, nz):
        copy = net.make(GZS, GZ.at[z], dev((z + d) % nz, x, y, c))
        net.start(copy)
        got.append(copy)
    keep = local(GZS, GZ.at[z])
    keep.start()
    tick(30)
    keep.wait()
    for copy in got:
        copy.wait_recv()
    total = GZ[0]
    for d in range(1, nz):
        total = total + GZ[d]
    gains[...] = total
    sent()
    sent_in()
    for copy in flushes:
        copy.wait()
    net.finish()


def spread_kernel(nz, ff_half, ff_cut, f0, f1, f2, fo, fq, out_in, gin_in, gains, *refs):
    out, gin, gn1, gwq, gwk, gwv, gwo, gn2, gwg, gwu, gwd = refs[:11]
    I0, I1, I2, IO, IQ, OG, OU, OD, OO, OQ, PO, PG, PF, sem, sem_out = refs[11:]
    moves = ((f0, I0), (f1, I1), (f2, I2), (fo, IO), (fq, IQ), (out_in, PO), (gin_in, PG))
    loads = [pltpu.make_async_copy(a, b, sem.at[i]) for i, (a, b) in enumerate(moves)]
    for i in (5, 6, 4, 3, 0, 1, 2):
        loads[i].start()
    stores = []

    def store(buf, dst):
        stores.append(pltpu.make_async_copy(buf, dst, sem_out.at[len(stores)]))
        stores[-1].start()

    gn1[...] = gains[0:1, :]
    gn2[...] = gains[1:2, :]
    x = lax.axis_index("row") // 2
    chips = (x, 1 - x)
    loads[5].wait()
    store(PO, out)
    loads[6].wait()
    PF[...] = PG[...].astype(F32)
    store(PF, gin)
    loads[4].wait()
    for i, dst in enumerate((gwq, gwk, gwv)):
        for u, xx in enumerate(chips):
            for q in range(nz):
                OQ[i, q * 64 : q * 64 + 64, pl.ds(pl.multiple_of(xx * 256, 256), 256)] = IQ[q, u, :, i * 256 : i * 256 + 256].astype(F32)
        store(OQ.at[i], dst)
    loads[3].wait()
    for u, xx in enumerate(chips):
        for q in range(nz):
            OO[pl.ds(pl.multiple_of(xx * 256, 256) + q * 64, 64), :] = IO[q, u].astype(F32)
    store(OO, gwo)

    def store_part(at, width):
        cols = pl.ds(at, width)
        store(OG.at[:, cols], gwg.at[:, cols])
        store(OU.at[:, cols], gwu.at[:, cols])
        store(OD.at[cols, :], gwd.at[cols, :])

    for n, I in enumerate((I0, I1)):
        loads[n].wait()
        for u, xx in enumerate(chips):
            at = pl.multiple_of(xx * ff_half + n * 256, 128)
            for q in range(nz):
                OG[q * 64 : q * 64 + 64, pl.ds(at, 256)] = I[q, u, :, 0:256].astype(F32)
                OU[q * 64 : q * 64 + 64, pl.ds(at, 256)] = I[q, u, :, 256:512].astype(F32)
                OD[pl.ds(at + q * 64, 64), :] = I[q, u, :, 512:768].astype(F32)
            store_part(at, 256)
    loads[2].wait()
    for u, at in enumerate((x * ff_half + ff_half - 256, ff_cut, (1 - x) * ff_half + ff_half - 256)):
        at = pl.multiple_of(at, 128) if u != 1 else at
        for q in range(nz):
            OG[q * 64 : q * 64 + 64, pl.ds(at, 128)] = I2[q, u, :, 0:128].astype(F32)
            OU[q * 64 : q * 64 + 64, pl.ds(at, 128)] = I2[q, u, :, 128:256].astype(F32)
            side = q // 2 * 128
            OD[pl.ds(at + q % 2 * 64, 64), side : side + 128] = I2[q, u, :, 256:384].astype(F32)
        store_part(at, 128)
    for copy in stores:
        copy.wait()


def fused(nz, tokens, cotangent, seg_ids, norm_one, wq, wk, wv, wo, norm_two, w_gate, w_up, w_down):
    ff = w_gate.shape[1]
    ff_half = -(-ff // 512) * 256
    ff_cut = ff - ff_half
    vm = pltpu.VMEM
    zshapes = [(2, 256, 768)] * 2 + [(3, 256, 384), (2, 256, 256), (2, 256, 768)]
    zscratch, fshapes = [], []
    for units, rows, cols in zshapes:
        fshapes.append((nz, units, rows // nz, cols))
        zscratch += [
            vm((2, units, rows, cols), BF),
            vm((units, rows, cols), BF),
            vm((2, nz - 1, units, rows // nz, cols), BF),
            vm((nz, rows // nz, cols) if len(fshapes) in LATE else (rows // nz, cols), BF),
            vm(fshapes[-1], BF),
        ]
    scratch = [
        vm((512, D), BF), vm((512, D), BF), vm((D, 768), BF), vm((D, D), BF),
        vm((D, ff_half), BF), vm((D, ff_half), BF), vm((ff_half, D), BF), vm((1, D), F32), vm((1, D), F32),
        vm((512, D), BF), vm((512, 256), BF), vm((768, 256), BF), vm((768, 256), BF), vm((2, 256, 512), F32),
        vm((8, 256, 512), F32), vm((512, D), BF),
        vm((2, 512, D), BF), vm((3, 3, 128, D), BF),
        vm((512, D), BF), vm((512, D), F32), vm((128, D), F32), vm((512, ff_half), BF), vm((512, ff_half), BF),
        vm((512, ff_half), BF), vm((512, D), BF), vm((512, 256), BF), vm((512, ff_half), F32), vm((512, ff_half), F32), vm((3, 512, 256), BF),
        vm((768, 256), F32), vm((768, 256), F32), vm((512, 768), BF), vm((256, 512), BF), vm((256, 512), BF),
        vm((128, D), BF), vm((128, D), BF), vm((8, D), F32), vm((8, 8, 256), F32), vm((nz, 8, 256), F32), vm((8, 256), F32),
        *zscratch,
        pltpu.SemaphoreType.DMA((10,)), pltpu.SemaphoreType.DMA((258,)), pltpu.SemaphoreType.DMA((28,)),
    ]
    hbm, vmem = pl.BlockSpec(memory_space=pl.ANY), pl.BlockSpec(memory_space=pltpu.VMEM)
    sds = jax.ShapeDtypeStruct
    done = pl.pallas_call(
        functools.partial(layer_kernel, nz, ff_half, ff_cut),
        out_shape=(sds((512, 256), BF), sds((512, 256), BF), sds((8, 256), F32), *(sds(f, BF) for f in fshapes)),
        in_specs=[hbm, hbm, vmem, vmem, hbm, hbm, hbm, hbm, vmem, hbm, hbm, hbm],
        out_specs=(hbm, hbm, vmem, *(hbm for f in fshapes)),
        scratch_shapes=scratch,
        compiler_params=pltpu.CompilerParams(collective_id=0, has_side_effects=True, vmem_limit_bytes=62 << 20),
        name="layer",
    )(
        tokens, cotangent, seg_ids, norm_one[None], wq, wk, wv, wo, norm_two[None], w_gate, w_up, w_down,
    )
    out, gin, gains, *sums = done
    grads = (
        sds((512, 256), BF), sds((512, 256), F32), sds((1, 256), F32),
        sds((256, 512), F32), sds((256, 512), F32), sds((256, 512), F32), sds((512, 256), F32),
        sds((1, 256), F32), sds((256, ff), F32), sds((256, ff), F32), sds((ff, 256), F32),
    )
    res = pl.pallas_call(
        functools.partial(spread_kernel, nz, ff_half, ff_cut),
        out_shape=grads,
        in_specs=[hbm] * 7 + [vmem],
        out_specs=tuple(vmem if i in (2, 7) else hbm for i in range(11)),
        scratch_shapes=[vm(f, BF) for f in fshapes]
        + [vm((256, ff), F32), vm((256, ff), F32), vm((ff, 256), F32), vm((512, 256), F32), vm((3, 256, 512), F32)]
        + [vm((512, 256), BF), vm((512, 256), BF), vm((512, 256), F32), pltpu.SemaphoreType.DMA((7,)), pltpu.SemaphoreType.DMA((27,))],
        compiler_params=pltpu.CompilerParams(vmem_limit_bytes=63 << 20),
        name="spread",
    )(*sums, out, gin, gains)
    res = list(res)
    res[2], res[7] = res[2][0], res[7][0]
    return tuple(res)


def solution(mesh):
    in_specs = (
        P(("dp", "col"), "row"),
        P(("dp", "col"), "row"),
        P("dp", None),
        P("row"),
        P("row", "col"),
        P("row", "col"),
        P("row", "col"),
        P("col", "row"),
        P("row"),
        P("row", "col"),
        P("row", "col"),
        P("col", "row"),
    )
    out_specs = (
        P(("dp", "col"), "row"),
        P(("dp", "col"), "row"),
        P("row"),
        P("row", "col"),
        P("row", "col"),
        P("row", "col"),
        P("col", "row"),
        P("row"),
        P("row", "col"),
        P("row", "col"),
        P("col", "row"),
    )
    sizes = dict(mesh.shape)
    body = per_device
    if sizes["row"] == 4 and sizes["col"] == 2:
        body = functools.partial(fused, sizes["dp"])
    return jax.shard_map(
        body, mesh=mesh, in_specs=in_specs, out_specs=out_specs, check_vma=False
    )
```

```python
import functools

import jax
import jax.numpy as jnp
from jax import lax
from jax.experimental import pallas as pl
from jax.experimental.pallas import tpu as pltpu
from jax.sharding import PartitionSpec as P

D = 1024
HEAD_DIM = 64


EPSILON = 1e-05
NEGATIVE = -1e30


def for_sending(array):

    def short(part):
        return part.astype(jnp.bfloat16) if part.dtype == jnp.float32 else part

    return jax.tree.map(short, array)


def shifted(block, axis, distance):
    devices = range(lax.axis_size(axis))
    route = [(i - distance, i) for i in devices if i - distance in devices]
    return lax.ppermute(block, axis, route)


def matmul(first_op, second_op):
    return jnp.dot(first_op, second_op, preferred_element_type=jnp.float32)


def matmul_tn(first_op, second_op):
    return lax.dot_general(
        first_op, second_op, (((0,), (0,)), ((), ())), preferred_element_type=jnp.float32
    )


def matmul_nt(first_op, second_op):
    return lax.dot_general(
        first_op, second_op, (((1,), (1,)), ((), ())), preferred_element_type=jnp.float32
    )


def tokens_col(array_in):
    return lax.all_gather(array_in, "col", axis=0, tiled=True)


def tokens_row(array_in):
    return lax.all_gather(for_sending(array_in), "row", axis=0, tiled=True).astype(array_in.dtype)


def summed_row(array_in):
    return lax.psum_scatter(
        array_in.astype(jnp.bfloat16), "row", scatter_dimension=0, tiled=True
    ).astype(jnp.float32)


def summed_col(array_in):
    return lax.psum_scatter(
        array_in.astype(jnp.bfloat16), "col", scatter_dimension=0, tiled=True
    ).astype(jnp.float32)


def feature_total(array_in):
    return lax.psum(array_in, "row")


def window_parts(queries, keys_all, ids_ext, offset, head_cols):
    t_local = queries.shape[0]
    block_rows = min(512, t_local)
    key_reach = min(2048, t_local)
    window = key_reach + block_rows
    head_count = head_cols // HEAD_DIM
    anchor = offset + t_local - key_reach
    q_blk = lax.dynamic_slice_in_dim(queries, offset, block_rows, 0).reshape(
        block_rows, head_count, HEAD_DIM
    )
    k_win = lax.dynamic_slice_in_dim(keys_all, anchor, window, 0)
    k_blk = k_win[:, :head_cols].reshape(window, head_count, HEAD_DIM)
    v_blk = k_win[:, head_cols:].reshape(window, head_count, HEAD_DIM)
    q_ids = lax.dynamic_slice_in_dim(ids_ext, offset + t_local, block_rows, 0)
    k_ids = lax.dynamic_slice_in_dim(ids_ext, anchor, window, 0)
    q_pos = offset + lax.iota(jnp.int32, block_rows)
    k_pos = offset - key_reach + lax.iota(jnp.int32, window)
    allowed = (q_ids[:, None] == k_ids[None, :]) & (k_pos[None, :] <= q_pos[:, None])
    scores = jnp.einsum(
        "qhd,khd->hqk", q_blk, k_blk, preferred_element_type=jnp.float32
    ) * HEAD_DIM ** (-0.5)
    scores = jnp.where(allowed[None], scores, NEGATIVE)
    return (q_blk, k_blk, v_blk, scores)


def forward(tokens, seg_ids, norm_one, wq, wk, wv, wo, norm_two, w_gate, w_up, w_down):
    token_vals = tokens.astype(jnp.float32)
    scale_one = lax.rsqrt(feature_total(jnp.sum(token_vals * token_vals, axis=1)) / D + EPSILON)
    normed = (token_vals * scale_one[:, None] * norm_one).astype(jnp.bfloat16)
    normed_all = tokens_col(normed)
    w_qkv = jnp.concatenate([wq, wk, wv], axis=1)
    head_cols = wq.shape[1]
    qkv = summed_row(matmul(normed_all, w_qkv)).astype(jnp.bfloat16)
    queries = qkv[:, :head_cols]
    kv_local = qkv[:, head_cols:]
    prior_keys = shifted(kv_local, "row", 1)
    keys_all = jnp.concatenate([prior_keys, kv_local], axis=0)
    t_local = queries.shape[0]
    block_rows = min(512, t_local)
    padded_ids = jnp.concatenate([jnp.full((t_local,), -1, jnp.int32), seg_ids[0]])
    ids_ext = lax.dynamic_slice_in_dim(padded_ids, lax.axis_index("row") * t_local, 2 * t_local, 0)

    def attend(offset):
        q_blk, k_blk, v_blk, scores = window_parts(queries, keys_all, ids_ext, offset, head_cols)
        row_max = jnp.max(scores, axis=2, keepdims=True)
        exp_total = jnp.sum(jnp.exp(scores - row_max), axis=2, keepdims=True)
        log_total = row_max + jnp.log(exp_total)
        prob_low = jnp.exp(scores - log_total).astype(jnp.bfloat16)
        mixed_out = jnp.einsum("hqk,khd->qhd", prob_low, v_blk, preferred_element_type=jnp.float32)
        return (mixed_out.reshape(block_rows, head_cols).astype(jnp.bfloat16), log_total[:, :, 0])

    offsets = lax.iota(jnp.int32, t_local // block_rows) * block_rows
    pieces, log_totals = lax.map(attend, offsets)
    attn_out = pieces.reshape(t_local, head_cols)
    attn_all = tokens_row(attn_out)
    residual = token_vals + summed_col(matmul(attn_all, wo))
    stored = {
        "token_vals": token_vals,
        "scale_one": scale_one,
        "normed_all": normed_all,
        "queries": queries,
        "keys_all": keys_all,
        "ids_ext": ids_ext,
        "log_totals": log_totals,
        "attn_all": attn_all,
        "offsets": offsets,
    }
    f_col = w_gate.shape[1]
    scale_two = lax.rsqrt(feature_total(jnp.sum(residual * residual, axis=1)) / D + EPSILON)
    hidden_in = (residual * scale_two[:, None] * norm_two).astype(jnp.bfloat16)
    hidden_all = tokens_col(hidden_in)
    w_pair = jnp.concatenate([w_gate, w_up], axis=1)
    pair_sum = summed_row(matmul(hidden_all, w_pair))
    gate_pre = pair_sum[:, :f_col]
    up_pre = pair_sum[:, f_col:]
    act_low = (jax.nn.silu(gate_pre) * up_pre).astype(jnp.bfloat16)
    act_all = tokens_row(act_low)
    final_sum = residual + summed_col(matmul(act_all, w_down))
    stored.update(
        {
            "residual": residual,
            "scale_two": scale_two,
            "hidden_all": hidden_all,
            "gate_pre": gate_pre,
            "up_pre": up_pre,
            "act_all": act_all,
        }
    )
    return (final_sum.astype(jnp.bfloat16), stored)


def swiglu_grads(dact, gate_pre, up_pre):
    sigmoid_gate = jax.nn.sigmoid(gate_pre)
    gate_grad = (dact * up_pre * sigmoid_gate * (1.0 + gate_pre * (1.0 - sigmoid_gate))).astype(
        jnp.bfloat16
    )
    up_grad = (dact * gate_pre * sigmoid_gate).astype(jnp.bfloat16)
    return (gate_grad, up_grad)


def per_device(
    tokens, cotangent, seg_ids, norm_one, wq, wk, wv, wo, norm_two, w_gate, w_up, w_down
):
    weights = (tokens, seg_ids, norm_one, wq, wk, wv, wo, norm_two, w_gate, w_up, w_down)
    output, stored = forward(*weights)
    f_col = w_gate.shape[1]
    grad_out = cotangent.astype(jnp.float32)
    grad_all = tokens_col(cotangent)
    dact = summed_row(matmul_nt(grad_all, w_down))
    grad_down = matmul_tn(stored["act_all"], grad_all)
    gate_grad, up_grad = swiglu_grads(dact, stored["gate_pre"], stored["up_pre"])
    dpair = jnp.concatenate([gate_grad, up_grad], axis=1)
    dpair_all = tokens_row(dpair)
    w_pair = jnp.concatenate([w_gate, w_up], axis=1)
    dhidden = summed_col(matmul_nt(dpair_all, w_pair))
    grad_pair = matmul_tn(stored["hidden_all"], dpair_all)
    grad_gate = grad_pair[:, :f_col]
    grad_up = grad_pair[:, f_col:]
    residual = stored["residual"]
    scale_two = stored["scale_two"]
    weighted = dhidden * norm_two
    inner_sum = feature_total(jnp.sum(weighted * residual, axis=1)) / D
    dresid = (
        grad_out + scale_two[:, None] * weighted - residual * (scale_two**3 * inner_sum)[:, None]
    )
    grad_norm_two = jnp.sum(dhidden * residual * scale_two[:, None], axis=0)
    dbranch = dresid.astype(jnp.bfloat16)
    dbranch_all = tokens_col(dbranch)
    attn_grad = summed_row(matmul_nt(dbranch_all, wo)).astype(jnp.bfloat16)
    grad_wo = matmul_tn(stored["attn_all"], dbranch_all)
    queries = stored["queries"]
    keys_all = stored["keys_all"]
    ids_ext = stored["ids_ext"]
    head_cols = wq.shape[1]
    head_count = head_cols // HEAD_DIM
    t_local = queries.shape[0]
    block_rows = min(512, t_local)
    key_reach = min(2048, t_local)
    window = key_reach + block_rows
    inv_root = HEAD_DIM ** (-0.5)

    def attend_back(accum_dkv, inputs):
        offset, log_total = inputs
        q_blk, k_blk, v_blk, scores = window_parts(queries, keys_all, ids_ext, offset, head_cols)
        prob_full = jnp.exp(scores - log_total[:, :, None])
        prob_low = prob_full.astype(jnp.bfloat16)
        d_blk = lax.dynamic_slice_in_dim(attn_grad, offset, block_rows, 0).reshape(
            block_rows, head_count, HEAD_DIM
        )
        dprobs = jnp.einsum("qhd,khd->hqk", d_blk, v_blk, preferred_element_type=jnp.float32)
        dvalue = jnp.einsum("hqk,qhd->khd", prob_low, d_blk, preferred_element_type=jnp.float32)
        center = jnp.sum(prob_full * dprobs, axis=2, keepdims=True)
        dscores = (prob_full * (dprobs - center)).astype(jnp.bfloat16)
        dquery = (
            jnp.einsum("hqk,khd->qhd", dscores, k_blk, preferred_element_type=jnp.float32)
            * inv_root
        )
        dkey = (
            jnp.einsum("hqk,qhd->khd", dscores, q_blk, preferred_element_type=jnp.float32)
            * inv_root
        )
        update = jnp.concatenate(
            [dkey.reshape(window, head_cols), dvalue.reshape(window, head_cols)], axis=1
        )
        anchor = offset + t_local - key_reach
        current = lax.dynamic_slice_in_dim(accum_dkv, anchor, window, 0)
        accum_dkv = lax.dynamic_update_slice_in_dim(accum_dkv, current + update, anchor, 0)
        return (accum_dkv, dquery.reshape(block_rows, head_cols))

    start_grads = jnp.zeros((2 * t_local, 2 * head_cols), jnp.float32)
    accum_dkv, query_grads = lax.scan(
        attend_back, start_grads, (stored["offsets"], stored["log_totals"])
    )
    returned = shifted(accum_dkv[:t_local].astype(jnp.bfloat16), "row", -1).astype(jnp.float32)
    key_grads = accum_dkv[t_local:] + returned
    dqkv = jnp.concatenate([query_grads.reshape(t_local, head_cols), key_grads], axis=1).astype(
        jnp.bfloat16
    )
    dqkv_all = tokens_row(dqkv)
    w_qkv = jnp.concatenate([wq, wk, wv], axis=1)
    dnormed = summed_col(matmul_nt(dqkv_all, w_qkv))
    grad_qkv = matmul_tn(stored["normed_all"], dqkv_all)
    grad_wq = grad_qkv[:, :head_cols]
    grad_wk = grad_qkv[:, head_cols : 2 * head_cols]
    grad_wv = grad_qkv[:, 2 * head_cols :]
    token_vals = stored["token_vals"]
    scale_one = stored["scale_one"]
    weighted_one = dnormed * norm_one
    inner_one = feature_total(jnp.sum(weighted_one * token_vals, axis=1)) / D
    grad_input = (
        dresid
        + scale_one[:, None] * weighted_one
        - token_vals * (scale_one**3 * inner_one)[:, None]
    )
    grad_norm_one = jnp.sum(dnormed * token_vals * scale_one[:, None], axis=0)
    grad_sums = (
        lax.psum(grad_wq.astype(jnp.bfloat16), "dp").astype(jnp.float32),
        lax.psum(grad_wk.astype(jnp.bfloat16), "dp").astype(jnp.float32),
        lax.psum(grad_wv.astype(jnp.bfloat16), "dp").astype(jnp.float32),
        lax.psum(grad_wo.astype(jnp.bfloat16), "dp").astype(jnp.float32),
        lax.psum(grad_gate.astype(jnp.bfloat16), "dp").astype(jnp.float32),
        lax.psum(grad_up.astype(jnp.bfloat16), "dp").astype(jnp.float32),
        lax.psum(grad_down.astype(jnp.bfloat16), "dp").astype(jnp.float32),
    )
    gain_sums = lax.psum((grad_norm_one, grad_norm_two), ("dp", "col"))
    return (
        output,
        grad_input,
        gain_sums[0],
        grad_sums[0],
        grad_sums[1],
        grad_sums[2],
        grad_sums[3],
        gain_sums[1],
        grad_sums[4],
        grad_sums[5],
        grad_sums[6],
    )


MESH = pl.DeviceIdType.MESH
BF = jnp.bfloat16
F32 = jnp.float32
NPLANE = 8
TAIL, HELD = (1, 2), (0, 3)
LATE = (1, 3, 4)
NEWFIRST, LAG = True, 4
FWAIT, OWAIT, QWAIT = (4, 6, 0), 0, 0


def contract(a, b, ca, cb):
    return lax.dot_general(a, b, (((ca,), (cb,)), ((), ())), preferred_element_type=F32)


class Copies:
    def __init__(self, send, recv):
        self.send, self.recv, self.used, self.kept, self.open = send, recv, 0, 1, []

    def take(self, amount=1):
        base = self.used
        self.used += amount
        return base

    def make(self, src, dst, to, site=None, own=False):
        site = self.take() if site is None else site
        self.kept += own
        return pltpu.make_async_remote_copy(
            src_ref=src,
            dst_ref=dst,
            send_sem=self.send.at[self.kept - 1 if own else 0],
            recv_sem=self.recv.at[site],
            device_id=to,
            device_id_type=MESH,
        )

    def start(self, copy, when=None):
        self.open.append((copy, when))
        if when is None:
            copy.start()
        else:
            pl.when(when)(copy.start)

    def finish(self):
        for copy, when in self.open:
            if when is None:
                copy.wait_send()
            else:
                pl.when(when)(copy.wait_send)
        self.open = []


def layer_kernel(nz, ff_half, ff_cut, *refs):
    it = iter(refs)
    take = lambda n: [next(it) for _ in range(n)]
    tok, cot, seg, n1, wq, wk, wv, wo, n2, wg, wu, wd = take(12)
    out, gin, gains, f0, f1, f2, fo, fq = take(8)
    X, G, WQKV, WO, WG, WU, WD, NG1, NG2 = take(9)
    XN, Q, K, V, BIAS, PM, AF = take(7)
    PART, RX = take(2)
    HN, RES, DRES, ACT, DGA, DUP, DB, DAT, BYG, BYU, T3 = take(11)
    DK, DV, DQKV, HS, HR = take(5)
    OS, GS, GP, GR, GZ, GZS = take(6)
    zbufs = [take(5) for _ in range(5)]
    send, recv, loc = take(3)

    z, row, y = lax.axis_index("dp"), lax.axis_index("row"), lax.axis_index("col")
    x, c = row // 2, row % 2
    net = Copies(send, recv)
    nloc = [0]

    def local(src, dst):
        nloc[0] += 1
        return pltpu.make_async_copy(src, dst, loc.at[nloc[0] - 1])

    def dev(zz, xx, yy, cc):
        return (zz, 2 * xx + cc, yy)

    core_nb, x_nb, y_nb = dev(z, x, y, 1 - c), dev(z, 1 - x, y, c), dev(z, x, 1 - y, c)
    z_up, z_dn = dev(z + 1, x, y, c), dev(z - 1, x, y, c)
    lanes = lambda i, n=256: pl.ds(pl.multiple_of(i * n, 128), n)
    rows = lambda i, n: pl.ds(pl.multiple_of(i * n, n if n % 16 else 16), n)
    flip = lambda v, bit: 1 - v if bit else v

    barrier = pltpu.get_barrier_semaphore()
    for d in range(1, NPLANE):
        pl.semaphore_signal(
            barrier, inc=1, device_id=dev(z, flip(x, d & 1), flip(y, d & 2), flip(c, d & 4)), device_id_type=MESH
        )
    for d in range(1, nz):
        pl.semaphore_signal(barrier, inc=1, device_id=dev((z + d) % nz, x, y, c), device_id_type=MESH)
    for _, _, ZR, _, _ in zbufs:

        @pl.when(z == 0)
        def _(ZR=ZR):
            ZR[0, nz - 2] = jnp.zeros(ZR.shape[2:], BF)

        @pl.when(z == nz - 1)
        def _(ZR=ZR):
            ZR[1, nz - 2] = jnp.zeros(ZR.shape[2:], BF)

    seg_f = seg[...].astype(F32)
    own = jnp.where(c == 0, seg_f[:, :512], seg_f[:, 512:])
    before = jnp.where(c == 0, jnp.full((1, 256), -1.0, F32), seg_f[:, 256:512])
    ids = jnp.concatenate([before, own], axis=1)
    for b in range(2):
        k_id = jnp.broadcast_to(ids[:, b * 256 : b * 256 + 512], (256, 512))
        q_id = jnp.broadcast_to(ids[:, 256 + b * 256 : 512 + b * 256], (512, 256)).T
        q_pos = lax.broadcasted_iota(jnp.int32, (256, 512), 0) + 256
        k_pos = lax.broadcasted_iota(jnp.int32, (256, 512), 1)
        BIAS[b] = jnp.where((q_id == k_id) & (k_pos <= q_pos), 0.0, NEGATIVE)

    @pl.when(c == 0)
    def _():
        K[0:256, :] = jnp.zeros((256, 256), BF)
        V[0:256, :] = jnp.zeros((256, 256), BF)

    pl.semaphore_wait(barrier, NPLANE - 1 + nz - 1)

    def gather_tokens(src, buf):
        col = lambda rr: buf.at[:, lanes(rr)]
        mine = c == y
        other = jnp.logical_not(mine)
        keep = local(src, col(row))
        over = net.make(src, col(row), core_nb)
        bx, by = net.take(2), net.take(2)
        to_x = net.make(src, col(row), dev(z, 1 - x, y, y), bx + c)
        to_y = net.make(src, col(row), dev(z, x, 1 - y, y), by + c)
        far = 2 * (1 - x)
        by_y = net.make(col(far), col(far), y_nb)
        by_x = net.make(col(2 * x + 1), col(2 * x + 1), x_nb)
        got_x = [net.make(src, col(row), core_nb, bx + k) for k in range(2)]
        got_y = [net.make(src, col(row), core_nb, by + k) for k in range(2)]

        def start():
            pl.when(mine)(keep.start)
            net.start(to_x)
            net.start(to_y)
            net.start(over, other)

        def arrive():
            @pl.when(mine)
            def _():
                got_x[0].wait_recv()
                by_y.start()

            @pl.when(other)
            def _():
                got_y[1].wait_recv()
                by_x.start()

            net.open += [(by_y, mine), (by_x, other)]

        def rest():
            @pl.when(mine)
            def _():
                got_x[1].wait_recv()
                over.wait_recv()
                keep.wait()

            @pl.when(other)
            def _():
                got_y[0].wait_recv()
                by_y.wait_recv()
                by_x.wait_recv()

        return start, arrive, rest

    def relay(src_of, dst_of):
        keep = local(src_of(x), dst_of(row))
        across = net.make(src_of(x), dst_of(row), core_nb)
        far = net.make(src_of(1 - x), dst_of(row), x_nb)
        theirs = dst_of(2 * (1 - x) + c)
        fwd = net.make(theirs, theirs, core_nb)

        def start():
            keep.start()
            net.start(far)
            net.start(across)

        def arrive():
            far.wait_recv()
            net.start(fwd)

        def rest():
            keep.wait()
            across.wait_recv()
            fwd.wait_recv()

        return start, arrive, rest

    def z_gather(at):
        sites = (net.take(nz - 1), net.take(nz - 1))

        def step(s):
            for way, to in ((0, z_up), (1, z_dn)):
                zz = z if way == 0 else nz - 1 - z
                ref = at(z - s if way == 0 else z + s)
                have = zz >= s
                if s > 0:
                    pl.when(have)(net.make(ref, ref, to, sites[way] + s - 1).wait_recv)
                if s < nz - 1:
                    net.start(net.make(ref, ref, to, sites[way] + s), have & (zz < nz - 1))

        return step

    def relay_z(pairs, whole, n_rows):
        n = n_rows // nz
        keep = [local(a, b) for a, b in pairs(x, row, 0, n_rows)]
        across = [net.make(a, b, core_nb) for a, b in pairs(x, row, 0, n_rows)]
        far = [net.make(a, b, x_nb) for a, b in pairs(1 - x, row, z * n, n)]
        hop = z_gather(lambda q: whole(2 * (1 - x) + c, q * n, n))
        theirs = whole(2 * (1 - x) + c, 0, n_rows)
        fwd = net.make(theirs, theirs, core_nb)

        def begin():
            for copy in far:
                net.start(copy)
            for copy in keep:
                copy.start()
            for copy in across:
                net.start(copy)

        def step(s):
            if s == 0:
                for copy in far:
                    copy.wait_recv()
            hop(s)
            if s == nz - 1:
                net.start(fwd)

        def rest():
            for copy in keep:
                copy.wait()
            for copy in across:
                copy.wait_recv()
            fwd.wait_recv()

        return begin, step, rest

    def gather_wo():
        at = lambda yy, rr: WO.at[rows(yy, 512), lanes(rr)]
        keep = local(wo, at(y, row))
        across = net.make(wo, at(y, row), core_nb)
        to_x, to_y = net.make(wo, at(y, row), x_nb), net.make(wo, at(y, row), y_nb)
        rx = 2 * (1 - x) + c
        on_y = net.make(at(y, rx), at(y, rx), y_nb)
        others = (at(y, rx), at(1 - y, row), at(1 - y, rx))
        fwd = [net.make(ref, ref, core_nb) for ref in others]

        def start():
            net.start(to_x)
            net.start(to_y)
            keep.start()
            net.start(across)

        def arrive():
            to_x.wait_recv()
            net.start(on_y)
            net.start(fwd[0])

        def pass_on():
            to_y.wait_recv()
            net.start(fwd[1])
            on_y.wait_recv()
            net.start(fwd[2])

        def rest():
            keep.wait()
            across.wait_recv()
            for copy in fwd:
                copy.wait_recv()

        return start, arrive, pass_on, rest

    def gather_gain(src, dst):
        keep = local(src, dst.at[:, lanes(row)])
        keep.start()
        got = []
        for to in (core_nb, x_nb, dev(z, 1 - x, y, 1 - c)):
            got.append(net.make(src, dst.at[:, lanes(row)], to))
            net.start(got[-1])

        def rest():
            keep.wait()
            for g in got:
                g.wait_recv()

        return rest

    gx, gg = gather_tokens(tok, X), gather_tokens(cot, G)
    some = lambda r0, n: pl.ds(pl.multiple_of(r0, 16), n)
    rqkv = []
    for i, w in ((1, wk), (2, wv), (0, wq)):
        at = lambda rr, r0, n, i=i: WQKV.at[some(rr * 256 + r0, n), pl.ds(i * 256, 256)]
        rqkv.append(relay_z(lambda xx, rr, r0, n, w=w, at=at: [(w.at[some(r0, n), lanes(xx)], at(rr, r0, n))], at, 256))
    ro = gather_wo()
    both = ff_half - ff_cut
    rff = []
    for w, W in ((wg, WG), (wu, WU)):
        at = lambda rr, r0, n, W=W: W.at[some(rr * 256 + r0, n), :]

        def pairs(xx, rr, r0, n, w=w, W=W):
            out = []
            for src, dst, width in ((pl.multiple_of(xx * ff_half, 128), 0, ff_cut), (ff_cut, ff_cut, both)):
                out.append((w.at[some(r0, n), pl.ds(src, width)], W.at[some(rr * 256 + r0, n), pl.ds(dst, width)]))
            return out

        rff.append(relay_z(pairs, at, 256))

    def pairs_down(xx, rr, r0, n):
        if n == ff_half:
            parts = ((xx * ff_half, 0, ff_cut), (ff_cut, ff_cut, both))
        else:
            tail = jnp.where(z == nz - 1, ff_cut, xx * ff_half + r0 + n - both)
            parts = ((xx * ff_half + r0, r0, n - both), (tail, r0 + n - both, both))
        return [(wd.at[some(src, k), :], WD.at[some(dst, k), lanes(rr)]) for src, dst, k in parts]

    rd = relay_z(pairs_down, lambda rr, r0, n: WD.at[some(r0, n), lanes(rr)], ff_half)
    for r in rqkv:
        r[0]()
    gx[0]()
    ga = [gather_gain(n1, NG1), gather_gain(n2, NG2)]
    for r in rqkv:
        r[1](0)
    for r in rqkv:
        r[1](1)
    gx[1]()
    for s in range(2, nz):
        for r in rqkv:
            r[1](s)
    for g in ga:
        g()
    for r in (*rff, rd):
        r[0]()
    gx[2]()
    ro[0]()
    for t in range(4):
        v = X[t * 128 : t * 128 + 128, :].astype(F32)
        scale = lax.rsqrt(jnp.mean(v * v, axis=1, keepdims=True) + EPSILON)
        XN[t * 128 : t * 128 + 128, :] = (v * scale * NG1[...]).astype(BF)
    for r in rqkv:
        r[2]()
    K[256:768, :] = contract(XN[...], WQKV[:, 256:512], 1, 0).astype(BF)
    V[256:768, :] = contract(XN[...], WQKV[:, 512:768], 1, 0).astype(BF)
    hk = net.make(K.at[pl.ds(512, 256), :], K.at[pl.ds(0, 256), :], core_nb)
    hv = net.make(V.at[pl.ds(512, 256), :], V.at[pl.ds(0, 256), :], core_nb)
    net.start(hk, c == 0)
    net.start(hv, c == 0)
    Q[...] = (contract(XN[...], WQKV[:, 0:256], 1, 0).astype(BF) * 0.125).astype(BF)
    @pl.when(c == 1)
    def _():
        hk.wait_recv()
        hv.wait_recv()

    lane_id = lax.broadcasted_iota(jnp.int32, (1, 128), 1)
    head_mask = [jnp.where(lane_id < 64, 1.0, 0.0).astype(BF), jnp.where(lane_id < 64, 0.0, 1.0).astype(BF)]

    heads_at = lambda xx, yy, b: AF.at[pl.ds(b * 256, 256), lanes(2 * yy + xx)]
    a_x = [net.make(heads_at(x, y, b), heads_at(x, y, b), x_nb) for b in range(2)]
    a_y = [net.make(heads_at(x, y, b), heads_at(x, y, b), y_nb) for b in range(2)]
    a_far = (
        net.make(heads_at(1 - x, y, 0), heads_at(1 - x, y, 0), y_nb),
        net.make(heads_at(x, 1 - y, 1), heads_at(x, 1 - y, 1), x_nb),
    )
    base = (2 * y + x) * 256
    for b in range(2):
        for hp in range(2):
            cols = slice(hp * 128, hp * 128 + 128)
            q_b, k_b, v_b = Q[b * 256 : b * 256 + 256, cols], K[b * 256 : b * 256 + 512, cols], V[b * 256 : b * 256 + 512, cols]
            total = None
            for h in range(2):
                s = contract(q_b * head_mask[h], k_b, 1, 1) + BIAS[b]
                e = jnp.exp(s - jnp.max(s, axis=1, keepdims=True))
                p = e * (1.0 / jnp.sum(e, axis=1, keepdims=True))
                PM[b * 4 + hp * 2 + h] = p
                part = contract(p.astype(BF), v_b * head_mask[h], 1, 0)
                total = part if total is None else total + part
            AF[b * 256 : b * 256 + 256, pl.ds(pl.multiple_of(base + hp * 128, 128), 128)] = total.astype(BF)
        net.start(a_x[b])
        net.start(a_y[b])
        if b == 0:
            for r in rff:
                r[1](0)
    for r in rff:
        r[1](1)
    rd[1](0)
    ro[1]()
    a_x[0].wait_recv()
    net.start(a_far[0])
    a_y[1].wait_recv()
    net.start(a_far[1])
    gg[0]()
    for r in rff:
        r[1](2)
    rd[1](1)
    ro[2]()
    for r in rff:
        r[1](3)
    rd[1](2)

    j = 2 * x + y
    shard = lambda buf, jj: buf.at[rows(jj, 128), :]

    peers = ((x_nb, 2 * (1 - x) + y), (y_nb, 2 * x + 1 - y), (dev(z, 1 - x, 1 - y, c), 2 * (1 - x) + 1 - y))

    def reduce_start(k, p):
        sent = [net.make(shard(PART.at[p], jj), RX.at[k, i], to, own=True) for i, (to, jj) in enumerate(peers)]
        for copy in (sent[2], sent[0], sent[1]):
            copy.start()

        def end():
            for copy in sent:
                copy.wait_recv()
            for copy in sent:
                copy.wait_send()
            total = PART[p, rows(j, 128), :].astype(F32)
            for i in range(3):
                total = total + RX[k, i].astype(F32)
            return total

        return end

    def gather_start(buf):
        sent = [net.make(shard(buf, j), shard(buf, j), to) for to, _ in peers]
        for copy in (sent[2], sent[0], sent[1]):
            net.start(copy)

        def end():
            for copy in sent:
                copy.wait_recv()

        return end

    def send_blocks(src, dst):
        base_r = net.take(4)
        waits = []
        for dx in range(2):
            for cc in range(2):
                xx = flip(x, dx)
                piece, place = src.at[:, lanes(2 * xx + cc)], dst.at[rows(j, 128), :]
                copy = pltpu.make_async_remote_copy(
                    src_ref=piece,
                    dst_ref=place,
                    send_sem=net.send.at[0],
                    recv_sem=net.recv.at[base_r + dx * 2 + y],
                    device_id=dev(z, xx, c, cc),
                    device_id_type=MESH,
                )
                if dx == 0:
                    here = (c == y) & (c == cc)
                    keep = local(piece, place)
                    pl.when(here)(keep.start)
                    net.start(copy, jnp.logical_not(here))
                    waits.append((keep, here))
                else:
                    net.start(copy)
        piece, place = src.at[:, pl.ds(0, 256)], dst.at[pl.ds(0, 128), :]
        arrivals = [
            (net.make(piece, place, core_nb, base_r + dx * 2 + yy), jnp.logical_not((c == y) & (y == yy)) if dx == 0 else None)
            for dx in range(2)
            for yy in range(2)
        ]

        def end():
            for keep, here in waits:
                pl.when(here)(keep.wait)
            for got, when in arrivals:
                if when is None:
                    got.wait_recv()
                else:
                    pl.when(when)(got.wait_recv)

        return end

    def along_z(tag, dst):
        GB, CR, ZR, RL, FF = zbufs[tag]
        n_rows = CR.shape[1] // nz
        n = n_rows // 2
        last = CR.shape[0] - 1
        part = lambda q, i: pl.ds(pl.multiple_of(q * n_rows + i * n, 16), n)
        own = lambda i: pl.ds(i * n, n)
        over = net.make(GB.at[1 - c], CR, core_nb)
        net.start(over)
        yield
        over.wait_recv()
        for u in range(CR.shape[0]):
            CR[u] = (CR[u].astype(F32) + GB[c, u].astype(F32)).astype(BF)
        sites = [[net.take(nz - 1) for _ in range(2)] for _ in range(2)]
        for s in range(1, nz):
            for i in range(2):
                for way, to in ((0, z_up), (1, z_dn)):
                    zz = z if way == 0 else nz - 1 - z
                    q = nz - s + zz
                    q = q if way == 0 else nz - 1 - q
                    go = (zz < nz - 1) & (zz <= s - 1)
                    first, later = go & (zz == 0), go & (zz > 0)
                    site = sites[way][i] + s - 1
                    there = ZR.at[way, s - 1, :, own(i), :]
                    net.start(net.make(CR.at[:, part(q, i), :], there, to, site), first)
                    if s >= 2:
                        acc = ZR.at[way, s - 2, :, own(i), :]
                        got = net.make(acc, acc, to, site - 1)

                        @pl.when(later)
                        def _(got=got, acc=acc, q=q, i=i):
                            got.wait_recv()
                            acc[...] = (acc[...].astype(F32) + CR[:, part(q, i), :].astype(F32)).astype(BF)

                        net.start(net.make(acc, there, to, site), later)
                yield
        late = len(RL.shape) == 3
        backs = [[net.take(nz - 1) for _ in range(2)] for _ in range(2)]
        here = lambda q, i: FF.at[q, :, own(i), :]
        side = []

        def send_back(i):
            net.start(net.make(here(z, i), here(z, i), z_up, backs[0][i]), z < nz - 1)
            net.start(net.make(here(z, i), here(z, i), z_dn, backs[1][i]), z > 0)

        for i in range(2):
            for way in range(2):
                zz = z if way == 0 else nz - 1 - z
                acc = ZR.at[way, nz - 2, :, own(i), :]
                pl.when(zz > 0)(net.make(acc, acc, z_up, sites[way][i] + nz - 2).wait_recv)
            total = (
                CR[:, part(z, i), :].astype(F32)
                + ZR[0, nz - 2, :, own(i), :].astype(F32)
                + ZR[1, nz - 2, :, own(i), :].astype(F32)
            ).astype(BF)
            if late:
                FF[z, :, own(i), :] = total
                send_back(i)
            else:
                RL[own(i), :] = total[-1]
                side.append(net.make(RL.at[own(i), :], FF.at[z, last, own(i), :], x_nb))
                net.start(side[i])
                FF[z, 0:last, own(i), :] = total[:-1]
            yield
        if not late:
            for i in range(2):
                side[i].wait_recv()
                send_back(i)
                if tag == 4 and i == 0:
                    gates.append(tag)
                yield
        sites = backs
        for s in range(2, nz + 1):
            for i in range(2):
                for way, to in ((0, z_up), (1, z_dn)):
                    zz = z if way == 0 else nz - 1 - z
                    q = z - (s - 1) if way == 0 else z + (s - 1)
                    have = zz >= s - 1
                    ref = here(q, i)
                    pl.when(have)(net.make(ref, ref, to, sites[way][i] + s - 2).wait_recv)
                    if s < nz:
                        net.start(net.make(ref, ref, to, sites[way][i] + s - 1), have & (zz < nz - 1))
                yield
        if late:
            trade = net.make(FF.at[:, last], RL, x_nb)
            while tag in HELD and not gates:
                yield
            net.start(trade)
            for _ in range(LAG):
                yield
            trade.wait_recv()
            flush(FF.at[:, 0:last], dst.at[:, 0:last])
            flush(RL, dst.at[:, last])
        else:
            flush(FF, dst)
        yield

    def flush(buf, dst):
        copy = local(buf, dst)
        copy.start()
        flushes.append(copy)

    flushes, gates = [], []

    lines = []

    def begin(i, dst, wait):
        line = along_z(i, dst)
        next(line)
        lines.append([line, wait])

    def tick(n=1):
        for _ in range(max(1, int(n))):
            for _ in range(2 if n >= 1 else 1):
                for line in (lines[::-1] if NEWFIRST else lines):
                    if line[1] > 0:
                        line[1] -= 1
                    else:
                        next(line[0], None)

    ro[3]()
    for copy in (a_x[1], a_y[0], *a_far):
        copy.wait_recv()
    for t in range(4):
        tile = slice(t * 128, t * 128 + 128)
        res = X[tile, :].astype(F32) + contract(AF[tile, :], WO[...], 1, 0)
        RES[tile, :] = res
        scale = lax.rsqrt(jnp.mean(res * res, axis=1, keepdims=True) + EPSILON)
        HN[tile, :] = (res * scale * NG2[...]).astype(BF)
    gg[1]()
    for r in rff:
        r[2]()
    rd[1](3)
    unit = lambda r: jnp.where(x == r // 2, 0, 1)
    shared = (lax.broadcasted_iota(jnp.int32, (1, 256), 1) >= 256 - both) & (x == 1)

    def tile_grads(n):
        cols = slice(n * 256, n * 256 + 256)
        GB = zbufs[n][0]
        for i, made in enumerate((DGA, DUP)):
            whole = contract(HN[...], made[:, cols], 0, 0)
            for r in range(4):
                GB[r % 2, unit(r), :, i * 256 : i * 256 + 256] = whole[r * 256 : r * 256 + 256].astype(BF)
        whole = contract(ACT[:, cols], G[...], 0, 0)
        for r in range(4):
            GB[r % 2, unit(r), :, 512:768] = whole[:, r * 256 : r * 256 + 256].astype(BF)

    def last_tile_grads(n):
        GB = zbufs[n][0]

        def put(r, cols, a, b):
            GB[r % 2, jnp.where(x == r // 2, 0, 2), :, cols] = a.astype(BF)

            @pl.when(x == r // 2)
            def _():
                GB[r % 2, 1, :, cols] = b.astype(BF)

        for i in range(2):
            whole = contract(HN[...], T3[i], 0, 0)
            for r in range(4):
                rws = whole[r * 256 : r * 256 + 256]
                put(r, slice(i * 128, i * 128 + 128), rws[:, :128], rws[:, 128:])
        whole = contract(T3[2], G[...], 0, 0)
        for r in range(4):
            left, right = whole[:, r * 256 : r * 256 + 128], whole[:, r * 256 + 128 : r * 256 + 256]
            put(
                r,
                slice(256, 384),
                jnp.concatenate([left[:128], right[:128]], axis=0),
                jnp.concatenate([left[128:], right[128:]], axis=0),
            )

    tiles = ff_half // 256
    for n in range(tiles):
        cols = slice(n * 256, n * 256 + 256)
        gate = contract(HN[...], WG[:, cols], 1, 0)
        up = contract(HN[...], WU[:, cols], 1, 0)
        sig = jax.nn.sigmoid(gate)
        silu = gate * sig
        act = (silu * up).astype(BF)
        if n == tiles - 1:
            T3[2] = act
            act = jnp.where(shared, jnp.zeros_like(act), act)
        ACT[:, cols] = act
        BYG[:, cols] = up * sig * (1.0 + gate * (1.0 - sig))
        BYU[:, cols] = silu
    gg[2]()
    rd[2]()
    for n in (tiles - 1, *range(tiles - 1)):
        cols = slice(n * 256, n * 256 + 256)
        dact = contract(G[...], WD[cols, :], 1, 1)
        dgate, dup = (dact * BYG[:, cols]).astype(BF), (dact * BYU[:, cols]).astype(BF)
        if n == tiles - 1:
            T3[0], T3[1] = dgate, dup
            dgate, dup = (jnp.where(shared, jnp.zeros_like(v), v) for v in (dgate, dup))
        DGA[:, cols] = dgate
        DUP[:, cols] = dup
        (last_tile_grads if n == tiles - 1 else tile_grads)(n)
        begin(n, (f0, f1, f2)[n], FWAIT[n])
        if n == 0:
            tick()
    blocks = lambda i, f: [zbufs[i][0].__setitem__((r % 2, unit(r)), f(slice(r * 256, r * 256 + 256)).astype(BF)) for r in range(4)]
    tick()
    for n in range(4):
        cols = slice(n * 256, n * 256 + 256)
        PART[0, :, cols] = (contract(DGA[...], WG[cols, :], 1, 1) + contract(DUP[...], WU[cols, :], 1, 1)).astype(BF)
    hid = reduce_start(0, 0)
    tick()
    for n in range(4):
        cols = slice(n * 256, n * 256 + 256)
        PART[1, :, cols] = contract(ACT[...], WD[:, cols], 1, 0).astype(BF)
    tick()
    tick(0.5)
    dh = hid()
    res = RES[rows(j, 128), :]
    scale = lax.rsqrt(jnp.mean(res * res, axis=1, keepdims=True) + EPSILON)
    w = dh * NG2[...]
    inner = jnp.mean(w * res, axis=1, keepdims=True)
    dres = G[rows(j, 128), :].astype(F32) + scale * w - res * (scale * scale * scale * inner)
    DRES[...] = dres
    GP[...] = jnp.zeros_like(GP)
    GP[1:2, :] = jnp.sum(dh * res * scale, axis=0, keepdims=True)
    DB[rows(j, 128), :] = dres.astype(BF)
    dbg = gather_start(DB)
    tick(0.5)
    tick()
    dbg()
    fin = reduce_start(1, 1)

    DAT[...] = contract(DB[...], WO[pl.ds(pl.multiple_of(base, 256), 256), :], 1, 1).astype(BF)
    own_heads = AF[:, pl.ds(pl.multiple_of(base, 256), 256)]
    blocks(3, lambda cols: contract(own_heads, DB[:, cols], 0, 0))
    begin(3, fo, OWAIT)
    DK[...] = jnp.zeros_like(DK)
    DV[...] = jnp.zeros_like(DV)

    def attend_back(b):
        qs, ks = pl.ds(b * 256, 256), pl.ds(b * 256, 512)
        for hp in range(2):
            cols = slice(hp * 128, hp * 128 + 128)
            q_b, k_b, v_b, d_b = Q[qs, cols], K[ks, cols], V[ks, cols], DAT[qs, cols]
            dq = dk = dv = None
            for h in range(2):
                m = head_mask[h]
                d_h = d_b * m
                p = PM[b * 4 + hp * 2 + h]
                dp = contract(d_h, v_b, 1, 1)
                ds = (p * (dp - jnp.sum(p * dp, axis=1, keepdims=True))).astype(BF)
                one = (contract(ds, k_b * m, 1, 0), contract(ds, q_b * m, 0, 0), contract(p.astype(BF), d_h, 0, 0))
                dq, dk, dv = one if dq is None else (dq + one[0], dk + one[1], dv + one[2])
            DQKV[qs, cols] = (dq * 0.125).astype(BF)
            DK[ks, cols] += dk
            DV[ks, cols] += dv

    attend_back(0)
    tick()
    attend_back(1)
    HS[:, 0:256] = DK[0:256, :].astype(BF)
    HS[:, 256:512] = DV[0:256, :].astype(BF)
    back = net.make(HS, HR, core_nb)
    net.start(back, c == 1)

    @pl.when(c == 0)
    def _():
        back.wait_recv()
        DK[512:768, :] += HR[:, 0:256].astype(F32)
        DV[512:768, :] += HR[:, 256:512].astype(F32)

    DQKV[:, 256:512] = DK[256:768, :].astype(BF)
    DQKV[:, 512:768] = DV[256:768, :].astype(BF)
    blocks(4, lambda cols: contract(XN[:, cols], DQKV[...], 0, 0))
    begin(4, fq, QWAIT)
    for n in range(4):
        cols = slice(n * 256, n * 256 + 256)
        PART[0, :, cols] = contract(DQKV[...], WQKV[cols, :], 1, 1).astype(BF)
    tick()
    OS[...] = (RES[rows(j, 128), :] + fin()).astype(BF)
    sent = send_blocks(OS, out)
    tick(TAIL[0])
    last = reduce_start(2, 0)
    tick(TAIL[1])
    dx = last()
    v = X[rows(j, 128), :].astype(F32)
    scale = lax.rsqrt(jnp.mean(v * v, axis=1, keepdims=True) + EPSILON)
    w = dx * NG1[...]
    inner = jnp.mean(w * v, axis=1, keepdims=True)
    GS[...] = (DRES[...] + scale * w - v * (scale * scale * scale * inner)).astype(BF)
    GP[0:1, :] = jnp.sum(dx * v * scale, axis=0, keepdims=True)
    sent_in = send_blocks(GS, gin)

    me = 4 * x + 2 * y + c
    got = []
    for d in range(1, NPLANE):
        xx, yy, cc = flip(x, d & 1), flip(y, d & 2), flip(c, d & 4)
        copy = net.make(GP.at[:, lanes(2 * xx + cc)], GR.at[me], dev(z, xx, yy, cc))
        net.start(copy)
        got.append(copy)
    keep = local(GP.at[:, lanes(row)], GR.at[me])
    keep.start()
    tick(2)
    keep.wait()
    for copy in got:
        copy.wait_recv()
    total = GR[0]
    for d in range(1, NPLANE):
        total = total + GR[d]
    GZS[...] = total
    got = []
    for d in range(1, nz):
        copy = net.make(GZS, GZ.at[z], dev((z + d) % nz, x, y, c))
        net.start(copy)
        got.append(copy)
    keep = local(GZS, GZ.at[z])
    keep.start()
    tick(30)
    keep.wait()
    for copy in got:
        copy.wait_recv()
    total = GZ[0]
    for d in range(1, nz):
        total = total + GZ[d]
    gains[...] = total
    sent()
    sent_in()
    for copy in flushes:
        copy.wait()
    net.finish()


def spread_kernel(nz, ff_half, ff_cut, f0, f1, f2, fo, fq, out_in, gin_in, gains, *refs):
    out, gin, gn1, gwq, gwk, gwv, gwo, gn2, gwg, gwu, gwd = refs[:11]
    I0, I1, I2, IO, IQ, OG, OU, OD, OO, OQ, PO, PG, PF, sem, sem_out = refs[11:]
    moves = ((f0, I0), (f1, I1), (f2, I2), (fo, IO), (fq, IQ), (out_in, PO), (gin_in, PG))
    loads = [pltpu.make_async_copy(a, b, sem.at[i]) for i, (a, b) in enumerate(moves)]
    for i in (5, 6, 4, 3, 0, 1, 2):
        loads[i].start()
    stores = []

    def store(buf, dst):
        stores.append(pltpu.make_async_copy(buf, dst, sem_out.at[len(stores)]))
        stores[-1].start()

    gn1[...] = gains[0:1, :]
    gn2[...] = gains[1:2, :]
    x = lax.axis_index("row") // 2
    chips = (x, 1 - x)
    loads[5].wait()
    store(PO, out)
    loads[6].wait()
    PF[...] = PG[...].astype(F32)
    store(PF, gin)
    loads[4].wait()
    for i, dst in enumerate((gwq, gwk, gwv)):
        for u, xx in enumerate(chips):
            for q in range(nz):
                OQ[i, q * 64 : q * 64 + 64, pl.ds(pl.multiple_of(xx * 256, 256), 256)] = IQ[q, u, :, i * 256 : i * 256 + 256].astype(F32)
        store(OQ.at[i], dst)
    loads[3].wait()
    for u, xx in enumerate(chips):
        for q in range(nz):
            OO[pl.ds(pl.multiple_of(xx * 256, 256) + q * 64, 64), :] = IO[q, u].astype(F32)
    store(OO, gwo)

    def store_part(at, width):
        cols = pl.ds(at, width)
        store(OG.at[:, cols], gwg.at[:, cols])
        store(OU.at[:, cols], gwu.at[:, cols])
        store(OD.at[cols, :], gwd.at[cols, :])

    for n, I in enumerate((I0, I1)):
        loads[n].wait()
        for u, xx in enumerate(chips):
            at = pl.multiple_of(xx * ff_half + n * 256, 128)
            for q in range(nz):
                OG[q * 64 : q * 64 + 64, pl.ds(at, 256)] = I[q, u, :, 0:256].astype(F32)
                OU[q * 64 : q * 64 + 64, pl.ds(at, 256)] = I[q, u, :, 256:512].astype(F32)
                OD[pl.ds(at + q * 64, 64), :] = I[q, u, :, 512:768].astype(F32)
            store_part(at, 256)
    loads[2].wait()
    for u, at in enumerate((x * ff_half + ff_half - 256, ff_cut, (1 - x) * ff_half + ff_half - 256)):
        at = pl.multiple_of(at, 128) if u != 1 else at
        for q in range(nz):
            OG[q * 64 : q * 64 + 64, pl.ds(at, 128)] = I2[q, u, :, 0:128].astype(F32)
            OU[q * 64 : q * 64 + 64, pl.ds(at, 128)] = I2[q, u, :, 128:256].astype(F32)
            side = q // 2 * 128
            OD[pl.ds(at + q % 2 * 64, 64), side : side + 128] = I2[q, u, :, 256:384].astype(F32)
        store_part(at, 128)
    for copy in stores:
        copy.wait()


def fused(nz, tokens, cotangent, seg_ids, norm_one, wq, wk, wv, wo, norm_two, w_gate, w_up, w_down):
    ff = w_gate.shape[1]
    ff_half = -(-ff // 512) * 256
    ff_cut = ff - ff_half
    vm = pltpu.VMEM
    zshapes = [(2, 256, 768)] * 2 + [(3, 256, 384), (2, 256, 256), (2, 256, 768)]
    zscratch, fshapes = [], []
    for units, rows, cols in zshapes:
        fshapes.append((nz, units, rows // nz, cols))
        zscratch += [
            vm((2, units, rows, cols), BF),
            vm((units, rows, cols), BF),
            vm((2, nz - 1, units, rows // nz, cols), BF),
            vm((nz, rows // nz, cols) if len(fshapes) in LATE else (rows // nz, cols), BF),
            vm(fshapes[-1], BF),
        ]
    scratch = [
        vm((512, D), BF), vm((512, D), BF), vm((D, 768), BF), vm((D, D), BF),
        vm((D, ff_half), BF), vm((D, ff_half), BF), vm((ff_half, D), BF), vm((1, D), F32), vm((1, D), F32),
        vm((512, D), BF), vm((512, 256), BF), vm((768, 256), BF), vm((768, 256), BF), vm((2, 256, 512), F32),
        vm((8, 256, 512), F32), vm((512, D), BF),
        vm((2, 512, D), BF), vm((3, 3, 128, D), BF),
        vm((512, D), BF), vm((512, D), F32), vm((128, D), F32), vm((512, ff_half), BF), vm((512, ff_half), BF),
        vm((512, ff_half), BF), vm((512, D), BF), vm((512, 256), BF), vm((512, ff_half), F32), vm((512, ff_half), F32), vm((3, 512, 256), BF),
        vm((768, 256), F32), vm((768, 256), F32), vm((512, 768), BF), vm((256, 512), BF), vm((256, 512), BF),
        vm((128, D), BF), vm((128, D), BF), vm((8, D), F32), vm((8, 8, 256), F32), vm((nz, 8, 256), F32), vm((8, 256), F32),
        *zscratch,
        pltpu.SemaphoreType.DMA((10,)), pltpu.SemaphoreType.DMA((258,)), pltpu.SemaphoreType.DMA((28,)),
    ]
    hbm, vmem = pl.BlockSpec(memory_space=pl.ANY), pl.BlockSpec(memory_space=pltpu.VMEM)
    sds = jax.ShapeDtypeStruct
    done = pl.pallas_call(
        functools.partial(layer_kernel, nz, ff_half, ff_cut),
        out_shape=(sds((512, 256), BF), sds((512, 256), BF), sds((8, 256), F32), *(sds(f, BF) for f in fshapes)),
        in_specs=[hbm, hbm, vmem, vmem, hbm, hbm, hbm, hbm, vmem, hbm, hbm, hbm],
        out_specs=(hbm, hbm, vmem, *(hbm for f in fshapes)),
        scratch_shapes=scratch,
        compiler_params=pltpu.CompilerParams(collective_id=0, has_side_effects=True, vmem_limit_bytes=62 << 20),
        name="layer",
    )(
        tokens, cotangent, seg_ids, norm_one[None], wq, wk, wv, wo, norm_two[None], w_gate, w_up, w_down,
    )
    out, gin, gains, *sums = done
    grads = (
        sds((512, 256), BF), sds((512, 256), F32), sds((1, 256), F32),
        sds((256, 512), F32), sds((256, 512), F32), sds((256, 512), F32), sds((512, 256), F32),
        sds((1, 256), F32), sds((256, ff), F32), sds((256, ff), F32), sds((ff, 256), F32),
    )
    res = pl.pallas_call(
        functools.partial(spread_kernel, nz, ff_half, ff_cut),
        out_shape=grads,
        in_specs=[hbm] * 7 + [vmem],
        out_specs=tuple(vmem if i in (2, 7) else hbm for i in range(11)),
        scratch_shapes=[vm(f, BF) for f in fshapes]
        + [vm((256, ff), F32), vm((256, ff), F32), vm((ff, 256), F32), vm((512, 256), F32), vm((3, 256, 512), F32)]
        + [vm((512, 256), BF), vm((512, 256), BF), vm((512, 256), F32), pltpu.SemaphoreType.DMA((7,)), pltpu.SemaphoreType.DMA((27,))],
        compiler_params=pltpu.CompilerParams(vmem_limit_bytes=63 << 20),
        name="spread",
    )(*sums, out, gin, gains)
    res = list(res)
    res[2], res[7] = res[2][0], res[7][0]
    return tuple(res)


def solution(mesh):
    in_specs = (
        P(("dp", "col"), "row"),
        P(("dp", "col"), "row"),
        P("dp", None),
        P("row"),
        P("row", "col"),
        P("row", "col"),
        P("row", "col"),
        P("col", "row"),
        P("row"),
        P("row", "col"),
        P("row", "col"),
        P("col", "row"),
    )
    out_specs = (
        P(("dp", "col"), "row"),
        P(("dp", "col"), "row"),
        P("row"),
        P("row", "col"),
        P("row", "col"),
        P("row", "col"),
        P("col", "row"),
        P("row"),
        P("row", "col"),
        P("row", "col"),
        P("col", "row"),
    )
    sizes = dict(mesh.shape)
    body = per_device
    if sizes["row"] == 4 and sizes["col"] == 2:
        body = functools.partial(fused, sizes["dp"])
    return jax.shard_map(
        body, mesh=mesh, in_specs=in_specs, out_specs=out_specs, check_vma=False
    )
```

```python
import functools

import jax
import jax.numpy as jnp
from jax import lax
from jax.experimental import pallas as pl
from jax.experimental.pallas import tpu as pltpu
from jax.sharding import PartitionSpec as P

D = 1024
HEAD_DIM = 64


EPSILON = 1e-05
NEGATIVE = -1e30


def for_sending(array):

    def short(part):
        return part.astype(jnp.bfloat16) if part.dtype == jnp.float32 else part

    return jax.tree.map(short, array)


def shifted(block, axis, distance):
    devices = range(lax.axis_size(axis))
    route = [(i - distance, i) for i in devices if i - distance in devices]
    return lax.ppermute(block, axis, route)


def matmul(first_op, second_op):
    return jnp.dot(first_op, second_op, preferred_element_type=jnp.float32)


def matmul_tn(first_op, second_op):
    return lax.dot_general(
        first_op, second_op, (((0,), (0,)), ((), ())), preferred_element_type=jnp.float32
    )


def matmul_nt(first_op, second_op):
    return lax.dot_general(
        first_op, second_op, (((1,), (1,)), ((), ())), preferred_element_type=jnp.float32
    )


def tokens_col(array_in):
    return lax.all_gather(array_in, "col", axis=0, tiled=True)


def tokens_row(array_in):
    return lax.all_gather(for_sending(array_in), "row", axis=0, tiled=True).astype(array_in.dtype)


def summed_row(array_in):
    return lax.psum_scatter(
        array_in.astype(jnp.bfloat16), "row", scatter_dimension=0, tiled=True
    ).astype(jnp.float32)


def summed_col(array_in):
    return lax.psum_scatter(
        array_in.astype(jnp.bfloat16), "col", scatter_dimension=0, tiled=True
    ).astype(jnp.float32)


def feature_total(array_in):
    return lax.psum(array_in, "row")


def window_parts(queries, keys_all, ids_ext, offset, head_cols):
    t_local = queries.shape[0]
    block_rows = min(512, t_local)
    key_reach = min(2048, t_local)
    window = key_reach + block_rows
    head_count = head_cols // HEAD_DIM
    anchor = offset + t_local - key_reach
    q_blk = lax.dynamic_slice_in_dim(queries, offset, block_rows, 0).reshape(
        block_rows, head_count, HEAD_DIM
    )
    k_win = lax.dynamic_slice_in_dim(keys_all, anchor, window, 0)
    k_blk = k_win[:, :head_cols].reshape(window, head_count, HEAD_DIM)
    v_blk = k_win[:, head_cols:].reshape(window, head_count, HEAD_DIM)
    q_ids = lax.dynamic_slice_in_dim(ids_ext, offset + t_local, block_rows, 0)
    k_ids = lax.dynamic_slice_in_dim(ids_ext, anchor, window, 0)
    q_pos = offset + lax.iota(jnp.int32, block_rows)
    k_pos = offset - key_reach + lax.iota(jnp.int32, window)
    allowed = (q_ids[:, None] == k_ids[None, :]) & (k_pos[None, :] <= q_pos[:, None])
    scores = jnp.einsum(
        "qhd,khd->hqk", q_blk, k_blk, preferred_element_type=jnp.float32
    ) * HEAD_DIM ** (-0.5)
    scores = jnp.where(allowed[None], scores, NEGATIVE)
    return (q_blk, k_blk, v_blk, scores)


def forward(tokens, seg_ids, norm_one, wq, wk, wv, wo, norm_two, w_gate, w_up, w_down):
    token_vals = tokens.astype(jnp.float32)
    scale_one = lax.rsqrt(feature_total(jnp.sum(token_vals * token_vals, axis=1)) / D + EPSILON)
    normed = (token_vals * scale_one[:, None] * norm_one).astype(jnp.bfloat16)
    normed_all = tokens_col(normed)
    w_qkv = jnp.concatenate([wq, wk, wv], axis=1)
    head_cols = wq.shape[1]
    qkv = summed_row(matmul(normed_all, w_qkv)).astype(jnp.bfloat16)
    queries = qkv[:, :head_cols]
    kv_local = qkv[:, head_cols:]
    prior_keys = shifted(kv_local, "row", 1)
    keys_all = jnp.concatenate([prior_keys, kv_local], axis=0)
    t_local = queries.shape[0]
    block_rows = min(512, t_local)
    padded_ids = jnp.concatenate([jnp.full((t_local,), -1, jnp.int32), seg_ids[0]])
    ids_ext = lax.dynamic_slice_in_dim(padded_ids, lax.axis_index("row") * t_local, 2 * t_local, 0)

    def attend(offset):
        q_blk, k_blk, v_blk, scores = window_parts(queries, keys_all, ids_ext, offset, head_cols)
        row_max = jnp.max(scores, axis=2, keepdims=True)
        exp_total = jnp.sum(jnp.exp(scores - row_max), axis=2, keepdims=True)
        log_total = row_max + jnp.log(exp_total)
        prob_low = jnp.exp(scores - log_total).astype(jnp.bfloat16)
        mixed_out = jnp.einsum("hqk,khd->qhd", prob_low, v_blk, preferred_element_type=jnp.float32)
        return (mixed_out.reshape(block_rows, head_cols).astype(jnp.bfloat16), log_total[:, :, 0])

    offsets = lax.iota(jnp.int32, t_local // block_rows) * block_rows
    pieces, log_totals = lax.map(attend, offsets)
    attn_out = pieces.reshape(t_local, head_cols)
    attn_all = tokens_row(attn_out)
    residual = token_vals + summed_col(matmul(attn_all, wo))
    stored = {
        "token_vals": token_vals,
        "scale_one": scale_one,
        "normed_all": normed_all,
        "queries": queries,
        "keys_all": keys_all,
        "ids_ext": ids_ext,
        "log_totals": log_totals,
        "attn_all": attn_all,
        "offsets": offsets,
    }
    f_col = w_gate.shape[1]
    scale_two = lax.rsqrt(feature_total(jnp.sum(residual * residual, axis=1)) / D + EPSILON)
    hidden_in = (residual * scale_two[:, None] * norm_two).astype(jnp.bfloat16)
    hidden_all = tokens_col(hidden_in)
    w_pair = jnp.concatenate([w_gate, w_up], axis=1)
    pair_sum = summed_row(matmul(hidden_all, w_pair))
    gate_pre = pair_sum[:, :f_col]
    up_pre = pair_sum[:, f_col:]
    act_low = (jax.nn.silu(gate_pre) * up_pre).astype(jnp.bfloat16)
    act_all = tokens_row(act_low)
    final_sum = residual + summed_col(matmul(act_all, w_down))
    stored.update(
        {
            "residual": residual,
            "scale_two": scale_two,
            "hidden_all": hidden_all,
            "gate_pre": gate_pre,
            "up_pre": up_pre,
            "act_all": act_all,
        }
    )
    return (final_sum.astype(jnp.bfloat16), stored)


def swiglu_grads(dact, gate_pre, up_pre):
    sigmoid_gate = jax.nn.sigmoid(gate_pre)
    gate_grad = (dact * up_pre * sigmoid_gate * (1.0 + gate_pre * (1.0 - sigmoid_gate))).astype(
        jnp.bfloat16
    )
    up_grad = (dact * gate_pre * sigmoid_gate).astype(jnp.bfloat16)
    return (gate_grad, up_grad)


def per_device(
    tokens, cotangent, seg_ids, norm_one, wq, wk, wv, wo, norm_two, w_gate, w_up, w_down
):
    weights = (tokens, seg_ids, norm_one, wq, wk, wv, wo, norm_two, w_gate, w_up, w_down)
    output, stored = forward(*weights)
    f_col = w_gate.shape[1]
    grad_out = cotangent.astype(jnp.float32)
    grad_all = tokens_col(cotangent)
    dact = summed_row(matmul_nt(grad_all, w_down))
    grad_down = matmul_tn(stored["act_all"], grad_all)
    gate_grad, up_grad = swiglu_grads(dact, stored["gate_pre"], stored["up_pre"])
    dpair = jnp.concatenate([gate_grad, up_grad], axis=1)
    dpair_all = tokens_row(dpair)
    w_pair = jnp.concatenate([w_gate, w_up], axis=1)
    dhidden = summed_col(matmul_nt(dpair_all, w_pair))
    grad_pair = matmul_tn(stored["hidden_all"], dpair_all)
    grad_gate = grad_pair[:, :f_col]
    grad_up = grad_pair[:, f_col:]
    residual = stored["residual"]
    scale_two = stored["scale_two"]
    weighted = dhidden * norm_two
    inner_sum = feature_total(jnp.sum(weighted * residual, axis=1)) / D
    dresid = (
        grad_out + scale_two[:, None] * weighted - residual * (scale_two**3 * inner_sum)[:, None]
    )
    grad_norm_two = jnp.sum(dhidden * residual * scale_two[:, None], axis=0)
    dbranch = dresid.astype(jnp.bfloat16)
    dbranch_all = tokens_col(dbranch)
    attn_grad = summed_row(matmul_nt(dbranch_all, wo)).astype(jnp.bfloat16)
    grad_wo = matmul_tn(stored["attn_all"], dbranch_all)
    queries = stored["queries"]
    keys_all = stored["keys_all"]
    ids_ext = stored["ids_ext"]
    head_cols = wq.shape[1]
    head_count = head_cols // HEAD_DIM
    t_local = queries.shape[0]
    block_rows = min(512, t_local)
    key_reach = min(2048, t_local)
    window = key_reach + block_rows
    inv_root = HEAD_DIM ** (-0.5)

    def attend_back(accum_dkv, inputs):
        offset, log_total = inputs
        q_blk, k_blk, v_blk, scores = window_parts(queries, keys_all, ids_ext, offset, head_cols)
        prob_full = jnp.exp(scores - log_total[:, :, None])
        prob_low = prob_full.astype(jnp.bfloat16)
        d_blk = lax.dynamic_slice_in_dim(attn_grad, offset, block_rows, 0).reshape(
            block_rows, head_count, HEAD_DIM
        )
        dprobs = jnp.einsum("qhd,khd->hqk", d_blk, v_blk, preferred_element_type=jnp.float32)
        dvalue = jnp.einsum("hqk,qhd->khd", prob_low, d_blk, preferred_element_type=jnp.float32)
        center = jnp.sum(prob_full * dprobs, axis=2, keepdims=True)
        dscores = (prob_full * (dprobs - center)).astype(jnp.bfloat16)
        dquery = (
            jnp.einsum("hqk,khd->qhd", dscores, k_blk, preferred_element_type=jnp.float32)
            * inv_root
        )
        dkey = (
            jnp.einsum("hqk,qhd->khd", dscores, q_blk, preferred_element_type=jnp.float32)
            * inv_root
        )
        update = jnp.concatenate(
            [dkey.reshape(window, head_cols), dvalue.reshape(window, head_cols)], axis=1
        )
        anchor = offset + t_local - key_reach
        current = lax.dynamic_slice_in_dim(accum_dkv, anchor, window, 0)
        accum_dkv = lax.dynamic_update_slice_in_dim(accum_dkv, current + update, anchor, 0)
        return (accum_dkv, dquery.reshape(block_rows, head_cols))

    start_grads = jnp.zeros((2 * t_local, 2 * head_cols), jnp.float32)
    accum_dkv, query_grads = lax.scan(
        attend_back, start_grads, (stored["offsets"], stored["log_totals"])
    )
    returned = shifted(accum_dkv[:t_local].astype(jnp.bfloat16), "row", -1).astype(jnp.float32)
    key_grads = accum_dkv[t_local:] + returned
    dqkv = jnp.concatenate([query_grads.reshape(t_local, head_cols), key_grads], axis=1).astype(
        jnp.bfloat16
    )
    dqkv_all = tokens_row(dqkv)
    w_qkv = jnp.concatenate([wq, wk, wv], axis=1)
    dnormed = summed_col(matmul_nt(dqkv_all, w_qkv))
    grad_qkv = matmul_tn(stored["normed_all"], dqkv_all)
    grad_wq = grad_qkv[:, :head_cols]
    grad_wk = grad_qkv[:, head_cols : 2 * head_cols]
    grad_wv = grad_qkv[:, 2 * head_cols :]
    token_vals = stored["token_vals"]
    scale_one = stored["scale_one"]
    weighted_one = dnormed * norm_one
    inner_one = feature_total(jnp.sum(weighted_one * token_vals, axis=1)) / D
    grad_input = (
        dresid
        + scale_one[:, None] * weighted_one
        - token_vals * (scale_one**3 * inner_one)[:, None]
    )
    grad_norm_one = jnp.sum(dnormed * token_vals * scale_one[:, None], axis=0)
    grad_sums = (
        lax.psum(grad_wq.astype(jnp.bfloat16), "dp").astype(jnp.float32),
        lax.psum(grad_wk.astype(jnp.bfloat16), "dp").astype(jnp.float32),
        lax.psum(grad_wv.astype(jnp.bfloat16), "dp").astype(jnp.float32),
        lax.psum(grad_wo.astype(jnp.bfloat16), "dp").astype(jnp.float32),
        lax.psum(grad_gate.astype(jnp.bfloat16), "dp").astype(jnp.float32),
        lax.psum(grad_up.astype(jnp.bfloat16), "dp").astype(jnp.float32),
        lax.psum(grad_down.astype(jnp.bfloat16), "dp").astype(jnp.float32),
    )
    gain_sums = lax.psum((grad_norm_one, grad_norm_two), ("dp", "col"))
    return (
        output,
        grad_input,
        gain_sums[0],
        grad_sums[0],
        grad_sums[1],
        grad_sums[2],
        grad_sums[3],
        gain_sums[1],
        grad_sums[4],
        grad_sums[5],
        grad_sums[6],
    )


MESH = pl.DeviceIdType.MESH
BF = jnp.bfloat16
F32 = jnp.float32
NPLANE = 8
TAIL, HELD = (1, 2), (0, 3)
LATE = (1, 3, 4)
NEWFIRST, LAG = True, 10
FWAIT, OWAIT, QWAIT = (4, 6, 0), 0, 0


def contract(a, b, ca, cb):
    return lax.dot_general(a, b, (((ca,), (cb,)), ((), ())), preferred_element_type=F32)


class Copies:
    def __init__(self, send, recv):
        self.send, self.recv, self.used, self.kept, self.open = send, recv, 0, 1, []

    def take(self, amount=1):
        base = self.used
        self.used += amount
        return base

    def make(self, src, dst, to, site=None, own=False):
        site = self.take() if site is None else site
        self.kept += own
        return pltpu.make_async_remote_copy(
            src_ref=src,
            dst_ref=dst,
            send_sem=self.send.at[self.kept - 1 if own else 0],
            recv_sem=self.recv.at[site],
            device_id=to,
            device_id_type=MESH,
        )

    def start(self, copy, when=None):
        self.open.append((copy, when))
        if when is None:
            copy.start()
        else:
            pl.when(when)(copy.start)

    def finish(self):
        for copy, when in self.open:
            if when is None:
                copy.wait_send()
            else:
                pl.when(when)(copy.wait_send)
        self.open = []


def layer_kernel(nz, ff_half, ff_cut, *refs):
    it = iter(refs)
    take = lambda n: [next(it) for _ in range(n)]
    tok, cot, seg, n1, wq, wk, wv, wo, n2, wg, wu, wd = take(12)
    out, gin, gains, f0, f1, f2, fo, fq = take(8)
    X, G, WQKV, WO, WG, WU, WD, NG1, NG2 = take(9)
    XN, Q, K, V, BIAS, PM, AF = take(7)
    PART, RX = take(2)
    HN, RES, DRES, ACT, DGA, DUP, DB, DAT, BYG, BYU, T3 = take(11)
    DK, DV, DQKV, HS, HR = take(5)
    OS, GS, GP, GR, GZ, GZS = take(6)
    zbufs = [take(5) for _ in range(5)]
    send, recv, loc = take(3)

    z, row, y = lax.axis_index("dp"), lax.axis_index("row"), lax.axis_index("col")
    x, c = row // 2, row % 2
    net = Copies(send, recv)
    nloc = [0]

    def local(src, dst):
        nloc[0] += 1
        return pltpu.make_async_copy(src, dst, loc.at[nloc[0] - 1])

    def dev(zz, xx, yy, cc):
        return (zz, 2 * xx + cc, yy)

    core_nb, x_nb, y_nb = dev(z, x, y, 1 - c), dev(z, 1 - x, y, c), dev(z, x, 1 - y, c)
    z_up, z_dn = dev(z + 1, x, y, c), dev(z - 1, x, y, c)
    lanes = lambda i, n=256: pl.ds(pl.multiple_of(i * n, 128), n)
    rows = lambda i, n: pl.ds(pl.multiple_of(i * n, n if n % 16 else 16), n)
    flip = lambda v, bit: 1 - v if bit else v

    barrier = pltpu.get_barrier_semaphore()
    for d in range(1, NPLANE):
        pl.semaphore_signal(
            barrier, inc=1, device_id=dev(z, flip(x, d & 1), flip(y, d & 2), flip(c, d & 4)), device_id_type=MESH
        )
    for d in range(1, nz):
        pl.semaphore_signal(barrier, inc=1, device_id=dev((z + d) % nz, x, y, c), device_id_type=MESH)
    for _, _, ZR, _, _ in zbufs:

        @pl.when(z == 0)
        def _(ZR=ZR):
            ZR[0, nz - 2] = jnp.zeros(ZR.shape[2:], BF)

        @pl.when(z == nz - 1)
        def _(ZR=ZR):
            ZR[1, nz - 2] = jnp.zeros(ZR.shape[2:], BF)

    seg_f = seg[...].astype(F32)
    own = jnp.where(c == 0, seg_f[:, :512], seg_f[:, 512:])
    before = jnp.where(c == 0, jnp.full((1, 256), -1.0, F32), seg_f[:, 256:512])
    ids = jnp.concatenate([before, own], axis=1)
    for b in range(2):
        k_id = jnp.broadcast_to(ids[:, b * 256 : b * 256 + 512], (256, 512))
        q_id = jnp.broadcast_to(ids[:, 256 + b * 256 : 512 + b * 256], (512, 256)).T
        q_pos = lax.broadcasted_iota(jnp.int32, (256, 512), 0) + 256
        k_pos = lax.broadcasted_iota(jnp.int32, (256, 512), 1)
        BIAS[b] = jnp.where((q_id == k_id) & (k_pos <= q_pos), 0.0, NEGATIVE)

    @pl.when(c == 0)
    def _():
        K[0:256, :] = jnp.zeros((256, 256), BF)
        V[0:256, :] = jnp.zeros((256, 256), BF)

    pl.semaphore_wait(barrier, NPLANE - 1 + nz - 1)

    def gather_tokens(src, buf):
        col = lambda rr: buf.at[:, lanes(rr)]
        mine = c == y
        other = jnp.logical_not(mine)
        keep = local(src, col(row))
        over = net.make(src, col(row), core_nb)
        bx, by = net.take(2), net.take(2)
        to_x = net.make(src, col(row), dev(z, 1 - x, y, y), bx + c)
        to_y = net.make(src, col(row), dev(z, x, 1 - y, y), by + c)
        far = 2 * (1 - x)
        by_y = net.make(col(far), col(far), y_nb)
        by_x = net.make(col(2 * x + 1), col(2 * x + 1), x_nb)
        got_x = [net.make(src, col(row), core_nb, bx + k) for k in range(2)]
        got_y = [net.make(src, col(row), core_nb, by + k) for k in range(2)]

        def start():
            pl.when(mine)(keep.start)
            net.start(to_x)
            net.start(to_y)
            net.start(over, other)

        def arrive():
            @pl.when(mine)
            def _():
                got_x[0].wait_recv()
                by_y.start()

            @pl.when(other)
            def _():
                got_y[1].wait_recv()
                by_x.start()

            net.open += [(by_y, mine), (by_x, other)]

        def rest():
            @pl.when(mine)
            def _():
                got_x[1].wait_recv()
                over.wait_recv()
                keep.wait()

            @pl.when(other)
            def _():
                got_y[0].wait_recv()
                by_y.wait_recv()
                by_x.wait_recv()

        return start, arrive, rest

    def relay(src_of, dst_of):
        keep = local(src_of(x), dst_of(row))
        across = net.make(src_of(x), dst_of(row), core_nb)
        far = net.make(src_of(1 - x), dst_of(row), x_nb)
        theirs = dst_of(2 * (1 - x) + c)
        fwd = net.make(theirs, theirs, core_nb)

        def start():
            keep.start()
            net.start(far)
            net.start(across)

        def arrive():
            far.wait_recv()
            net.start(fwd)

        def rest():
            keep.wait()
            across.wait_recv()
            fwd.wait_recv()

        return start, arrive, rest

    def z_gather(at):
        sites = (net.take(nz - 1), net.take(nz - 1))

        def step(s):
            for way, to in ((0, z_up), (1, z_dn)):
                zz = z if way == 0 else nz - 1 - z
                ref = at(z - s if way == 0 else z + s)
                have = zz >= s
                if s > 0:
                    pl.when(have)(net.make(ref, ref, to, sites[way] + s - 1).wait_recv)
                if s < nz - 1:
                    net.start(net.make(ref, ref, to, sites[way] + s), have & (zz < nz - 1))

        return step

    def relay_z(pairs, whole, n_rows):
        n = n_rows // nz
        keep = [local(a, b) for a, b in pairs(x, row, 0, n_rows)]
        across = [net.make(a, b, core_nb) for a, b in pairs(x, row, 0, n_rows)]
        far = [net.make(a, b, x_nb) for a, b in pairs(1 - x, row, z * n, n)]
        hop = z_gather(lambda q: whole(2 * (1 - x) + c, q * n, n))
        theirs = whole(2 * (1 - x) + c, 0, n_rows)
        fwd = net.make(theirs, theirs, core_nb)

        def begin():
            for copy in far:
                net.start(copy)
            for copy in keep:
                copy.start()
            for copy in across:
                net.start(copy)

        def step(s):
            if s == 0:
                for copy in far:
                    copy.wait_recv()
            hop(s)
            if s == nz - 1:
                net.start(fwd)

        def rest():
            for copy in keep:
                copy.wait()
            for copy in across:
                copy.wait_recv()
            fwd.wait_recv()

        return begin, step, rest

    def gather_wo():
        at = lambda yy, rr: WO.at[rows(yy, 512), lanes(rr)]
        keep = local(wo, at(y, row))
        across = net.make(wo, at(y, row), core_nb)
        to_x, to_y = net.make(wo, at(y, row), x_nb), net.make(wo, at(y, row), y_nb)
        rx = 2 * (1 - x) + c
        on_y = net.make(at(y, rx), at(y, rx), y_nb)
        others = (at(y, rx), at(1 - y, row), at(1 - y, rx))
        fwd = [net.make(ref, ref, core_nb) for ref in others]

        def start():
            net.start(to_x)
            net.start(to_y)
            keep.start()
            net.start(across)

        def arrive():
            to_x.wait_recv()
            net.start(on_y)
            net.start(fwd[0])

        def pass_on():
            to_y.wait_recv()
            net.start(fwd[1])
            on_y.wait_recv()
            net.start(fwd[2])

        def rest():
            keep.wait()
            across.wait_recv()
            for copy in fwd:
                copy.wait_recv()

        return start, arrive, pass_on, rest

    def gather_gain(src, dst):
        keep = local(src, dst.at[:, lanes(row)])
        keep.start()
        got = []
        for to in (core_nb, x_nb, dev(z, 1 - x, y, 1 - c)):
            got.append(net.make(src, dst.at[:, lanes(row)], to))
            net.start(got[-1])

        def rest():
            keep.wait()
            for g in got:
                g.wait_recv()

        return rest

    gx, gg = gather_tokens(tok, X), gather_tokens(cot, G)
    some = lambda r0, n: pl.ds(pl.multiple_of(r0, 16), n)
    rqkv = []
    for i, w in ((1, wk), (2, wv), (0, wq)):
        at = lambda rr, r0, n, i=i: WQKV.at[some(rr * 256 + r0, n), pl.ds(i * 256, 256)]
        rqkv.append(relay_z(lambda xx, rr, r0, n, w=w, at=at: [(w.at[some(r0, n), lanes(xx)], at(rr, r0, n))], at, 256))
    ro = gather_wo()
    both = ff_half - ff_cut
    rff = []
    for w, W in ((wg, WG), (wu, WU)):
        at = lambda rr, r0, n, W=W: W.at[some(rr * 256 + r0, n), :]

        def pairs(xx, rr, r0, n, w=w, W=W):
            out = []
            for src, dst, width in ((pl.multiple_of(xx * ff_half, 128), 0, ff_cut), (ff_cut, ff_cut, both)):
                out.append((w.at[some(r0, n), pl.ds(src, width)], W.at[some(rr * 256 + r0, n), pl.ds(dst, width)]))
            return out

        rff.append(relay_z(pairs, at, 256))

    def pairs_down(xx, rr, r0, n):
        if n == ff_half:
            parts = ((xx * ff_half, 0, ff_cut), (ff_cut, ff_cut, both))
        else:
            tail = jnp.where(z == nz - 1, ff_cut, xx * ff_half + r0 + n - both)
            parts = ((xx * ff_half + r0, r0, n - both), (tail, r0 + n - both, both))
        return [(wd.at[some(src, k), :], WD.at[some(dst, k), lanes(rr)]) for src, dst, k in parts]

    rd = relay_z(pairs_down, lambda rr, r0, n: WD.at[some(r0, n), lanes(rr)], ff_half)
    for r in rqkv:
        r[0]()
    gx[0]()
    ga = [gather_gain(n1, NG1), gather_gain(n2, NG2)]
    for r in rqkv:
        r[1](0)
    for r in rqkv:
        r[1](1)
    gx[1]()
    for s in range(2, nz):
        for r in rqkv:
            r[1](s)
    for g in ga:
        g()
    for r in (*rff, rd):
        r[0]()
    gx[2]()
    ro[0]()
    for t in range(4):
        v = X[t * 128 : t * 128 + 128, :].astype(F32)
        scale = lax.rsqrt(jnp.mean(v * v, axis=1, keepdims=True) + EPSILON)
        XN[t * 128 : t * 128 + 128, :] = (v * scale * NG1[...]).astype(BF)
    for r in rqkv:
        r[2]()
    K[256:768, :] = contract(XN[...], WQKV[:, 256:512], 1, 0).astype(BF)
    V[256:768, :] = contract(XN[...], WQKV[:, 512:768], 1, 0).astype(BF)
    hk = net.make(K.at[pl.ds(512, 256), :], K.at[pl.ds(0, 256), :], core_nb)
    hv = net.make(V.at[pl.ds(512, 256), :], V.at[pl.ds(0, 256), :], core_nb)
    net.start(hk, c == 0)
    net.start(hv, c == 0)
    Q[...] = (contract(XN[...], WQKV[:, 0:256], 1, 0).astype(BF) * 0.125).astype(BF)
    @pl.when(c == 1)
    def _():
        hk.wait_recv()
        hv.wait_recv()

    lane_id = lax.broadcasted_iota(jnp.int32, (1, 128), 1)
    head_mask = [jnp.where(lane_id < 64, 1.0, 0.0).astype(BF), jnp.where(lane_id < 64, 0.0, 1.0).astype(BF)]

    heads_at = lambda xx, yy, b: AF.at[pl.ds(b * 256, 256), lanes(2 * yy + xx)]
    a_x = [net.make(heads_at(x, y, b), heads_at(x, y, b), x_nb) for b in range(2)]
    a_y = [net.make(heads_at(x, y, b), heads_at(x, y, b), y_nb) for b in range(2)]
    a_far = (
        net.make(heads_at(1 - x, y, 0), heads_at(1 - x, y, 0), y_nb),
        net.make(heads_at(x, 1 - y, 1), heads_at(x, 1 - y, 1), x_nb),
    )
    base = (2 * y + x) * 256
    for b in range(2):
        for hp in range(2):
            cols = slice(hp * 128, hp * 128 + 128)
            q_b, k_b, v_b = Q[b * 256 : b * 256 + 256, cols], K[b * 256 : b * 256 + 512, cols], V[b * 256 : b * 256 + 512, cols]
            total = None
            for h in range(2):
                s = contract(q_b * head_mask[h], k_b, 1, 1) + BIAS[b]
                e = jnp.exp(s - jnp.max(s, axis=1, keepdims=True))
                p = e * (1.0 / jnp.sum(e, axis=1, keepdims=True))
                PM[b * 4 + hp * 2 + h] = p
                part = contract(p.astype(BF), v_b * head_mask[h], 1, 0)
                total = part if total is None else total + part
            AF[b * 256 : b * 256 + 256, pl.ds(pl.multiple_of(base + hp * 128, 128), 128)] = total.astype(BF)
        net.start(a_x[b])
        net.start(a_y[b])
        if b == 0:
            for r in rff:
                r[1](0)
    for r in rff:
        r[1](1)
    rd[1](0)
    ro[1]()
    a_x[0].wait_recv()
    net.start(a_far[0])
    a_y[1].wait_recv()
    net.start(a_far[1])
    gg[0]()
    for r in rff:
        r[1](2)
    rd[1](1)
    ro[2]()
    for r in rff:
        r[1](3)
    rd[1](2)

    j = 2 * x + y
    shard = lambda buf, jj: buf.at[rows(jj, 128), :]

    peers = ((x_nb, 2 * (1 - x) + y), (y_nb, 2 * x + 1 - y), (dev(z, 1 - x, 1 - y, c), 2 * (1 - x) + 1 - y))

    def reduce_start(k, p):
        sent = [net.make(shard(PART.at[p], jj), RX.at[k, i], to, own=True) for i, (to, jj) in enumerate(peers)]
        for copy in (sent[2], sent[0], sent[1]):
            copy.start()

        def end():
            for copy in sent:
                copy.wait_recv()
            for copy in sent:
                copy.wait_send()
            total = PART[p, rows(j, 128), :].astype(F32)
            for i in range(3):
                total = total + RX[k, i].astype(F32)
            return total

        return end

    def gather_start(buf):
        sent = [net.make(shard(buf, j), shard(buf, j), to) for to, _ in peers]
        for copy in (sent[2], sent[0], sent[1]):
            net.start(copy)

        def end():
            for copy in sent:
                copy.wait_recv()

        return end

    def send_blocks(src, dst):
        base_r = net.take(4)
        waits = []
        for dx in range(2):
            for cc in range(2):
                xx = flip(x, dx)
                piece, place = src.at[:, lanes(2 * xx + cc)], dst.at[rows(j, 128), :]
                copy = pltpu.make_async_remote_copy(
                    src_ref=piece,
                    dst_ref=place,
                    send_sem=net.send.at[0],
                    recv_sem=net.recv.at[base_r + dx * 2 + y],
                    device_id=dev(z, xx, c, cc),
                    device_id_type=MESH,
                )
                if dx == 0:
                    here = (c == y) & (c == cc)
                    keep = local(piece, place)
                    pl.when(here)(keep.start)
                    net.start(copy, jnp.logical_not(here))
                    waits.append((keep, here))
                else:
                    net.start(copy)
        piece, place = src.at[:, pl.ds(0, 256)], dst.at[pl.ds(0, 128), :]
        arrivals = [
            (net.make(piece, place, core_nb, base_r + dx * 2 + yy), jnp.logical_not((c == y) & (y == yy)) if dx == 0 else None)
            for dx in range(2)
            for yy in range(2)
        ]

        def end():
            for keep, here in waits:
                pl.when(here)(keep.wait)
            for got, when in arrivals:
                if when is None:
                    got.wait_recv()
                else:
                    pl.when(when)(got.wait_recv)

        return end

    def along_z(tag, dst):
        GB, CR, ZR, RL, FF = zbufs[tag]
        n_rows = CR.shape[1] // nz
        n = n_rows // 2
        last = CR.shape[0] - 1
        part = lambda q, i: pl.ds(pl.multiple_of(q * n_rows + i * n, 16), n)
        own = lambda i: pl.ds(i * n, n)
        over = net.make(GB.at[1 - c], CR, core_nb)
        net.start(over)
        yield
        over.wait_recv()
        for u in range(CR.shape[0]):
            CR[u] = (CR[u].astype(F32) + GB[c, u].astype(F32)).astype(BF)
        sites = [[net.take(nz - 1) for _ in range(2)] for _ in range(2)]
        for s in range(1, nz):
            for i in range(2):
                for way, to in ((0, z_up), (1, z_dn)):
                    zz = z if way == 0 else nz - 1 - z
                    q = nz - s + zz
                    q = q if way == 0 else nz - 1 - q
                    go = (zz < nz - 1) & (zz <= s - 1)
                    first, later = go & (zz == 0), go & (zz > 0)
                    site = sites[way][i] + s - 1
                    there = ZR.at[way, s - 1, :, own(i), :]
                    net.start(net.make(CR.at[:, part(q, i), :], there, to, site), first)
                    if s >= 2:
                        acc = ZR.at[way, s - 2, :, own(i), :]
                        got = net.make(acc, acc, to, site - 1)

                        @pl.when(later)
                        def _(got=got, acc=acc, q=q, i=i):
                            got.wait_recv()
                            acc[...] = (acc[...].astype(F32) + CR[:, part(q, i), :].astype(F32)).astype(BF)

                        net.start(net.make(acc, there, to, site), later)
                yield
        late = len(RL.shape) == 3
        backs = [[net.take(nz - 1) for _ in range(2)] for _ in range(2)]
        here = lambda q, i: FF.at[q, :, own(i), :]
        side = []

        def send_back(i):
            net.start(net.make(here(z, i), here(z, i), z_up, backs[0][i]), z < nz - 1)
            net.start(net.make(here(z, i), here(z, i), z_dn, backs[1][i]), z > 0)

        for i in range(2):
            for way in range(2):
                zz = z if way == 0 else nz - 1 - z
                acc = ZR.at[way, nz - 2, :, own(i), :]
                pl.when(zz > 0)(net.make(acc, acc, z_up, sites[way][i] + nz - 2).wait_recv)
            total = (
                CR[:, part(z, i), :].astype(F32)
                + ZR[0, nz - 2, :, own(i), :].astype(F32)
                + ZR[1, nz - 2, :, own(i), :].astype(F32)
            ).astype(BF)
            if late:
                FF[z, :, own(i), :] = total
                send_back(i)
            else:
                RL[own(i), :] = total[-1]
                side.append(net.make(RL.at[own(i), :], FF.at[z, last, own(i), :], x_nb))
                net.start(side[i])
                FF[z, 0:last, own(i), :] = total[:-1]
            yield
        if not late:
            for i in range(2):
                side[i].wait_recv()
                send_back(i)
                if tag == 4 and i == 1:
                    gates.append(tag)
                yield
        sites = backs
        for s in range(2, nz + 1):
            for i in range(2):
                for way, to in ((0, z_up), (1, z_dn)):
                    zz = z if way == 0 else nz - 1 - z
                    q = z - (s - 1) if way == 0 else z + (s - 1)
                    have = zz >= s - 1
                    ref = here(q, i)
                    pl.when(have)(net.make(ref, ref, to, sites[way][i] + s - 2).wait_recv)
                    if s < nz:
                        net.start(net.make(ref, ref, to, sites[way][i] + s - 1), have & (zz < nz - 1))
                yield
        if late:
            trade = net.make(FF.at[:, last], RL, x_nb)
            while tag in HELD and not gates:
                yield
            net.start(trade)
            for _ in range(LAG):
                yield
            trade.wait_recv()
            flush(FF.at[:, 0:last], dst.at[:, 0:last])
            flush(RL, dst.at[:, last])
        else:
            flush(FF, dst)
        yield

    def flush(buf, dst):
        copy = local(buf, dst)
        copy.start()
        flushes.append(copy)

    flushes, gates = [], []

    lines = []

    def begin(i, dst, wait):
        line = along_z(i, dst)
        next(line)
        lines.append([line, wait])

    def tick(n=1):
        for _ in range(n):
            for _ in range(2):
                for line in (lines[::-1] if NEWFIRST else lines):
                    if line[1] > 0:
                        line[1] -= 1
                    else:
                        next(line[0], None)

    ro[3]()
    for copy in (a_x[1], a_y[0], *a_far):
        copy.wait_recv()
    for t in range(4):
        tile = slice(t * 128, t * 128 + 128)
        res = X[tile, :].astype(F32) + contract(AF[tile, :], WO[...], 1, 0)
        RES[tile, :] = res
        scale = lax.rsqrt(jnp.mean(res * res, axis=1, keepdims=True) + EPSILON)
        HN[tile, :] = (res * scale * NG2[...]).astype(BF)
    gg[1]()
    for r in rff:
        r[2]()
    rd[1](3)
    unit = lambda r: jnp.where(x == r // 2, 0, 1)
    shared = (lax.broadcasted_iota(jnp.int32, (1, 256), 1) >= 256 - both) & (x == 1)

    def tile_grads(n):
        cols = slice(n * 256, n * 256 + 256)
        GB = zbufs[n][0]
        for i, made in enumerate((DGA, DUP)):
            whole = contract(HN[...], made[:, cols], 0, 0)
            for r in range(4):
                GB[r % 2, unit(r), :, i * 256 : i * 256 + 256] = whole[r * 256 : r * 256 + 256].astype(BF)
        whole = contract(ACT[:, cols], G[...], 0, 0)
        for r in range(4):
            GB[r % 2, unit(r), :, 512:768] = whole[:, r * 256 : r * 256 + 256].astype(BF)

    def last_tile_grads(n):
        GB = zbufs[n][0]

        def put(r, cols, a, b):
            GB[r % 2, jnp.where(x == r // 2, 0, 2), :, cols] = a.astype(BF)

            @pl.when(x == r // 2)
            def _():
                GB[r % 2, 1, :, cols] = b.astype(BF)

        for i in range(2):
            whole = contract(HN[...], T3[i], 0, 0)
            for r in range(4):
                rws = whole[r * 256 : r * 256 + 256]
                put(r, slice(i * 128, i * 128 + 128), rws[:, :128], rws[:, 128:])
        whole = contract(T3[2], G[...], 0, 0)
        for r in range(4):
            left, right = whole[:, r * 256 : r * 256 + 128], whole[:, r * 256 + 128 : r * 256 + 256]
            put(
                r,
                slice(256, 384),
                jnp.concatenate([left[:128], right[:128]], axis=0),
                jnp.concatenate([left[128:], right[128:]], axis=0),
            )

    tiles = ff_half // 256
    for n in range(tiles):
        cols = slice(n * 256, n * 256 + 256)
        gate = contract(HN[...], WG[:, cols], 1, 0)
        up = contract(HN[...], WU[:, cols], 1, 0)
        sig = jax.nn.sigmoid(gate)
        silu = gate * sig
        act = (silu * up).astype(BF)
        if n == tiles - 1:
            T3[2] = act
            act = jnp.where(shared, jnp.zeros_like(act), act)
        ACT[:, cols] = act
        BYG[:, cols] = up * sig * (1.0 + gate * (1.0 - sig))
        BYU[:, cols] = silu
    gg[2]()
    rd[2]()
    for n in (tiles - 1, *range(tiles - 1)):
        cols = slice(n * 256, n * 256 + 256)
        dact = contract(G[...], WD[cols, :], 1, 1)
        dgate, dup = (dact * BYG[:, cols]).astype(BF), (dact * BYU[:, cols]).astype(BF)
        if n == tiles - 1:
            T3[0], T3[1] = dgate, dup
            dgate, dup = (jnp.where(shared, jnp.zeros_like(v), v) for v in (dgate, dup))
        DGA[:, cols] = dgate
        DUP[:, cols] = dup
        (last_tile_grads if n == tiles - 1 else tile_grads)(n)
        begin(n, (f0, f1, f2)[n], FWAIT[n])
        if n == 0:
            tick()
    blocks = lambda i, f: [zbufs[i][0].__setitem__((r % 2, unit(r)), f(slice(r * 256, r * 256 + 256)).astype(BF)) for r in range(4)]
    tick()
    for n in range(4):
        cols = slice(n * 256, n * 256 + 256)
        PART[0, :, cols] = (contract(DGA[...], WG[cols, :], 1, 1) + contract(DUP[...], WU[cols, :], 1, 1)).astype(BF)
    hid = reduce_start(0, 0)
    tick()
    for n in range(4):
        cols = slice(n * 256, n * 256 + 256)
        PART[1, :, cols] = contract(ACT[...], WD[:, cols], 1, 0).astype(BF)
    tick()
    dh = hid()
    res = RES[rows(j, 128), :]
    scale = lax.rsqrt(jnp.mean(res * res, axis=1, keepdims=True) + EPSILON)
    w = dh * NG2[...]
    inner = jnp.mean(w * res, axis=1, keepdims=True)
    dres = G[rows(j, 128), :].astype(F32) + scale * w - res * (scale * scale * scale * inner)
    DRES[...] = dres
    GP[...] = jnp.zeros_like(GP)
    GP[1:2, :] = jnp.sum(dh * res * scale, axis=0, keepdims=True)
    DB[rows(j, 128), :] = dres.astype(BF)
    dbg = gather_start(DB)
    tick()
    tick()
    dbg()
    fin = reduce_start(1, 1)

    DAT[...] = contract(DB[...], WO[pl.ds(pl.multiple_of(base, 256), 256), :], 1, 1).astype(BF)
    own_heads = AF[:, pl.ds(pl.multiple_of(base, 256), 256)]
    blocks(3, lambda cols: contract(own_heads, DB[:, cols], 0, 0))
    begin(3, fo, OWAIT)
    DK[...] = jnp.zeros_like(DK)
    DV[...] = jnp.zeros_like(DV)

    def attend_back(b):
        qs, ks = pl.ds(b * 256, 256), pl.ds(b * 256, 512)
        for hp in range(2):
            cols = slice(hp * 128, hp * 128 + 128)
            q_b, k_b, v_b, d_b = Q[qs, cols], K[ks, cols], V[ks, cols], DAT[qs, cols]
            dq = dk = dv = None
            for h in range(2):
                m = head_mask[h]
                d_h = d_b * m
                p = PM[b * 4 + hp * 2 + h]
                dp = contract(d_h, v_b, 1, 1)
                ds = (p * (dp - jnp.sum(p * dp, axis=1, keepdims=True))).astype(BF)
                one = (contract(ds, k_b * m, 1, 0), contract(ds, q_b * m, 0, 0), contract(p.astype(BF), d_h, 0, 0))
                dq, dk, dv = one if dq is None else (dq + one[0], dk + one[1], dv + one[2])
            DQKV[qs, cols] = (dq * 0.125).astype(BF)
            DK[ks, cols] += dk
            DV[ks, cols] += dv

    attend_back(0)
    tick()
    attend_back(1)
    HS[:, 0:256] = DK[0:256, :].astype(BF)
    HS[:, 256:512] = DV[0:256, :].astype(BF)
    back = net.make(HS, HR, core_nb)
    net.start(back, c == 1)

    @pl.when(c == 0)
    def _():
        back.wait_recv()
        DK[512:768, :] += HR[:, 0:256].astype(F32)
        DV[512:768, :] += HR[:, 256:512].astype(F32)

    DQKV[:, 256:512] = DK[256:768, :].astype(BF)
    DQKV[:, 512:768] = DV[256:768, :].astype(BF)
    blocks(4, lambda cols: contract(XN[:, cols], DQKV[...], 0, 0))
    begin(4, fq, QWAIT)
    for n in range(4):
        cols = slice(n * 256, n * 256 + 256)
        PART[0, :, cols] = contract(DQKV[...], WQKV[cols, :], 1, 1).astype(BF)
    tick()
    OS[...] = (RES[rows(j, 128), :] + fin()).astype(BF)
    sent = send_blocks(OS, out)
    tick(TAIL[0])
    last = reduce_start(2, 0)
    tick(TAIL[1])
    dx = last()
    v = X[rows(j, 128), :].astype(F32)
    scale = lax.rsqrt(jnp.mean(v * v, axis=1, keepdims=True) + EPSILON)
    w = dx * NG1[...]
    inner = jnp.mean(w * v, axis=1, keepdims=True)
    GS[...] = (DRES[...] + scale * w - v * (scale * scale * scale * inner)).astype(BF)
    GP[0:1, :] = jnp.sum(dx * v * scale, axis=0, keepdims=True)
    sent_in = send_blocks(GS, gin)

    me = 4 * x + 2 * y + c
    got = []
    for d in range(1, NPLANE):
        xx, yy, cc = flip(x, d & 1), flip(y, d & 2), flip(c, d & 4)
        copy = net.make(GP.at[:, lanes(2 * xx + cc)], GR.at[me], dev(z, xx, yy, cc))
        net.start(copy)
        got.append(copy)
    keep = local(GP.at[:, lanes(row)], GR.at[me])
    keep.start()
    tick(2)
    keep.wait()
    for copy in got:
        copy.wait_recv()
    total = GR[0]
    for d in range(1, NPLANE):
        total = total + GR[d]
    GZS[...] = total
    got = []
    for d in range(1, nz):
        copy = net.make(GZS, GZ.at[z], dev((z + d) % nz, x, y, c))
        net.start(copy)
        got.append(copy)
    keep = local(GZS, GZ.at[z])
    keep.start()
    tick(30)
    keep.wait()
    for copy in got:
        copy.wait_recv()
    total = GZ[0]
    for d in range(1, nz):
        total = total + GZ[d]
    gains[...] = total
    sent()
    sent_in()
    for copy in flushes:
        copy.wait()
    net.finish()


def spread_kernel(nz, ff_half, ff_cut, f0, f1, f2, fo, fq, out_in, gin_in, gains, *refs):
    out, gin, gn1, gwq, gwk, gwv, gwo, gn2, gwg, gwu, gwd = refs[:11]
    I0, I1, I2, IO, IQ, OG, OU, OD, OO, OQ, PO, PG, PF, sem, sem_out = refs[11:]
    moves = ((f0, I0), (f1, I1), (f2, I2), (fo, IO), (fq, IQ), (out_in, PO), (gin_in, PG))
    loads = [pltpu.make_async_copy(a, b, sem.at[i]) for i, (a, b) in enumerate(moves)]
    for i in (5, 6, 4, 3, 0, 1, 2):
        loads[i].start()
    stores = []

    def store(buf, dst):
        stores.append(pltpu.make_async_copy(buf, dst, sem_out.at[len(stores)]))
        stores[-1].start()

    gn1[...] = gains[0:1, :]
    gn2[...] = gains[1:2, :]
    x = lax.axis_index("row") // 2
    chips = (x, 1 - x)
    loads[5].wait()
    store(PO, out)
    loads[6].wait()
    PF[...] = PG[...].astype(F32)
    store(PF, gin)
    loads[4].wait()
    for i, dst in enumerate((gwq, gwk, gwv)):
        for u, xx in enumerate(chips):
            for q in range(nz):
                OQ[i, q * 64 : q * 64 + 64, pl.ds(pl.multiple_of(xx * 256, 256), 256)] = IQ[q, u, :, i * 256 : i * 256 + 256].astype(F32)
        store(OQ.at[i], dst)
    loads[3].wait()
    for u, xx in enumerate(chips):
        for q in range(nz):
            OO[pl.ds(pl.multiple_of(xx * 256, 256) + q * 64, 64), :] = IO[q, u].astype(F32)
    store(OO, gwo)

    def store_part(at, width):
        cols = pl.ds(at, width)
        store(OG.at[:, cols], gwg.at[:, cols])
        store(OU.at[:, cols], gwu.at[:, cols])
        store(OD.at[cols, :], gwd.at[cols, :])

    for n, I in enumerate((I0, I1)):
        loads[n].wait()
        for u, xx in enumerate(chips):
            at = pl.multiple_of(xx * ff_half + n * 256, 128)
            for q in range(nz):
                OG[q * 64 : q * 64 + 64, pl.ds(at, 256)] = I[q, u, :, 0:256].astype(F32)
                OU[q * 64 : q * 64 + 64, pl.ds(at, 256)] = I[q, u, :, 256:512].astype(F32)
                OD[pl.ds(at + q * 64, 64), :] = I[q, u, :, 512:768].astype(F32)
            store_part(at, 256)
    loads[2].wait()
    for u, at in enumerate((x * ff_half + ff_half - 256, ff_cut, (1 - x) * ff_half + ff_half - 256)):
        at = pl.multiple_of(at, 128) if u != 1 else at
        for q in range(nz):
            OG[q * 64 : q * 64 + 64, pl.ds(at, 128)] = I2[q, u, :, 0:128].astype(F32)
            OU[q * 64 : q * 64 + 64, pl.ds(at, 128)] = I2[q, u, :, 128:256].astype(F32)
            side = q // 2 * 128
            OD[pl.ds(at + q % 2 * 64, 64), side : side + 128] = I2[q, u, :, 256:384].astype(F32)
        store_part(at, 128)
    for copy in stores:
        copy.wait()


def fused(nz, tokens, cotangent, seg_ids, norm_one, wq, wk, wv, wo, norm_two, w_gate, w_up, w_down):
    ff = w_gate.shape[1]
    ff_half = -(-ff // 512) * 256
    ff_cut = ff - ff_half
    vm = pltpu.VMEM
    zshapes = [(2, 256, 768)] * 2 + [(3, 256, 384), (2, 256, 256), (2, 256, 768)]
    zscratch, fshapes = [], []
    for units, rows, cols in zshapes:
        fshapes.append((nz, units, rows // nz, cols))
        zscratch += [
            vm((2, units, rows, cols), BF),
            vm((units, rows, cols), BF),
            vm((2, nz - 1, units, rows // nz, cols), BF),
            vm((nz, rows // nz, cols) if len(fshapes) in LATE else (rows // nz, cols), BF),
            vm(fshapes[-1], BF),
        ]
    scratch = [
        vm((512, D), BF), vm((512, D), BF), vm((D, 768), BF), vm((D, D), BF),
        vm((D, ff_half), BF), vm((D, ff_half), BF), vm((ff_half, D), BF), vm((1, D), F32), vm((1, D), F32),
        vm((512, D), BF), vm((512, 256), BF), vm((768, 256), BF), vm((768, 256), BF), vm((2, 256, 512), F32),
        vm((8, 256, 512), F32), vm((512, D), BF),
        vm((2, 512, D), BF), vm((3, 3, 128, D), BF),
        vm((512, D), BF), vm((512, D), F32), vm((128, D), F32), vm((512, ff_half), BF), vm((512, ff_half), BF),
        vm((512, ff_half), BF), vm((512, D), BF), vm((512, 256), BF), vm((512, ff_half), F32), vm((512, ff_half), F32), vm((3, 512, 256), BF),
        vm((768, 256), F32), vm((768, 256), F32), vm((512, 768), BF), vm((256, 512), BF), vm((256, 512), BF),
        vm((128, D), BF), vm((128, D), BF), vm((8, D), F32), vm((8, 8, 256), F32), vm((nz, 8, 256), F32), vm((8, 256), F32),
        *zscratch,
        pltpu.SemaphoreType.DMA((10,)), pltpu.SemaphoreType.DMA((258,)), pltpu.SemaphoreType.DMA((28,)),
    ]
    hbm, vmem = pl.BlockSpec(memory_space=pl.ANY), pl.BlockSpec(memory_space=pltpu.VMEM)
    sds = jax.ShapeDtypeStruct
    done = pl.pallas_call(
        functools.partial(layer_kernel, nz, ff_half, ff_cut),
        out_shape=(sds((512, 256), BF), sds((512, 256), BF), sds((8, 256), F32), *(sds(f, BF) for f in fshapes)),
        in_specs=[hbm, hbm, vmem, vmem, hbm, hbm, hbm, hbm, vmem, hbm, hbm, hbm],
        out_specs=(hbm, hbm, vmem, *(hbm for f in fshapes)),
        scratch_shapes=scratch,
        compiler_params=pltpu.CompilerParams(collective_id=0, has_side_effects=True, vmem_limit_bytes=62 << 20),
        name="layer",
    )(
        tokens, cotangent, seg_ids, norm_one[None], wq, wk, wv, wo, norm_two[None], w_gate, w_up, w_down,
    )
    out, gin, gains, *sums = done
    grads = (
        sds((512, 256), BF), sds((512, 256), F32), sds((1, 256), F32),
        sds((256, 512), F32), sds((256, 512), F32), sds((256, 512), F32), sds((512, 256), F32),
        sds((1, 256), F32), sds((256, ff), F32), sds((256, ff), F32), sds((ff, 256), F32),
    )
    res = pl.pallas_call(
        functools.partial(spread_kernel, nz, ff_half, ff_cut),
        out_shape=grads,
        in_specs=[hbm] * 7 + [vmem],
        out_specs=tuple(vmem if i in (2, 7) else hbm for i in range(11)),
        scratch_shapes=[vm(f, BF) for f in fshapes]
        + [vm((256, ff), F32), vm((256, ff), F32), vm((ff, 256), F32), vm((512, 256), F32), vm((3, 256, 512), F32)]
        + [vm((512, 256), BF), vm((512, 256), BF), vm((512, 256), F32), pltpu.SemaphoreType.DMA((7,)), pltpu.SemaphoreType.DMA((27,))],
        compiler_params=pltpu.CompilerParams(vmem_limit_bytes=63 << 20),
        name="spread",
    )(*sums, out, gin, gains)
    res = list(res)
    res[2], res[7] = res[2][0], res[7][0]
    return tuple(res)


def solution(mesh):
    in_specs = (
        P(("dp", "col"), "row"),
        P(("dp", "col"), "row"),
        P("dp", None),
        P("row"),
        P("row", "col"),
        P("row", "col"),
        P("row", "col"),
        P("col", "row"),
        P("row"),
        P("row", "col"),
        P("row", "col"),
        P("col", "row"),
    )
    out_specs = (
        P(("dp", "col"), "row"),
        P(("dp", "col"), "row"),
        P("row"),
        P("row", "col"),
        P("row", "col"),
        P("row", "col"),
        P("col", "row"),
        P("row"),
        P("row", "col"),
        P("row", "col"),
        P("col", "row"),
    )
    sizes = dict(mesh.shape)
    body = per_device
    if sizes["row"] == 4 and sizes["col"] == 2:
        body = functools.partial(fused, sizes["dp"])
    return jax.shard_map(
        body, mesh=mesh, in_specs=in_specs, out_specs=out_specs, check_vma=False
    )
```
